32 devices in a mesh: expert: 8 (over z, x), tensor: 4 (over y, core).
Axes of the slice: x: 2, y: 2, z: 4, core: 2. Of those that a mesh axis runs over, the one named last changes fastest.
Arguments:
- tokens: bfloat16 [4096, 2048], P('expert'), may hold values from -6 to 6
- attn_gain: bfloat16 [2048], P('expert'), may hold values from 0.5 to 1.5
- w_query: bfloat16 [2048, 2048], P('expert', 'tensor'), may hold values from -0.125 to 0.125
- w_key: bfloat16 [2048, 2048], P('expert', 'tensor'), may hold values from -0.125 to 0.125
- w_value: bfloat16 [2048, 2048], P('expert', 'tensor'), may hold values from -0.125 to 0.125
- w_out: bfloat16 [2048, 2048], P('tensor', 'expert'), may hold values from -1 to 1
- query_gain: bfloat16 [2048], P('expert'), may hold values from 0.5 to 1.5
- key_gain: bfloat16 [2048], P('expert'), may hold values from 0.5 to 1.5
- ffn_gain: bfloat16 [2048], P('expert'), may hold values from 0.5 to 1.5
- w_router: bfloat16 [2048, 16], P('expert'), may hold values from -0.0625 to 0.0625
- w_gate: bfloat16 [16, 2048, 1024], P('expert', None, 'tensor'), may hold values from -0.125 to 0.125
- w_up: bfloat16 [16, 2048, 1024], P('expert', None, 'tensor'), may hold values from -0.125 to 0.125
- w_down: bfloat16 [16, 1024, 2048], P('expert', 'tensor'), may hold values from -4 to 4
- doc_ids: int32 [4096], P('expert'), may hold values from 0 to 3, as said below
- routes: int32 [4096, 8], P('expert'), may hold values from 0 to 15, all different within a row; in each aligned block of 512 rows (0 to 511, 512 to 1023, ...) at most 320 rows name the same one
- deal: int32 [4096], replicated, may hold values from 0 to 4095, as said below
- out_grad: bfloat16 [4096, 2048], P('expert'), may hold values from -6 to 6
Outputs:
- output: bfloat16 [4096, 2048], P('expert')
- d_tokens: bfloat16 [4096, 2048], P('expert')
- d_attn_gain: float32 [2048], P('expert')
- d_w_query: float32 [2048, 2048], P('expert', 'tensor')
- d_w_key: float32 [2048, 2048], P('expert', 'tensor')
- d_w_value: float32 [2048, 2048], P('expert', 'tensor')
- d_w_out: float32 [2048, 2048], P('tensor', 'expert')
- d_query_gain: float32 [2048], P('expert')
- d_key_gain: float32 [2048], P('expert')
- d_ffn_gain: float32 [2048], P('expert')
- d_w_router: float32 [2048, 16], P('expert')
- d_w_gate: float32 [16, 2048, 1024], P('expert', None, 'tensor')
- d_w_up: float32 [16, 2048, 1024], P('expert', None, 'tensor')
- d_w_down: float32 [16, 1024, 2048], P('expert', 'tensor')
The draws below stay inside these ranges and needn't reach their ends.
Inputs may be any that keep to these rules, and one draw needn't show every extreme that they name: `doc_ids`: within each aligned block of 512 places the numbers never fall and start at 0; in some block a single document fills all 512 places, in another block all four numbers occur. `routes`: each row names 8 different experts. Within the 512 rows of one device no expert is named by more than 320 rows, a bound that some block reaches. `deal`: each token is named exactly once. Within every aligned block of 512 places, the places k * 64 to (k + 1) * 64 - 1 of the block name tokens of the k-th aligned block of 512 tokens.
All inputs are finite; a program needn't handle non-finite values.
Results may differ from the reference program's by a relative error of at most 0.019.
Values may be sent and summed in bfloat16 or wider, within the bound.
A program may use at most 320 MiB of HBM per device.

```python
import math
import jax
import jax.numpy as jnp
import numpy as np
from jax import lax

D = 2048
HEADS = 16
HEAD_DIM = 128
FF = 1024
TOP = 8
TOK_DEV = 512
EXPERTS = 16
TOKENS = 4096
CAP = 320


def draw_doc_ids(key, part):
    blocks = TOKENS // TOK_DEV
    cut_key, use_key, whole_key, full_key = jax.random.split(key, 4)
    cuts = jax.random.randint(cut_key, (blocks, 3), 1, TOK_DEV)
    used = jax.random.randint(use_key, (blocks, 3), 0, 2)
    whole_block = jax.random.randint(whole_key, (), 0, blocks)
    full_block = (whole_block + 1 + jax.random.randint(full_key, (), 0, blocks - 1)) % blocks
    block_ids = jnp.arange(blocks, dtype=jnp.int32)[:, None]
    keep = jnp.where(block_ids == full_block, 1, jnp.where(block_ids == whole_block, 0, used))
    where_rows = jnp.arange(TOK_DEV, dtype=jnp.int32)[None, None, :]
    passed = (where_rows >= cuts[:, :, None]).astype(jnp.int32) * keep[:, :, None]
    return jnp.sum(passed, axis=1).reshape(TOKENS).astype(jnp.int32)


def draw_deal(key, part):
    blocks = TOKENS // TOK_DEV
    share_rows = TOK_DEV // blocks
    block_keys = jax.random.split(jax.random.fold_in(key, 7), blocks)
    orders = jax.vmap(lambda one_key: jax.random.permutation(one_key, TOK_DEV))(block_keys).astype(jnp.int32)
    grid = orders.reshape(blocks, blocks, share_rows)
    sources = jnp.arange(blocks, dtype=jnp.int32)[:, None, None] * TOK_DEV + grid
    return jnp.transpose(sources, (1, 0, 2)).reshape(TOKENS).astype(jnp.int32)


def spiked(entries, rng, source, target, parts, factor):
    def block_of(position):
        return (jnp.arange(entries.shape[position]) // (entries.shape[position] // parts)).reshape((-1,) + (1,) * (entries.ndim - 1 - position))

    one_side = jax.random.permutation(rng, parts)[block_of(target)]
    second = (block_of(target) + parts // 2) % parts
    return jnp.where((block_of(source) == one_side) | (block_of(source) == second), factor * entries, entries)


def level_of(key, shape, pieces, smallest, high):
    loudness, own = 1.0, jax.random.fold_in(key, 6)
    for position, shards_of in pieces:
        heights = jnp.exp(jax.random.uniform(jax.random.fold_in(own, position), (shards_of,), jnp.float32, smallest / len(pieces), high / len(pieces)))
        loudness = loudness * jnp.repeat(heights, shape[position] // shards_of).reshape([-1 if axis == position else 1 for axis in range(len(shape))])
    return loudness


def deal_out(stream_key, own, number, rows, count, top, reach, skew):
    sequence = jax.random.permutation(stream_key, count)
    crowded, ordinary = load_shares(count, rows * top, reach, skew, True), load_shares(count, rows * top, reach, skew, False)
    places = jnp.arange(count)

    def named(sizes, offset_by):
        used = int((sizes > 0).sum())
        fixed = max(1, used // 4)
        moved = fixed + (places - fixed + offset_by * (used - fixed)) % max(1, count - fixed)
        return jnp.zeros((count,), jnp.int32).at[sequence[jnp.where(places < fixed, places, moved)]].set(jnp.asarray(sizes, jnp.int32))

    sizes = jnp.where(number % 4 == 0, named(crowded, number // 4), named(ordinary, number - number // 4 - 1))
    mixed = jax.random.permutation(jax.random.fold_in(own, 3), count)
    donor, taker = mixed[0:count // 2 * 2:2], mixed[1:count // 2 * 2:2]
    margin = jnp.minimum(sizes[donor] - 1, reach - sizes[taker]) // 2
    margin = jnp.where((donor == sequence[0]) | (taker == sequence[0]) | (sizes[taker] == 0), 0, jnp.maximum(margin, 0))
    moved = jax.random.randint(jax.random.fold_in(own, 4), (count // 2,), 0, 1 << 20) % (margin + 1)
    sizes = sizes.at[donor].add(-moved).at[taker].add(moved)
    items = jnp.searchsorted(jnp.cumsum(sizes), jnp.arange(rows * top), side="right").astype(jnp.int32)
    table = items.reshape(top, rows).T
    table = table[jax.random.permutation(jax.random.fold_in(own, 1), rows)]
    offset_by = jax.random.randint(jax.random.fold_in(own, 2), (rows, 1), 0, top)
    return jnp.take_along_axis(table, (jnp.arange(top)[None, :] + offset_by) % top, axis=1)


def load_shares(count, total, reach, lean, full):
    portions = [(1 << 20) // math.isqrt(rank ** lean) + 1 for rank in range(1, count + 1)]
    largest = reach if full else min(reach, max(-(-total // count), total * portions[0] // sum(portions)))
    least = 1 if total - largest >= count - 1 else 0
    given, surplus = [largest] + [least] * (count - 1), total - largest - least * (count - 1)
    while surplus > 0:
        movable = [i for i in range(1, count) if given[i] < largest] or [i for i in range(1, count) if given[i] < reach]
        pool, remaining = sum([portions[i] for i in movable]), surplus
        for i in movable:
            more = min(reach - given[i], max(1, remaining * portions[i] // pool), surplus)
            given[i] = given[i] + more
            surplus = surplus - more
    return np.array(given)


def noise(own_key, shape, spread, most, cuts=(), kind=jnp.bfloat16):
    array = jax.random.normal(own_key, shape, jnp.float32) * spread
    if len(cuts) > 0:
        array = level_of(own_key, shape, cuts, -0.22, 0.18) * array
    return jnp.clip(array, min=-most, max=most).astype(kind)


def gaussian_with(own_key, extent, scale, most, pieces, heavy, kind=jnp.bfloat16):
    array = scale * jax.random.normal(own_key, extent, jnp.float32)
    if pieces:
        array = array * level_of(own_key, extent, pieces, -0.22, 0.18)
    return jnp.clip(spiked(array, jax.random.fold_in(own_key, 3), *heavy), -most, most).astype(kind)


def setup_inputs(seed: int = 0) -> dict:
    keys = jax.random.split(jax.random.key(seed), 18)
    tokens = gaussian_with(keys[0], (TOKENS, D), 1.0, 6.0, ((0, 8),), (0, 1, 8, 2.0))
    attn_gain = jnp.clip(1.0 + 0.1 * jax.random.normal(keys[1], (D,), jnp.float32), 0.5, 1.5).astype(jnp.bfloat16)
    w_query = noise(keys[2], (D, D), D ** -0.5, 0.125, ((0, 8), (1, 4)))
    w_key = noise(keys[3], (D, D), D ** -0.5, 0.125, ((0, 8), (1, 4)))
    w_value = noise(keys[4], (D, D), D ** -0.5, 0.125, ((0, 8), (1, 4)))
    w_out = noise(keys[5], (D, D), (max(1, D // 64)) ** -0.5, 1.0, ((0, 4), (1, 8)))
    query_gain = jnp.clip(1.0 + 0.1 * jax.random.normal(keys[6], (D,), jnp.float32), 0.5, 1.5).astype(jnp.bfloat16)
    key_gain = jnp.clip(1.0 + 0.1 * jax.random.normal(keys[7], (D,), jnp.float32), 0.5, 1.5).astype(jnp.bfloat16)
    ffn_gain = jnp.clip(1.0 + 0.1 * jax.random.normal(keys[8], (D,), jnp.float32), 0.5, 1.5).astype(jnp.bfloat16)
    w_router = noise(keys[9], (D, EXPERTS), (4 * D) ** -0.5, 0.0625, ((0, 8),))
    w_gate = noise(keys[10], (EXPERTS, D, FF), D ** -0.5, 0.125, ((0, 8), (2, 4)))
    w_up = noise(keys[11], (EXPERTS, D, FF), D ** -0.5, 0.125, ((0, 8), (2, 4)))
    w_down = noise(keys[12], (EXPERTS, FF, D), (max(1, FF // 512)) ** -0.5, 4.0, ((0, 8), (1, 4)))
    doc_ids = draw_doc_ids(jax.random.fold_in(keys[17], 71), 0)
    routes_keys = jax.random.split(jax.random.fold_in(keys[14], 1), TOKENS // TOK_DEV)
    routes_turns = jax.random.permutation(jax.random.fold_in(keys[14], 3), TOKENS // TOK_DEV)
    routes = jax.vmap(lambda own, number: deal_out(jax.random.fold_in(keys[14], 2), own, number, TOK_DEV, EXPERTS, TOP, CAP, 1))(routes_keys, routes_turns).reshape((TOKENS, TOP))
    deal = draw_deal(jax.random.fold_in(keys[17], 71), 0)
    out_grad = gaussian_with(keys[16], (TOKENS, D), 1.0, 6.0, ((0, 8),), (0, 1, 8, 2.0))
    return {"tokens": tokens, "attn_gain": attn_gain, "w_query": w_query, "w_key": w_key, "w_value": w_value, "w_out": w_out, "query_gain": query_gain, "key_gain": key_gain, "ffn_gain": ffn_gain, "w_router": w_router, "w_gate": w_gate, "w_up": w_up, "w_down": w_down, "doc_ids": doc_ids, "routes": routes, "deal": deal, "out_grad": out_grad}


NORM_EPS = 1e-05
ROPE_BASE = 10000.0

@jax.custom_vjp
def low(v):
    return lax.optimization_barrier(v.astype(jnp.bfloat16)).astype(jnp.float32)

@jax.custom_vjp
def low_back(v):
    return v

def low_keep(v):
    return (low(v), None)

def low_pass(kept, grad):
    return (grad,)

def back_keep(v):
    return (v, None)

def back_low(kept, grad):
    return (low(grad),)
low.defvjp(low_keep, low_pass)
low_back.defvjp(back_keep, back_low)

def matmul(left, right):
    return jnp.dot(left, right, precision=lax.Precision.HIGHEST, preferred_element_type=jnp.float32)

def rms_scaled(values, gain):
    return values * lax.rsqrt(lax.optimization_barrier(jnp.mean(values * values, axis=-1, keepdims=True)) + NORM_EPS) * gain

def rope_tables(documents, head_size):
    row_count = documents.shape[0]
    positions = jnp.arange(row_count, dtype=jnp.int32)
    new_doc = jnp.concatenate([jnp.ones((1,), jnp.int32), (documents[1:] != documents[:-1]).astype(jnp.int32)])
    starts = lax.cummax(jnp.where(new_doc > 0, positions, 0), axis=0)
    places = (positions - starts).astype(jnp.float32)
    half_dim = head_size // 2
    frequency = jnp.exp(jnp.arange(half_dim, dtype=jnp.float32) * (-2.0 * math.log(ROPE_BASE) / head_size))
    angles = places[:, None] * frequency[None, :]
    return (jnp.cos(angles), jnp.sin(angles))

def rotate(values, cosines, sines):
    half_dim = values.shape[-1] // 2
    first_half = values[..., :half_dim]
    second_half = values[..., half_dim:]
    cos_rows = cosines[:, None, :]
    sin_rows = sines[:, None, :]
    return jnp.concatenate([first_half * cos_rows - second_half * sin_rows, second_half * cos_rows + first_half * sin_rows], axis=-1)

def attention_block(x_block, documents, attn_gain, w_query, w_key, w_value, w_out, query_gain, key_gain):
    row_count = x_block.shape[0]
    normed = low(rms_scaled(x_block, attn_gain))
    query_pre = low_back(matmul(normed, w_query))
    key_pre = low_back(matmul(normed, w_key))
    value_rows = low(low_back(matmul(normed, w_value))).reshape(row_count, HEADS, HEAD_DIM)
    cosines, sines = rope_tables(documents, HEAD_DIM)
    queries = low(rotate(rms_scaled(query_pre, query_gain).reshape(row_count, HEADS, HEAD_DIM), cosines, sines))
    key_rows = low(rotate(rms_scaled(key_pre, key_gain).reshape(row_count, HEADS, HEAD_DIM), cosines, sines))
    raw_scores = low_back(jnp.einsum('qhd,khd->hqk', queries, key_rows, precision=lax.Precision.HIGHEST))
    positions = jnp.arange(row_count, dtype=jnp.int32)
    allowed = (documents[:, None] == documents[None, :]) & (positions[None, :] <= positions[:, None])
    scores = jnp.where(allowed[None], raw_scores * (1.0 / math.sqrt(HEAD_DIM)), -1e+30)
    weights = low(jax.nn.softmax(scores, axis=-1))
    mixed = jnp.einsum('hqk,khd->qhd', weights, value_rows, precision=lax.Precision.HIGHEST)
    attended = low(low_back(mixed)).reshape(row_count, D)
    return x_block + low_back(matmul(attended, w_out))

def expert_rows(packed):
    rows_in, gate_w, up_w, down_w = packed
    gate_pre = low_back(matmul(rows_in, gate_w))
    up_pre = low_back(matmul(rows_in, up_w))
    hidden = low(jax.nn.silu(gate_pre) * up_pre)
    return low(low_back(matmul(hidden, down_w)))

def expert_tables(routes):
    blocks = TOKENS // TOK_DEV
    flat_routes = routes.reshape(blocks, TOK_DEV * TOP)
    expert_ids = jnp.arange(EXPERTS, dtype=jnp.int32)
    onehot = (flat_routes[:, :, None] == expert_ids[None, None, :]).astype(jnp.int32)
    slot_rank = lax.optimization_barrier(jnp.sum((jnp.cumsum(onehot, axis=1) - onehot) * onehot, axis=2))
    block_ids = jnp.arange(blocks, dtype=jnp.int32)[:, None]
    row_ids = (flat_routes * blocks + block_ids) * CAP + slot_rank
    token_ids = block_ids * TOK_DEV + jnp.arange(TOK_DEV * TOP, dtype=jnp.int32)[None, :] // TOP
    slot_token = jnp.full((EXPERTS * blocks * CAP,), TOKENS, jnp.int32).at[row_ids.reshape(-1)].set(token_ids.reshape(-1))
    return (slot_token, row_ids.reshape(TOKENS, TOP))

def reference(tokens, attn_gain, w_query, w_key, w_value, w_out, query_gain, key_gain, ffn_gain, w_router, w_gate, w_up, w_down, doc_ids, routes, deal, out_grad):
    blocks = TOKENS // TOK_DEV
    slot_token, pick_rows = expert_tables(routes)

    def forward(inputs, gain_a, weight_q, weight_k, weight_v, weight_o, gain_q, gain_k, gain_f, weight_r, weight_g, weight_u, weight_d):
        dealt = inputs[deal]

        def attend(carry, packed):
            x_block, documents = packed
            return (carry, attention_block(x_block, documents, gain_a, weight_q, weight_k, weight_v, weight_o, gain_q, gain_k))
        _, residual = lax.scan(jax.checkpoint(attend), jnp.zeros((), jnp.float32), (dealt.reshape(blocks, TOK_DEV, D), doc_ids.reshape(blocks, TOK_DEV)))
        residual = residual.reshape(TOKENS, D)
        ffn_in = low(rms_scaled(residual, gain_f))
        router_probs = jax.nn.softmax(low_back(matmul(ffn_in, weight_r)), axis=-1)
        gate_probs = jnp.take_along_axis(router_probs, routes, axis=1)
        padded = jnp.concatenate([ffn_in, jnp.zeros((1, D), jnp.float32)], axis=0)
        rows_in = low_back(padded[slot_token]).reshape(EXPERTS, blocks * CAP, D)
        expert_out = lax.map(jax.checkpoint(expert_rows), (rows_in, weight_g, weight_u, weight_d)).reshape(EXPERTS * blocks * CAP, D)
        mixed = residual
        for route_slot in range(TOP):
            mixed = mixed + gate_probs[:, route_slot:route_slot + 1] * expert_out[pick_rows[:, route_slot]]
        return jnp.zeros((TOKENS, D), jnp.float32).at[deal].set(mixed)
    floats = [arg.astype(jnp.float32) for arg in (tokens, attn_gain, w_query, w_key, w_value, w_out, query_gain, key_gain, ffn_gain, w_router, w_gate, w_up, w_down)]
    result, pullback = jax.vjp(forward, *floats)
    grads = pullback(out_grad.astype(jnp.float32))
    return (result.astype(jnp.bfloat16), grads[0].astype(jnp.bfloat16), grads[1], grads[2], grads[3], grads[4], grads[5], grads[6], grads[7], grads[8], grads[9], grads[10], grads[11], grads[12])
```

```python
import math

import jax
import jax.numpy as jnp
from jax import lax
from jax.sharding import PartitionSpec as P

HEAD_DIM = 128


NORM_EPS = 1e-05
ROPE_BASE = 10000.0


def rope_tables(documents, head_size):
    row_count = documents.shape[0]
    positions = jnp.arange(row_count, dtype=jnp.int32)
    new_doc = jnp.concatenate(
        [jnp.ones((1,), jnp.int32), (documents[1:] != documents[:-1]).astype(jnp.int32)]
    )
    starts = lax.cummax(jnp.where(new_doc > 0, positions, 0), axis=0)
    places = (positions - starts).astype(jnp.float32)
    half_dim = head_size // 2
    frequency = jnp.exp(
        jnp.arange(half_dim, dtype=jnp.float32) * (-2.0 * math.log(ROPE_BASE) / head_size)
    )
    angles = places[:, None] * frequency[None, :]
    return (jnp.cos(angles), jnp.sin(angles))


def rotate(values, cosines, sines):
    half_dim = values.shape[-1] // 2
    first_half = values[..., :half_dim]
    second_half = values[..., half_dim:]
    cos_rows = cosines[:, None, :]
    sin_rows = sines[:, None, :]
    return jnp.concatenate(
        [
            first_half * cos_rows - second_half * sin_rows,
            second_half * cos_rows + first_half * sin_rows,
        ],
        axis=-1,
    )


def unrotate(grads_in, cosines, sines):
    half_dim = grads_in.shape[-1] // 2
    first_half = grads_in[..., :half_dim]
    second_half = grads_in[..., half_dim:]
    cos_rows = cosines[:, None, :]
    sin_rows = sines[:, None, :]
    return jnp.concatenate(
        [
            first_half * cos_rows + second_half * sin_rows,
            second_half * cos_rows - first_half * sin_rows,
        ],
        axis=-1,
    )


def to_experts(rows):
    return lax.all_to_all(rows, "expert", split_axis=0, concat_axis=0, tiled=True)


def from_experts(rows):
    return lax.all_to_all(rows, "expert", split_axis=0, concat_axis=0, tiled=True)


def hidden_sums(terms):
    return lax.psum_scatter(terms, "tensor", scatter_dimension=3, tiled=True)


def routed_body(
    tokens,
    attn_gain,
    w_query,
    w_key,
    w_value,
    w_out,
    query_gain,
    key_gain,
    ffn_gain,
    w_router,
    w_gate,
    w_up,
    w_down,
    doc_ids,
    routes,
    deal,
    out_grad,
):
    row_count, width = tokens.shape
    tensor_parts = lax.axis_size("tensor")
    expert_parts = lax.axis_size("expert")
    column = lax.axis_index("tensor")
    device_idx = lax.axis_index("expert")
    quarter = width // tensor_parts
    share_rows = row_count // expert_parts
    deal_rows = lax.dynamic_slice_in_dim(
        deal.reshape(expert_parts, row_count), device_idx * share_rows, share_rows, 1
    )
    local_pick = deal_rows - device_idx * row_count
    dealt_tokens, dealt_grad = (
        lax.all_to_all(tokens[local_pick], "expert", split_axis=0, concat_axis=0, tiled=True),
        lax.all_to_all(out_grad[local_pick], "expert", split_axis=0, concat_axis=0, tiled=True),
    )
    dealt_tokens = dealt_tokens.reshape(row_count, width)
    dealt_grad = dealt_grad.reshape(row_count, width)
    gain_stack = jnp.stack([attn_gain, query_gain, key_gain, ffn_gain])
    wq_full, wk_full, wv_full, wo_full, router_full, gain_full = (
        lax.all_gather(w_query, "expert", axis=0, tiled=True),
        lax.all_gather(w_key, "expert", axis=0, tiled=True),
        lax.all_gather(w_value, "expert", axis=0, tiled=True),
        lax.all_gather(w_out, "expert", axis=1, tiled=True),
        lax.all_gather(w_router, "expert", axis=0, tiled=True),
        lax.all_gather(gain_stack, "expert", axis=1, tiled=True),
    )
    local_width = wq_full.shape[1]
    head_count = local_width // HEAD_DIM
    gain_attn = gain_full[0].astype(jnp.float32)
    gain_query = lax.dynamic_slice_in_dim(
        gain_full[1].astype(jnp.float32), column * local_width, local_width
    )
    gain_key = lax.dynamic_slice_in_dim(
        gain_full[2].astype(jnp.float32), column * local_width, local_width
    )
    gain_ffn = gain_full[3].astype(jnp.float32)
    scale = 1.0 / math.sqrt(HEAD_DIM)
    inputs = dealt_tokens.astype(jnp.float32)
    input_inv = lax.rsqrt(jnp.mean(inputs * inputs, axis=-1, keepdims=True) + NORM_EPS)
    input_hat = inputs * input_inv
    normed = (input_hat * gain_attn).astype(jnp.bfloat16)
    query_pre = jnp.dot(normed, wq_full, preferred_element_type=jnp.float32)
    key_pre = jnp.dot(normed, wk_full, preferred_element_type=jnp.float32)
    value_rows = (
        jnp.dot(normed, wv_full, preferred_element_type=jnp.float32)
        .astype(jnp.bfloat16)
        .reshape(row_count, head_count, HEAD_DIM)
    )
    query_sq, key_sq = lax.psum(
        (jnp.sum(query_pre * query_pre, axis=-1), jnp.sum(key_pre * key_pre, axis=-1)), "tensor"
    )
    query_inv = lax.rsqrt(query_sq / width + NORM_EPS)[:, None]
    key_inv = lax.rsqrt(key_sq / width + NORM_EPS)[:, None]
    query_hat = query_pre * query_inv
    key_hat = key_pre * key_inv
    cosines, sines = rope_tables(doc_ids, HEAD_DIM)
    query_rot = rotate(
        (query_hat * gain_query).reshape(row_count, head_count, HEAD_DIM), cosines, sines
    ).astype(jnp.bfloat16)
    key_rot = rotate(
        (key_hat * gain_key).reshape(row_count, head_count, HEAD_DIM), cosines, sines
    ).astype(jnp.bfloat16)
    positions = jnp.arange(row_count, dtype=jnp.int32)
    allowed = (doc_ids[:, None] == doc_ids[None, :]) & (positions[None, :] <= positions[:, None])

    def masked_scores():
        raw_scores = jnp.einsum(
            "qhd,khd->hqk", query_rot, key_rot, preferred_element_type=jnp.float32
        )
        return jnp.where(allowed[None], raw_scores * scale, -1e30)

    scores = masked_scores()
    top_score = jnp.max(scores, axis=-1, keepdims=True)
    log_total = top_score + jnp.log(jnp.sum(jnp.exp(scores - top_score), axis=-1, keepdims=True))
    weights = jnp.exp(scores - log_total).astype(jnp.bfloat16)
    attended = (
        jnp.einsum("hqk,khd->qhd", weights, value_rows, preferred_element_type=jnp.float32)
        .astype(jnp.bfloat16)
        .reshape(row_count, local_width)
    )
    branch = lax.psum(jnp.dot(attended, wo_full, preferred_element_type=jnp.float32), "tensor")
    residual = inputs + branch
    resid_inv = lax.rsqrt(jnp.mean(residual * residual, axis=-1, keepdims=True) + NORM_EPS)
    resid_hat = residual * resid_inv
    ffn_in = (resid_hat * gain_ffn).astype(jnp.bfloat16)
    logits = jnp.dot(ffn_in, router_full, preferred_element_type=jnp.float32)
    router_probs = jax.nn.softmax(logits, axis=-1)
    expert_count = router_full.shape[1]
    top_count = routes.shape[1]
    local_experts = expert_count // expert_parts
    capacity = tensor_parts * max(
        1,
        (row_count * top_count + expert_count * tensor_parts - 1) // (expert_count * tensor_parts),
        row_count * top_count * 5 // (4 * expert_count * tensor_parts),
    )
    expert_ids = jnp.arange(expert_count, dtype=jnp.int32)
    route_match = routes[:, :, None] == expert_ids[None, None, :]
    gate_probs = jnp.sum(jnp.where(route_match, router_probs[:, None, :], 0.0), axis=-1)
    flat_routes = routes.reshape(-1)
    onehot = (flat_routes[:, None] == expert_ids[None, :]).astype(jnp.int32)
    slot_rank = jnp.sum((jnp.cumsum(onehot, axis=0) - onehot) * onehot, axis=-1)
    row_ids = flat_routes * capacity + slot_rank
    token_ids = jnp.arange(row_count * top_count, dtype=jnp.int32) // top_count
    slot_token = (
        jnp.full((expert_count * capacity,), row_count, jnp.int32).at[row_ids].set(token_ids)
    )
    slot_gates = (
        jnp.zeros((expert_count * capacity,), jnp.float32).at[row_ids].set(gate_probs.reshape(-1))
    )
    pick_rows = row_ids.reshape(row_count, top_count)
    padded_in = jnp.concatenate([ffn_in, jnp.zeros((1, width), jnp.bfloat16)], axis=0)
    grad_full = dealt_grad.astype(jnp.float32)
    grad_padded = jnp.concatenate([grad_full, jnp.zeros((1, width), jnp.float32)], axis=0)
    received = to_experts(
        padded_in[slot_token].reshape(expert_parts, local_experts, capacity, width)
    )
    gate_pre = jnp.einsum("secd,edf->secf", received, w_gate, preferred_element_type=jnp.float32)
    up_pre = jnp.einsum("secd,edf->secf", received, w_up, preferred_element_type=jnp.float32)
    sigmoid_gate = jax.nn.sigmoid(gate_pre)
    silu_gate = gate_pre * sigmoid_gate
    hidden = (silu_gate * up_pre).astype(jnp.bfloat16)
    partial_out = jnp.einsum("secf,efd->secd", hidden, w_down, preferred_element_type=jnp.float32)
    own_columns = hidden_sums(partial_out).astype(jnp.bfloat16)
    returned = from_experts(own_columns).reshape(expert_count * capacity, quarter)
    chosen = returned[pick_rows].astype(jnp.float32)
    mix_own = jnp.sum(gate_probs[:, :, None] * chosen, axis=1)
    mix_part = lax.dynamic_update_slice_in_dim(
        jnp.zeros((row_count, width), jnp.float32), mix_own, column * quarter, 1
    )
    grad_own = lax.dynamic_slice_in_dim(grad_full, column * quarter, quarter, 1)
    gate_grad_part = jnp.sum(grad_own[:, None, :] * chosen, axis=-1)
    send_grad = (
        (grad_padded[slot_token] * slot_gates[:, None])
        .astype(jnp.bfloat16)
        .reshape(expert_parts, local_experts, capacity, width)
    )
    recv_grad = to_experts(send_grad)
    d_w_down = jnp.einsum("secf,secd->efd", hidden, recv_grad, preferred_element_type=jnp.float32)
    hidden_grad = jnp.einsum(
        "secd,efd->secf", recv_grad, w_down, preferred_element_type=jnp.float32
    )
    gate_grad_pre = (
        hidden_grad * up_pre * sigmoid_gate * (1.0 + gate_pre * (1.0 - sigmoid_gate))
    ).astype(jnp.bfloat16)
    up_grad_pre = (hidden_grad * silu_gate).astype(jnp.bfloat16)
    d_w_gate = jnp.einsum(
        "secd,secf->edf", received, gate_grad_pre, preferred_element_type=jnp.float32
    )
    d_w_up = jnp.einsum("secd,secf->edf", received, up_grad_pre, preferred_element_type=jnp.float32)
    joined_grad = jnp.concatenate([gate_grad_pre, up_grad_pre], axis=-1)
    joined_weight = jnp.concatenate([w_gate, w_up], axis=-1)
    row_terms = jnp.einsum(
        "secf,edf->secd", joined_grad, joined_weight, preferred_element_type=jnp.float32
    )
    row_own = hidden_sums(row_terms).astype(jnp.bfloat16)
    row_back = from_experts(row_own).reshape(expert_count * capacity, quarter)
    ffn_grad_own = jnp.sum(row_back[pick_rows].astype(jnp.float32), axis=1)
    placed = lax.dynamic_update_slice_in_dim(
        jnp.zeros((row_count, width), jnp.float32), ffn_grad_own, column * quarter, 1
    )
    ffn_grad_rows, gate_grad, mix_total = lax.psum((placed, gate_grad_part, mix_part), "tensor")
    output = (residual + mix_total).astype(jnp.bfloat16)
    prob_grad = jnp.sum(jnp.where(route_match, gate_grad[:, :, None], 0.0), axis=1)
    logit_grad = (
        router_probs * (prob_grad - jnp.sum(router_probs * prob_grad, axis=-1, keepdims=True))
    ).astype(jnp.bfloat16)
    d_router = jnp.einsum("rd,re->de", ffn_in, logit_grad, preferred_element_type=jnp.float32)
    ffn_grad = ffn_grad_rows + jnp.einsum(
        "re,de->rd", logit_grad, router_full, preferred_element_type=jnp.float32
    )
    d_ffn_gain = jnp.sum(ffn_grad * resid_hat, axis=0)
    scaled_ffn = ffn_grad * gain_ffn
    resid_grad = grad_full + resid_inv * (
        scaled_ffn - resid_hat * jnp.mean(scaled_ffn * resid_hat, axis=-1, keepdims=True)
    )
    branch_grad = resid_grad.astype(jnp.bfloat16)
    d_wo = jnp.einsum("rk,rd->kd", attended, branch_grad, preferred_element_type=jnp.float32)
    attended_grad = (
        jnp.einsum("rd,kd->rk", branch_grad, wo_full, preferred_element_type=jnp.float32)
        .astype(jnp.bfloat16)
        .reshape(row_count, head_count, HEAD_DIM)
    )
    probs_again = jnp.exp(masked_scores() - log_total)
    prob_grads = jnp.einsum(
        "qhd,khd->hqk", attended_grad, value_rows, preferred_element_type=jnp.float32
    )
    value_grad = (
        jnp.einsum(
            "hqk,qhd->khd",
            probs_again.astype(jnp.bfloat16),
            attended_grad,
            preferred_element_type=jnp.float32,
        )
        .astype(jnp.bfloat16)
        .reshape(row_count, local_width)
    )
    row_delta = jnp.sum(probs_again * prob_grads, axis=-1, keepdims=True)
    score_grad = (probs_again * (prob_grads - row_delta) * scale).astype(jnp.bfloat16)
    query_rot_grad = jnp.einsum(
        "hqk,khd->qhd", score_grad, key_rot, preferred_element_type=jnp.float32
    )
    key_rot_grad = jnp.einsum(
        "hqk,qhd->khd", score_grad, query_rot, preferred_element_type=jnp.float32
    )
    query_norm_grad = unrotate(query_rot_grad, cosines, sines).reshape(row_count, local_width)
    key_norm_grad = unrotate(key_rot_grad, cosines, sines).reshape(row_count, local_width)
    query_hat_grad = query_norm_grad * gain_query
    key_hat_grad = key_norm_grad * gain_key
    gain_pieces = jnp.stack(
        [jnp.sum(query_norm_grad * query_hat, axis=0), jnp.sum(key_norm_grad * key_hat, axis=0)]
    )
    gain_parts = lax.dynamic_update_slice_in_dim(
        jnp.zeros((2, width), jnp.float32), gain_pieces, column * local_width, 1
    )
    query_dot, key_dot, qk_gains = lax.psum(
        (
            jnp.sum(query_hat_grad * query_hat, axis=-1),
            jnp.sum(key_hat_grad * key_hat, axis=-1),
            gain_parts,
        ),
        "tensor",
    )
    query_grad = (query_inv * (query_hat_grad - query_hat * (query_dot / width)[:, None])).astype(
        jnp.bfloat16
    )
    key_grad = (key_inv * (key_hat_grad - key_hat * (key_dot / width)[:, None])).astype(
        jnp.bfloat16
    )
    d_wq = jnp.einsum("rd,rk->dk", normed, query_grad, preferred_element_type=jnp.float32)
    d_wk = jnp.einsum("rd,rk->dk", normed, key_grad, preferred_element_type=jnp.float32)
    d_wv = jnp.einsum("rd,rk->dk", normed, value_grad, preferred_element_type=jnp.float32)
    input_terms = jnp.einsum("rk,dk->rd", query_grad, wq_full, preferred_element_type=jnp.float32)
    input_terms = input_terms + jnp.einsum(
        "rk,dk->rd", key_grad, wk_full, preferred_element_type=jnp.float32
    )
    input_terms = input_terms + jnp.einsum(
        "rk,dk->rd", value_grad, wv_full, preferred_element_type=jnp.float32
    )
    normed_grad = lax.psum(input_terms, "tensor")
    d_attn_part = jnp.sum(normed_grad * input_hat, axis=0)
    scaled_attn = normed_grad * gain_attn
    input_grad = resid_grad + input_inv * (
        scaled_attn - input_hat * jnp.mean(scaled_attn * input_hat, axis=-1, keepdims=True)
    )
    dealt_dtokens = input_grad.astype(jnp.bfloat16)
    gain_grads = jnp.stack([d_attn_part, qk_gains[0], qk_gains[1], d_ffn_gain])
    sum_wq, sum_wk, sum_wv, sum_wo, sum_router, sum_gains = (
        lax.psum_scatter(d_wq, "expert", scatter_dimension=0, tiled=True),
        lax.psum_scatter(d_wk, "expert", scatter_dimension=0, tiled=True),
        lax.psum_scatter(d_wv, "expert", scatter_dimension=0, tiled=True),
        lax.psum_scatter(d_wo, "expert", scatter_dimension=1, tiled=True),
        lax.psum_scatter(d_router, "expert", scatter_dimension=0, tiled=True),
        lax.psum_scatter(gain_grads, "expert", scatter_dimension=1, tiled=True),
    )
    back_out, back_dtok = (
        lax.all_to_all(
            output.reshape(expert_parts, share_rows, width),
            "expert",
            split_axis=0,
            concat_axis=0,
            tiled=True,
        ),
        lax.all_to_all(
            dealt_dtokens.reshape(expert_parts, share_rows, width),
            "expert",
            split_axis=0,
            concat_axis=0,
            tiled=True,
        ),
    )
    flat_pick = local_pick.reshape(-1)
    output_rows = (
        jnp.zeros((row_count, width), jnp.bfloat16)
        .at[flat_pick]
        .set(back_out.reshape(row_count, width))
    )
    d_tokens = (
        jnp.zeros((row_count, width), jnp.bfloat16)
        .at[flat_pick]
        .set(back_dtok.reshape(row_count, width))
    )
    return (
        output_rows,
        d_tokens,
        sum_gains[0],
        sum_wq,
        sum_wk,
        sum_wv,
        sum_wo,
        sum_gains[1],
        sum_gains[2],
        sum_gains[3],
        sum_router,
        d_w_gate,
        d_w_up,
        d_w_down,
    )


BOTH = ("expert", "tensor")


def gather_all(rows):
    return lax.all_gather(rows, BOTH, axis=0, tiled=True)


def sum_all(rows):
    return lax.psum_scatter(rows, BOTH, scatter_dimension=0, tiled=True)


def dot32(left, right, dims):
    return lax.dot_general(left, right, (dims, ((), ())), preferred_element_type=jnp.float32)


NN = ((1,), (0,))
NT = ((1,), (1,))
TN = ((0,), (0,))


def rms_inv(values):
    return lax.rsqrt(jnp.mean(values * values, axis=-1, keepdims=True) + NORM_EPS)


def dense_body(
    tokens,
    attn_gain,
    w_query,
    w_key,
    w_value,
    w_out,
    query_gain,
    key_gain,
    ffn_gain,
    w_router,
    w_gate,
    w_up,
    w_down,
    doc_ids,
    routes,
    deal,
    out_grad,
):
    rows, width = tokens.shape
    parts = lax.axis_size("tensor")
    blocks = lax.axis_size("expert")
    column = lax.axis_index("tensor")
    block = lax.axis_index("expert")
    own = rows // parts
    share = rows // blocks
    piece = share // parts
    bf16, f32 = jnp.bfloat16, jnp.float32

    def reorder(per_place):
        grid = per_place.reshape((blocks, parts, piece) + per_place.shape[1:])
        return jnp.swapaxes(grid, 0, 1).reshape(per_place.shape)

    qkv_own = jnp.concatenate([w_query, w_key, w_value], axis=1)
    qkv_full = lax.all_gather(qkv_own, "expert", axis=0, tiled=True)
    local_width = w_query.shape[1]
    head_count = local_width // HEAD_DIM
    gain_stack = jnp.stack([attn_gain, query_gain, key_gain, ffn_gain])
    gain_full = lax.all_gather(gain_stack, "expert", axis=1, tiled=True).astype(f32)
    router_full = lax.all_gather(w_router, "expert", axis=0, tiled=True)
    gain_attn, gain_ffn = gain_full[0], gain_full[3]
    gain_query = lax.dynamic_slice_in_dim(gain_full[1], column * local_width, local_width)
    gain_key = lax.dynamic_slice_in_dim(gain_full[2], column * local_width, local_width)

    deal_grid = deal.reshape(blocks, blocks, parts, piece)
    picks = lax.dynamic_slice(deal_grid, (0, block, column, 0), (blocks, 1, 1, piece)).reshape(-1)
    picks = picks - block * rows
    sent = jnp.stack(
        [
            tokens[picks].reshape(blocks, piece, width),
            out_grad[picks].reshape(blocks, piece, width),
        ],
        axis=1,
    )
    dealt = lax.all_to_all(sent, "expert", split_axis=0, concat_axis=0, tiled=True)
    own_low = dealt[:, 0].reshape(own, width)
    own_grad_low = dealt[:, 1].reshape(own, width)
    inputs = lax.all_gather(own_low, "tensor", axis=0, tiled=True).astype(f32)
    out_full = lax.all_gather(w_out, "expert", axis=0)
    grads_all = gather_all(own_grad_low)
    own_in = own_low.astype(f32)
    own_grad = own_grad_low.astype(f32)

    scale = 1.0 / math.sqrt(HEAD_DIM)
    normed = (inputs * rms_inv(inputs) * gain_attn).astype(bf16)
    qkv = dot32(normed, qkv_full, NN)
    query_pre = qkv[:, :local_width]
    key_pre = qkv[:, local_width : 2 * local_width]
    value_rows = qkv[:, 2 * local_width :].astype(bf16).reshape(rows, head_count, HEAD_DIM)
    squares = lax.psum(
        jnp.stack([jnp.sum(query_pre * query_pre, axis=-1), jnp.sum(key_pre * key_pre, axis=-1)]),
        "tensor",
    )
    query_inv = lax.rsqrt(squares[0] / width + NORM_EPS)[:, None]
    key_inv = lax.rsqrt(squares[1] / width + NORM_EPS)[:, None]
    query_hat = query_pre * query_inv
    key_hat = key_pre * key_inv
    cosines, sines = rope_tables(doc_ids, HEAD_DIM)
    cosines, sines = reorder(cosines), reorder(sines)
    query_rot = rotate(
        (query_hat * gain_query).reshape(rows, head_count, HEAD_DIM), cosines, sines
    ).astype(bf16)
    key_rot = rotate(
        (key_hat * gain_key).reshape(rows, head_count, HEAD_DIM), cosines, sines
    ).astype(bf16)
    positions = reorder(jnp.arange(rows, dtype=jnp.int32))
    documents = reorder(doc_ids)
    allowed = (documents[:, None] == documents[None, :]) & (positions[None, :] <= positions[:, None])

    def masked_scores():
        raw_scores = jnp.einsum("qhd,khd->hqk", query_rot, key_rot, preferred_element_type=f32)
        return jnp.where(allowed[None], raw_scores * scale, -1e30)

    scores = masked_scores()
    top_score = jnp.max(scores, axis=-1, keepdims=True)
    log_total = top_score + jnp.log(jnp.sum(jnp.exp(scores - top_score), axis=-1, keepdims=True))
    weights = jnp.exp(scores - log_total).astype(bf16)
    attended = (
        jnp.einsum("hqk,khd->qhd", weights, value_rows, preferred_element_type=f32)
        .astype(bf16)
        .reshape(rows, local_width)
    )
    branch = jnp.einsum("rk,ekd->red", attended, out_full, preferred_element_type=f32)
    branch = branch.astype(bf16).reshape(rows, width)
    branch_own = lax.psum_scatter(branch, "tensor", scatter_dimension=0, tiled=True)

    residual = own_in + branch_own.astype(f32)
    resid_inv = rms_inv(residual)
    resid_hat = residual * resid_inv
    ffn_in = (resid_hat * gain_ffn).astype(bf16)
    logits = dot32(ffn_in, router_full, NN)
    router_probs = jax.nn.softmax(logits, axis=-1)
    expert_count = router_full.shape[1]
    local_experts = w_gate.shape[0]
    hidden_width = w_gate.shape[2]
    own_routes = lax.dynamic_slice(
        routes.reshape(blocks, parts, piece, -1),
        (0, column, 0, 0),
        (blocks, 1, piece, routes.shape[1]),
    ).reshape(own, -1)
    expert_ids = jnp.arange(expert_count, dtype=jnp.int32)
    routed = jnp.any(own_routes[:, :, None] == expert_ids[None, None, :], axis=1)
    gates_own = jnp.where(routed, router_probs, 0.0)

    rows_all = gather_all(ffn_in)
    gates_all = gather_all(gates_own)
    gates = lax.dynamic_slice_in_dim(gates_all, block * local_experts, local_experts, 1)

    joined_weight = jnp.concatenate(
        [w_gate[i] for i in range(local_experts)] + [w_up[i] for i in range(local_experts)], axis=1
    )
    down_weight = w_down.reshape(local_experts * hidden_width, width)
    joined = dot32(rows_all, joined_weight, NN)
    half = local_experts * hidden_width
    gate_pre, up_pre = joined[:, :half], joined[:, half:]
    wide_gates = jnp.concatenate(
        [
            jnp.broadcast_to(gates[:, i : i + 1], (gates.shape[0], hidden_width))
            for i in range(local_experts)
        ],
        axis=1,
    )
    sigmoid_gate = jax.nn.sigmoid(gate_pre)
    silu_gate = gate_pre * sigmoid_gate
    hidden = (silu_gate * up_pre).astype(bf16)
    gated_hidden = (hidden.astype(f32) * wide_gates).astype(bf16)
    mixed = dot32(gated_hidden, down_weight, NN).astype(bf16)
    mix_own = sum_all(mixed)
    output_own = (residual + mix_own.astype(f32)).astype(bf16)

    hidden_raw = dot32(grads_all, down_weight, NT)
    gate_grads = jnp.sum(
        (hidden.astype(f32) * hidden_raw).reshape(-1, local_experts, hidden_width), axis=-1
    )
    d_w_down = dot32(gated_hidden, grads_all, TN).reshape(w_down.shape)
    hidden_grad = hidden_raw * wide_gates
    gate_grad_pre = (
        hidden_grad * up_pre * sigmoid_gate * (1.0 + gate_pre * (1.0 - sigmoid_gate))
    ).astype(bf16)
    up_grad_pre = (hidden_grad * silu_gate).astype(bf16)
    joined_grad = jnp.concatenate([gate_grad_pre, up_grad_pre], axis=1)
    row_terms = dot32(joined_grad, joined_weight, NT).astype(bf16)
    row_own = sum_all(row_terms)
    placed = lax.dynamic_update_slice_in_dim(
        jnp.zeros((gate_grads.shape[0], expert_count), f32), gate_grads, block * local_experts, 1
    )
    gate_grad_own = sum_all(placed)
    d_w_gate = jnp.stack(
        [
            dot32(rows_all, gate_grad_pre[:, i * hidden_width : (i + 1) * hidden_width], TN)
            for i in range(local_experts)
        ]
    )
    d_w_up = jnp.stack(
        [
            dot32(rows_all, up_grad_pre[:, i * hidden_width : (i + 1) * hidden_width], TN)
            for i in range(local_experts)
        ]
    )

    prob_grad = jnp.where(routed, gate_grad_own, 0.0)
    logit_grad = (
        router_probs * (prob_grad - jnp.sum(router_probs * prob_grad, axis=-1, keepdims=True))
    ).astype(bf16)
    d_router = dot32(ffn_in, logit_grad, TN)
    ffn_grad = row_own.astype(f32) + dot32(logit_grad, router_full, NT)
    d_ffn_gain = jnp.sum(ffn_grad * resid_hat, axis=0)
    scaled_ffn = ffn_grad * gain_ffn
    resid_grad = own_grad + resid_inv * (
        scaled_ffn - resid_hat * jnp.mean(scaled_ffn * resid_hat, axis=-1, keepdims=True)
    )
    branch_grad = lax.all_gather(resid_grad.astype(bf16), "tensor", axis=0, tiled=True)

    branch_cols = branch_grad.reshape(rows, blocks, width // blocks)
    d_wo = jnp.einsum("rk,red->ekd", attended, branch_cols, preferred_element_type=f32).astype(bf16)
    sum_wo = lax.psum_scatter(d_wo, "expert", scatter_dimension=0, tiled=False)
    attended_grad = (
        jnp.einsum("red,ekd->rk", branch_cols, out_full, preferred_element_type=f32)
        .astype(bf16)
        .reshape(rows, head_count, HEAD_DIM)
    )
    probs_again = jnp.exp(masked_scores() - log_total)
    prob_grads = jnp.einsum("qhd,khd->hqk", attended_grad, value_rows, preferred_element_type=f32)
    value_grad = (
        jnp.einsum(
            "hqk,qhd->khd", probs_again.astype(bf16), attended_grad, preferred_element_type=f32
        )
        .astype(bf16)
        .reshape(rows, local_width)
    )
    row_delta = jnp.sum(probs_again * prob_grads, axis=-1, keepdims=True)
    score_grad = (probs_again * (prob_grads - row_delta) * scale).astype(bf16)
    query_rot_grad = jnp.einsum("hqk,khd->qhd", score_grad, key_rot, preferred_element_type=f32)
    key_rot_grad = jnp.einsum("hqk,qhd->khd", score_grad, query_rot, preferred_element_type=f32)
    query_norm_grad = unrotate(query_rot_grad, cosines, sines).reshape(rows, local_width)
    key_norm_grad = unrotate(key_rot_grad, cosines, sines).reshape(rows, local_width)
    query_hat_grad = query_norm_grad * gain_query
    key_hat_grad = key_norm_grad * gain_key
    d_query_gain = jnp.sum(query_norm_grad * query_hat, axis=0)
    d_key_gain = jnp.sum(key_norm_grad * key_hat, axis=0)
    dots = lax.psum(
        jnp.stack(
            [
                jnp.sum(query_hat_grad * query_hat, axis=-1),
                jnp.sum(key_hat_grad * key_hat, axis=-1),
            ]
        ),
        "tensor",
    )
    query_grad = (query_inv * (query_hat_grad - query_hat * (dots[0] / width)[:, None])).astype(
        bf16
    )
    key_grad = (key_inv * (key_hat_grad - key_hat * (dots[1] / width)[:, None])).astype(bf16)
    qkv_grad = jnp.concatenate([query_grad, key_grad, value_grad], axis=1)
    input_terms = dot32(qkv_grad, qkv_full, NT).astype(bf16)
    normed_grad = lax.psum_scatter(
        input_terms, "tensor", scatter_dimension=0, tiled=True
    ).astype(f32)
    d_qkv = dot32(normed, qkv_grad, TN).astype(bf16)
    sum_qkv = lax.psum_scatter(d_qkv, "expert", scatter_dimension=0, tiled=True).astype(f32)

    own_inv = rms_inv(own_in)
    own_hat = own_in * own_inv
    d_attn_gain = jnp.sum(normed_grad * own_hat, axis=0)
    scaled_attn = normed_grad * gain_attn
    input_grad = resid_grad + own_inv * (
        scaled_attn - own_hat * jnp.mean(scaled_attn * own_hat, axis=-1, keepdims=True)
    )

    def widen(slots):
        return lax.dynamic_update_slice_in_dim(
            jnp.zeros((width,), f32), slots, column * local_width, 0
        )

    small = jnp.concatenate(
        [
            d_router.T,
            jnp.stack([d_attn_gain, widen(d_query_gain), widen(d_key_gain), d_ffn_gain]),
        ]
    )
    small = lax.psum_scatter(small, "expert", scatter_dimension=1, tiled=True)
    small = lax.psum(small, "tensor")
    sum_router = small[:expert_count].T
    sum_gains = small[expert_count:]

    def back(own_rows):
        moved = lax.all_to_all(
            own_rows.reshape(blocks, piece, width), "expert", split_axis=0, concat_axis=0, tiled=True
        )
        return lax.all_gather(moved.reshape(own, width), "tensor", axis=0, tiled=True)

    came = lax.dynamic_slice(deal_grid, (0, block, 0, 0), (blocks, 1, parts, piece))
    came = jnp.swapaxes(came.reshape(blocks, parts, piece), 0, 1).reshape(-1) - block * rows
    chooser = (jnp.arange(rows, dtype=jnp.int32)[:, None] == came[None, :]).astype(bf16)
    output = dot32(chooser, back(output_own), NN).astype(bf16)
    d_tokens = dot32(chooser, back(input_grad.astype(bf16)), NN).astype(bf16)
    return (
        output,
        d_tokens,
        sum_gains[0],
        sum_qkv[:, :local_width],
        sum_qkv[:, local_width : 2 * local_width],
        sum_qkv[:, 2 * local_width :],
        sum_wo.astype(f32),
        sum_gains[1],
        sum_gains[2],
        sum_gains[3],
        sum_router,
        d_w_gate,
        d_w_up,
        d_w_down,
    )


def pick_body(*args):
    routes, experts = args[14], args[9].shape[1]
    body = dense_body if experts <= 2 * routes.shape[1] else routed_body
    return body(*args)


def solution(mesh):
    in_specs = (
        P("expert", None),
        P("expert"),
        P("expert", "tensor"),
        P("expert", "tensor"),
        P("expert", "tensor"),
        P("tensor", "expert"),
        P("expert"),
        P("expert"),
        P("expert"),
        P("expert", None),
        P("expert", None, "tensor"),
        P("expert", None, "tensor"),
        P("expert", "tensor", None),
        P("expert"),
        P("expert", None),
        P(),
        P("expert", None),
    )
    out_specs = (
        P("expert", None),
        P("expert", None),
        P("expert"),
        P("expert", "tensor"),
        P("expert", "tensor"),
        P("expert", "tensor"),
        P("tensor", "expert"),
        P("expert"),
        P("expert"),
        P("expert"),
        P("expert", None),
        P("expert", None, "tensor"),
        P("expert", None, "tensor"),
        P("expert", "tensor", None),
    )
    return jax.shard_map(pick_body, mesh=mesh, in_specs=in_specs, out_specs=out_specs, check_vma=False)
```

```python
import functools
import math

import jax
import jax.numpy as jnp
from jax import lax
from jax.experimental import pallas as pl
from jax.experimental.pallas import tpu as pltpu
from jax.sharding import PartitionSpec as P

HEAD_DIM = 128


NORM_EPS = 1e-05
ROPE_BASE = 10000.0


def rope_tables(documents, head_size):
    row_count = documents.shape[0]
    positions = jnp.arange(row_count, dtype=jnp.int32)
    new_doc = jnp.concatenate(
        [jnp.ones((1,), jnp.int32), (documents[1:] != documents[:-1]).astype(jnp.int32)]
    )
    starts = lax.cummax(jnp.where(new_doc > 0, positions, 0), axis=0)
    places = (positions - starts).astype(jnp.float32)
    half_dim = head_size // 2
    frequency = jnp.exp(
        jnp.arange(half_dim, dtype=jnp.float32) * (-2.0 * math.log(ROPE_BASE) / head_size)
    )
    angles = places[:, None] * frequency[None, :]
    return (jnp.cos(angles), jnp.sin(angles))


def rotate(values, cosines, sines):
    half_dim = values.shape[-1] // 2
    first_half = values[..., :half_dim]
    second_half = values[..., half_dim:]
    cos_rows = cosines[:, None, :]
    sin_rows = sines[:, None, :]
    return jnp.concatenate(
        [
            first_half * cos_rows - second_half * sin_rows,
            second_half * cos_rows + first_half * sin_rows,
        ],
        axis=-1,
    )


def unrotate(grads_in, cosines, sines):
    half_dim = grads_in.shape[-1] // 2
    first_half = grads_in[..., :half_dim]
    second_half = grads_in[..., half_dim:]
    cos_rows = cosines[:, None, :]
    sin_rows = sines[:, None, :]
    return jnp.concatenate(
        [
            first_half * cos_rows + second_half * sin_rows,
            second_half * cos_rows - first_half * sin_rows,
        ],
        axis=-1,
    )


def to_experts(rows):
    return lax.all_to_all(rows, "expert", split_axis=0, concat_axis=0, tiled=True)


def from_experts(rows):
    return lax.all_to_all(rows, "expert", split_axis=0, concat_axis=0, tiled=True)


def hidden_sums(terms):
    return lax.psum_scatter(terms, "tensor", scatter_dimension=3, tiled=True)


def routed_body(
    tokens,
    attn_gain,
    w_query,
    w_key,
    w_value,
    w_out,
    query_gain,
    key_gain,
    ffn_gain,
    w_router,
    w_gate,
    w_up,
    w_down,
    doc_ids,
    routes,
    deal,
    out_grad,
):
    row_count, width = tokens.shape
    tensor_parts = lax.axis_size("tensor")
    expert_parts = lax.axis_size("expert")
    column = lax.axis_index("tensor")
    device_idx = lax.axis_index("expert")
    quarter = width // tensor_parts
    share_rows = row_count // expert_parts
    deal_rows = lax.dynamic_slice_in_dim(
        deal.reshape(expert_parts, row_count), device_idx * share_rows, share_rows, 1
    )
    local_pick = deal_rows - device_idx * row_count
    dealt_tokens, dealt_grad = (
        lax.all_to_all(tokens[local_pick], "expert", split_axis=0, concat_axis=0, tiled=True),
        lax.all_to_all(out_grad[local_pick], "expert", split_axis=0, concat_axis=0, tiled=True),
    )
    dealt_tokens = dealt_tokens.reshape(row_count, width)
    dealt_grad = dealt_grad.reshape(row_count, width)
    gain_stack = jnp.stack([attn_gain, query_gain, key_gain, ffn_gain])
    wq_full, wk_full, wv_full, wo_full, router_full, gain_full = (
        lax.all_gather(w_query, "expert", axis=0, tiled=True),
        lax.all_gather(w_key, "expert", axis=0, tiled=True),
        lax.all_gather(w_value, "expert", axis=0, tiled=True),
        lax.all_gather(w_out, "expert", axis=1, tiled=True),
        lax.all_gather(w_router, "expert", axis=0, tiled=True),
        lax.all_gather(gain_stack, "expert", axis=1, tiled=True),
    )
    local_width = wq_full.shape[1]
    head_count = local_width // HEAD_DIM
    gain_attn = gain_full[0].astype(jnp.float32)
    gain_query = lax.dynamic_slice_in_dim(
        gain_full[1].astype(jnp.float32), column * local_width, local_width
    )
    gain_key = lax.dynamic_slice_in_dim(
        gain_full[2].astype(jnp.float32), column * local_width, local_width
    )
    gain_ffn = gain_full[3].astype(jnp.float32)
    scale = 1.0 / math.sqrt(HEAD_DIM)
    inputs = dealt_tokens.astype(jnp.float32)
    input_inv = lax.rsqrt(jnp.mean(inputs * inputs, axis=-1, keepdims=True) + NORM_EPS)
    input_hat = inputs * input_inv
    normed = (input_hat * gain_attn).astype(jnp.bfloat16)
    query_pre = jnp.dot(normed, wq_full, preferred_element_type=jnp.float32)
    key_pre = jnp.dot(normed, wk_full, preferred_element_type=jnp.float32)
    value_rows = (
        jnp.dot(normed, wv_full, preferred_element_type=jnp.float32)
        .astype(jnp.bfloat16)
        .reshape(row_count, head_count, HEAD_DIM)
    )
    query_sq, key_sq = lax.psum(
        (jnp.sum(query_pre * query_pre, axis=-1), jnp.sum(key_pre * key_pre, axis=-1)), "tensor"
    )
    query_inv = lax.rsqrt(query_sq / width + NORM_EPS)[:, None]
    key_inv = lax.rsqrt(key_sq / width + NORM_EPS)[:, None]
    query_hat = query_pre * query_inv
    key_hat = key_pre * key_inv
    cosines, sines = rope_tables(doc_ids, HEAD_DIM)
    query_rot = rotate(
        (query_hat * gain_query).reshape(row_count, head_count, HEAD_DIM), cosines, sines
    ).astype(jnp.bfloat16)
    key_rot = rotate(
        (key_hat * gain_key).reshape(row_count, head_count, HEAD_DIM), cosines, sines
    ).astype(jnp.bfloat16)
    positions = jnp.arange(row_count, dtype=jnp.int32)
    allowed = (doc_ids[:, None] == doc_ids[None, :]) & (positions[None, :] <= positions[:, None])

    def masked_scores():
        raw_scores = jnp.einsum(
            "qhd,khd->hqk", query_rot, key_rot, preferred_element_type=jnp.float32
        )
        return jnp.where(allowed[None], raw_scores * scale, -1e30)

    scores = masked_scores()
    top_score = jnp.max(scores, axis=-1, keepdims=True)
    log_total = top_score + jnp.log(jnp.sum(jnp.exp(scores - top_score), axis=-1, keepdims=True))
    weights = jnp.exp(scores - log_total).astype(jnp.bfloat16)
    attended = (
        jnp.einsum("hqk,khd->qhd", weights, value_rows, preferred_element_type=jnp.float32)
        .astype(jnp.bfloat16)
        .reshape(row_count, local_width)
    )
    branch = lax.psum(jnp.dot(attended, wo_full, preferred_element_type=jnp.float32), "tensor")
    residual = inputs + branch
    resid_inv = lax.rsqrt(jnp.mean(residual * residual, axis=-1, keepdims=True) + NORM_EPS)
    resid_hat = residual * resid_inv
    ffn_in = (resid_hat * gain_ffn).astype(jnp.bfloat16)
    logits = jnp.dot(ffn_in, router_full, preferred_element_type=jnp.float32)
    router_probs = jax.nn.softmax(logits, axis=-1)
    expert_count = router_full.shape[1]
    top_count = routes.shape[1]
    local_experts = expert_count // expert_parts
    capacity = tensor_parts * max(
        1,
        (row_count * top_count + expert_count * tensor_parts - 1) // (expert_count * tensor_parts),
        row_count * top_count * 5 // (4 * expert_count * tensor_parts),
    )
    expert_ids = jnp.arange(expert_count, dtype=jnp.int32)
    route_match = routes[:, :, None] == expert_ids[None, None, :]
    gate_probs = jnp.sum(jnp.where(route_match, router_probs[:, None, :], 0.0), axis=-1)
    flat_routes = routes.reshape(-1)
    onehot = (flat_routes[:, None] == expert_ids[None, :]).astype(jnp.int32)
    slot_rank = jnp.sum((jnp.cumsum(onehot, axis=0) - onehot) * onehot, axis=-1)
    row_ids = flat_routes * capacity + slot_rank
    token_ids = jnp.arange(row_count * top_count, dtype=jnp.int32) // top_count
    slot_token = (
        jnp.full((expert_count * capacity,), row_count, jnp.int32).at[row_ids].set(token_ids)
    )
    slot_gates = (
        jnp.zeros((expert_count * capacity,), jnp.float32).at[row_ids].set(gate_probs.reshape(-1))
    )
    pick_rows = row_ids.reshape(row_count, top_count)
    padded_in = jnp.concatenate([ffn_in, jnp.zeros((1, width), jnp.bfloat16)], axis=0)
    grad_full = dealt_grad.astype(jnp.float32)
    grad_padded = jnp.concatenate([grad_full, jnp.zeros((1, width), jnp.float32)], axis=0)
    received = to_experts(
        padded_in[slot_token].reshape(expert_parts, local_experts, capacity, width)
    )
    gate_pre = jnp.einsum("secd,edf->secf", received, w_gate, preferred_element_type=jnp.float32)
    up_pre = jnp.einsum("secd,edf->secf", received, w_up, preferred_element_type=jnp.float32)
    sigmoid_gate = jax.nn.sigmoid(gate_pre)
    silu_gate = gate_pre * sigmoid_gate
    hidden = (silu_gate * up_pre).astype(jnp.bfloat16)
    partial_out = jnp.einsum("secf,efd->secd", hidden, w_down, preferred_element_type=jnp.float32)
    own_columns = hidden_sums(partial_out).astype(jnp.bfloat16)
    returned = from_experts(own_columns).reshape(expert_count * capacity, quarter)
    chosen = returned[pick_rows].astype(jnp.float32)
    mix_own = jnp.sum(gate_probs[:, :, None] * chosen, axis=1)
    mix_part = lax.dynamic_update_slice_in_dim(
        jnp.zeros((row_count, width), jnp.float32), mix_own, column * quarter, 1
    )
    grad_own = lax.dynamic_slice_in_dim(grad_full, column * quarter, quarter, 1)
    gate_grad_part = jnp.sum(grad_own[:, None, :] * chosen, axis=-1)
    send_grad = (
        (grad_padded[slot_token] * slot_gates[:, None])
        .astype(jnp.bfloat16)
        .reshape(expert_parts, local_experts, capacity, width)
    )
    recv_grad = to_experts(send_grad)
    d_w_down = jnp.einsum("secf,secd->efd", hidden, recv_grad, preferred_element_type=jnp.float32)
    hidden_grad = jnp.einsum(
        "secd,efd->secf", recv_grad, w_down, preferred_element_type=jnp.float32
    )
    gate_grad_pre = (
        hidden_grad * up_pre * sigmoid_gate * (1.0 + gate_pre * (1.0 - sigmoid_gate))
    ).astype(jnp.bfloat16)
    up_grad_pre = (hidden_grad * silu_gate).astype(jnp.bfloat16)
    d_w_gate = jnp.einsum(
        "secd,secf->edf", received, gate_grad_pre, preferred_element_type=jnp.float32
    )
    d_w_up = jnp.einsum("secd,secf->edf", received, up_grad_pre, preferred_element_type=jnp.float32)
    joined_grad = jnp.concatenate([gate_grad_pre, up_grad_pre], axis=-1)
    joined_weight = jnp.concatenate([w_gate, w_up], axis=-1)
    row_terms = jnp.einsum(
        "secf,edf->secd", joined_grad, joined_weight, preferred_element_type=jnp.float32
    )
    row_own = hidden_sums(row_terms).astype(jnp.bfloat16)
    row_back = from_experts(row_own).reshape(expert_count * capacity, quarter)
    ffn_grad_own = jnp.sum(row_back[pick_rows].astype(jnp.float32), axis=1)
    placed = lax.dynamic_update_slice_in_dim(
        jnp.zeros((row_count, width), jnp.float32), ffn_grad_own, column * quarter, 1
    )
    ffn_grad_rows, gate_grad, mix_total = lax.psum((placed, gate_grad_part, mix_part), "tensor")
    output = (residual + mix_total).astype(jnp.bfloat16)
    prob_grad = jnp.sum(jnp.where(route_match, gate_grad[:, :, None], 0.0), axis=1)
    logit_grad = (
        router_probs * (prob_grad - jnp.sum(router_probs * prob_grad, axis=-1, keepdims=True))
    ).astype(jnp.bfloat16)
    d_router = jnp.einsum("rd,re->de", ffn_in, logit_grad, preferred_element_type=jnp.float32)
    ffn_grad = ffn_grad_rows + jnp.einsum(
        "re,de->rd", logit_grad, router_full, preferred_element_type=jnp.float32
    )
    d_ffn_gain = jnp.sum(ffn_grad * resid_hat, axis=0)
    scaled_ffn = ffn_grad * gain_ffn
    resid_grad = grad_full + resid_inv * (
        scaled_ffn - resid_hat * jnp.mean(scaled_ffn * resid_hat, axis=-1, keepdims=True)
    )
    branch_grad = resid_grad.astype(jnp.bfloat16)
    d_wo = jnp.einsum("rk,rd->kd", attended, branch_grad, preferred_element_type=jnp.float32)
    attended_grad = (
        jnp.einsum("rd,kd->rk", branch_grad, wo_full, preferred_element_type=jnp.float32)
        .astype(jnp.bfloat16)
        .reshape(row_count, head_count, HEAD_DIM)
    )
    probs_again = jnp.exp(masked_scores() - log_total)
    prob_grads = jnp.einsum(
        "qhd,khd->hqk", attended_grad, value_rows, preferred_element_type=jnp.float32
    )
    value_grad = (
        jnp.einsum(
            "hqk,qhd->khd",
            probs_again.astype(jnp.bfloat16),
            attended_grad,
            preferred_element_type=jnp.float32,
        )
        .astype(jnp.bfloat16)
        .reshape(row_count, local_width)
    )
    row_delta = jnp.sum(probs_again * prob_grads, axis=-1, keepdims=True)
    score_grad = (probs_again * (prob_grads - row_delta) * scale).astype(jnp.bfloat16)
    query_rot_grad = jnp.einsum(
        "hqk,khd->qhd", score_grad, key_rot, preferred_element_type=jnp.float32
    )
    key_rot_grad = jnp.einsum(
        "hqk,qhd->khd", score_grad, query_rot, preferred_element_type=jnp.float32
    )
    query_norm_grad = unrotate(query_rot_grad, cosines, sines).reshape(row_count, local_width)
    key_norm_grad = unrotate(key_rot_grad, cosines, sines).reshape(row_count, local_width)
    query_hat_grad = query_norm_grad * gain_query
    key_hat_grad = key_norm_grad * gain_key
    gain_pieces = jnp.stack(
        [jnp.sum(query_norm_grad * query_hat, axis=0), jnp.sum(key_norm_grad * key_hat, axis=0)]
    )
    gain_parts = lax.dynamic_update_slice_in_dim(
        jnp.zeros((2, width), jnp.float32), gain_pieces, column * local_width, 1
    )
    query_dot, key_dot, qk_gains = lax.psum(
        (
            jnp.sum(query_hat_grad * query_hat, axis=-1),
            jnp.sum(key_hat_grad * key_hat, axis=-1),
            gain_parts,
        ),
        "tensor",
    )
    query_grad = (query_inv * (query_hat_grad - query_hat * (query_dot / width)[:, None])).astype(
        jnp.bfloat16
    )
    key_grad = (key_inv * (key_hat_grad - key_hat * (key_dot / width)[:, None])).astype(
        jnp.bfloat16
    )
    d_wq = jnp.einsum("rd,rk->dk", normed, query_grad, preferred_element_type=jnp.float32)
    d_wk = jnp.einsum("rd,rk->dk", normed, key_grad, preferred_element_type=jnp.float32)
    d_wv = jnp.einsum("rd,rk->dk", normed, value_grad, preferred_element_type=jnp.float32)
    input_terms = jnp.einsum("rk,dk->rd", query_grad, wq_full, preferred_element_type=jnp.float32)
    input_terms = input_terms + jnp.einsum(
        "rk,dk->rd", key_grad, wk_full, preferred_element_type=jnp.float32
    )
    input_terms = input_terms + jnp.einsum(
        "rk,dk->rd", value_grad, wv_full, preferred_element_type=jnp.float32
    )
    normed_grad = lax.psum(input_terms, "tensor")
    d_attn_part = jnp.sum(normed_grad * input_hat, axis=0)
    scaled_attn = normed_grad * gain_attn
    input_grad = resid_grad + input_inv * (
        scaled_attn - input_hat * jnp.mean(scaled_attn * input_hat, axis=-1, keepdims=True)
    )
    dealt_dtokens = input_grad.astype(jnp.bfloat16)
    gain_grads = jnp.stack([d_attn_part, qk_gains[0], qk_gains[1], d_ffn_gain])
    sum_wq, sum_wk, sum_wv, sum_wo, sum_router, sum_gains = (
        lax.psum_scatter(d_wq, "expert", scatter_dimension=0, tiled=True),
        lax.psum_scatter(d_wk, "expert", scatter_dimension=0, tiled=True),
        lax.psum_scatter(d_wv, "expert", scatter_dimension=0, tiled=True),
        lax.psum_scatter(d_wo, "expert", scatter_dimension=1, tiled=True),
        lax.psum_scatter(d_router, "expert", scatter_dimension=0, tiled=True),
        lax.psum_scatter(gain_grads, "expert", scatter_dimension=1, tiled=True),
    )
    back_out, back_dtok = (
        lax.all_to_all(
            output.reshape(expert_parts, share_rows, width),
            "expert",
            split_axis=0,
            concat_axis=0,
            tiled=True,
        ),
        lax.all_to_all(
            dealt_dtokens.reshape(expert_parts, share_rows, width),
            "expert",
            split_axis=0,
            concat_axis=0,
            tiled=True,
        ),
    )
    flat_pick = local_pick.reshape(-1)
    output_rows = (
        jnp.zeros((row_count, width), jnp.bfloat16)
        .at[flat_pick]
        .set(back_out.reshape(row_count, width))
    )
    d_tokens = (
        jnp.zeros((row_count, width), jnp.bfloat16)
        .at[flat_pick]
        .set(back_dtok.reshape(row_count, width))
    )
    return (
        output_rows,
        d_tokens,
        sum_gains[0],
        sum_wq,
        sum_wk,
        sum_wv,
        sum_wo,
        sum_gains[1],
        sum_gains[2],
        sum_gains[3],
        sum_router,
        d_w_gate,
        d_w_up,
        d_w_down,
    )


MESH_ID = pl.DeviceIdType.MESH
ANY = pl.BlockSpec(memory_space=pl.ANY)
IN_VMEM = pl.BlockSpec(memory_space=pltpu.VMEM)
def cost_of(micros):
    return pl.CostEstimate(flops=0, bytes_accessed=micros * 3_000_000, transcendentals=0)


SELF, NEAR, FAR, BOTH_FLIPPED = 0, 1, 2, 3


def place_of(device):
    expert, tensor = device
    return expert // 2, expert % 2, tensor // 2, tensor % 2


def flipped(device, role):
    expert, tensor = device
    _, x, y, core = place_of(device)
    step_x, step_y = 1 - 2 * x, 2 - 4 * y
    if role == NEAR:
        return expert + (1 - core) * step_x, tensor + core * step_y
    if role == FAR:
        return expert + core * step_x, tensor + (1 - core) * step_y
    if role == BOTH_FLIPPED:
        return expert + step_x, tensor + step_y
    return expert, tensor


def moved_z(device, hops):
    expert, tensor = device
    return lax.rem(expert + 2 * hops, 8), tensor


def sibling(device):
    expert, tensor = device
    return expert, tensor + 1 - 2 * (tensor % 2)


def slot_of(device):
    return device[0] * 4 + device[1]


def here():
    return lax.axis_index("expert"), lax.axis_index("tensor")


def greet(partners):
    barrier = pltpu.get_barrier_semaphore()
    for partner in partners:
        pl.semaphore_signal(barrier, inc=1, device_id=partner, device_id_type=MESH_ID)
    pl.semaphore_wait(barrier, len(partners))


def push(source, target, send_sem, recv_sem, device):
    return pltpu.make_async_remote_copy(
        src_ref=source,
        dst_ref=target,
        send_sem=send_sem,
        recv_sem=recv_sem,
        device_id=device,
        device_id_type=MESH_ID,
    )


def gather_kernel(count, *refs):
    ins, outs = refs[:count], refs[count : 2 * count]
    send_sem, recv_sem, local_sem = refs[2 * count :]
    me = here()
    near, far, sib = flipped(me, NEAR), flipped(me, FAR), sibling(me)
    greet([near, far, sib] + [moved_z(me, d) for d in (1, 2, 3)])
    started = []

    def send(k, role, device, tag, recv_tag):
        origin = moved_z(flipped(me, role), k)
        for i in range(count):
            block = outs[i].at[slot_of(origin)]
            source = ins[i] if (k, role) == (0, SELF) else block
            copy = push(source, block, send_sem.at[i, tag], recv_sem.at[i, recv_tag], device)
            copy.start()
            started.append(copy)

    def wait(k, role):
        origin = moved_z(flipped(me, role), k)
        for i in range(count):
            block = outs[i].at[slot_of(origin)]
            push(block, block, send_sem.at[i, 0], recv_sem.at[i, k * 4 + role], near).wait_recv()

    def forward(k, role):
        if role == SELF:
            send(k, SELF, far, 4 + k, k * 4 + FAR)
            send(k, SELF, near, k, k * 4 + NEAR)
        if role == NEAR:
            send(k, NEAR, far, 8 + k, k * 4 + BOTH_FLIPPED)
        send(k, role, sib, 16 + k * 4 + role, 16 + k * 4 + role)

    local = [
        pltpu.make_async_copy(ins[i], outs[i].at[slot_of(me)], local_sem.at[i])
        for i in range(count)
    ]
    forward(0, SELF)
    for d in (1, 3, 2):
        send(0, SELF, moved_z(me, d), 11 + d, (4 - d) * 4 + SELF)
    for copy in local:
        copy.start()
    for k, role in (
        (0, NEAR), (1, SELF), (3, SELF), (0, FAR), (1, NEAR), (0, BOTH_FLIPPED), (2, SELF), (3, NEAR),
        (1, FAR), (1, BOTH_FLIPPED), (2, NEAR), (3, FAR), (3, BOTH_FLIPPED), (2, FAR), (2, BOTH_FLIPPED),
    ):
        wait(k, role)
        forward(k, role)
    for k in range(4):
        for role in range(4):
            origin = sibling(moved_z(me, k))
            origin = moved_z(flipped(sib, role), k)
            for i in range(count):
                block = outs[i].at[slot_of(origin)]
                push(
                    block, block, send_sem.at[i, 0], recv_sem.at[i, 16 + k * 4 + role], near
                ).wait_recv()
    for copy in started:
        copy.wait_send()
    for copy in local:
        copy.wait()


def gather_all(*shards):
    count = len(shards)
    out = pl.pallas_call(
        functools.partial(gather_kernel, count),
        out_shape=[jax.ShapeDtypeStruct((32,) + s.shape, s.dtype) for s in shards],
        in_specs=[IN_VMEM] * count,
        out_specs=[ANY] * count,
        scratch_shapes=[
            pltpu.SemaphoreType.DMA((count, 32)),
            pltpu.SemaphoreType.DMA((count, 32)),
            pltpu.SemaphoreType.DMA((count,)),
        ],
        compiler_params=pltpu.CompilerParams(
            collective_id=count, has_side_effects=True, vmem_limit_bytes=16 * 2**20
        ),
        cost_estimate=cost_of(90),
        name=f"gather_all_{count}",
    )(*shards)
    return [o.reshape((-1,) + s.shape[1:]) for o, s in zip(out, shards)]


def sum_kernel(part, out, mine, from_sib, from_far, from_near, from_z, send_sem, recv_sem, load_sem):
    me = here()
    near, far, sib = flipped(me, NEAR), flipped(me, FAR), sibling(me)
    greet([near, far, sib] + [moved_z(me, d) for d in (1, 2, 3)])
    order = (2, 1, 3, 0)
    started = []

    def send(source, target, tag, recv_tag, device):
        copy = push(source, target, send_sem.at[tag], recv_sem.at[recv_tag], device)
        copy.start()
        started.append(copy)

    def wait(target, recv_tag):
        push(target, target, send_sem.at[0], recv_sem.at[recv_tag], near).wait_recv()

    loads = {}
    for roles in ((BOTH_FLIPPED, FAR), (NEAR, SELF)):
        for k in order:
            for role in roles:
                tag = k * 4 + role
                send(part.at[slot_of(moved_z(flipped(sib, role), k))], from_sib.at[tag], tag, tag, sib)
                loads[tag] = pltpu.make_async_copy(
                    part.at[slot_of(moved_z(flipped(me, role), k))], mine.at[tag], load_sem.at[tag]
                )
                loads[tag].start()

    def total(k, role, others):
        tag = k * 4 + role
        loads[tag].wait()
        wait(from_sib.at[tag], tag)
        terms = [from_sib.at[tag]]
        for ref, recv_tag in others:
            wait(ref, recv_tag)
            terms.append(ref)
        return tag, terms

    def add(target, tag, terms):
        rows = mine.shape[1]
        step = 16

        def body(i, carry):
            window = pl.ds(pl.multiple_of(i * step, step), step)
            value = mine[tag, window, :].astype(jnp.float32)
            for ref in terms:
                value = value + ref[window, :].astype(jnp.float32)
            target[window, :] = value.astype(target.dtype)
            return carry

        lax.fori_loop(0, rows // step, body, 0)

    for k in order:
        for role in (BOTH_FLIPPED, FAR):
            tag, terms = total(k, role, [])
            add(mine.at[tag], tag, terms)
            at = k * 2 + (role == BOTH_FLIPPED)
            send(mine.at[tag], from_far.at[at], 16 + at, 16 + at, far)

    def second(k):
        tag, terms = total(k, NEAR, [(from_far.at[k * 2 + 1], 16 + k * 2 + 1)])
        add(mine.at[tag], tag, terms)
        send(mine.at[tag], from_near.at[k], 24 + k, 24 + k, near)

    def third(k):
        tag, terms = total(
            k, SELF, [(from_far.at[k * 2], 16 + k * 2), (from_near.at[k], 24 + k)]
        )
        if k > 0:
            add(mine.at[tag], tag, terms)
            send(mine.at[tag], from_z.at[3 - k], 27 + k, 28 + 3 - k, moved_z(me, k))
        else:
            for d in range(3):
                wait(from_z.at[d], 28 + d)
                terms.append(from_z.at[d])
            add(out, tag, terms)

    second(order[0])
    second(order[1])
    third(order[0])
    second(order[2])
    third(order[1])
    second(order[3])
    third(order[2])
    third(order[3])
    for copy in started:
        copy.wait_send()


def sum_all(partial):
    rows, width = partial.shape[0] // 32, partial.shape[1]
    block = (rows, width)
    return pl.pallas_call(
        sum_kernel,
        out_shape=jax.ShapeDtypeStruct(block, jnp.float32),
        in_specs=[ANY],
        out_specs=IN_VMEM,
        scratch_shapes=[
            pltpu.VMEM((16,) + block, partial.dtype),
            pltpu.VMEM((16,) + block, partial.dtype),
            pltpu.VMEM((8,) + block, partial.dtype),
            pltpu.VMEM((4,) + block, partial.dtype),
            pltpu.VMEM((3,) + block, partial.dtype),
            pltpu.SemaphoreType.DMA((32,)),
            pltpu.SemaphoreType.DMA((32,)),
            pltpu.SemaphoreType.DMA((16,)),
        ],
        compiler_params=pltpu.CompilerParams(
            collective_id=3, has_side_effects=True, vmem_limit_bytes=40 * 2**20
        ),
        cost_estimate=cost_of(80),
        name="sum_all",
    )(partial.reshape((32,) + block))


def hop(device, flips, hops):
    expert, tensor = device
    return lax.rem(expert + flips * (1 - 2 * lax.rem(expert, 2)) + 2 * hops, 8), tensor


def across_y(device):
    expert, tensor = device
    return expert, lax.rem(tensor + 2, 4)


class Line:
    def __init__(self, send_sem, recv_sem):
        self.send_sem, self.recv_sem = send_sem, recv_sem
        self.started = []

    def send(self, source, target, tag, recv_tag, device):
        copy = push(source, target, self.send_sem.at[tag], self.recv_sem.at[recv_tag], device)
        copy.start()
        self.started.append(copy)

    def wait(self, target, tag, device):
        push(target, target, self.send_sem.at[0], self.recv_sem.at[tag], device).wait_recv()

    def finish(self):
        for copy in self.started:
            copy.wait_send()


PIECES = ((0, 1), (1, 0), (3, 0), (1, 1), (3, 1), (2, 0), (2, 1))


def exchange_steps(source, out, gathered, line, local_sem):
    me = here()
    tensor = me[1]
    side, sib = across_y(me), sibling(me)

    def at(column, expert):
        return out.at[column, expert] if gathered else out.at[expert]

    local = pltpu.make_async_copy(source.at[me[0]], at(tensor, me[0]), local_sem)
    local.start()
    if gathered:
        line.send(source.at[me[0]], at(tensor, me[0]), 8, 8, side)
        line.send(source.at[me[0]], at(tensor, me[0]), 16, 16, sib)
    for k, flips in PIECES:
        target = hop(me, flips, k)
        line.send(
            source.at[target[0]], at(tensor, me[0]), k * 2 + flips, (4 - k) % 4 * 2 + flips, target
        )
    yield
    for k, flips in PIECES:
        expert = hop(me, flips, k)[0]
        tag = k * 2 + flips
        line.wait(at(tensor, expert), tag, sib)
        if gathered:
            line.send(at(tensor, expert), at(tensor, expert), 8 + tag, 8 + tag, side)
            line.send(at(tensor, expert), at(tensor, expert), 16 + tag, 16 + tag, sib)
        yield
    if gathered:
        for k, flips in ((0, 0),) + PIECES:
            expert = hop(me, flips, k)[0]
            tag = k * 2 + flips
            line.wait(at(side[1], expert), 8 + tag, sib)
            line.send(at(side[1], expert), at(side[1], expert), 24 + tag, 24 + tag, sib)
            yield
        for k, flips in ((0, 0),) + PIECES:
            expert = hop(me, flips, k)[0]
            tag = k * 2 + flips
            line.wait(at(sib[1], expert), 16 + tag, sib)
            line.wait(at(across_y(sib)[1], expert), 24 + tag, sib)
    local.wait()
    line.finish()


def gather_expert_steps(source, out, chunks, line, local_sem):
    me = here()
    z = me[0] // 2
    beside = hop(me, 1, 0)
    step = source.shape[0] // chunks

    def part(ref, i):
        return ref.at[pl.ds(i * step, step), :]

    local = pltpu.make_async_copy(source, out.at[me[0]], local_sem)
    local.start()

    def passes(ref, target, i, tag, origin_tag, up):
        device = hop(me, 0, 1 if up else 3)

        @pl.when((z < 3) if up else (z > 0))
        def _():
            push(ref, target, line.send_sem.at[tag], line.recv_sem.at[origin_tag], device).start()

    def base(distance, up, i):
        return ((distance - 1) * 2 + up) * chunks + i

    for i in range(chunks):
        line.send(part(source, i), part(out.at[me[0]], i), 12 * chunks + i, 12 * chunks + i, beside)
        for up in (1, 0):
            passes(part(source, i), part(out.at[me[0]], i), i, base(1, up, i), base(1, up, i), up)
    yield
    for distance in (1, 2, 3):
        for i in range(chunks):
            for up in (1, 0):
                held = (z >= distance) if up else (z + distance <= 3)
                expert = lax.rem(me[0] + (8 - 2 * distance if up else 2 * distance), 8)
                block = part(out.at[expert], i)
                tag = base(distance, up, i)

                @pl.when(held)
                def _():
                    line.wait(block, tag, beside)
                    cross = 6 * chunks + tag
                    push(block, block, line.send_sem.at[cross], line.recv_sem.at[cross], beside).start()

                if distance < 3:
                    more = base(distance + 1, up, i)

                    @pl.when(held & ((z < 3) if up else (z > 0)))
                    def _():
                        push(
                            block,
                            block,
                            line.send_sem.at[more],
                            line.recv_sem.at[more],
                            hop(me, 0, 1 if up else 3),
                        ).start()

                yield
    for i in range(chunks):
        line.wait(part(out.at[beside[0]], i), 12 * chunks + i, beside)
    for distance in (1, 2, 3):
        for i in range(chunks):
            for up in (1, 0):
                held = (z >= distance) if up else (z + distance <= 3)
                expert = lax.rem(beside[0] + (8 - 2 * distance if up else 2 * distance), 8)
                block = part(out.at[expert], i)
                cross = 6 * chunks + base(distance, up, i)
                sent_on = (z + 1 >= distance) & (z < 3) if up else (z - 1 + distance <= 3) & (z > 0)

                @pl.when(held)
                def _():
                    both = push(block, block, line.send_sem.at[cross], line.recv_sem.at[cross], beside)
                    both.wait()

                @pl.when(sent_on)
                def _():
                    tag = base(distance, up, i)
                    push(
                        block, block, line.send_sem.at[tag], line.recv_sem.at[tag], beside
                    ).wait_send()

        yield
    local.wait()
    line.finish()


def sum_rows(target, terms, step=16):
    def body(i, carry):
        window = pl.ds(pl.multiple_of(i * step, step), step)
        value = terms[0][window, :].astype(jnp.float32)
        for ref in terms[1:]:
            value = value + ref[window, :].astype(jnp.float32)
        target[window, :] = value.astype(target.dtype)
        return carry

    lax.fori_loop(0, target.shape[0] // step, body, 0)


def sum_expert_steps(part, out, mine, from_x, from_z, line, load_sem):
    me = here()
    beside = hop(me, 1, 0)
    loads = {}
    for k in (2, 1, 3, 0):
        line.send(part.at[hop(me, 1, k)[0]], from_x.at[k], k, k, beside)
        loads[k] = pltpu.make_async_copy(part.at[hop(me, 0, k)[0]], mine.at[k], load_sem.at[k])
        loads[k].start()
    yield
    for k in (2, 1, 3, 0):
        loads[k].wait()
        line.wait(from_x.at[k], k, beside)
        if k:
            sum_rows(mine.at[k], [mine.at[k], from_x.at[k]])
            line.send(mine.at[k], from_z.at[3 - k], 3 + k, 4 + 3 - k, hop(me, 0, k))
            yield
            yield
    for i in range(3):
        line.wait(from_z.at[i], 4 + i, beside)
    sum_rows(out, [mine.at[0], from_x.at[0], from_z.at[0], from_z.at[1], from_z.at[2]])
    line.finish()


def take_turns(steps):
    steps = list(steps)
    while steps:
        steps = [s for s in steps if next(s, steps) is not steps]


DMA = pltpu.SemaphoreType.DMA


def start_kernel(tokens, grads, weights, small, o_tokens, o_grads, o_weights, o_small, *sems):
    me = here()
    pieces = [hop(me, flips, k) for k, flips in PIECES]
    greet(pieces + [across_y(me), sibling(me)])
    local = sems[8]
    take_turns(
        [
            exchange_steps(tokens, o_tokens, True, Line(sems[0], sems[1]), local.at[0]),
            exchange_steps(grads, o_grads, False, Line(sems[2], sems[3]), local.at[1]),
            gather_expert_steps(small, o_small, 1, Line(sems[6], sems[7]), local.at[3]),
            gather_expert_steps(weights, o_weights, 4, Line(sems[4], sems[5]), local.at[2]),
        ]
    )


def start_exchange(tokens, grads, weights, small):
    piece = tokens.shape[1:]
    sds = jax.ShapeDtypeStruct
    return pl.pallas_call(
        start_kernel,
        out_shape=[
            sds((4, 8) + piece, tokens.dtype),
            sds((8,) + piece, grads.dtype),
            sds((8,) + weights.shape, weights.dtype),
            sds((8,) + small.shape, small.dtype),
        ],
        in_specs=[IN_VMEM] * 4,
        out_specs=[ANY] * 4,
        scratch_shapes=[DMA((32,)), DMA((32,)), DMA((8,)), DMA((8,))]
        + [DMA((52,)), DMA((52,)), DMA((13,)), DMA((13,)), DMA((4,))],
        compiler_params=pltpu.CompilerParams(
            collective_id=4, has_side_effects=True, vmem_limit_bytes=16 * 2**20
        ),
        cost_estimate=cost_of(100),
        name="start_exchange",
    )(tokens, grads, weights, small)


def last_kernel(rows, more, part, o_rows, o_more, out, mine, from_x, from_z, *sems):
    me = here()
    pieces = [hop(me, flips, k) for k, flips in PIECES]
    greet(pieces + [across_y(me), sibling(me)])
    take_turns(
        [
            exchange_steps(more, o_more, True, Line(sems[2], sems[3]), sems[7].at[1]),
            exchange_steps(rows, o_rows, True, Line(sems[0], sems[1]), sems[7].at[0]),
            sum_expert_steps(part, out, mine, from_x, from_z, Line(sems[4], sems[5]), sems[6]),
        ]
    )


def last_exchange(rows, more, part):
    piece = rows.shape[1:]
    block = part.shape[1:]
    sds = jax.ShapeDtypeStruct
    return pl.pallas_call(
        last_kernel,
        out_shape=[
            sds((4, 8) + piece, rows.dtype),
            sds((4, 8) + piece, more.dtype),
            sds(block, jnp.float32),
        ],
        in_specs=[IN_VMEM, IN_VMEM, ANY],
        out_specs=[ANY, ANY, IN_VMEM],
        scratch_shapes=[
            pltpu.VMEM((4,) + block, part.dtype),
            pltpu.VMEM((4,) + block, part.dtype),
            pltpu.VMEM((3,) + block, part.dtype),
        ]
        + [DMA((32,))] * 4
        + [DMA((8,)), DMA((8,)), DMA((4,)), DMA((2,))],
        compiler_params=pltpu.CompilerParams(
            collective_id=5, has_side_effects=True, vmem_limit_bytes=32 * 2**20
        ),
        cost_estimate=cost_of(100),
        name="last_exchange",
    )(rows, more, part)


def gather_tensor_kernel(source, out, send_sem, recv_sem, local_sem):
    me = here()
    side, sib = across_y(me), sibling(me)
    greet([side, sib])
    line = Line(send_sem, recv_sem)
    halves = 4
    step = source.shape[0] // halves

    def part(ref, i):
        return ref.at[pl.ds(i * step, step), :]

    local = pltpu.make_async_copy(source, out.at[me[1]], local_sem)
    for i in range(halves):
        line.send(part(source, i), part(out.at[me[1]], i), i, i, side)
        line.send(part(source, i), part(out.at[me[1]], i), 4 + i, 4 + i, sib)
    local.start()
    for i in range(halves):
        got = part(out.at[side[1]], i)
        line.wait(got, i, sib)
        line.send(got, got, 8 + i, 8 + i, sib)
    for i in range(halves):
        line.wait(part(out.at[sib[1]], i), 4 + i, sib)
        line.wait(part(out.at[across_y(sib)[1]], i), 8 + i, sib)
    local.wait()
    line.finish()


def gather_tensor(rows):
    out = pl.pallas_call(
        gather_tensor_kernel,
        out_shape=jax.ShapeDtypeStruct((4,) + rows.shape, rows.dtype),
        in_specs=[IN_VMEM],
        out_specs=ANY,
        scratch_shapes=[DMA((12,)), DMA((12,)), DMA],
        compiler_params=pltpu.CompilerParams(
            collective_id=6, has_side_effects=True, vmem_limit_bytes=8 * 2**20
        ),
        cost_estimate=cost_of(15),
        name="gather_tensor",
    )(rows)
    return out.reshape((-1,) + rows.shape[1:])


def sum_tensor_kernel(part, out, from_sib, from_side, total, send_sem, recv_sem):
    me = here()
    side, sib = across_y(me), sibling(me)
    greet([side, sib])
    line = Line(send_sem, recv_sem)
    pieces = 4
    step = out.shape[0] // pieces

    def rows(ref, i):
        return ref.at[pl.ds(i * step, step), :]

    for j, column in ((0, across_y(sib)[1]), (1, sib[1])):
        for i in range(pieces):
            line.send(
                rows(part.at[column], i), rows(from_sib.at[j], i), 4 * j + i, 4 * j + i, sib
            )
    for i in range(pieces):
        got = rows(from_sib.at[0], i)
        line.wait(got, i, sib)
        sum_rows(rows(total, i), [rows(part.at[side[1]], i), got])
        line.send(rows(total, i), rows(from_side, i), 8 + i, 8 + i, side)
    for i in range(pieces):
        got = rows(from_sib.at[1], i)
        line.wait(got, 4 + i, sib)
        line.wait(rows(from_side, i), 8 + i, sib)
        sum_rows(rows(out, i), [rows(part.at[me[1]], i), got, rows(from_side, i)])
    line.finish()


def sum_tensor(partial):
    block = (partial.shape[0] // 4, partial.shape[1])
    return pl.pallas_call(
        sum_tensor_kernel,
        out_shape=jax.ShapeDtypeStruct(block, jnp.float32),
        in_specs=[IN_VMEM],
        out_specs=IN_VMEM,
        scratch_shapes=[
            pltpu.VMEM((2,) + block, partial.dtype),
            pltpu.VMEM(block, partial.dtype),
            pltpu.VMEM(block, partial.dtype),
            DMA((12,)),
            DMA((12,)),
        ],
        compiler_params=pltpu.CompilerParams(
            collective_id=7, has_side_effects=True, vmem_limit_bytes=12 * 2**20
        ),
        cost_estimate=cost_of(15),
        name="sum_tensor",
    )(partial.reshape((4,) + block))


BOTH = ("expert", "tensor")


def sum_small(rows):
    return lax.psum_scatter(rows, BOTH, scatter_dimension=0, tiled=True)


def dot32(left, right, dims):
    return lax.dot_general(left, right, (dims, ((), ())), preferred_element_type=jnp.float32)


NN = ((1,), (0,))
NT = ((1,), (1,))
TN = ((0,), (0,))


def rms_inv(values):
    return lax.rsqrt(jnp.mean(values * values, axis=-1, keepdims=True) + NORM_EPS)


def dense_body(
    tokens,
    attn_gain,
    w_query,
    w_key,
    w_value,
    w_out,
    query_gain,
    key_gain,
    ffn_gain,
    w_router,
    w_gate,
    w_up,
    w_down,
    doc_ids,
    routes,
    deal,
    out_grad,
):
    rows, width = tokens.shape
    parts = lax.axis_size("tensor")
    blocks = lax.axis_size("expert")
    column = lax.axis_index("tensor")
    block = lax.axis_index("expert")
    own = rows // parts
    share = rows // blocks
    piece = share // parts
    bf16, f32 = jnp.bfloat16, jnp.float32

    def reorder(per_place):
        grid = per_place.reshape((blocks, parts, piece) + per_place.shape[1:])
        return jnp.swapaxes(grid, 0, 1).reshape(per_place.shape)

    local_width = w_query.shape[1]
    head_count = local_width // HEAD_DIM
    expert_count = w_router.shape[1]
    qkv_own = jnp.concatenate([w_query, w_key, w_value], axis=1)
    gain_stack = jnp.stack([attn_gain, query_gain, key_gain, ffn_gain], axis=1)
    small_own = jnp.concatenate([w_router, gain_stack], axis=1)
    small_own = jnp.pad(small_own, ((0, 0), (0, 128 - small_own.shape[1])))
    deal_grid = deal.reshape(blocks, blocks, parts, piece)
    picks = lax.dynamic_slice(deal_grid, (0, block, column, 0), (blocks, 1, 1, piece)).reshape(-1)
    picks = picks - block * rows
    inputs, dealt_grads, qkv_full, small_full = start_exchange(
        tokens[picks].reshape(blocks, piece, width),
        out_grad[picks].reshape(blocks, piece, width),
        qkv_own,
        small_own,
    )
    own_low = lax.dynamic_slice_in_dim(inputs, column, 1, 0).reshape(own, width)
    inputs = inputs.reshape(rows, width).astype(f32)
    qkv_full = qkv_full.reshape(width, -1)
    small_full = small_full.reshape(width, -1)
    router_full = small_full[:, :expert_count]
    gain_full = small_full[:, expert_count : expert_count + 4].T.astype(f32)
    gain_attn, gain_ffn = gain_full[0], gain_full[3]
    gain_query = lax.dynamic_slice_in_dim(gain_full[1], column * local_width, local_width)
    gain_key = lax.dynamic_slice_in_dim(gain_full[2], column * local_width, local_width)
    out_full = lax.all_gather(w_out, "expert", axis=0)
    own_grad_low = dealt_grads.reshape(own, width)
    grads_all = lax.all_gather(own_grad_low, BOTH, axis=0, tiled=True)
    own_in = own_low.astype(f32)
    own_grad = own_grad_low.astype(f32)

    scale = 1.0 / math.sqrt(HEAD_DIM)
    normed = (inputs * rms_inv(inputs) * gain_attn).astype(bf16)
    qkv = dot32(normed, qkv_full, NN)
    query_pre = qkv[:, :local_width]
    key_pre = qkv[:, local_width : 2 * local_width]
    value_rows = qkv[:, 2 * local_width :].astype(bf16).reshape(rows, head_count, HEAD_DIM)
    squares = lax.psum(
        jnp.stack([jnp.sum(query_pre * query_pre, axis=-1), jnp.sum(key_pre * key_pre, axis=-1)]),
        "tensor",
    )
    query_inv = lax.rsqrt(squares[0] / width + NORM_EPS)[:, None]
    key_inv = lax.rsqrt(squares[1] / width + NORM_EPS)[:, None]
    query_hat = query_pre * query_inv
    key_hat = key_pre * key_inv
    cosines, sines = rope_tables(doc_ids, HEAD_DIM)
    cosines, sines = reorder(cosines), reorder(sines)
    query_rot = rotate(
        (query_hat * gain_query).reshape(rows, head_count, HEAD_DIM), cosines, sines
    ).astype(bf16)
    key_rot = rotate(
        (key_hat * gain_key).reshape(rows, head_count, HEAD_DIM), cosines, sines
    ).astype(bf16)
    positions = reorder(jnp.arange(rows, dtype=jnp.int32))
    documents = reorder(doc_ids)
    allowed = (documents[:, None] == documents[None, :]) & (positions[None, :] <= positions[:, None])

    def masked_scores():
        raw_scores = jnp.einsum("qhd,khd->hqk", query_rot, key_rot, preferred_element_type=f32)
        return jnp.where(allowed[None], raw_scores * scale, -1e30)

    scores = masked_scores()
    top_score = jnp.max(scores, axis=-1, keepdims=True)
    log_total = top_score + jnp.log(jnp.sum(jnp.exp(scores - top_score), axis=-1, keepdims=True))
    weights = jnp.exp(scores - log_total).astype(bf16)
    attended = (
        jnp.einsum("hqk,khd->qhd", weights, value_rows, preferred_element_type=f32)
        .astype(bf16)
        .reshape(rows, local_width)
    )
    branch = jnp.einsum("rk,ekd->red", attended, out_full, preferred_element_type=f32)
    branch = branch.astype(bf16).reshape(rows, width)
    branch_own = sum_tensor(branch)

    residual = own_in + branch_own
    resid_inv = rms_inv(residual)
    resid_hat = residual * resid_inv
    ffn_in = (resid_hat * gain_ffn).astype(bf16)
    logits = dot32(ffn_in, router_full, NN)
    router_probs = jax.nn.softmax(logits, axis=-1)
    local_experts = w_gate.shape[0]
    hidden_width = w_gate.shape[2]
    own_routes = lax.dynamic_slice(
        routes.reshape(blocks, parts, piece, -1),
        (0, column, 0, 0),
        (blocks, 1, piece, routes.shape[1]),
    ).reshape(own, -1)
    expert_ids = jnp.arange(expert_count, dtype=jnp.int32)
    routed = jnp.any(own_routes[:, :, None] == expert_ids[None, None, :], axis=1)
    gates_own = jnp.where(routed, router_probs, 0.0)

    rows_all, gates_all = gather_all(ffn_in, gates_own.T)
    gates_all = gates_all.reshape(blocks * parts, expert_count, own)
    gates = lax.dynamic_slice_in_dim(gates_all, block * local_experts, local_experts, 1)
    gates = jnp.swapaxes(gates, 1, 2).reshape(-1, local_experts)

    joined_weight = jnp.concatenate(
        [w_gate[i] for i in range(local_experts)] + [w_up[i] for i in range(local_experts)], axis=1
    )
    down_weight = w_down.reshape(local_experts * hidden_width, width)
    joined = dot32(rows_all, joined_weight, NN)
    half = local_experts * hidden_width
    gate_pre, up_pre = joined[:, :half], joined[:, half:]
    wide_gates = jnp.concatenate(
        [
            jnp.broadcast_to(gates[:, i : i + 1], (gates.shape[0], hidden_width))
            for i in range(local_experts)
        ],
        axis=1,
    )
    sigmoid_gate = jax.nn.sigmoid(gate_pre)
    silu_gate = gate_pre * sigmoid_gate
    hidden = (silu_gate * up_pre).astype(bf16)
    gated_hidden = (hidden.astype(f32) * wide_gates).astype(bf16)
    mixed = dot32(gated_hidden, down_weight, NN).astype(bf16)
    mix_own = lax.psum_scatter(mixed, BOTH, scatter_dimension=0, tiled=True)
    output_own = (residual + mix_own.astype(f32)).astype(bf16)

    hidden_raw = dot32(grads_all, down_weight, NT)
    gate_grads = jnp.sum(
        (hidden.astype(f32) * hidden_raw).reshape(-1, local_experts, hidden_width), axis=-1
    )
    d_w_down = dot32(gated_hidden, grads_all, TN).reshape(w_down.shape)
    hidden_grad = hidden_raw * wide_gates
    gate_grad_pre = (
        hidden_grad * up_pre * sigmoid_gate * (1.0 + gate_pre * (1.0 - sigmoid_gate))
    ).astype(bf16)
    up_grad_pre = (hidden_grad * silu_gate).astype(bf16)
    joined_grad = jnp.concatenate([gate_grad_pre, up_grad_pre], axis=1)
    row_terms = dot32(joined_grad, joined_weight, NT).astype(bf16)
    row_own = sum_all(row_terms)
    placed = lax.dynamic_update_slice_in_dim(
        jnp.zeros((gate_grads.shape[0], expert_count), f32), gate_grads, block * local_experts, 1
    )
    gate_grad_own = sum_small(placed)
    d_w_gate = jnp.stack(
        [
            dot32(rows_all, gate_grad_pre[:, i * hidden_width : (i + 1) * hidden_width], TN)
            for i in range(local_experts)
        ]
    )
    d_w_up = jnp.stack(
        [
            dot32(rows_all, up_grad_pre[:, i * hidden_width : (i + 1) * hidden_width], TN)
            for i in range(local_experts)
        ]
    )

    prob_grad = jnp.where(routed, gate_grad_own, 0.0)
    logit_grad = (
        router_probs * (prob_grad - jnp.sum(router_probs * prob_grad, axis=-1, keepdims=True))
    ).astype(bf16)
    d_router = dot32(ffn_in, logit_grad, TN)
    ffn_grad = row_own + dot32(logit_grad, router_full, NT)
    d_ffn_gain = jnp.sum(ffn_grad * resid_hat, axis=0)
    scaled_ffn = ffn_grad * gain_ffn
    resid_grad = own_grad + resid_inv * (
        scaled_ffn - resid_hat * jnp.mean(scaled_ffn * resid_hat, axis=-1, keepdims=True)
    )
    branch_grad = gather_tensor(resid_grad.astype(bf16))

    branch_cols = branch_grad.reshape(rows, blocks, width // blocks)
    d_wo = jnp.einsum("rk,red->ekd", attended, branch_cols, preferred_element_type=f32).astype(bf16)
    sum_wo = lax.psum_scatter(d_wo, "expert", scatter_dimension=0, tiled=False)
    attended_grad = (
        jnp.einsum("red,ekd->rk", branch_cols, out_full, preferred_element_type=f32)
        .astype(bf16)
        .reshape(rows, head_count, HEAD_DIM)
    )
    probs_again = jnp.exp(masked_scores() - log_total)
    prob_grads = jnp.einsum("qhd,khd->hqk", attended_grad, value_rows, preferred_element_type=f32)
    value_grad = (
        jnp.einsum(
            "hqk,qhd->khd", probs_again.astype(bf16), attended_grad, preferred_element_type=f32
        )
        .astype(bf16)
        .reshape(rows, local_width)
    )
    row_delta = jnp.sum(probs_again * prob_grads, axis=-1, keepdims=True)
    score_grad = (probs_again * (prob_grads - row_delta) * scale).astype(bf16)
    query_rot_grad = jnp.einsum("hqk,khd->qhd", score_grad, key_rot, preferred_element_type=f32)
    key_rot_grad = jnp.einsum("hqk,qhd->khd", score_grad, query_rot, preferred_element_type=f32)
    query_norm_grad = unrotate(query_rot_grad, cosines, sines).reshape(rows, local_width)
    key_norm_grad = unrotate(key_rot_grad, cosines, sines).reshape(rows, local_width)
    query_hat_grad = query_norm_grad * gain_query
    key_hat_grad = key_norm_grad * gain_key
    d_query_gain = jnp.sum(query_norm_grad * query_hat, axis=0)
    d_key_gain = jnp.sum(key_norm_grad * key_hat, axis=0)
    dots = lax.psum(
        jnp.stack(
            [
                jnp.sum(query_hat_grad * query_hat, axis=-1),
                jnp.sum(key_hat_grad * key_hat, axis=-1),
            ]
        ),
        "tensor",
    )
    query_grad = (query_inv * (query_hat_grad - query_hat * (dots[0] / width)[:, None])).astype(
        bf16
    )
    key_grad = (key_inv * (key_hat_grad - key_hat * (dots[1] / width)[:, None])).astype(bf16)
    qkv_grad = jnp.concatenate([query_grad, key_grad, value_grad], axis=1)
    input_terms = dot32(qkv_grad, qkv_full, NT).astype(bf16)
    normed_grad = sum_tensor(input_terms)
    d_qkv = dot32(normed, qkv_grad, TN).astype(bf16)

    own_inv = rms_inv(own_in)
    own_hat = own_in * own_inv
    d_attn_gain = jnp.sum(normed_grad * own_hat, axis=0)
    scaled_attn = normed_grad * gain_attn
    input_grad = resid_grad + own_inv * (
        scaled_attn - own_hat * jnp.mean(scaled_attn * own_hat, axis=-1, keepdims=True)
    )

    def widen(slots):
        return lax.dynamic_update_slice_in_dim(
            jnp.zeros((width,), f32), slots, column * local_width, 0
        )

    small = jnp.concatenate(
        [
            d_router.T,
            jnp.stack([d_attn_gain, widen(d_query_gain), widen(d_key_gain), d_ffn_gain]),
        ]
    )
    small = lax.psum_scatter(small, "expert", scatter_dimension=1, tiled=True)
    small = lax.psum(small, "tensor")
    sum_router = small[:expert_count].T
    sum_gains = small[expert_count:]

    back_out, back_in, sum_qkv = last_exchange(
        output_own.reshape(blocks, piece, width),
        input_grad.astype(bf16).reshape(blocks, piece, width),
        d_qkv.reshape(blocks, -1, d_qkv.shape[1]),
    )
    came = lax.dynamic_slice(deal_grid, (0, block, 0, 0), (blocks, 1, parts, piece))
    came = jnp.swapaxes(came.reshape(blocks, parts, piece), 0, 1).reshape(-1) - block * rows
    chooser = (jnp.arange(rows, dtype=jnp.int32)[:, None] == came[None, :]).astype(bf16)
    output = dot32(chooser, back_out.reshape(rows, width), NN).astype(bf16)
    d_tokens = dot32(chooser, back_in.reshape(rows, width), NN).astype(bf16)
    return (
        output,
        d_tokens,
        sum_gains[0],
        sum_qkv[:, :local_width],
        sum_qkv[:, local_width : 2 * local_width],
        sum_qkv[:, 2 * local_width :],
        sum_wo.astype(f32),
        sum_gains[1],
        sum_gains[2],
        sum_gains[3],
        sum_router,
        d_w_gate,
        d_w_up,
        d_w_down,
    )


def pick_body(*args):
    routes, experts = args[14], args[9].shape[1]
    mesh_fits = (lax.axis_size("expert"), lax.axis_size("tensor")) == (8, 4)
    body = dense_body if mesh_fits and experts <= 2 * routes.shape[1] else routed_body
    return body(*args)


def solution(mesh):
    in_specs = (
        P("expert", None),
        P("expert"),
        P("expert", "tensor"),
        P("expert", "tensor"),
        P("expert", "tensor"),
        P("tensor", "expert"),
        P("expert"),
        P("expert"),
        P("expert"),
        P("expert", None),
        P("expert", None, "tensor"),
        P("expert", None, "tensor"),
        P("expert", "tensor", None),
        P("expert"),
        P("expert", None),
        P(),
        P("expert", None),
    )
    out_specs = (
        P("expert", None),
        P("expert", None),
        P("expert"),
        P("expert", "tensor"),
        P("expert", "tensor"),
        P("expert", "tensor"),
        P("tensor", "expert"),
        P("expert"),
        P("expert"),
        P("expert"),
        P("expert", None),
        P("expert", None, "tensor"),
        P("expert", None, "tensor"),
        P("expert", "tensor", None),
    )
    return jax.shard_map(pick_body, mesh=mesh, in_specs=in_specs, out_specs=out_specs, check_vma=False)
```

```python
import functools
import math

import jax
import jax.numpy as jnp
from jax import lax
from jax.experimental import pallas as pl
from jax.experimental.pallas import tpu as pltpu
from jax.sharding import PartitionSpec as P

HEAD_DIM = 128


NORM_EPS = 1e-05
ROPE_BASE = 10000.0


def rope_tables(documents, head_size):
    row_count = documents.shape[0]
    positions = jnp.arange(row_count, dtype=jnp.int32)
    new_doc = jnp.concatenate(
        [jnp.ones((1,), jnp.int32), (documents[1:] != documents[:-1]).astype(jnp.int32)]
    )
    starts = lax.cummax(jnp.where(new_doc > 0, positions, 0), axis=0)
    places = (positions - starts).astype(jnp.float32)
    half_dim = head_size // 2
    frequency = jnp.exp(
        jnp.arange(half_dim, dtype=jnp.float32) * (-2.0 * math.log(ROPE_BASE) / head_size)
    )
    angles = places[:, None] * frequency[None, :]
    return (jnp.cos(angles), jnp.sin(angles))


def rotate(values, cosines, sines):
    half_dim = values.shape[-1] // 2
    first_half = values[..., :half_dim]
    second_half = values[..., half_dim:]
    cos_rows = cosines[:, None, :]
    sin_rows = sines[:, None, :]
    return jnp.concatenate(
        [
            first_half * cos_rows - second_half * sin_rows,
            second_half * cos_rows + first_half * sin_rows,
        ],
        axis=-1,
    )


def unrotate(grads_in, cosines, sines):
    half_dim = grads_in.shape[-1] // 2
    first_half = grads_in[..., :half_dim]
    second_half = grads_in[..., half_dim:]
    cos_rows = cosines[:, None, :]
    sin_rows = sines[:, None, :]
    return jnp.concatenate(
        [
            first_half * cos_rows + second_half * sin_rows,
            second_half * cos_rows - first_half * sin_rows,
        ],
        axis=-1,
    )


def to_experts(rows):
    return lax.all_to_all(rows, "expert", split_axis=0, concat_axis=0, tiled=True)


def from_experts(rows):
    return lax.all_to_all(rows, "expert", split_axis=0, concat_axis=0, tiled=True)


def hidden_sums(terms):
    return lax.psum_scatter(terms, "tensor", scatter_dimension=3, tiled=True)


def routed_body(
    tokens,
    attn_gain,
    w_query,
    w_key,
    w_value,
    w_out,
    query_gain,
    key_gain,
    ffn_gain,
    w_router,
    w_gate,
    w_up,
    w_down,
    doc_ids,
    routes,
    deal,
    out_grad,
):
    row_count, width = tokens.shape
    tensor_parts = lax.axis_size("tensor")
    expert_parts = lax.axis_size("expert")
    column = lax.axis_index("tensor")
    device_idx = lax.axis_index("expert")
    quarter = width // tensor_parts
    share_rows = row_count // expert_parts
    deal_rows = lax.dynamic_slice_in_dim(
        deal.reshape(expert_parts, row_count), device_idx * share_rows, share_rows, 1
    )
    local_pick = deal_rows - device_idx * row_count
    dealt_tokens, dealt_grad = (
        lax.all_to_all(tokens[local_pick], "expert", split_axis=0, concat_axis=0, tiled=True),
        lax.all_to_all(out_grad[local_pick], "expert", split_axis=0, concat_axis=0, tiled=True),
    )
    dealt_tokens = dealt_tokens.reshape(row_count, width)
    dealt_grad = dealt_grad.reshape(row_count, width)
    gain_stack = jnp.stack([attn_gain, query_gain, key_gain, ffn_gain])
    wq_full, wk_full, wv_full, wo_full, router_full, gain_full = (
        lax.all_gather(w_query, "expert", axis=0, tiled=True),
        lax.all_gather(w_key, "expert", axis=0, tiled=True),
        lax.all_gather(w_value, "expert", axis=0, tiled=True),
        lax.all_gather(w_out, "expert", axis=1, tiled=True),
        lax.all_gather(w_router, "expert", axis=0, tiled=True),
        lax.all_gather(gain_stack, "expert", axis=1, tiled=True),
    )
    local_width = wq_full.shape[1]
    head_count = local_width // HEAD_DIM
    gain_attn = gain_full[0].astype(jnp.float32)
    gain_query = lax.dynamic_slice_in_dim(
        gain_full[1].astype(jnp.float32), column * local_width, local_width
    )
    gain_key = lax.dynamic_slice_in_dim(
        gain_full[2].astype(jnp.float32), column * local_width, local_width
    )
    gain_ffn = gain_full[3].astype(jnp.float32)
    scale = 1.0 / math.sqrt(HEAD_DIM)
    inputs = dealt_tokens.astype(jnp.float32)
    input_inv = lax.rsqrt(jnp.mean(inputs * inputs, axis=-1, keepdims=True) + NORM_EPS)
    input_hat = inputs * input_inv
    normed = (input_hat * gain_attn).astype(jnp.bfloat16)
    query_pre = jnp.dot(normed, wq_full, preferred_element_type=jnp.float32)
    key_pre = jnp.dot(normed, wk_full, preferred_element_type=jnp.float32)
    value_rows = (
        jnp.dot(normed, wv_full, preferred_element_type=jnp.float32)
        .astype(jnp.bfloat16)
        .reshape(row_count, head_count, HEAD_DIM)
    )
    query_sq, key_sq = lax.psum(
        (jnp.sum(query_pre * query_pre, axis=-1), jnp.sum(key_pre * key_pre, axis=-1)), "tensor"
    )
    query_inv = lax.rsqrt(query_sq / width + NORM_EPS)[:, None]
    key_inv = lax.rsqrt(key_sq / width + NORM_EPS)[:, None]
    query_hat = query_pre * query_inv
    key_hat = key_pre * key_inv
    cosines, sines = rope_tables(doc_ids, HEAD_DIM)
    query_rot = rotate(
        (query_hat * gain_query).reshape(row_count, head_count, HEAD_DIM), cosines, sines
    ).astype(jnp.bfloat16)
    key_rot = rotate(
        (key_hat * gain_key).reshape(row_count, head_count, HEAD_DIM), cosines, sines
    ).astype(jnp.bfloat16)
    positions = jnp.arange(row_count, dtype=jnp.int32)
    allowed = (doc_ids[:, None] == doc_ids[None, :]) & (positions[None, :] <= positions[:, None])

    def masked_scores():
        raw_scores = jnp.einsum(
            "qhd,khd->hqk", query_rot, key_rot, preferred_element_type=jnp.float32
        )
        return jnp.where(allowed[None], raw_scores * scale, -1e30)

    scores = masked_scores()
    top_score = jnp.max(scores, axis=-1, keepdims=True)
    log_total = top_score + jnp.log(jnp.sum(jnp.exp(scores - top_score), axis=-1, keepdims=True))
    weights = jnp.exp(scores - log_total).astype(jnp.bfloat16)
    attended = (
        jnp.einsum("hqk,khd->qhd", weights, value_rows, preferred_element_type=jnp.float32)
        .astype(jnp.bfloat16)
        .reshape(row_count, local_width)
    )
    branch = lax.psum(jnp.dot(attended, wo_full, preferred_element_type=jnp.float32), "tensor")
    residual = inputs + branch
    resid_inv = lax.rsqrt(jnp.mean(residual * residual, axis=-1, keepdims=True) + NORM_EPS)
    resid_hat = residual * resid_inv
    ffn_in = (resid_hat * gain_ffn).astype(jnp.bfloat16)
    logits = jnp.dot(ffn_in, router_full, preferred_element_type=jnp.float32)
    router_probs = jax.nn.softmax(logits, axis=-1)
    expert_count = router_full.shape[1]
    top_count = routes.shape[1]
    local_experts = expert_count // expert_parts
    capacity = tensor_parts * max(
        1,
        (row_count * top_count + expert_count * tensor_parts - 1) // (expert_count * tensor_parts),
        row_count * top_count * 5 // (4 * expert_count * tensor_parts),
    )
    expert_ids = jnp.arange(expert_count, dtype=jnp.int32)
    route_match = routes[:, :, None] == expert_ids[None, None, :]
    gate_probs = jnp.sum(jnp.where(route_match, router_probs[:, None, :], 0.0), axis=-1)
    flat_routes = routes.reshape(-1)
    onehot = (flat_routes[:, None] == expert_ids[None, :]).astype(jnp.int32)
    slot_rank = jnp.sum((jnp.cumsum(onehot, axis=0) - onehot) * onehot, axis=-1)
    row_ids = flat_routes * capacity + slot_rank
    token_ids = jnp.arange(row_count * top_count, dtype=jnp.int32) // top_count
    slot_token = (
        jnp.full((expert_count * capacity,), row_count, jnp.int32).at[row_ids].set(token_ids)
    )
    slot_gates = (
        jnp.zeros((expert_count * capacity,), jnp.float32).at[row_ids].set(gate_probs.reshape(-1))
    )
    pick_rows = row_ids.reshape(row_count, top_count)
    padded_in = jnp.concatenate([ffn_in, jnp.zeros((1, width), jnp.bfloat16)], axis=0)
    grad_full = dealt_grad.astype(jnp.float32)
    grad_padded = jnp.concatenate([grad_full, jnp.zeros((1, width), jnp.float32)], axis=0)
    received = to_experts(
        padded_in[slot_token].reshape(expert_parts, local_experts, capacity, width)
    )
    gate_pre = jnp.einsum("secd,edf->secf", received, w_gate, preferred_element_type=jnp.float32)
    up_pre = jnp.einsum("secd,edf->secf", received, w_up, preferred_element_type=jnp.float32)
    sigmoid_gate = jax.nn.sigmoid(gate_pre)
    silu_gate = gate_pre * sigmoid_gate
    hidden = (silu_gate * up_pre).astype(jnp.bfloat16)
    partial_out = jnp.einsum("secf,efd->secd", hidden, w_down, preferred_element_type=jnp.float32)
    own_columns = hidden_sums(partial_out).astype(jnp.bfloat16)
    returned = from_experts(own_columns).reshape(expert_count * capacity, quarter)
    chosen = returned[pick_rows].astype(jnp.float32)
    mix_own = jnp.sum(gate_probs[:, :, None] * chosen, axis=1)
    mix_part = lax.dynamic_update_slice_in_dim(
        jnp.zeros((row_count, width), jnp.float32), mix_own, column * quarter, 1
    )
    grad_own = lax.dynamic_slice_in_dim(grad_full, column * quarter, quarter, 1)
    gate_grad_part = jnp.sum(grad_own[:, None, :] * chosen, axis=-1)
    send_grad = (
        (grad_padded[slot_token] * slot_gates[:, None])
        .astype(jnp.bfloat16)
        .reshape(expert_parts, local_experts, capacity, width)
    )
    recv_grad = to_experts(send_grad)
    d_w_down = jnp.einsum("secf,secd->efd", hidden, recv_grad, preferred_element_type=jnp.float32)
    hidden_grad = jnp.einsum(
        "secd,efd->secf", recv_grad, w_down, preferred_element_type=jnp.float32
    )
    gate_grad_pre = (
        hidden_grad * up_pre * sigmoid_gate * (1.0 + gate_pre * (1.0 - sigmoid_gate))
    ).astype(jnp.bfloat16)
    up_grad_pre = (hidden_grad * silu_gate).astype(jnp.bfloat16)
    d_w_gate = jnp.einsum(
        "secd,secf->edf", received, gate_grad_pre, preferred_element_type=jnp.float32
    )
    d_w_up = jnp.einsum("secd,secf->edf", received, up_grad_pre, preferred_element_type=jnp.float32)
    joined_grad = jnp.concatenate([gate_grad_pre, up_grad_pre], axis=-1)
    joined_weight = jnp.concatenate([w_gate, w_up], axis=-1)
    row_terms = jnp.einsum(
        "secf,edf->secd", joined_grad, joined_weight, preferred_element_type=jnp.float32
    )
    row_own = hidden_sums(row_terms).astype(jnp.bfloat16)
    row_back = from_experts(row_own).reshape(expert_count * capacity, quarter)
    ffn_grad_own = jnp.sum(row_back[pick_rows].astype(jnp.float32), axis=1)
    placed = lax.dynamic_update_slice_in_dim(
        jnp.zeros((row_count, width), jnp.float32), ffn_grad_own, column * quarter, 1
    )
    ffn_grad_rows, gate_grad, mix_total = lax.psum((placed, gate_grad_part, mix_part), "tensor")
    output = (residual + mix_total).astype(jnp.bfloat16)
    prob_grad = jnp.sum(jnp.where(route_match, gate_grad[:, :, None], 0.0), axis=1)
    logit_grad = (
        router_probs * (prob_grad - jnp.sum(router_probs * prob_grad, axis=-1, keepdims=True))
    ).astype(jnp.bfloat16)
    d_router = jnp.einsum("rd,re->de", ffn_in, logit_grad, preferred_element_type=jnp.float32)
    ffn_grad = ffn_grad_rows + jnp.einsum(
        "re,de->rd", logit_grad, router_full, preferred_element_type=jnp.float32
    )
    d_ffn_gain = jnp.sum(ffn_grad * resid_hat, axis=0)
    scaled_ffn = ffn_grad * gain_ffn
    resid_grad = grad_full + resid_inv * (
        scaled_ffn - resid_hat * jnp.mean(scaled_ffn * resid_hat, axis=-1, keepdims=True)
    )
    branch_grad = resid_grad.astype(jnp.bfloat16)
    d_wo = jnp.einsum("rk,rd->kd", attended, branch_grad, preferred_element_type=jnp.float32)
    attended_grad = (
        jnp.einsum("rd,kd->rk", branch_grad, wo_full, preferred_element_type=jnp.float32)
        .astype(jnp.bfloat16)
        .reshape(row_count, head_count, HEAD_DIM)
    )
    probs_again = jnp.exp(masked_scores() - log_total)
    prob_grads = jnp.einsum(
        "qhd,khd->hqk", attended_grad, value_rows, preferred_element_type=jnp.float32
    )
    value_grad = (
        jnp.einsum(
            "hqk,qhd->khd",
            probs_again.astype(jnp.bfloat16),
            attended_grad,
            preferred_element_type=jnp.float32,
        )
        .astype(jnp.bfloat16)
        .reshape(row_count, local_width)
    )
    row_delta = jnp.sum(probs_again * prob_grads, axis=-1, keepdims=True)
    score_grad = (probs_again * (prob_grads - row_delta) * scale).astype(jnp.bfloat16)
    query_rot_grad = jnp.einsum(
        "hqk,khd->qhd", score_grad, key_rot, preferred_element_type=jnp.float32
    )
    key_rot_grad = jnp.einsum(
        "hqk,qhd->khd", score_grad, query_rot, preferred_element_type=jnp.float32
    )
    query_norm_grad = unrotate(query_rot_grad, cosines, sines).reshape(row_count, local_width)
    key_norm_grad = unrotate(key_rot_grad, cosines, sines).reshape(row_count, local_width)
    query_hat_grad = query_norm_grad * gain_query
    key_hat_grad = key_norm_grad * gain_key
    gain_pieces = jnp.stack(
        [jnp.sum(query_norm_grad * query_hat, axis=0), jnp.sum(key_norm_grad * key_hat, axis=0)]
    )
    gain_parts = lax.dynamic_update_slice_in_dim(
        jnp.zeros((2, width), jnp.float32), gain_pieces, column * local_width, 1
    )
    query_dot, key_dot, qk_gains = lax.psum(
        (
            jnp.sum(query_hat_grad * query_hat, axis=-1),
            jnp.sum(key_hat_grad * key_hat, axis=-1),
            gain_parts,
        ),
        "tensor",
    )
    query_grad = (query_inv * (query_hat_grad - query_hat * (query_dot / width)[:, None])).astype(
        jnp.bfloat16
    )
    key_grad = (key_inv * (key_hat_grad - key_hat * (key_dot / width)[:, None])).astype(
        jnp.bfloat16
    )
    d_wq = jnp.einsum("rd,rk->dk", normed, query_grad, preferred_element_type=jnp.float32)
    d_wk = jnp.einsum("rd,rk->dk", normed, key_grad, preferred_element_type=jnp.float32)
    d_wv = jnp.einsum("rd,rk->dk", normed, value_grad, preferred_element_type=jnp.float32)
    input_terms = jnp.einsum("rk,dk->rd", query_grad, wq_full, preferred_element_type=jnp.float32)
    input_terms = input_terms + jnp.einsum(
        "rk,dk->rd", key_grad, wk_full, preferred_element_type=jnp.float32
    )
    input_terms = input_terms + jnp.einsum(
        "rk,dk->rd", value_grad, wv_full, preferred_element_type=jnp.float32
    )
    normed_grad = lax.psum(input_terms, "tensor")
    d_attn_part = jnp.sum(normed_grad * input_hat, axis=0)
    scaled_attn = normed_grad * gain_attn
    input_grad = resid_grad + input_inv * (
        scaled_attn - input_hat * jnp.mean(scaled_attn * input_hat, axis=-1, keepdims=True)
    )
    dealt_dtokens = input_grad.astype(jnp.bfloat16)
    gain_grads = jnp.stack([d_attn_part, qk_gains[0], qk_gains[1], d_ffn_gain])
    sum_wq, sum_wk, sum_wv, sum_wo, sum_router, sum_gains = (
        lax.psum_scatter(d_wq, "expert", scatter_dimension=0, tiled=True),
        lax.psum_scatter(d_wk, "expert", scatter_dimension=0, tiled=True),
        lax.psum_scatter(d_wv, "expert", scatter_dimension=0, tiled=True),
        lax.psum_scatter(d_wo, "expert", scatter_dimension=1, tiled=True),
        lax.psum_scatter(d_router, "expert", scatter_dimension=0, tiled=True),
        lax.psum_scatter(gain_grads, "expert", scatter_dimension=1, tiled=True),
    )
    back_out, back_dtok = (
        lax.all_to_all(
            output.reshape(expert_parts, share_rows, width),
            "expert",
            split_axis=0,
            concat_axis=0,
            tiled=True,
        ),
        lax.all_to_all(
            dealt_dtokens.reshape(expert_parts, share_rows, width),
            "expert",
            split_axis=0,
            concat_axis=0,
            tiled=True,
        ),
    )
    flat_pick = local_pick.reshape(-1)
    output_rows = (
        jnp.zeros((row_count, width), jnp.bfloat16)
        .at[flat_pick]
        .set(back_out.reshape(row_count, width))
    )
    d_tokens = (
        jnp.zeros((row_count, width), jnp.bfloat16)
        .at[flat_pick]
        .set(back_dtok.reshape(row_count, width))
    )
    return (
        output_rows,
        d_tokens,
        sum_gains[0],
        sum_wq,
        sum_wk,
        sum_wv,
        sum_wo,
        sum_gains[1],
        sum_gains[2],
        sum_gains[3],
        sum_router,
        d_w_gate,
        d_w_up,
        d_w_down,
    )


MESH_ID = pl.DeviceIdType.MESH
ANY = pl.BlockSpec(memory_space=pl.ANY)
IN_VMEM = pl.BlockSpec(memory_space=pltpu.VMEM)
def cost_of(micros):
    return pl.CostEstimate(flops=0, bytes_accessed=micros * 3_000_000, transcendentals=0)


SELF, NEAR, FAR, BOTH_FLIPPED = 0, 1, 2, 3


def place_of(device):
    expert, tensor = device
    return expert // 2, expert % 2, tensor // 2, tensor % 2


def flipped(device, role):
    expert, tensor = device
    _, x, y, core = place_of(device)
    step_x, step_y = 1 - 2 * x, 2 - 4 * y
    if role == NEAR:
        return expert + (1 - core) * step_x, tensor + core * step_y
    if role == FAR:
        return expert + core * step_x, tensor + (1 - core) * step_y
    if role == BOTH_FLIPPED:
        return expert + step_x, tensor + step_y
    return expert, tensor


def moved_z(device, hops):
    expert, tensor = device
    return lax.rem(expert + 2 * hops, 8), tensor


def sibling(device):
    expert, tensor = device
    return expert, tensor + 1 - 2 * (tensor % 2)


def slot_of(device):
    return device[0] * 4 + device[1]


def here():
    return lax.axis_index("expert"), lax.axis_index("tensor")


def greet(partners):
    barrier = pltpu.get_barrier_semaphore()
    for partner in partners:
        pl.semaphore_signal(barrier, inc=1, device_id=partner, device_id_type=MESH_ID)
    pl.semaphore_wait(barrier, len(partners))


def push(source, target, send_sem, recv_sem, device):
    return pltpu.make_async_remote_copy(
        src_ref=source,
        dst_ref=target,
        send_sem=send_sem,
        recv_sem=recv_sem,
        device_id=device,
        device_id_type=MESH_ID,
    )


def hop(device, flips, hops):
    expert, tensor = device
    return lax.rem(expert + flips * (1 - 2 * lax.rem(expert, 2)) + 2 * hops, 8), tensor


def across_y(device):
    expert, tensor = device
    return expert, lax.rem(tensor + 2, 4)


class Line:
    def __init__(self, send_sem, recv_sem):
        self.send_sem, self.recv_sem = send_sem, recv_sem
        self.started = []

    def send(self, source, target, tag, recv_tag, device):
        copy = push(source, target, self.send_sem.at[tag], self.recv_sem.at[recv_tag], device)
        copy.start()
        self.started.append(copy)

    def wait(self, target, tag, device):
        push(target, target, self.send_sem.at[0], self.recv_sem.at[tag], device).wait_recv()

    def finish(self):
        for copy in self.started:
            copy.wait_send()


PIECES = ((0, 1), (1, 0), (3, 0), (1, 1), (3, 1), (2, 0), (2, 1))


def exchange_steps(source, out, gathered, line, local_sem):
    me = here()
    tensor = me[1]
    side, sib = across_y(me), sibling(me)

    def at(column, expert):
        return out.at[column, expert] if gathered else out.at[expert]

    local = pltpu.make_async_copy(source.at[me[0]], at(tensor, me[0]), local_sem)
    local.start()
    if gathered:
        line.send(source.at[me[0]], at(tensor, me[0]), 8, 8, side)
        line.send(source.at[me[0]], at(tensor, me[0]), 16, 16, sib)
    for k, flips in PIECES:
        target = hop(me, flips, k)
        line.send(
            source.at[target[0]], at(tensor, me[0]), k * 2 + flips, (4 - k) % 4 * 2 + flips, target
        )
    yield
    for k, flips in PIECES:
        expert = hop(me, flips, k)[0]
        tag = k * 2 + flips
        line.wait(at(tensor, expert), tag, sib)
        if gathered:
            line.send(at(tensor, expert), at(tensor, expert), 8 + tag, 8 + tag, side)
            line.send(at(tensor, expert), at(tensor, expert), 16 + tag, 16 + tag, sib)
        yield
    if gathered:
        for k, flips in ((0, 0),) + PIECES:
            expert = hop(me, flips, k)[0]
            tag = k * 2 + flips
            line.wait(at(side[1], expert), 8 + tag, sib)
            line.send(at(side[1], expert), at(side[1], expert), 24 + tag, 24 + tag, sib)
            yield
        for k, flips in ((0, 0),) + PIECES:
            expert = hop(me, flips, k)[0]
            tag = k * 2 + flips
            line.wait(at(sib[1], expert), 16 + tag, sib)
            line.wait(at(across_y(sib)[1], expert), 24 + tag, sib)
    local.wait()
    line.finish()


def gather_expert_steps(source, out, chunks, line, local_sem):
    me = here()
    z = me[0] // 2
    beside = hop(me, 1, 0)
    step = source.shape[0] // chunks

    def part(ref, i):
        return ref.at[pl.ds(i * step, step), :]

    local = pltpu.make_async_copy(source, out.at[me[0]], local_sem)
    local.start()

    def passes(ref, target, i, tag, origin_tag, up):
        device = hop(me, 0, 1 if up else 3)

        @pl.when((z < 3) if up else (z > 0))
        def _():
            push(ref, target, line.send_sem.at[tag], line.recv_sem.at[origin_tag], device).start()

    def base(distance, up, i):
        return ((distance - 1) * 2 + up) * chunks + i

    for i in range(chunks):
        line.send(part(source, i), part(out.at[me[0]], i), 12 * chunks + i, 12 * chunks + i, beside)
        for up in (1, 0):
            passes(part(source, i), part(out.at[me[0]], i), i, base(1, up, i), base(1, up, i), up)
    yield
    for distance in (1, 2, 3):
        for i in range(chunks):
            for up in (1, 0):
                held = (z >= distance) if up else (z + distance <= 3)
                expert = lax.rem(me[0] + (8 - 2 * distance if up else 2 * distance), 8)
                block = part(out.at[expert], i)
                tag = base(distance, up, i)

                @pl.when(held)
                def _():
                    line.wait(block, tag, beside)
                    cross = 6 * chunks + tag
                    push(block, block, line.send_sem.at[cross], line.recv_sem.at[cross], beside).start()

                if distance < 3:
                    more = base(distance + 1, up, i)

                    @pl.when(held & ((z < 3) if up else (z > 0)))
                    def _():
                        push(
                            block,
                            block,
                            line.send_sem.at[more],
                            line.recv_sem.at[more],
                            hop(me, 0, 1 if up else 3),
                        ).start()

                yield
    for i in range(chunks):
        line.wait(part(out.at[beside[0]], i), 12 * chunks + i, beside)
    for distance in (1, 2, 3):
        for i in range(chunks):
            for up in (1, 0):
                held = (z >= distance) if up else (z + distance <= 3)
                expert = lax.rem(beside[0] + (8 - 2 * distance if up else 2 * distance), 8)
                block = part(out.at[expert], i)
                cross = 6 * chunks + base(distance, up, i)
                sent_on = (z + 1 >= distance) & (z < 3) if up else (z - 1 + distance <= 3) & (z > 0)

                @pl.when(held)
                def _():
                    both = push(block, block, line.send_sem.at[cross], line.recv_sem.at[cross], beside)
                    both.wait()

                @pl.when(sent_on)
                def _():
                    tag = base(distance, up, i)
                    push(
                        block, block, line.send_sem.at[tag], line.recv_sem.at[tag], beside
                    ).wait_send()

        yield
    local.wait()
    line.finish()


def sum_rows(target, terms, step=16):
    def body(i, carry):
        window = pl.ds(pl.multiple_of(i * step, step), step)
        value = terms[0][window, :].astype(jnp.float32)
        for ref in terms[1:]:
            value = value + ref[window, :].astype(jnp.float32)
        target[window, :] = value.astype(target.dtype)
        return carry

    lax.fori_loop(0, target.shape[0] // step, body, 0)


def sum_expert_steps(part, out, mine, from_x, from_z, line, load_sem):
    me = here()
    beside = hop(me, 1, 0)
    loads = {}
    for k in (2, 1, 3, 0):
        line.send(part.at[hop(me, 1, k)[0]], from_x.at[k], k, k, beside)
        loads[k] = pltpu.make_async_copy(part.at[hop(me, 0, k)[0]], mine.at[k], load_sem.at[k])
        loads[k].start()
    yield
    for k in (2, 1, 3, 0):
        loads[k].wait()
        line.wait(from_x.at[k], k, beside)
        if k:
            sum_rows(mine.at[k], [mine.at[k], from_x.at[k]])
            line.send(mine.at[k], from_z.at[3 - k], 3 + k, 4 + 3 - k, hop(me, 0, k))
            yield
            yield
    for i in range(3):
        line.wait(from_z.at[i], 4 + i, beside)
    sum_rows(out, [mine.at[0], from_x.at[0], from_z.at[0], from_z.at[1], from_z.at[2]])
    line.finish()


def take_turns(steps):
    steps = list(steps)
    while steps:
        steps = [s for s in steps if next(s, steps) is not steps]


DMA = pltpu.SemaphoreType.DMA


def start_kernel(tokens, grads, weights, small, o_tokens, o_grads, o_weights, o_small, *sems):
    me = here()
    pieces = [hop(me, flips, k) for k, flips in PIECES]
    greet(pieces + [across_y(me), sibling(me)])
    local = sems[8]
    take_turns(
        [
            exchange_steps(tokens, o_tokens, True, Line(sems[0], sems[1]), local.at[0]),
            exchange_steps(grads, o_grads, False, Line(sems[2], sems[3]), local.at[1]),
            gather_expert_steps(small, o_small, 1, Line(sems[6], sems[7]), local.at[3]),
            gather_expert_steps(weights, o_weights, 4, Line(sems[4], sems[5]), local.at[2]),
        ]
    )


def start_exchange(tokens, grads, weights, small):
    piece = tokens.shape[1:]
    sds = jax.ShapeDtypeStruct
    return pl.pallas_call(
        start_kernel,
        out_shape=[
            sds((4, 8) + piece, tokens.dtype),
            sds((8,) + piece, grads.dtype),
            sds((8,) + weights.shape, weights.dtype),
            sds((8,) + small.shape, small.dtype),
        ],
        in_specs=[IN_VMEM] * 4,
        out_specs=[ANY] * 4,
        scratch_shapes=[DMA((32,)), DMA((32,)), DMA((8,)), DMA((8,))]
        + [DMA((52,)), DMA((52,)), DMA((13,)), DMA((13,)), DMA((4,))],
        compiler_params=pltpu.CompilerParams(
            collective_id=4, has_side_effects=True, vmem_limit_bytes=16 * 2**20
        ),
        cost_estimate=cost_of(100),
        name="start_exchange",
    )(tokens, grads, weights, small)


def last_kernel(rows, more, part, o_rows, o_more, out, mine, from_x, from_z, *sems):
    me = here()
    pieces = [hop(me, flips, k) for k, flips in PIECES]
    greet(pieces + [across_y(me), sibling(me)])
    take_turns(
        [
            exchange_steps(more, o_more, True, Line(sems[2], sems[3]), sems[7].at[1]),
            exchange_steps(rows, o_rows, True, Line(sems[0], sems[1]), sems[7].at[0]),
            sum_expert_steps(part, out, mine, from_x, from_z, Line(sems[4], sems[5]), sems[6]),
        ]
    )


def last_exchange(rows, more, part):
    piece = rows.shape[1:]
    block = part.shape[1:]
    sds = jax.ShapeDtypeStruct
    return pl.pallas_call(
        last_kernel,
        out_shape=[
            sds((4, 8) + piece, rows.dtype),
            sds((4, 8) + piece, more.dtype),
            sds(block, jnp.float32),
        ],
        in_specs=[IN_VMEM, IN_VMEM, ANY],
        out_specs=[ANY, ANY, IN_VMEM],
        scratch_shapes=[
            pltpu.VMEM((4,) + block, part.dtype),
            pltpu.VMEM((4,) + block, part.dtype),
            pltpu.VMEM((3,) + block, part.dtype),
        ]
        + [DMA((32,))] * 4
        + [DMA((8,)), DMA((8,)), DMA((4,)), DMA((2,))],
        compiler_params=pltpu.CompilerParams(
            collective_id=5, has_side_effects=True, vmem_limit_bytes=32 * 2**20
        ),
        cost_estimate=cost_of(100),
        name="last_exchange",
    )(rows, more, part)


def gather_tensor_kernel(source, out, send_sem, recv_sem, local_sem):
    me = here()
    side, sib = across_y(me), sibling(me)
    greet([side, sib])
    line = Line(send_sem, recv_sem)
    halves = 4
    step = source.shape[0] // halves

    def part(ref, i):
        return ref.at[pl.ds(i * step, step), :]

    local = pltpu.make_async_copy(source, out.at[me[1]], local_sem)
    for i in range(halves):
        line.send(part(source, i), part(out.at[me[1]], i), i, i, side)
        line.send(part(source, i), part(out.at[me[1]], i), 4 + i, 4 + i, sib)
    local.start()
    for i in range(halves):
        got = part(out.at[side[1]], i)
        line.wait(got, i, sib)
        line.send(got, got, 8 + i, 8 + i, sib)
    for i in range(halves):
        line.wait(part(out.at[sib[1]], i), 4 + i, sib)
        line.wait(part(out.at[across_y(sib)[1]], i), 8 + i, sib)
    local.wait()
    line.finish()


def gather_tensor(rows):
    out = pl.pallas_call(
        gather_tensor_kernel,
        out_shape=jax.ShapeDtypeStruct((4,) + rows.shape, rows.dtype),
        in_specs=[IN_VMEM],
        out_specs=ANY,
        scratch_shapes=[DMA((12,)), DMA((12,)), DMA],
        compiler_params=pltpu.CompilerParams(
            collective_id=6, has_side_effects=True, vmem_limit_bytes=8 * 2**20
        ),
        cost_estimate=cost_of(15),
        name="gather_tensor",
    )(rows)
    return out.reshape((-1,) + rows.shape[1:])


def sum_tensor_kernel(part, out, from_sib, from_side, total, send_sem, recv_sem):
    me = here()
    side, sib = across_y(me), sibling(me)
    greet([side, sib])
    line = Line(send_sem, recv_sem)
    pieces = 4
    step = out.shape[0] // pieces

    def rows(ref, i):
        return ref.at[pl.ds(i * step, step), :]

    for j, column in ((0, across_y(sib)[1]), (1, sib[1])):
        for i in range(pieces):
            line.send(
                rows(part.at[column], i), rows(from_sib.at[j], i), 4 * j + i, 4 * j + i, sib
            )
    for i in range(pieces):
        got = rows(from_sib.at[0], i)
        line.wait(got, i, sib)
        sum_rows(rows(total, i), [rows(part.at[side[1]], i), got])
        line.send(rows(total, i), rows(from_side, i), 8 + i, 8 + i, side)
    for i in range(pieces):
        got = rows(from_sib.at[1], i)
        line.wait(got, 4 + i, sib)
        line.wait(rows(from_side, i), 8 + i, sib)
        sum_rows(rows(out, i), [rows(part.at[me[1]], i), got, rows(from_side, i)])
    line.finish()


def sum_tensor(partial):
    block = (partial.shape[0] // 4, partial.shape[1])
    return pl.pallas_call(
        sum_tensor_kernel,
        out_shape=jax.ShapeDtypeStruct(block, jnp.float32),
        in_specs=[IN_VMEM],
        out_specs=IN_VMEM,
        scratch_shapes=[
            pltpu.VMEM((2,) + block, partial.dtype),
            pltpu.VMEM(block, partial.dtype),
            pltpu.VMEM(block, partial.dtype),
            DMA((12,)),
            DMA((12,)),
        ],
        compiler_params=pltpu.CompilerParams(
            collective_id=7, has_side_effects=True, vmem_limit_bytes=12 * 2**20
        ),
        cost_estimate=cost_of(15),
        name="sum_tensor",
    )(partial.reshape((4,) + block))


def rows_at(ref, slot, size, count=1):
    return ref.at[pl.ds(pl.multiple_of(slot * size, size), size * count), :]


class Plan:
    def __init__(self, send_sem, recv_sem):
        self.send_sem, self.recv_sem, self.made = send_sem, recv_sem, []

    def send(self, make):
        make().start()
        self.made.append(make)

    def finish(self):
        for make in self.made:
            make().wait_send()


def gather_plan(ins, outs, sizes, send_sem, recv_sem):
    me = here()
    near, far, sib = flipped(me, NEAR), flipped(me, FAR), sibling(me)
    plan = Plan(send_sem, recv_sem)
    count = len(ins)

    def send(k, role, device, tag, recv_tag):
        for i in range(count):

            def make(i=i):
                block = rows_at(outs[i], slot_of(moved_z(flipped(me, role), k)), sizes[i])
                source = ins[i] if (k, role) == (0, SELF) else block
                return push(source, block, send_sem.at[i, tag], recv_sem.at[i, recv_tag], device)

            plan.send(make)

    def arrive(k, role):
        for i in range(count):
            block = rows_at(outs[i], slot_of(moved_z(flipped(me, role), k)), sizes[i])
            push(block, block, send_sem.at[i, 0], recv_sem.at[i, k * 4 + role], near).wait_recv()

    def forward(k, role):
        if role == SELF:
            send(k, SELF, far, 4 + k, k * 4 + FAR)
            send(k, SELF, near, k, k * 4 + NEAR)
        if role == NEAR:
            send(k, NEAR, far, 8 + k, k * 4 + BOTH_FLIPPED)
        send(k, role, sib, 16 + k * 4 + role, 16 + k * 4 + role)

    def event(k, role):
        arrive(k, role)
        forward(k, role)

    def from_sibling(k, role):
        for i in range(count):
            block = rows_at(outs[i], 0, sizes[i])
            push(
                block, block, send_sem.at[i, 0], recv_sem.at[i, 16 + k * 4 + role], near
            ).wait_recv()

    def begin():
        forward(0, SELF)
        for d in (1, 3, 2):
            send(0, SELF, moved_z(me, d), 11 + d, (4 - d) * 4 + SELF)

    return plan, begin, event, from_sibling


def gate_columns(gates_ref, slot, columns, first):
    lane = lax.broadcasted_iota(jnp.int32, (128, 128), 1)
    for s in range(4):
        block = gates_ref[pl.ds(pl.multiple_of((slot + s) * 16, 16), 16), :]
        turned = jnp.concatenate([block, jnp.zeros((112, 128), jnp.float32)], axis=0).T
        for i in range(2):
            column = jnp.sum(jnp.where(lane == first + i, turned, 0.0), axis=1, keepdims=True)
            columns[i, pl.ds(s * 128, 128), :] = jnp.broadcast_to(column, (128, 128))


def tiles(count, width, body):
    def step(n, carry):
        body(pl.ds(pl.multiple_of(n * width, width), width))
        return carry

    lax.fori_loop(0, count, step, 0)


STAGES = ((0, 0), (0, 1), (1, 0), (1, 1), (3, 0), (3, 1), (2, 0), (2, 1))
BLOCK = 512


def stage_expert(me, j):
    half = j // 2
    k = half + jnp.where(half == 2, 1, 0) - jnp.where(half == 3, 1, 0)
    flips = lax.rem(j, 2)
    expert = me[0]
    return lax.rem(expert + flips * (1 - 2 * lax.rem(expert, 2)) + 2 * k, 8)


def forward_kernel(
    x_own, g_own, w_joined, w_down, x_out, g_out, pre_out, gated_out, y_out,
    x_all, g_all, columns, pre, gated, y, send_sem, recv_sem, local_sem, out_sem,
):
    me = here()
    core = lax.rem(me[1], 2)
    greet(
        [flipped(me, NEAR), flipped(me, FAR), sibling(me)] + [moved_z(me, d) for d in (1, 2, 3)]
    )
    plan, begin, event, from_sibling = gather_plan(
        [x_own, g_own], [x_all, g_all], [128, 16], send_sem, recv_sem
    )
    local = [
        pltpu.make_async_copy(x_own, rows_at(x_all, slot_of(me), 128), local_sem.at[0]),
        pltpu.make_async_copy(g_own, rows_at(g_all, slot_of(me), 16), local_sem.at[1]),
    ]
    begin()
    for copy in local:
        copy.start()
    for copy in local:
        copy.wait()
    before = {
        0: [(1, SELF), (0, NEAR), (0, FAR)],
        1: [(0, BOTH_FLIPPED)],
        3: [(1, BOTH_FLIPPED)],
        5: [(3, BOTH_FLIPPED)],
        7: [(2, BOTH_FLIPPED)],
    }
    middle = {
        0: [(3, SELF), (1, NEAR)],
        1: [(1, FAR)],
        2: [(2, SELF), (3, NEAR)],
        3: [(3, FAR)],
        4: [(2, NEAR)],
        5: [(2, FAR)],
    }
    half = w_joined.shape[1] // 2

    def results(expert, slot):
        return [
            pltpu.make_async_copy(
                rows_at(x_all, expert, BLOCK), rows_at(x_out, expert, BLOCK), out_sem.at[0, slot]
            ),
            pltpu.make_async_copy(pre.at[slot], rows_at(pre_out, expert, BLOCK), out_sem.at[1, slot]),
            pltpu.make_async_copy(
                gated.at[slot], rows_at(gated_out, expert, BLOCK), out_sem.at[2, slot]
            ),
            pltpu.make_async_copy(y.at[slot], rows_at(y_out, expert, BLOCK), out_sem.at[3, slot]),
        ]

    def block(j, carry):
        slot = lax.rem(j, 2)
        expert = stage_expert(me, j)
        for n, (k, flips) in enumerate(STAGES):

            @pl.when(j == n)
            def _():
                for at in before.get(n, []):
                    event(*at)
                if n:
                    from_sibling(k, 2 - core if flips else SELF)
                    from_sibling(k, BOTH_FLIPPED if flips else 1 + core)
                else:
                    from_sibling(k, SELF)
                    from_sibling(k, 1 + core)

        @pl.when(j >= 2)
        def _():
            for copy in results(stage_expert(me, j - 2), slot):
                copy.wait()

        gate_columns(g_all, expert * 4, columns, me[0] * 2)
        x_rows = rows_at(x_all, expert, BLOCK)

        def first(cols):
            pre[slot, :, cols] = jnp.dot(
                x_rows[...], w_joined[:, cols], preferred_element_type=jnp.float32
            )

        tiles(w_joined.shape[1] // 1024, 1024, first)
        for n in middle:

            @pl.when(j == n)
            def _():
                for at in middle[n]:
                    event(*at)

        def act(r):
            for c in range(half // 128):
                cols = slice(c * 128, (c + 1) * 128)
                g = pre[slot, r, cols]
                u = pre[slot, r, half + c * 128 : half + (c + 1) * 128]
                hidden = (g * (1.0 / (1.0 + jnp.exp(-g))) * u).astype(jnp.bfloat16)
                gate = columns[c * 128 * 2 // half, r, :]
                gated[slot, r, cols] = (hidden.astype(jnp.float32) * gate).astype(jnp.bfloat16)

        tiles(BLOCK // 64, 64, act)

        def second(cols):
            y[slot, :, cols] = jnp.dot(
                gated[slot], w_down[:, cols], preferred_element_type=jnp.float32
            ).astype(jnp.bfloat16)

        tiles(w_down.shape[1] // 1024, 1024, second)
        for copy in results(expert, slot):
            copy.start()
        return carry

    lax.fori_loop(0, 8, block, 0)
    for j in (6, 7):
        for copy in results(stage_expert(me, jnp.int32(j)), j % 2):
            copy.wait()
    g_out[...] = g_all[...]
    plan.finish()


def experts_forward(ffn_in, gates_own, w_joined, w_down):
    rows, width = ffn_in.shape[0] * 32, ffn_in.shape[1]
    joined, hidden = w_joined.shape[1], w_down.shape[0]
    bf16, f32, sds = jnp.bfloat16, jnp.float32, jax.ShapeDtypeStruct
    return pl.pallas_call(
        forward_kernel,
        out_shape=[
            sds((rows, width), bf16),
            sds((512, 128), f32),
            sds((rows, joined), f32),
            sds((rows, hidden), bf16),
            sds((rows, width), bf16),
        ],
        in_specs=[IN_VMEM] * 4,
        out_specs=[ANY, IN_VMEM, ANY, ANY, ANY],
        scratch_shapes=[
            pltpu.VMEM((rows, width), bf16),
            pltpu.VMEM((512, 128), f32),
            pltpu.VMEM((2, BLOCK, 128), f32),
            pltpu.VMEM((2, BLOCK, joined), f32),
            pltpu.VMEM((2, BLOCK, hidden), bf16),
            pltpu.VMEM((2, BLOCK, width), bf16),
            DMA((2, 32)),
            DMA((2, 32)),
            DMA((2,)),
            DMA((4, 2)),
        ],
        compiler_params=pltpu.CompilerParams(
            collective_id=1, has_side_effects=True, vmem_limit_bytes=48 * 2**20
        ),
        cost_estimate=cost_of(90),
        name="experts_forward",
    )(ffn_in, gates_own, w_joined, w_down)


def sum_plan(arrays, send_sem, recv_sem, load_sem):
    me = here()
    near, far, sib = flipped(me, NEAR), flipped(me, FAR), sibling(me)
    plan = Plan(send_sem, recv_sem)
    order = (2, 1, 3, 0)

    def send(i, source, target, tag, recv_tag, device):
        plan.send(
            lambda: push(source(), target(), send_sem.at[i, tag], recv_sem.at[i, recv_tag], device())
        )

    def arrive(i, ref, tag):
        push(ref, ref, send_sem.at[i, 0], recv_sem.at[i, tag], near).wait_recv()

    def load(i, k, role):
        part, _, size, mine = arrays[i][:4]
        tag = k * 4 + role
        return pltpu.make_async_copy(
            rows_at(part, slot_of(moved_z(flipped(me, role), k)), size), mine.at[tag], load_sem.at[i, tag]
        )

    def begin():
        for roles in ((BOTH_FLIPPED, FAR), (NEAR, SELF)):
            for k in order:
                for role in roles:
                    for i, (part, _, size, _, from_sib, _, _, _) in enumerate(arrays):
                        tag = k * 4 + role
                        send(
                            i,
                            lambda part=part, size=size, k=k, role=role: rows_at(
                                part, slot_of(moved_z(flipped(sib, role), k)), size
                            ),
                            lambda from_sib=from_sib, tag=tag: from_sib.at[tag],
                            tag,
                            tag,
                            lambda: sib,
                        )
                        load(i, k, role).start()

    def collect(i, k, role):
        tag = k * 4 + role
        load(i, k, role).wait()
        from_sib = arrays[i][4]
        arrive(i, from_sib.at[tag], tag)
        return [arrays[i][3].at[tag], from_sib.at[tag]]

    def first(k, role):
        for i, (_, _, _, mine, _, from_far, _, _) in enumerate(arrays):
            tag, at = k * 4 + role, k * 2 + (role == BOTH_FLIPPED)
            terms = collect(i, k, role)
            sum_rows(mine.at[tag], terms)
            send(
                i,
                lambda mine=mine, tag=tag: mine.at[tag],
                lambda from_far=from_far, at=at: from_far.at[at],
                16 + at,
                16 + at,
                lambda: far,
            )

    def second(k):
        for i, (_, _, _, mine, _, from_far, from_near, _) in enumerate(arrays):
            tag = k * 4 + NEAR
            terms = collect(i, k, NEAR)
            arrive(i, from_far.at[k * 2 + 1], 16 + k * 2 + 1)
            sum_rows(mine.at[tag], terms + [from_far.at[k * 2 + 1]])
            send(
                i,
                lambda mine=mine, tag=tag: mine.at[tag],
                lambda from_near=from_near, k=k: from_near.at[k],
                24 + k,
                24 + k,
                lambda: near,
            )

    def third(k):
        for i, (_, out, _, mine, _, from_far, from_near, from_z) in enumerate(arrays):
            tag = k * 4 + SELF
            terms = collect(i, k, SELF)
            arrive(i, from_far.at[k * 2], 16 + k * 2)
            arrive(i, from_near.at[k], 24 + k)
            terms = terms + [from_far.at[k * 2], from_near.at[k]]
            if k > 0:
                sum_rows(mine.at[tag], terms)
                send(
                    i,
                    lambda mine=mine, tag=tag: mine.at[tag],
                    lambda from_z=from_z, k=k: from_z.at[3 - k],
                    27 + k,
                    31 - k,
                    lambda k=k: moved_z(me, k),
                )
            else:
                for d in range(3):
                    arrive(i, from_z.at[d], 28 + d)
                    terms.append(from_z.at[d])
                sum_rows(out, terms)

    return plan, begin, first, second, third


def sum_scratch(size, width, dtype):
    return [pltpu.VMEM((n, size, width), dtype) for n in (16, 16, 8, 4, 3)]


SUM_BEFORE = {0: [(2, 3), (2, 2), (1, 3), (1, 2)], 3: [(2, "third")], 5: [(1, "third")]}
SUM_MIDDLE = {
    0: [(3, 3), (3, 2), (0, 3), (0, 2)],
    1: [(2, "second")],
    2: [(1, "second")],
    4: [(3, "second")],
    6: [(0, "second")],
}


def sum_events(table, j, first, second, third):
    for n, events in table.items():

        @pl.when(j == n)
        def _():
            for k, what in events:
                if what == "second":
                    second(k)
                elif what == "third":
                    third(k)
                else:
                    first(k, what)


def greet_all(me):
    greet(
        [flipped(me, NEAR), flipped(me, FAR), sibling(me)] + [moved_z(me, d) for d in (1, 2, 3)]
    )


def backward_kernel(
    y_part, grads, pre_all, gates, w_joined, w_down, mix_out, dpre_out, drow_out, gate_grads,
    mine, from_sib, from_far, from_near, from_z, dz, pre, raw, columns, products, dpre, drow,
    send_sem, recv_sem, load_sem, in_sem, out_sem,
):
    me = here()
    greet_all(me)
    plan, begin, first, second, third = sum_plan(
        [(y_part, mix_out, 128, mine, from_sib, from_far, from_near, from_z)],
        send_sem, recv_sem, load_sem,
    )
    half = w_joined.shape[1] // 2
    expert_lanes = half // 2

    def loads(block, slot):
        return [
            pltpu.make_async_copy(rows_at(grads, block, BLOCK), dz.at[slot], in_sem.at[0, slot]),
            pltpu.make_async_copy(rows_at(pre_all, block, BLOCK), pre.at[slot], in_sem.at[1, slot]),
        ]

    def results(block, slot):
        return [
            pltpu.make_async_copy(dpre.at[slot], rows_at(dpre_out, block, BLOCK), out_sem.at[0, slot]),
            pltpu.make_async_copy(drow.at[slot], rows_at(drow_out, block, BLOCK), out_sem.at[1, slot]),
        ]

    for copy in loads(0, 0):
        copy.start()
    begin()

    def step(j, carry):
        slot = lax.rem(j, 2)

        @pl.when(j < 7)
        def _():
            for copy in loads(j + 1, 1 - slot):
                copy.start()

        sum_events(SUM_BEFORE, j, first, second, third)
        for copy in loads(j, slot):
            copy.wait()

        @pl.when(j >= 2)
        def _():
            for copy in results(j - 2, slot):
                copy.wait()

        gate_columns(gates, j * 4, columns, me[0] * 2)
        raw[...] = lax.dot_general(
            dz[slot], w_down[...], (((1,), (1,)), ((), ())), preferred_element_type=jnp.float32
        )
        sum_events(SUM_MIDDLE, j, first, second, third)

        def act(r):
            for i in range(2):
                product = None
                for c in range(i * expert_lanes, (i + 1) * expert_lanes, 128):
                    g = pre[slot, r, c : c + 128]
                    u = pre[slot, r, half + c : half + c + 128]
                    t = raw[r, c : c + 128]
                    sig = 1.0 / (1.0 + jnp.exp(-g))
                    silu = g * sig
                    hidden = (silu * u).astype(jnp.bfloat16).astype(jnp.float32)
                    term = hidden * t
                    product = term if product is None else product + term
                    dh = t * columns[i, r, :]
                    dpre[slot, r, c : c + 128] = (
                        dh * u * sig * (1.0 + g * (1.0 - sig))
                    ).astype(jnp.bfloat16)
                    dpre[slot, r, half + c : half + c + 128] = (dh * silu).astype(jnp.bfloat16)
                products[i, r, :] = product

        tiles(BLOCK // 64, 64, act)
        place = lax.broadcasted_iota(jnp.int32, (16, 128), 0)
        for s in range(4):
            sums = jnp.zeros((16, 128), jnp.float32)
            for i in range(2):
                turned = products[i, pl.ds(s * 128, 128), :].T
                row = jnp.sum(turned, axis=0, keepdims=True)
                sums = jnp.where(place == me[0] * 2 + i, jnp.broadcast_to(row, (16, 128)), sums)
            gate_grads[pl.ds(pl.multiple_of((j * 4 + s) * 16, 16), 16), :] = sums

        def back(rows):
            drow[slot, :, rows] = lax.dot_general(
                dpre[slot],
                w_joined[rows, :],
                (((1,), (1,)), ((), ())),
                preferred_element_type=jnp.float32,
            ).astype(jnp.bfloat16)

        tiles(w_joined.shape[0] // 1024, 1024, back)
        for copy in results(j, slot):
            copy.start()
        return carry

    lax.fori_loop(0, 8, step, 0)
    third(3)
    third(0)
    for j in (6, 7):
        for copy in results(j, j % 2):
            copy.wait()
    plan.finish()


def experts_backward(y_part, grads, pre, gates, w_joined, w_down):
    rows, width = grads.shape
    joined, hidden = w_joined.shape[1], w_down.shape[0]
    bf16, f32, sds = jnp.bfloat16, jnp.float32, jax.ShapeDtypeStruct
    return pl.pallas_call(
        backward_kernel,
        out_shape=[
            sds((rows // 32, width), f32),
            sds((rows, joined), bf16),
            sds((rows, width), bf16),
            sds((512, 128), f32),
        ],
        in_specs=[ANY, ANY, ANY] + [IN_VMEM] * 3,
        out_specs=[IN_VMEM, ANY, ANY, IN_VMEM],
        scratch_shapes=sum_scratch(rows // 32, width, bf16)
        + [
            pltpu.VMEM((2, BLOCK, width), bf16),
            pltpu.VMEM((2, BLOCK, joined), f32),
            pltpu.VMEM((BLOCK, hidden), f32),
            pltpu.VMEM((2, BLOCK, 128), f32),
            pltpu.VMEM((2, BLOCK, 128), f32),
            pltpu.VMEM((2, BLOCK, joined), bf16),
            pltpu.VMEM((2, BLOCK, width), bf16),
            DMA((1, 32)),
            DMA((1, 32)),
            DMA((1, 16)),
            DMA((2, 2)),
            DMA((2, 2)),
        ],
        compiler_params=pltpu.CompilerParams(
            collective_id=2, has_side_effects=True, vmem_limit_bytes=56 * 2**20
        ),
        cost_estimate=cost_of(90),
        name="experts_backward",
    )(y_part, grads, pre, gates, w_joined, w_down)


def weights_kernel(
    drow, gate_grads, x_all, grads, dpre_all, gated_all, row_out, gate_out, d_gate, d_up, d_down,
    mine, from_sib, from_far, from_near, from_z, mine_g, sib_g, far_g, near_g, z_g,
    dpre, gated, tile, wide, send_sem, recv_sem, load_sem, in_sem, tile_sem, out_sem,
):
    me = here()
    greet_all(me)
    plan, begin, first, second, third = sum_plan(
        [
            (drow, row_out, 128, mine, from_sib, from_far, from_near, from_z),
            (gate_grads, gate_out, 16, mine_g, sib_g, far_g, near_g, z_g),
        ],
        send_sem, recv_sem, load_sem,
    )
    span = tile.shape[2]
    steps = x_all.shape[1] // span
    hidden = d_gate.shape[2]
    begin()
    held = [
        pltpu.make_async_copy(dpre_all, dpre, in_sem.at[0]),
        pltpu.make_async_copy(gated_all, gated, in_sem.at[1]),
    ]

    def columns_of(j):
        return pl.ds(pl.multiple_of(lax.rem(j, steps) * span, span), span)

    def fetch(j, slot, act):
        @pl.when(j < steps)
        def _():
            act(pltpu.make_async_copy(x_all.at[:, columns_of(j)], tile.at[slot], tile_sem.at[slot]))

        @pl.when((j >= steps) & (j < 2 * steps))
        def _():
            act(pltpu.make_async_copy(grads.at[:, columns_of(j)], tile.at[slot], tile_sem.at[slot]))

    def results(j, slot, act):
        cols = columns_of(j)

        @pl.when(j < steps)
        def _():
            for i in range(2):
                act(
                    pltpu.make_async_copy(
                        wide.at[slot, :, pl.ds(i * hidden, hidden)], d_gate.at[i, cols, :], out_sem.at[slot, i]
                    )
                )
                act(
                    pltpu.make_async_copy(
                        wide.at[slot, :, pl.ds((2 + i) * hidden, hidden)],
                        d_up.at[i, cols, :],
                        out_sem.at[slot, 2 + i],
                    )
                )

        @pl.when(j >= steps)
        def _():
            act(
                pltpu.make_async_copy(
                    wide.at[slot, :, pl.ds(0, span)], d_down.at[:, cols], out_sem.at[slot, 0]
                )
            )

    fetch(jnp.int32(0), 0, lambda copy: copy.start())
    for copy in held:
        copy.start()

    def step(j, carry):
        slot = lax.rem(j, 2)
        fetch(j + 1, 1 - slot, lambda copy: copy.start())
        sum_events(SUM_BEFORE, j, first, second, third)

        @pl.when(j == 0)
        def _():
            for copy in held:
                copy.wait()

        fetch(j, slot, lambda copy: copy.wait())

        @pl.when(j >= 2)
        def _():
            results(j - 2, slot, lambda copy: copy.wait())

        @pl.when(j < steps)
        def _():
            wide[slot] = lax.dot_general(
                tile[slot], dpre[...], (((0,), (0,)), ((), ())), preferred_element_type=jnp.float32
            )

        @pl.when(j >= steps)
        def _():
            wide[slot, :, 0:span] = lax.dot_general(
                gated[...], tile[slot], (((0,), (0,)), ((), ())), preferred_element_type=jnp.float32
            )

        results(j, slot, lambda copy: copy.start())
        sum_events(SUM_MIDDLE, j, first, second, third)
        return carry

    lax.fori_loop(0, 2 * steps, step, 0)
    third(3)
    third(0)
    for j in (2 * steps - 2, 2 * steps - 1):
        results(jnp.int32(j), j % 2, lambda copy: copy.wait())
    plan.finish()


def experts_weights(drow, gate_grads, x_all, grads, dpre, gated):
    rows, width = grads.shape
    joined, hidden = dpre.shape[1], gated.shape[1]
    span = width // 4
    bf16, f32, sds = jnp.bfloat16, jnp.float32, jax.ShapeDtypeStruct
    return pl.pallas_call(
        weights_kernel,
        out_shape=[
            sds((rows // 32, width), f32),
            sds((16, 128), f32),
            sds((2, width, joined // 4), f32),
            sds((2, width, joined // 4), f32),
            sds((hidden, width), f32),
        ],
        in_specs=[ANY] * 6,
        out_specs=[IN_VMEM, IN_VMEM, ANY, ANY, ANY],
        scratch_shapes=sum_scratch(rows // 32, width, bf16)
        + sum_scratch(16, 128, f32)
        + [
            pltpu.VMEM((rows, joined), bf16),
            pltpu.VMEM((rows, hidden), bf16),
            pltpu.VMEM((2, rows, span), bf16),
            pltpu.VMEM((2, span, joined), f32),
            DMA((2, 32)),
            DMA((2, 32)),
            DMA((2, 16)),
            DMA((2,)),
            DMA((2,)),
            DMA((2, 4)),
        ],
        compiler_params=pltpu.CompilerParams(
            collective_id=3, has_side_effects=True, vmem_limit_bytes=58 * 2**20
        ),
        cost_estimate=cost_of(90),
        name="experts_weights",
    )(drow, gate_grads, x_all, grads, dpre, gated)


BOTH = ("expert", "tensor")


def dot32(left, right, dims):
    return lax.dot_general(left, right, (dims, ((), ())), preferred_element_type=jnp.float32)


NN = ((1,), (0,))
NT = ((1,), (1,))
TN = ((0,), (0,))


def rms_inv(values):
    return lax.rsqrt(jnp.mean(values * values, axis=-1, keepdims=True) + NORM_EPS)


def dense_body(
    tokens,
    attn_gain,
    w_query,
    w_key,
    w_value,
    w_out,
    query_gain,
    key_gain,
    ffn_gain,
    w_router,
    w_gate,
    w_up,
    w_down,
    doc_ids,
    routes,
    deal,
    out_grad,
):
    rows, width = tokens.shape
    parts = lax.axis_size("tensor")
    blocks = lax.axis_size("expert")
    column = lax.axis_index("tensor")
    block = lax.axis_index("expert")
    own = rows // parts
    share = rows // blocks
    piece = share // parts
    bf16, f32 = jnp.bfloat16, jnp.float32

    def reorder(per_place):
        grid = per_place.reshape((blocks, parts, piece) + per_place.shape[1:])
        return jnp.swapaxes(grid, 0, 1).reshape(per_place.shape)

    local_width = w_query.shape[1]
    head_count = local_width // HEAD_DIM
    expert_count = w_router.shape[1]
    qkv_own = jnp.concatenate([w_query, w_key, w_value], axis=1)
    gain_stack = jnp.stack([attn_gain, query_gain, key_gain, ffn_gain], axis=1)
    small_own = jnp.concatenate([w_router, gain_stack], axis=1)
    small_own = jnp.pad(small_own, ((0, 0), (0, 128 - small_own.shape[1])))
    deal_grid = deal.reshape(blocks, blocks, parts, piece)
    picks = lax.dynamic_slice(deal_grid, (0, block, column, 0), (blocks, 1, 1, piece)).reshape(-1)
    picks = picks - block * rows
    inputs, dealt_grads, qkv_full, small_full = start_exchange(
        tokens[picks].reshape(blocks, piece, width),
        out_grad[picks].reshape(blocks, piece, width),
        qkv_own,
        small_own,
    )
    own_low = lax.dynamic_slice_in_dim(inputs, column, 1, 0).reshape(own, width)
    inputs = inputs.reshape(rows, width).astype(f32)
    qkv_full = qkv_full.reshape(width, -1)
    small_full = small_full.reshape(width, -1)
    router_full = small_full[:, :expert_count]
    gain_full = small_full[:, expert_count : expert_count + 4].T.astype(f32)
    gain_attn, gain_ffn = gain_full[0], gain_full[3]
    gain_query = lax.dynamic_slice_in_dim(gain_full[1], column * local_width, local_width)
    gain_key = lax.dynamic_slice_in_dim(gain_full[2], column * local_width, local_width)
    out_full = lax.all_gather(w_out, "expert", axis=0)
    own_grad_low = dealt_grads.reshape(own, width)
    grads_all = lax.all_gather(own_grad_low, BOTH, axis=0, tiled=True)
    own_in = own_low.astype(f32)
    own_grad = own_grad_low.astype(f32)

    scale = 1.0 / math.sqrt(HEAD_DIM)
    normed = (inputs * rms_inv(inputs) * gain_attn).astype(bf16)
    qkv = dot32(normed, qkv_full, NN)
    query_pre = qkv[:, :local_width]
    key_pre = qkv[:, local_width : 2 * local_width]
    value_rows = qkv[:, 2 * local_width :].astype(bf16).reshape(rows, head_count, HEAD_DIM)
    squares = lax.psum(
        jnp.stack([jnp.sum(query_pre * query_pre, axis=-1), jnp.sum(key_pre * key_pre, axis=-1)]),
        "tensor",
    )
    query_inv = lax.rsqrt(squares[0] / width + NORM_EPS)[:, None]
    key_inv = lax.rsqrt(squares[1] / width + NORM_EPS)[:, None]
    query_hat = query_pre * query_inv
    key_hat = key_pre * key_inv
    cosines, sines = rope_tables(doc_ids, HEAD_DIM)
    cosines, sines = reorder(cosines), reorder(sines)
    query_rot = rotate(
        (query_hat * gain_query).reshape(rows, head_count, HEAD_DIM), cosines, sines
    ).astype(bf16)
    key_rot = rotate(
        (key_hat * gain_key).reshape(rows, head_count, HEAD_DIM), cosines, sines
    ).astype(bf16)
    positions = reorder(jnp.arange(rows, dtype=jnp.int32))
    documents = reorder(doc_ids)
    allowed = (documents[:, None] == documents[None, :]) & (positions[None, :] <= positions[:, None])

    def masked_scores():
        raw_scores = jnp.einsum("qhd,khd->hqk", query_rot, key_rot, preferred_element_type=f32)
        return jnp.where(allowed[None], raw_scores * scale, -1e30)

    scores = masked_scores()
    top_score = jnp.max(scores, axis=-1, keepdims=True)
    log_total = top_score + jnp.log(jnp.sum(jnp.exp(scores - top_score), axis=-1, keepdims=True))
    weights = jnp.exp(scores - log_total).astype(bf16)
    attended = (
        jnp.einsum("hqk,khd->qhd", weights, value_rows, preferred_element_type=f32)
        .astype(bf16)
        .reshape(rows, local_width)
    )
    branch = jnp.einsum("rk,ekd->red", attended, out_full, preferred_element_type=f32)
    branch = branch.astype(bf16).reshape(rows, width)
    branch_own = sum_tensor(branch)

    residual = own_in + branch_own
    resid_inv = rms_inv(residual)
    resid_hat = residual * resid_inv
    ffn_in = (resid_hat * gain_ffn).astype(bf16)
    logits = dot32(ffn_in, router_full, NN)
    router_probs = jax.nn.softmax(logits, axis=-1)
    local_experts = w_gate.shape[0]
    own_routes = lax.dynamic_slice(
        routes.reshape(blocks, parts, piece, -1),
        (0, column, 0, 0),
        (blocks, 1, piece, routes.shape[1]),
    ).reshape(own, -1)
    expert_ids = jnp.arange(expert_count, dtype=jnp.int32)
    routed = jnp.any(own_routes[:, :, None] == expert_ids[None, None, :], axis=1)
    gates_own = jnp.where(routed, router_probs, 0.0)

    hidden_width = w_gate.shape[2]
    joined_weight = jnp.concatenate(
        [w_gate[i] for i in range(local_experts)] + [w_up[i] for i in range(local_experts)], axis=1
    )
    down_weight = w_down.reshape(local_experts * hidden_width, width)
    rows_all, gates_all, pre_all, gated_all, mixed = experts_forward(
        ffn_in, gates_own.T, joined_weight, down_weight
    )
    mix_own, joined_grad, row_terms, gate_grads = experts_backward(
        mixed, grads_all, pre_all, gates_all, joined_weight, down_weight
    )
    output_own = (residual + mix_own).astype(bf16)
    row_own, gate_grad_own, d_w_gate, d_w_up, d_w_down = experts_weights(
        row_terms, gate_grads, rows_all, grads_all, joined_grad, gated_all
    )
    gate_grad_own = gate_grad_own.T
    d_w_down = d_w_down.reshape(w_down.shape)

    prob_grad = jnp.where(routed, gate_grad_own, 0.0)
    logit_grad = (
        router_probs * (prob_grad - jnp.sum(router_probs * prob_grad, axis=-1, keepdims=True))
    ).astype(bf16)
    d_router = dot32(ffn_in, logit_grad, TN)
    ffn_grad = row_own + dot32(logit_grad, router_full, NT)
    d_ffn_gain = jnp.sum(ffn_grad * resid_hat, axis=0)
    scaled_ffn = ffn_grad * gain_ffn
    resid_grad = own_grad + resid_inv * (
        scaled_ffn - resid_hat * jnp.mean(scaled_ffn * resid_hat, axis=-1, keepdims=True)
    )
    branch_grad = gather_tensor(resid_grad.astype(bf16))

    branch_cols = branch_grad.reshape(rows, blocks, width // blocks)
    d_wo = jnp.einsum("rk,red->ekd", attended, branch_cols, preferred_element_type=f32).astype(bf16)
    sum_wo = lax.psum_scatter(d_wo, "expert", scatter_dimension=0, tiled=False)
    attended_grad = (
        jnp.einsum("red,ekd->rk", branch_cols, out_full, preferred_element_type=f32)
        .astype(bf16)
        .reshape(rows, head_count, HEAD_DIM)
    )
    probs_again = jnp.exp(masked_scores() - log_total)
    prob_grads = jnp.einsum("qhd,khd->hqk", attended_grad, value_rows, preferred_element_type=f32)
    value_grad = (
        jnp.einsum(
            "hqk,qhd->khd", probs_again.astype(bf16), attended_grad, preferred_element_type=f32
        )
        .astype(bf16)
        .reshape(rows, local_width)
    )
    row_delta = jnp.sum(probs_again * prob_grads, axis=-1, keepdims=True)
    score_grad = (probs_again * (prob_grads - row_delta) * scale).astype(bf16)
    query_rot_grad = jnp.einsum("hqk,khd->qhd", score_grad, key_rot, preferred_element_type=f32)
    key_rot_grad = jnp.einsum("hqk,qhd->khd", score_grad, query_rot, preferred_element_type=f32)
    query_norm_grad = unrotate(query_rot_grad, cosines, sines).reshape(rows, local_width)
    key_norm_grad = unrotate(key_rot_grad, cosines, sines).reshape(rows, local_width)
    query_hat_grad = query_norm_grad * gain_query
    key_hat_grad = key_norm_grad * gain_key
    d_query_gain = jnp.sum(query_norm_grad * query_hat, axis=0)
    d_key_gain = jnp.sum(key_norm_grad * key_hat, axis=0)
    dots = lax.psum(
        jnp.stack(
            [
                jnp.sum(query_hat_grad * query_hat, axis=-1),
                jnp.sum(key_hat_grad * key_hat, axis=-1),
            ]
        ),
        "tensor",
    )
    query_grad = (query_inv * (query_hat_grad - query_hat * (dots[0] / width)[:, None])).astype(
        bf16
    )
    key_grad = (key_inv * (key_hat_grad - key_hat * (dots[1] / width)[:, None])).astype(bf16)
    qkv_grad = jnp.concatenate([query_grad, key_grad, value_grad], axis=1)
    input_terms = dot32(qkv_grad, qkv_full, NT).astype(bf16)
    normed_grad = sum_tensor(input_terms)
    d_qkv = dot32(normed, qkv_grad, TN).astype(bf16)

    own_inv = rms_inv(own_in)
    own_hat = own_in * own_inv
    d_attn_gain = jnp.sum(normed_grad * own_hat, axis=0)
    scaled_attn = normed_grad * gain_attn
    input_grad = resid_grad + own_inv * (
        scaled_attn - own_hat * jnp.mean(scaled_attn * own_hat, axis=-1, keepdims=True)
    )

    def widen(slots):
        return lax.dynamic_update_slice_in_dim(
            jnp.zeros((width,), f32), slots, column * local_width, 0
        )

    small = jnp.concatenate(
        [
            d_router.T,
            jnp.stack([d_attn_gain, widen(d_query_gain), widen(d_key_gain), d_ffn_gain]),
        ]
    )
    small = lax.psum_scatter(small, "expert", scatter_dimension=1, tiled=True)
    small = lax.psum(small, "tensor")
    sum_router = small[:expert_count].T
    sum_gains = small[expert_count:]

    back_out, back_in, sum_qkv = last_exchange(
        output_own.reshape(blocks, piece, width),
        input_grad.astype(bf16).reshape(blocks, piece, width),
        d_qkv.reshape(blocks, -1, d_qkv.shape[1]),
    )
    came = lax.dynamic_slice(deal_grid, (0, block, 0, 0), (blocks, 1, parts, piece))
    came = jnp.swapaxes(came.reshape(blocks, parts, piece), 0, 1).reshape(-1) - block * rows
    chooser = (jnp.arange(rows, dtype=jnp.int32)[:, None] == came[None, :]).astype(bf16)
    output = dot32(chooser, back_out.reshape(rows, width), NN).astype(bf16)
    d_tokens = dot32(chooser, back_in.reshape(rows, width), NN).astype(bf16)
    return (
        output,
        d_tokens,
        sum_gains[0],
        sum_qkv[:, :local_width],
        sum_qkv[:, local_width : 2 * local_width],
        sum_qkv[:, 2 * local_width :],
        sum_wo.astype(f32),
        sum_gains[1],
        sum_gains[2],
        sum_gains[3],
        sum_router,
        d_w_gate,
        d_w_up,
        d_w_down,
    )


def pick_body(*args):
    routes, experts = args[14], args[9].shape[1]
    mesh_fits = (lax.axis_size("expert"), lax.axis_size("tensor")) == (8, 4)
    body = dense_body if mesh_fits and experts <= 2 * routes.shape[1] else routed_body
    return body(*args)


def solution(mesh):
    in_specs = (
        P("expert", None),
        P("expert"),
        P("expert", "tensor"),
        P("expert", "tensor"),
        P("expert", "tensor"),
        P("tensor", "expert"),
        P("expert"),
        P("expert"),
        P("expert"),
        P("expert", None),
        P("expert", None, "tensor"),
        P("expert", None, "tensor"),
        P("expert", "tensor", None),
        P("expert"),
        P("expert", None),
        P(),
        P("expert", None),
    )
    out_specs = (
        P("expert", None),
        P("expert", None),
        P("expert"),
        P("expert", "tensor"),
        P("expert", "tensor"),
        P("expert", "tensor"),
        P("tensor", "expert"),
        P("expert"),
        P("expert"),
        P("expert"),
        P("expert", None),
        P("expert", None, "tensor"),
        P("expert", None, "tensor"),
        P("expert", "tensor", None),
    )
    return jax.shard_map(pick_body, mesh=mesh, in_specs=in_specs, out_specs=out_specs, check_vma=False)
```

```python
import functools
import math

import jax
import jax.numpy as jnp
from jax import lax
from jax.experimental import pallas as pl
from jax.experimental.pallas import tpu as pltpu
from jax.sharding import PartitionSpec as P

HEAD_DIM = 128
EXPERT, TENSOR = "expert", "tensor"


NORM_EPS = 1e-05
ROPE_BASE = 10000.0


def rope_tables(documents, head_size):
    row_count = documents.shape[0]
    positions = jnp.arange(row_count, dtype=jnp.int32)
    new_doc = jnp.concatenate(
        [jnp.ones((1,), jnp.int32), (documents[1:] != documents[:-1]).astype(jnp.int32)]
    )
    starts = lax.cummax(jnp.where(new_doc > 0, positions, 0), axis=0)
    places = (positions - starts).astype(jnp.float32)
    half_dim = head_size // 2
    frequency = jnp.exp(
        jnp.arange(half_dim, dtype=jnp.float32) * (-2.0 * math.log(ROPE_BASE) / head_size)
    )
    angles = places[:, None] * frequency[None, :]
    return (jnp.cos(angles), jnp.sin(angles), starts)


def rotate(values, cosines, sines):
    half_dim = values.shape[-1] // 2
    first_half = values[..., :half_dim]
    second_half = values[..., half_dim:]
    cos_rows = cosines[:, None, :]
    sin_rows = sines[:, None, :]
    return jnp.concatenate(
        [
            first_half * cos_rows - second_half * sin_rows,
            second_half * cos_rows + first_half * sin_rows,
        ],
        axis=-1,
    )


def unrotate(grads_in, cosines, sines):
    half_dim = grads_in.shape[-1] // 2
    first_half = grads_in[..., :half_dim]
    second_half = grads_in[..., half_dim:]
    cos_rows = cosines[:, None, :]
    sin_rows = sines[:, None, :]
    return jnp.concatenate(
        [
            first_half * cos_rows + second_half * sin_rows,
            second_half * cos_rows - first_half * sin_rows,
        ],
        axis=-1,
    )


def to_experts(rows):
    return lax.all_to_all(rows, EXPERT, split_axis=0, concat_axis=0, tiled=True)


def from_experts(rows):
    return lax.all_to_all(rows, EXPERT, split_axis=0, concat_axis=0, tiled=True)


def hidden_sums(terms):
    return lax.psum_scatter(terms, TENSOR, scatter_dimension=3, tiled=True)


def routed_body(
    tokens,
    attn_gain,
    w_query,
    w_key,
    w_value,
    w_out,
    query_gain,
    key_gain,
    ffn_gain,
    w_router,
    w_gate,
    w_up,
    w_down,
    doc_ids,
    routes,
    deal,
    out_grad,
):
    row_count, width = tokens.shape
    tensor_parts = lax.axis_size(TENSOR)
    expert_parts = lax.axis_size(EXPERT)
    column = lax.axis_index(TENSOR)
    device_idx = lax.axis_index(EXPERT)
    quarter = width // tensor_parts
    share_rows = row_count // expert_parts
    deal_rows = lax.dynamic_slice_in_dim(
        deal.reshape(expert_parts, row_count), device_idx * share_rows, share_rows, 1
    )
    local_pick = deal_rows - device_idx * row_count
    dealt_tokens, dealt_grad = (
        lax.all_to_all(tokens[local_pick], EXPERT, split_axis=0, concat_axis=0, tiled=True),
        lax.all_to_all(out_grad[local_pick], EXPERT, split_axis=0, concat_axis=0, tiled=True),
    )
    dealt_tokens = dealt_tokens.reshape(row_count, width)
    dealt_grad = dealt_grad.reshape(row_count, width)
    gain_stack = jnp.stack([attn_gain, query_gain, key_gain, ffn_gain])
    wq_full, wk_full, wv_full, wo_full, router_full, gain_full = (
        lax.all_gather(w_query, EXPERT, axis=0, tiled=True),
        lax.all_gather(w_key, EXPERT, axis=0, tiled=True),
        lax.all_gather(w_value, EXPERT, axis=0, tiled=True),
        lax.all_gather(w_out, EXPERT, axis=1, tiled=True),
        lax.all_gather(w_router, EXPERT, axis=0, tiled=True),
        lax.all_gather(gain_stack, EXPERT, axis=1, tiled=True),
    )
    local_width = wq_full.shape[1]
    head_count = local_width // HEAD_DIM
    gain_attn = gain_full[0].astype(jnp.float32)
    gain_query = lax.dynamic_slice_in_dim(
        gain_full[1].astype(jnp.float32), column * local_width, local_width
    )
    gain_key = lax.dynamic_slice_in_dim(
        gain_full[2].astype(jnp.float32), column * local_width, local_width
    )
    gain_ffn = gain_full[3].astype(jnp.float32)
    scale = 1.0 / math.sqrt(HEAD_DIM)
    inputs = dealt_tokens.astype(jnp.float32)
    input_inv = lax.rsqrt(jnp.mean(inputs * inputs, axis=-1, keepdims=True) + NORM_EPS)
    input_hat = inputs * input_inv
    normed = (input_hat * gain_attn).astype(jnp.bfloat16)
    query_pre = jnp.dot(normed, wq_full, preferred_element_type=jnp.float32)
    key_pre = jnp.dot(normed, wk_full, preferred_element_type=jnp.float32)
    value_rows = (
        jnp.dot(normed, wv_full, preferred_element_type=jnp.float32)
        .astype(jnp.bfloat16)
        .reshape(row_count, head_count, HEAD_DIM)
    )
    query_sq, key_sq = lax.psum(
        (jnp.sum(query_pre * query_pre, axis=-1), jnp.sum(key_pre * key_pre, axis=-1)), TENSOR
    )
    query_inv = lax.rsqrt(query_sq / width + NORM_EPS)[:, None]
    key_inv = lax.rsqrt(key_sq / width + NORM_EPS)[:, None]
    query_hat = query_pre * query_inv
    key_hat = key_pre * key_inv
    cosines, sines, _ = rope_tables(doc_ids, HEAD_DIM)
    query_rot = rotate(
        (query_hat * gain_query).reshape(row_count, head_count, HEAD_DIM), cosines, sines
    ).astype(jnp.bfloat16)
    key_rot = rotate(
        (key_hat * gain_key).reshape(row_count, head_count, HEAD_DIM), cosines, sines
    ).astype(jnp.bfloat16)
    positions = jnp.arange(row_count, dtype=jnp.int32)
    allowed = (doc_ids[:, None] == doc_ids[None, :]) & (positions[None, :] <= positions[:, None])

    def masked_scores():
        raw_scores = jnp.einsum(
            "qhd,khd->hqk", query_rot, key_rot, preferred_element_type=jnp.float32
        )
        return jnp.where(allowed[None], raw_scores * scale, -1e30)

    scores = masked_scores()
    top_score = jnp.max(scores, axis=-1, keepdims=True)
    log_total = top_score + jnp.log(jnp.sum(jnp.exp(scores - top_score), axis=-1, keepdims=True))
    weights = jnp.exp(scores - log_total).astype(jnp.bfloat16)
    attended = (
        jnp.einsum("hqk,khd->qhd", weights, value_rows, preferred_element_type=jnp.float32)
        .astype(jnp.bfloat16)
        .reshape(row_count, local_width)
    )
    branch = lax.psum(jnp.dot(attended, wo_full, preferred_element_type=jnp.float32), TENSOR)
    residual = inputs + branch
    resid_inv = lax.rsqrt(jnp.mean(residual * residual, axis=-1, keepdims=True) + NORM_EPS)
    resid_hat = residual * resid_inv
    ffn_in = (resid_hat * gain_ffn).astype(jnp.bfloat16)
    logits = jnp.dot(ffn_in, router_full, preferred_element_type=jnp.float32)
    router_probs = jax.nn.softmax(logits, axis=-1)
    expert_count = router_full.shape[1]
    top_count = routes.shape[1]
    local_experts = expert_count // expert_parts
    capacity = tensor_parts * max(
        1,
        (row_count * top_count + expert_count * tensor_parts - 1) // (expert_count * tensor_parts),
        row_count * top_count * 5 // (4 * expert_count * tensor_parts),
    )
    expert_ids = jnp.arange(expert_count, dtype=jnp.int32)
    route_match = routes[:, :, None] == expert_ids[None, None, :]
    gate_probs = jnp.sum(jnp.where(route_match, router_probs[:, None, :], 0.0), axis=-1)
    flat_routes = routes.reshape(-1)
    onehot = (flat_routes[:, None] == expert_ids[None, :]).astype(jnp.int32)
    slot_rank = jnp.sum((jnp.cumsum(onehot, axis=0) - onehot) * onehot, axis=-1)
    row_ids = flat_routes * capacity + slot_rank
    token_ids = jnp.arange(row_count * top_count, dtype=jnp.int32) // top_count
    slot_token = (
        jnp.full((expert_count * capacity,), row_count, jnp.int32).at[row_ids].set(token_ids)
    )
    slot_gates = (
        jnp.zeros((expert_count * capacity,), jnp.float32).at[row_ids].set(gate_probs.reshape(-1))
    )
    pick_rows = row_ids.reshape(row_count, top_count)
    padded_in = jnp.concatenate([ffn_in, jnp.zeros((1, width), jnp.bfloat16)], axis=0)
    grad_full = dealt_grad.astype(jnp.float32)
    grad_padded = jnp.concatenate([grad_full, jnp.zeros((1, width), jnp.float32)], axis=0)
    received = to_experts(
        padded_in[slot_token].reshape(expert_parts, local_experts, capacity, width)
    )
    gate_pre = jnp.einsum("secd,edf->secf", received, w_gate, preferred_element_type=jnp.float32)
    up_pre = jnp.einsum("secd,edf->secf", received, w_up, preferred_element_type=jnp.float32)
    sigmoid_gate = jax.nn.sigmoid(gate_pre)
    silu_gate = gate_pre * sigmoid_gate
    hidden = (silu_gate * up_pre).astype(jnp.bfloat16)
    partial_out = jnp.einsum("secf,efd->secd", hidden, w_down, preferred_element_type=jnp.float32)
    own_columns = hidden_sums(partial_out).astype(jnp.bfloat16)
    returned = from_experts(own_columns).reshape(expert_count * capacity, quarter)
    chosen = returned[pick_rows].astype(jnp.float32)
    mix_own = jnp.sum(gate_probs[:, :, None] * chosen, axis=1)
    mix_part = lax.dynamic_update_slice_in_dim(
        jnp.zeros((row_count, width), jnp.float32), mix_own, column * quarter, 1
    )
    grad_own = lax.dynamic_slice_in_dim(grad_full, column * quarter, quarter, 1)
    gate_grad_part = jnp.sum(grad_own[:, None, :] * chosen, axis=-1)
    send_grad = (
        (grad_padded[slot_token] * slot_gates[:, None])
        .astype(jnp.bfloat16)
        .reshape(expert_parts, local_experts, capacity, width)
    )
    recv_grad = to_experts(send_grad)
    d_w_down = jnp.einsum("secf,secd->efd", hidden, recv_grad, preferred_element_type=jnp.float32)
    hidden_grad = jnp.einsum(
        "secd,efd->secf", recv_grad, w_down, preferred_element_type=jnp.float32
    )
    gate_grad_pre = (
        hidden_grad * up_pre * sigmoid_gate * (1.0 + gate_pre * (1.0 - sigmoid_gate))
    ).astype(jnp.bfloat16)
    up_grad_pre = (hidden_grad * silu_gate).astype(jnp.bfloat16)
    d_w_gate = jnp.einsum(
        "secd,secf->edf", received, gate_grad_pre, preferred_element_type=jnp.float32
    )
    d_w_up = jnp.einsum("secd,secf->edf", received, up_grad_pre, preferred_element_type=jnp.float32)
    joined_grad = jnp.concatenate([gate_grad_pre, up_grad_pre], axis=-1)
    joined_weight = jnp.concatenate([w_gate, w_up], axis=-1)
    row_terms = jnp.einsum(
        "secf,edf->secd", joined_grad, joined_weight, preferred_element_type=jnp.float32
    )
    row_own = hidden_sums(row_terms).astype(jnp.bfloat16)
    row_back = from_experts(row_own).reshape(expert_count * capacity, quarter)
    ffn_grad_own = jnp.sum(row_back[pick_rows].astype(jnp.float32), axis=1)
    placed = lax.dynamic_update_slice_in_dim(
        jnp.zeros((row_count, width), jnp.float32), ffn_grad_own, column * quarter, 1
    )
    ffn_grad_rows, gate_grad, mix_total = lax.psum((placed, gate_grad_part, mix_part), TENSOR)
    output = (residual + mix_total).astype(jnp.bfloat16)
    prob_grad = jnp.sum(jnp.where(route_match, gate_grad[:, :, None], 0.0), axis=1)
    logit_grad = (
        router_probs * (prob_grad - jnp.sum(router_probs * prob_grad, axis=-1, keepdims=True))
    ).astype(jnp.bfloat16)
    d_router = jnp.einsum("rd,re->de", ffn_in, logit_grad, preferred_element_type=jnp.float32)
    ffn_grad = ffn_grad_rows + jnp.einsum(
        "re,de->rd", logit_grad, router_full, preferred_element_type=jnp.float32
    )
    d_ffn_gain = jnp.sum(ffn_grad * resid_hat, axis=0)
    scaled_ffn = ffn_grad * gain_ffn
    resid_grad = grad_full + resid_inv * (
        scaled_ffn - resid_hat * jnp.mean(scaled_ffn * resid_hat, axis=-1, keepdims=True)
    )
    branch_grad = resid_grad.astype(jnp.bfloat16)
    d_wo = jnp.einsum("rk,rd->kd", attended, branch_grad, preferred_element_type=jnp.float32)
    attended_grad = (
        jnp.einsum("rd,kd->rk", branch_grad, wo_full, preferred_element_type=jnp.float32)
        .astype(jnp.bfloat16)
        .reshape(row_count, head_count, HEAD_DIM)
    )
    probs_again = jnp.exp(masked_scores() - log_total)
    prob_grads = jnp.einsum(
        "qhd,khd->hqk", attended_grad, value_rows, preferred_element_type=jnp.float32
    )
    value_grad = (
        jnp.einsum(
            "hqk,qhd->khd",
            probs_again.astype(jnp.bfloat16),
            attended_grad,
            preferred_element_type=jnp.float32,
        )
        .astype(jnp.bfloat16)
        .reshape(row_count, local_width)
    )
    row_delta = jnp.sum(probs_again * prob_grads, axis=-1, keepdims=True)
    score_grad = (probs_again * (prob_grads - row_delta) * scale).astype(jnp.bfloat16)
    query_rot_grad = jnp.einsum(
        "hqk,khd->qhd", score_grad, key_rot, preferred_element_type=jnp.float32
    )
    key_rot_grad = jnp.einsum(
        "hqk,qhd->khd", score_grad, query_rot, preferred_element_type=jnp.float32
    )
    query_norm_grad = unrotate(query_rot_grad, cosines, sines).reshape(row_count, local_width)
    key_norm_grad = unrotate(key_rot_grad, cosines, sines).reshape(row_count, local_width)
    query_hat_grad = query_norm_grad * gain_query
    key_hat_grad = key_norm_grad * gain_key
    gain_pieces = jnp.stack(
        [jnp.sum(query_norm_grad * query_hat, axis=0), jnp.sum(key_norm_grad * key_hat, axis=0)]
    )
    gain_parts = lax.dynamic_update_slice_in_dim(
        jnp.zeros((2, width), jnp.float32), gain_pieces, column * local_width, 1
    )
    query_dot, key_dot, qk_gains = lax.psum(
        (
            jnp.sum(query_hat_grad * query_hat, axis=-1),
            jnp.sum(key_hat_grad * key_hat, axis=-1),
            gain_parts,
        ),
        TENSOR,
    )
    query_grad = (query_inv * (query_hat_grad - query_hat * (query_dot / width)[:, None])).astype(
        jnp.bfloat16
    )
    key_grad = (key_inv * (key_hat_grad - key_hat * (key_dot / width)[:, None])).astype(
        jnp.bfloat16
    )
    d_wq = jnp.einsum("rd,rk->dk", normed, query_grad, preferred_element_type=jnp.float32)
    d_wk = jnp.einsum("rd,rk->dk", normed, key_grad, preferred_element_type=jnp.float32)
    d_wv = jnp.einsum("rd,rk->dk", normed, value_grad, preferred_element_type=jnp.float32)
    input_terms = jnp.einsum("rk,dk->rd", query_grad, wq_full, preferred_element_type=jnp.float32)
    input_terms = input_terms + jnp.einsum(
        "rk,dk->rd", key_grad, wk_full, preferred_element_type=jnp.float32
    )
    input_terms = input_terms + jnp.einsum(
        "rk,dk->rd", value_grad, wv_full, preferred_element_type=jnp.float32
    )
    normed_grad = lax.psum(input_terms, TENSOR)
    d_attn_part = jnp.sum(normed_grad * input_hat, axis=0)
    scaled_attn = normed_grad * gain_attn
    input_grad = resid_grad + input_inv * (
        scaled_attn - input_hat * jnp.mean(scaled_attn * input_hat, axis=-1, keepdims=True)
    )
    dealt_dtokens = input_grad.astype(jnp.bfloat16)
    gain_grads = jnp.stack([d_attn_part, qk_gains[0], qk_gains[1], d_ffn_gain])
    sum_wq, sum_wk, sum_wv, sum_wo, sum_router, sum_gains = (
        lax.psum_scatter(d_wq, EXPERT, scatter_dimension=0, tiled=True),
        lax.psum_scatter(d_wk, EXPERT, scatter_dimension=0, tiled=True),
        lax.psum_scatter(d_wv, EXPERT, scatter_dimension=0, tiled=True),
        lax.psum_scatter(d_wo, EXPERT, scatter_dimension=1, tiled=True),
        lax.psum_scatter(d_router, EXPERT, scatter_dimension=0, tiled=True),
        lax.psum_scatter(gain_grads, EXPERT, scatter_dimension=1, tiled=True),
    )
    back_out, back_dtok = (
        lax.all_to_all(
            output.reshape(expert_parts, share_rows, width),
            EXPERT,
            split_axis=0,
            concat_axis=0,
            tiled=True,
        ),
        lax.all_to_all(
            dealt_dtokens.reshape(expert_parts, share_rows, width),
            EXPERT,
            split_axis=0,
            concat_axis=0,
            tiled=True,
        ),
    )
    flat_pick = local_pick.reshape(-1)
    output_rows = (
        jnp.zeros((row_count, width), jnp.bfloat16)
        .at[flat_pick]
        .set(back_out.reshape(row_count, width))
    )
    d_tokens = (
        jnp.zeros((row_count, width), jnp.bfloat16)
        .at[flat_pick]
        .set(back_dtok.reshape(row_count, width))
    )
    return (
        output_rows,
        d_tokens,
        sum_gains[0],
        sum_wq,
        sum_wk,
        sum_wv,
        sum_wo,
        sum_gains[1],
        sum_gains[2],
        sum_gains[3],
        sum_router,
        d_w_gate,
        d_w_up,
        d_w_down,
    )


MESH_ID = pl.DeviceIdType.MESH
ANY = pl.BlockSpec(memory_space=pl.ANY)
IN_VMEM = pl.BlockSpec(memory_space=pltpu.VMEM)
def cost_of(micros):
    return pl.CostEstimate(flops=0, bytes_accessed=micros * 3_000_000, transcendentals=0)


SELF, NEAR, FAR, BOTH_FLIPPED = 0, 1, 2, 3


def place_of(device):
    expert, tensor = device
    return expert // 2, expert % 2, tensor // 2, tensor % 2


def flipped(device, role):
    expert, tensor = device
    _, x, y, core = place_of(device)
    step_x, step_y = 1 - 2 * x, 2 - 4 * y
    if role == NEAR:
        return expert + (1 - core) * step_x, tensor + core * step_y
    if role == FAR:
        return expert + core * step_x, tensor + (1 - core) * step_y
    if role == BOTH_FLIPPED:
        return expert + step_x, tensor + step_y
    return expert, tensor


def moved_z(device, hops):
    expert, tensor = device
    return lax.rem(expert + 2 * hops, 8), tensor


def sibling(device):
    expert, tensor = device
    return expert, tensor + 1 - 2 * (tensor % 2)


def slot_of(device):
    return device[0] * 4 + device[1]


def here():
    return lax.axis_index(EXPERT), lax.axis_index(TENSOR)


def greet(partners):
    barrier = pltpu.get_barrier_semaphore()
    for partner in partners:
        pl.semaphore_signal(barrier, inc=1, device_id=partner, device_id_type=MESH_ID)
    pl.semaphore_wait(barrier, len(partners))


def push(source, target, send_sem, recv_sem, device):
    return pltpu.make_async_remote_copy(
        src_ref=source,
        dst_ref=target,
        send_sem=send_sem,
        recv_sem=recv_sem,
        device_id=device,
        device_id_type=MESH_ID,
    )


def hop(device, flips, hops):
    expert, tensor = device
    return lax.rem(expert + flips * (1 - 2 * lax.rem(expert, 2)) + 2 * hops, 8), tensor


def across_y(device):
    expert, tensor = device
    return expert, lax.rem(tensor + 2, 4)


class Line:
    def __init__(self, send_sem, recv_sem):
        self.send_sem, self.recv_sem = send_sem, recv_sem
        self.started = []

    def send(self, source, target, tag, recv_tag, device):
        copy = push(source, target, self.send_sem.at[tag], self.recv_sem.at[recv_tag], device)
        copy.start()
        self.started.append(copy)

    def wait(self, target, tag, device):
        push(target, target, self.send_sem.at[0], self.recv_sem.at[tag], device).wait_recv()

    def finish(self):
        for copy in self.started:
            copy.wait_send()


PIECES = ((0, 1), (1, 0), (3, 0), (1, 1), (3, 1), (2, 0), (2, 1))


def exchange_steps(source, out, gathered, line, local_sem):
    me = here()
    tensor = me[1]
    side, sib = across_y(me), sibling(me)

    def at(column, expert):
        return out.at[column, expert] if gathered else out.at[expert]

    local = pltpu.make_async_copy(source.at[me[0]], at(tensor, me[0]), local_sem)
    local.start()
    if gathered:
        line.send(source.at[me[0]], at(tensor, me[0]), 8, 8, side)
        line.send(source.at[me[0]], at(tensor, me[0]), 16, 16, sib)
    for k, flips in PIECES:
        target = hop(me, flips, k)
        line.send(
            source.at[target[0]], at(tensor, me[0]), k * 2 + flips, (4 - k) % 4 * 2 + flips, target
        )
    yield
    for k, flips in PIECES:
        expert = hop(me, flips, k)[0]
        tag = k * 2 + flips
        line.wait(at(tensor, expert), tag, sib)
        if gathered:
            line.send(at(tensor, expert), at(tensor, expert), 8 + tag, 8 + tag, side)
            line.send(at(tensor, expert), at(tensor, expert), 16 + tag, 16 + tag, sib)
        yield
    if gathered:
        for k, flips in ((0, 0),) + PIECES:
            expert = hop(me, flips, k)[0]
            tag = k * 2 + flips
            line.wait(at(side[1], expert), 8 + tag, sib)
            line.send(at(side[1], expert), at(side[1], expert), 24 + tag, 24 + tag, sib)
            yield
        for k, flips in ((0, 0),) + PIECES:
            expert = hop(me, flips, k)[0]
            tag = k * 2 + flips
            line.wait(at(sib[1], expert), 16 + tag, sib)
            line.wait(at(across_y(sib)[1], expert), 24 + tag, sib)
    local.wait()
    line.finish()


def gather_expert_steps(source, out, chunks, line, local_sem):
    me = here()
    z = me[0] // 2
    beside = hop(me, 1, 0)
    step = source.shape[0] // chunks

    def part(ref, i):
        return ref.at[pl.ds(i * step, step), :]

    local = pltpu.make_async_copy(source, out.at[me[0]], local_sem)
    local.start()

    def passes(ref, target, i, tag, origin_tag, up):
        device = hop(me, 0, 1 if up else 3)

        @pl.when((z < 3) if up else (z > 0))
        def _():
            push(ref, target, line.send_sem.at[tag], line.recv_sem.at[origin_tag], device).start()

    def base(distance, up, i):
        return ((distance - 1) * 2 + up) * chunks + i

    for i in range(chunks):
        line.send(part(source, i), part(out.at[me[0]], i), 12 * chunks + i, 12 * chunks + i, beside)
        for up in (1, 0):
            passes(part(source, i), part(out.at[me[0]], i), i, base(1, up, i), base(1, up, i), up)
    yield
    for distance in (1, 2, 3):
        for i in range(chunks):
            for up in (1, 0):
                held = (z >= distance) if up else (z + distance <= 3)
                expert = lax.rem(me[0] + (8 - 2 * distance if up else 2 * distance), 8)
                block = part(out.at[expert], i)
                tag = base(distance, up, i)

                @pl.when(held)
                def _():
                    line.wait(block, tag, beside)
                    cross = 6 * chunks + tag
                    push(block, block, line.send_sem.at[cross], line.recv_sem.at[cross], beside).start()

                if distance < 3:
                    more = base(distance + 1, up, i)

                    @pl.when(held & ((z < 3) if up else (z > 0)))
                    def _():
                        push(
                            block,
                            block,
                            line.send_sem.at[more],
                            line.recv_sem.at[more],
                            hop(me, 0, 1 if up else 3),
                        ).start()

                yield
    for i in range(chunks):
        line.wait(part(out.at[beside[0]], i), 12 * chunks + i, beside)
    for distance in (1, 2, 3):
        for i in range(chunks):
            for up in (1, 0):
                held = (z >= distance) if up else (z + distance <= 3)
                expert = lax.rem(beside[0] + (8 - 2 * distance if up else 2 * distance), 8)
                block = part(out.at[expert], i)
                cross = 6 * chunks + base(distance, up, i)
                sent_on = (z + 1 >= distance) & (z < 3) if up else (z - 1 + distance <= 3) & (z > 0)

                @pl.when(held)
                def _():
                    both = push(block, block, line.send_sem.at[cross], line.recv_sem.at[cross], beside)
                    both.wait()

                @pl.when(sent_on)
                def _():
                    tag = base(distance, up, i)
                    push(
                        block, block, line.send_sem.at[tag], line.recv_sem.at[tag], beside
                    ).wait_send()

        yield
    local.wait()
    line.finish()


def sum_rows(target, terms, step=16):
    def body(i, carry):
        window = pl.ds(pl.multiple_of(i * step, step), step)
        value = terms[0][window, :].astype(jnp.float32)
        for ref in terms[1:]:
            value = value + ref[window, :].astype(jnp.float32)
        target[window, :] = value.astype(target.dtype)
        return carry

    lax.fori_loop(0, target.shape[0] // step, body, 0)


def sum_expert_steps(part, out, mine, from_x, from_z, line, load_sem, step=16):
    me = here()
    beside = hop(me, 1, 0)
    loads = {}
    for k in (2, 1, 3, 0):
        line.send(part.at[hop(me, 1, k)[0]], from_x.at[k], k, k, beside)
        loads[k] = pltpu.make_async_copy(part.at[hop(me, 0, k)[0]], mine.at[k], load_sem.at[k])
        loads[k].start()
    yield
    for k in (2, 1, 3, 0):
        loads[k].wait()
        line.wait(from_x.at[k], k, beside)
        if k:
            sum_rows(mine.at[k], [mine.at[k], from_x.at[k]], step)
            line.send(mine.at[k], from_z.at[3 - k], 3 + k, 4 + 3 - k, hop(me, 0, k))
            yield
            yield
    for i in range(3):
        line.wait(from_z.at[i], 4 + i, beside)
    sum_rows(out, [mine.at[0], from_x.at[0], from_z.at[0], from_z.at[1], from_z.at[2]], step)
    line.finish()


def sum_everywhere_steps(part, out, mine, from_x, from_z, total, shares, line, load_sem):
    me = here()
    yield from sum_expert_steps(part, total, mine, from_x, from_z, line, load_sem, 8)
    peers = [across_y(me), sibling(me), across_y(sibling(me))]
    for i, peer in enumerate(peers):
        line.send(total, shares.at[me[1]], 7 + i, 7 + i, peer)
    shares[me[1]] = total[...]
    yield
    for i, peer in enumerate(peers):
        line.wait(shares.at[peer[1]], 7 + i, peer)
    sum_rows(out, [shares.at[i] for i in range(4)], 8)
    for i in range(3):
        line.started[-3 + i].wait_send()


def take_turns(steps):
    steps = list(steps)
    while steps:
        steps = [s for s in steps if next(s, steps) is not steps]


DMA = pltpu.SemaphoreType.DMA


def start_kernel(tokens, grads, weights, small, o_tokens, o_grads, o_weights, o_small, *sems):
    me = here()
    pieces = [hop(me, flips, k) for k, flips in PIECES]
    greet(pieces + [across_y(me), sibling(me)])
    local = sems[8]
    take_turns(
        [
            exchange_steps(tokens, o_tokens, True, Line(sems[0], sems[1]), local.at[0]),
            exchange_steps(grads, o_grads, False, Line(sems[2], sems[3]), local.at[1]),
            gather_expert_steps(small, o_small, 1, Line(sems[6], sems[7]), local.at[3]),
            gather_expert_steps(weights, o_weights, 4, Line(sems[4], sems[5]), local.at[2]),
        ]
    )


def start_exchange(tokens, grads, weights, small):
    piece = tokens.shape[1:]
    sds = jax.ShapeDtypeStruct
    return pl.pallas_call(
        start_kernel,
        out_shape=[
            sds((4, 8) + piece, tokens.dtype),
            sds((8,) + piece, grads.dtype),
            sds((8,) + weights.shape, weights.dtype),
            sds((8,) + small.shape, small.dtype),
        ],
        in_specs=[IN_VMEM] * 4,
        out_specs=[ANY] * 4,
        scratch_shapes=[DMA((32,)), DMA((32,)), DMA((8,)), DMA((8,))]
        + [DMA((52,)), DMA((52,)), DMA((13,)), DMA((13,)), DMA((4,))],
        compiler_params=pltpu.CompilerParams(
            collective_id=4, has_side_effects=True, vmem_limit_bytes=16 * 2**20
        ),
        cost_estimate=cost_of(100),
        name="start_exchange",
    )(tokens, grads, weights, small)


def last_kernel(
    rows, more, part, small, o_rows, o_more, out, o_small,
    mine, from_x, from_z, mine_s, x_s, z_s, total_s, shares_s, *sems,
):
    me = here()
    pieces = [hop(me, flips, k) for k, flips in PIECES]
    greet(pieces + [across_y(me), sibling(me), across_y(sibling(me))])
    take_turns(
        [
            exchange_steps(more, o_more, True, Line(sems[2], sems[3]), sems[7].at[1]),
            exchange_steps(rows, o_rows, True, Line(sems[0], sems[1]), sems[7].at[0]),
            sum_everywhere_steps(
                small, o_small, mine_s, x_s, z_s, total_s, shares_s, Line(sems[8], sems[9]), sems[10]
            ),
            sum_expert_steps(part, out, mine, from_x, from_z, Line(sems[4], sems[5]), sems[6]),
        ]
    )


def last_exchange(rows, more, part, small):
    piece = rows.shape[1:]
    block, little = part.shape[1:], small.shape[1:]
    sds = jax.ShapeDtypeStruct
    return pl.pallas_call(
        last_kernel,
        out_shape=[
            sds((4, 8) + piece, rows.dtype),
            sds((4, 8) + piece, more.dtype),
            sds(block, jnp.float32),
            sds(little, jnp.float32),
        ],
        in_specs=[IN_VMEM, IN_VMEM, ANY, ANY],
        out_specs=[ANY, ANY, IN_VMEM, IN_VMEM],
        scratch_shapes=[
            pltpu.VMEM((4,) + block, part.dtype),
            pltpu.VMEM((4,) + block, part.dtype),
            pltpu.VMEM((3,) + block, part.dtype),
        ]
        + [pltpu.VMEM((n,) + little, jnp.float32) for n in (4, 4, 3)]
        + [pltpu.VMEM(little, jnp.float32), pltpu.VMEM((4,) + little, jnp.float32)]
        + [DMA((32,))] * 4
        + [DMA((8,)), DMA((8,)), DMA((4,)), DMA((2,))]
        + [DMA((10,)), DMA((10,)), DMA((4,))],
        compiler_params=pltpu.CompilerParams(
            collective_id=5, has_side_effects=True, vmem_limit_bytes=32 * 2**20
        ),
        cost_estimate=cost_of(100),
        name="last_exchange",
    )(rows, more, part, small)


def gather_tensor_kernel(source, out, send_sem, recv_sem, local_sem):
    me = here()
    side, sib = across_y(me), sibling(me)
    greet([side, sib])
    line = Line(send_sem, recv_sem)
    halves = 4
    step = source.shape[0] // halves

    def part(ref, i):
        return ref.at[pl.ds(i * step, step), :]

    local = pltpu.make_async_copy(source, out.at[me[1]], local_sem)
    for i in range(halves):
        line.send(part(source, i), part(out.at[me[1]], i), i, i, side)
        line.send(part(source, i), part(out.at[me[1]], i), 4 + i, 4 + i, sib)
    local.start()
    for i in range(halves):
        got = part(out.at[side[1]], i)
        line.wait(got, i, sib)
        line.send(got, got, 8 + i, 8 + i, sib)
    for i in range(halves):
        line.wait(part(out.at[sib[1]], i), 4 + i, sib)
        line.wait(part(out.at[across_y(sib)[1]], i), 8 + i, sib)
    local.wait()
    line.finish()


def gather_tensor(rows):
    out = pl.pallas_call(
        gather_tensor_kernel,
        out_shape=jax.ShapeDtypeStruct((4,) + rows.shape, rows.dtype),
        in_specs=[IN_VMEM],
        out_specs=ANY,
        scratch_shapes=[DMA((12,)), DMA((12,)), DMA],
        compiler_params=pltpu.CompilerParams(
            collective_id=6, has_side_effects=True, vmem_limit_bytes=8 * 2**20
        ),
        cost_estimate=cost_of(15),
        name="gather_tensor",
    )(rows)
    return out.reshape((-1,) + rows.shape[1:])


def sum_tensor_kernel(part, out, from_sib, from_side, total, send_sem, recv_sem):
    me = here()
    side, sib = across_y(me), sibling(me)
    greet([side, sib])
    line = Line(send_sem, recv_sem)
    pieces = 4
    step = out.shape[0] // pieces

    def rows(ref, i):
        return ref.at[pl.ds(i * step, step), :]

    for j, column in ((0, across_y(sib)[1]), (1, sib[1])):
        for i in range(pieces):
            line.send(
                rows(part.at[column], i), rows(from_sib.at[j], i), 4 * j + i, 4 * j + i, sib
            )
    for i in range(pieces):
        got = rows(from_sib.at[0], i)
        line.wait(got, i, sib)
        sum_rows(rows(total, i), [rows(part.at[side[1]], i), got])
        line.send(rows(total, i), rows(from_side, i), 8 + i, 8 + i, side)
    for i in range(pieces):
        got = rows(from_sib.at[1], i)
        line.wait(got, 4 + i, sib)
        line.wait(rows(from_side, i), 8 + i, sib)
        sum_rows(rows(out, i), [rows(part.at[me[1]], i), got, rows(from_side, i)])
    line.finish()


def sum_tensor(partial):
    block = (partial.shape[0] // 4, partial.shape[1])
    return pl.pallas_call(
        sum_tensor_kernel,
        out_shape=jax.ShapeDtypeStruct(block, jnp.float32),
        in_specs=[IN_VMEM],
        out_specs=IN_VMEM,
        scratch_shapes=[
            pltpu.VMEM((2,) + block, partial.dtype),
            pltpu.VMEM(block, partial.dtype),
            pltpu.VMEM(block, partial.dtype),
            DMA((12,)),
            DMA((12,)),
        ],
        compiler_params=pltpu.CompilerParams(
            collective_id=7, has_side_effects=True, vmem_limit_bytes=12 * 2**20
        ),
        cost_estimate=cost_of(15),
        name="sum_tensor",
    )(partial.reshape((4,) + block))


def rows_at(ref, slot, size, count=1):
    return ref.at[pl.ds(pl.multiple_of(slot * size, size), size * count), :]


class Plan:
    def __init__(self, send_sem, recv_sem):
        self.send_sem, self.recv_sem, self.made = send_sem, recv_sem, []

    def send(self, make):
        make().start()
        self.made.append(make)

    def finish(self):
        for make in self.made:
            make().wait_send()


def gather_plan(ins, outs, sizes, send_sem, recv_sem):
    me = here()
    near, far, sib = flipped(me, NEAR), flipped(me, FAR), sibling(me)
    plan = Plan(send_sem, recv_sem)
    count = len(ins)

    def send(k, role, device, tag, recv_tag):
        for i in range(count):

            def make(i=i):
                block = rows_at(outs[i], slot_of(moved_z(flipped(me, role), k)), sizes[i])
                source = ins[i] if (k, role) == (0, SELF) else block
                return push(source, block, send_sem.at[i, tag], recv_sem.at[i, recv_tag], device)

            plan.send(make)

    def arrive(k, role):
        for i in range(count):
            block = rows_at(outs[i], slot_of(moved_z(flipped(me, role), k)), sizes[i])
            push(block, block, send_sem.at[i, 0], recv_sem.at[i, k * 4 + role], near).wait_recv()

    def forward(k, role):
        if role == SELF:
            send(k, SELF, far, 4 + k, k * 4 + FAR)
            send(k, SELF, near, k, k * 4 + NEAR)
        if role == NEAR:
            send(k, NEAR, far, 8 + k, k * 4 + BOTH_FLIPPED)
        send(k, role, sib, 16 + k * 4 + role, 16 + k * 4 + role)

    def event(k, role):
        arrive(k, role)
        forward(k, role)

    def from_sibling(k, role):
        for i in range(count):
            block = rows_at(outs[i], 0, sizes[i])
            push(
                block, block, send_sem.at[i, 0], recv_sem.at[i, 16 + k * 4 + role], near
            ).wait_recv()

    def begin():
        forward(0, SELF)
        for d in (1, 3, 2):
            send(0, SELF, moved_z(me, d), 11 + d, (4 - d) * 4 + SELF)

    return plan, begin, event, from_sibling


def gate_columns(gates_ref, slot, columns, first):
    lane = lax.broadcasted_iota(jnp.int32, (128, 128), 1)
    for s in range(4):
        block = gates_ref[pl.ds(pl.multiple_of((slot + s) * 16, 16), 16), :]
        turned = jnp.concatenate([block, jnp.zeros((112, 128), jnp.float32)], axis=0).T
        for i in range(2):
            column = jnp.sum(jnp.where(lane == first + i, turned, 0.0), axis=1, keepdims=True)
            columns[i, pl.ds(s * 128, 128), :] = jnp.broadcast_to(column, (128, 128))


def tiles(count, width, body):
    def step(n, carry):
        body(pl.ds(pl.multiple_of(n * width, width), width))
        return carry

    lax.fori_loop(0, count, step, 0)


STAGES = ((0, 0), (0, 1), (1, 0), (1, 1), (3, 0), (3, 1), (2, 0), (2, 1))
BLOCK = 512


def stage_expert(me, j):
    half = j // 2
    k = half + jnp.where(half == 2, 1, 0) - jnp.where(half == 3, 1, 0)
    flips = lax.rem(j, 2)
    expert = me[0]
    return lax.rem(expert + flips * (1 - 2 * lax.rem(expert, 2)) + 2 * k, 8)


def forward_kernel(
    x_own, g_own, w_joined, w_down, x_out, g_out, pre_out, gated_out, y_out,
    x_all, g_all, columns, pre, gated, y, send_sem, recv_sem, local_sem, out_sem,
):
    me = here()
    core = lax.rem(me[1], 2)
    greet(
        [flipped(me, NEAR), flipped(me, FAR), sibling(me)] + [moved_z(me, d) for d in (1, 2, 3)]
    )
    plan, begin, event, from_sibling = gather_plan(
        [x_own, g_own], [x_all, g_all], [128, 16], send_sem, recv_sem
    )
    local = [
        pltpu.make_async_copy(x_own, rows_at(x_all, slot_of(me), 128), local_sem.at[0]),
        pltpu.make_async_copy(g_own, rows_at(g_all, slot_of(me), 16), local_sem.at[1]),
    ]
    begin()
    for copy in local:
        copy.start()
    for copy in local:
        copy.wait()
    before = {
        0: [(1, SELF), (0, NEAR), (0, FAR)],
        1: [(0, BOTH_FLIPPED)],
        3: [(1, BOTH_FLIPPED)],
        5: [(3, BOTH_FLIPPED)],
        7: [(2, BOTH_FLIPPED)],
    }
    middle = {
        0: [(3, SELF), (1, NEAR)],
        1: [(1, FAR)],
        2: [(2, SELF), (3, NEAR)],
        3: [(3, FAR)],
        4: [(2, NEAR)],
        5: [(2, FAR)],
    }
    half = w_joined.shape[1] // 2

    def results(expert, slot):
        return [
            pltpu.make_async_copy(
                rows_at(x_all, expert, BLOCK), rows_at(x_out, expert, BLOCK), out_sem.at[0, slot]
            ),
            pltpu.make_async_copy(pre.at[slot], rows_at(pre_out, expert, BLOCK), out_sem.at[1, slot]),
            pltpu.make_async_copy(
                gated.at[slot], rows_at(gated_out, expert, BLOCK), out_sem.at[2, slot]
            ),
            pltpu.make_async_copy(y.at[slot], rows_at(y_out, expert, BLOCK), out_sem.at[3, slot]),
        ]

    def block(j, carry):
        slot = lax.rem(j, 2)
        expert = stage_expert(me, j)
        for n, (k, flips) in enumerate(STAGES):

            @pl.when(j == n)
            def _():
                for at in before.get(n, []):
                    event(*at)
                if n:
                    from_sibling(k, 2 - core if flips else SELF)
                    from_sibling(k, BOTH_FLIPPED if flips else 1 + core)
                else:
                    from_sibling(k, SELF)
                    from_sibling(k, 1 + core)

        @pl.when(j >= 2)
        def _():
            for copy in results(stage_expert(me, j - 2), slot):
                copy.wait()

        gate_columns(g_all, expert * 4, columns, me[0] * 2)
        x_rows = rows_at(x_all, expert, BLOCK)

        def first(cols):
            pre[slot, :, cols] = jnp.dot(
                x_rows[...], w_joined[:, cols], preferred_element_type=jnp.float32
            )

        tiles(w_joined.shape[1] // 1024, 1024, first)
        for n in middle:

            @pl.when(j == n)
            def _():
                for at in middle[n]:
                    event(*at)

        def act(r):
            for c in range(half // 128):
                cols = slice(c * 128, (c + 1) * 128)
                g = pre[slot, r, cols]
                u = pre[slot, r, half + c * 128 : half + (c + 1) * 128]
                hidden = (g * (1.0 / (1.0 + jnp.exp(-g))) * u).astype(jnp.bfloat16)
                gate = columns[c * 128 * 2 // half, r, :]
                gated[slot, r, cols] = (hidden.astype(jnp.float32) * gate).astype(jnp.bfloat16)

        tiles(BLOCK // 64, 64, act)

        def second(cols):
            y[slot, :, cols] = jnp.dot(
                gated[slot], w_down[:, cols], preferred_element_type=jnp.float32
            ).astype(jnp.bfloat16)

        tiles(w_down.shape[1] // 1024, 1024, second)
        for copy in results(expert, slot):
            copy.start()
        return carry

    lax.fori_loop(0, 8, block, 0)
    for j in (6, 7):
        for copy in results(stage_expert(me, jnp.int32(j)), j % 2):
            copy.wait()
    g_out[...] = g_all[...]
    plan.finish()


def experts_forward(ffn_in, gates_own, w_joined, w_down):
    rows, width = ffn_in.shape[0] * 32, ffn_in.shape[1]
    joined, hidden = w_joined.shape[1], w_down.shape[0]
    bf16, f32, sds = jnp.bfloat16, jnp.float32, jax.ShapeDtypeStruct
    return pl.pallas_call(
        forward_kernel,
        out_shape=[
            sds((rows, width), bf16),
            sds((512, 128), f32),
            sds((rows, joined), f32),
            sds((rows, hidden), bf16),
            sds((rows, width), bf16),
        ],
        in_specs=[IN_VMEM] * 4,
        out_specs=[ANY, IN_VMEM, ANY, ANY, ANY],
        scratch_shapes=[
            pltpu.VMEM((rows, width), bf16),
            pltpu.VMEM((512, 128), f32),
            pltpu.VMEM((2, BLOCK, 128), f32),
            pltpu.VMEM((2, BLOCK, joined), f32),
            pltpu.VMEM((2, BLOCK, hidden), bf16),
            pltpu.VMEM((2, BLOCK, width), bf16),
            DMA((2, 32)),
            DMA((2, 32)),
            DMA((2,)),
            DMA((4, 2)),
        ],
        compiler_params=pltpu.CompilerParams(
            collective_id=1, has_side_effects=True, vmem_limit_bytes=48 * 2**20
        ),
        cost_estimate=cost_of(90),
        name="experts_forward",
    )(ffn_in, gates_own, w_joined, w_down)


def sum_plan(arrays, send_sem, recv_sem, load_sem):
    me = here()
    near, far, sib = flipped(me, NEAR), flipped(me, FAR), sibling(me)
    plan = Plan(send_sem, recv_sem)
    order = (2, 1, 3, 0)

    def send(i, source, target, tag, recv_tag, device):
        plan.send(
            lambda: push(source(), target(), send_sem.at[i, tag], recv_sem.at[i, recv_tag], device())
        )

    def arrive(i, ref, tag):
        push(ref, ref, send_sem.at[i, 0], recv_sem.at[i, tag], near).wait_recv()

    def load(i, k, role):
        part, _, size, mine = arrays[i][:4]
        tag = k * 4 + role
        return pltpu.make_async_copy(
            rows_at(part, slot_of(moved_z(flipped(me, role), k)), size), mine.at[tag], load_sem.at[i, tag]
        )

    def begin():
        for roles in ((BOTH_FLIPPED, FAR), (NEAR, SELF)):
            for k in order:
                for role in roles:
                    for i, (part, _, size, _, from_sib, _, _, _) in enumerate(arrays):
                        tag = k * 4 + role
                        send(
                            i,
                            lambda part=part, size=size, k=k, role=role: rows_at(
                                part, slot_of(moved_z(flipped(sib, role), k)), size
                            ),
                            lambda from_sib=from_sib, tag=tag: from_sib.at[tag],
                            tag,
                            tag,
                            lambda: sib,
                        )
                        load(i, k, role).start()

    def collect(i, k, role):
        tag = k * 4 + role
        load(i, k, role).wait()
        from_sib = arrays[i][4]
        arrive(i, from_sib.at[tag], tag)
        return [arrays[i][3].at[tag], from_sib.at[tag]]

    def first(k, role):
        for i, (_, _, _, mine, _, from_far, _, _) in enumerate(arrays):
            tag, at = k * 4 + role, k * 2 + (role == BOTH_FLIPPED)
            terms = collect(i, k, role)
            sum_rows(mine.at[tag], terms)
            send(
                i,
                lambda mine=mine, tag=tag: mine.at[tag],
                lambda from_far=from_far, at=at: from_far.at[at],
                16 + at,
                16 + at,
                lambda: far,
            )

    def second(k):
        for i, (_, _, _, mine, _, from_far, from_near, _) in enumerate(arrays):
            tag = k * 4 + NEAR
            terms = collect(i, k, NEAR)
            arrive(i, from_far.at[k * 2 + 1], 16 + k * 2 + 1)
            sum_rows(mine.at[tag], terms + [from_far.at[k * 2 + 1]])
            send(
                i,
                lambda mine=mine, tag=tag: mine.at[tag],
                lambda from_near=from_near, k=k: from_near.at[k],
                24 + k,
                24 + k,
                lambda: near,
            )

    def third(k):
        for i, (_, out, _, mine, _, from_far, from_near, from_z) in enumerate(arrays):
            tag = k * 4 + SELF
            terms = collect(i, k, SELF)
            arrive(i, from_far.at[k * 2], 16 + k * 2)
            arrive(i, from_near.at[k], 24 + k)
            terms = terms + [from_far.at[k * 2], from_near.at[k]]
            if k > 0:
                sum_rows(mine.at[tag], terms)
                send(
                    i,
                    lambda mine=mine, tag=tag: mine.at[tag],
                    lambda from_z=from_z, k=k: from_z.at[3 - k],
                    27 + k,
                    31 - k,
                    lambda k=k: moved_z(me, k),
                )
            else:
                for d in range(3):
                    arrive(i, from_z.at[d], 28 + d)
                    terms.append(from_z.at[d])
                sum_rows(out, terms)

    return plan, begin, first, second, third


def sum_scratch(size, width, dtype):
    return [pltpu.VMEM((n, size, width), dtype) for n in (16, 16, 8, 4, 3)]


SUM_BEFORE = {0: [(2, 3), (2, 2), (1, 3), (1, 2)], 3: [(2, "third")], 5: [(1, "third")]}
SUM_MIDDLE = {
    0: [(3, 3), (3, 2), (0, 3), (0, 2)],
    1: [(2, "second")],
    2: [(1, "second")],
    4: [(3, "second")],
    6: [(0, "second")],
}


def sum_events(table, j, first, second, third):
    for n, events in table.items():

        @pl.when(j == n)
        def _():
            for k, what in events:
                if what == "second":
                    second(k)
                elif what == "third":
                    third(k)
                else:
                    first(k, what)


def greet_all(me):
    greet(
        [flipped(me, NEAR), flipped(me, FAR), sibling(me)] + [moved_z(me, d) for d in (1, 2, 3)]
    )


def backward_kernel(
    y_part, grads, pre_all, gates, w_joined, w_down, mix_out, dpre_out, drow_out, gate_grads,
    mine, from_sib, from_far, from_near, from_z, dz, pre, raw, columns, products, dpre, drow,
    send_sem, recv_sem, load_sem, in_sem, out_sem,
):
    me = here()
    greet_all(me)
    plan, begin, first, second, third = sum_plan(
        [(y_part, mix_out, 128, mine, from_sib, from_far, from_near, from_z)],
        send_sem, recv_sem, load_sem,
    )
    half = w_joined.shape[1] // 2
    expert_lanes = half // 2

    def loads(block, slot):
        return [
            pltpu.make_async_copy(rows_at(grads, block, BLOCK), dz.at[slot], in_sem.at[0, slot]),
            pltpu.make_async_copy(rows_at(pre_all, block, BLOCK), pre.at[slot], in_sem.at[1, slot]),
        ]

    def results(block, slot):
        return [
            pltpu.make_async_copy(dpre.at[slot], rows_at(dpre_out, block, BLOCK), out_sem.at[0, slot]),
            pltpu.make_async_copy(drow.at[slot], rows_at(drow_out, block, BLOCK), out_sem.at[1, slot]),
        ]

    for copy in loads(0, 0):
        copy.start()
    begin()

    def step(j, carry):
        slot = lax.rem(j, 2)

        @pl.when(j < 7)
        def _():
            for copy in loads(j + 1, 1 - slot):
                copy.start()

        sum_events(SUM_BEFORE, j, first, second, third)
        for copy in loads(j, slot):
            copy.wait()

        @pl.when(j >= 2)
        def _():
            for copy in results(j - 2, slot):
                copy.wait()

        gate_columns(gates, j * 4, columns, me[0] * 2)
        raw[...] = lax.dot_general(
            dz[slot], w_down[...], (((1,), (1,)), ((), ())), preferred_element_type=jnp.float32
        )
        sum_events(SUM_MIDDLE, j, first, second, third)

        def act(r):
            for i in range(2):
                product = None
                for c in range(i * expert_lanes, (i + 1) * expert_lanes, 128):
                    g = pre[slot, r, c : c + 128]
                    u = pre[slot, r, half + c : half + c + 128]
                    t = raw[r, c : c + 128]
                    sig = 1.0 / (1.0 + jnp.exp(-g))
                    silu = g * sig
                    hidden = (silu * u).astype(jnp.bfloat16).astype(jnp.float32)
                    term = hidden * t
                    product = term if product is None else product + term
                    dh = t * columns[i, r, :]
                    dpre[slot, r, c : c + 128] = (
                        dh * u * sig * (1.0 + g * (1.0 - sig))
                    ).astype(jnp.bfloat16)
                    dpre[slot, r, half + c : half + c + 128] = (dh * silu).astype(jnp.bfloat16)
                products[i, r, :] = product

        tiles(BLOCK // 64, 64, act)
        place = lax.broadcasted_iota(jnp.int32, (16, 128), 0)
        for s in range(4):
            sums = jnp.zeros((16, 128), jnp.float32)
            for i in range(2):
                turned = products[i, pl.ds(s * 128, 128), :].T
                row = jnp.sum(turned, axis=0, keepdims=True)
                sums = jnp.where(place == me[0] * 2 + i, jnp.broadcast_to(row, (16, 128)), sums)
            gate_grads[pl.ds(pl.multiple_of((j * 4 + s) * 16, 16), 16), :] = sums

        def back(rows):
            drow[slot, :, rows] = lax.dot_general(
                dpre[slot],
                w_joined[rows, :],
                (((1,), (1,)), ((), ())),
                preferred_element_type=jnp.float32,
            ).astype(jnp.bfloat16)

        tiles(w_joined.shape[0] // 1024, 1024, back)
        for copy in results(j, slot):
            copy.start()
        return carry

    lax.fori_loop(0, 8, step, 0)
    third(3)
    third(0)
    for j in (6, 7):
        for copy in results(j, j % 2):
            copy.wait()
    plan.finish()


def experts_backward(y_part, grads, pre, gates, w_joined, w_down):
    rows, width = grads.shape
    joined, hidden = w_joined.shape[1], w_down.shape[0]
    bf16, f32, sds = jnp.bfloat16, jnp.float32, jax.ShapeDtypeStruct
    return pl.pallas_call(
        backward_kernel,
        out_shape=[
            sds((rows // 32, width), f32),
            sds((rows, joined), bf16),
            sds((rows, width), bf16),
            sds((512, 128), f32),
        ],
        in_specs=[ANY, ANY, ANY] + [IN_VMEM] * 3,
        out_specs=[IN_VMEM, ANY, ANY, IN_VMEM],
        scratch_shapes=sum_scratch(rows // 32, width, bf16)
        + [
            pltpu.VMEM((2, BLOCK, width), bf16),
            pltpu.VMEM((2, BLOCK, joined), f32),
            pltpu.VMEM((BLOCK, hidden), f32),
            pltpu.VMEM((2, BLOCK, 128), f32),
            pltpu.VMEM((2, BLOCK, 128), f32),
            pltpu.VMEM((2, BLOCK, joined), bf16),
            pltpu.VMEM((2, BLOCK, width), bf16),
            DMA((1, 32)),
            DMA((1, 32)),
            DMA((1, 16)),
            DMA((2, 2)),
            DMA((2, 2)),
        ],
        compiler_params=pltpu.CompilerParams(
            collective_id=2, has_side_effects=True, vmem_limit_bytes=56 * 2**20
        ),
        cost_estimate=cost_of(90),
        name="experts_backward",
    )(y_part, grads, pre, gates, w_joined, w_down)


def weights_kernel(
    drow, gate_grads, x_all, grads, dpre_all, gated_all, row_out, gate_out, d_gate, d_up, d_down,
    mine, from_sib, from_far, from_near, from_z, mine_g, sib_g, far_g, near_g, z_g,
    dpre, gated, tile, wide, send_sem, recv_sem, load_sem, in_sem, tile_sem, out_sem,
):
    me = here()
    greet_all(me)
    plan, begin, first, second, third = sum_plan(
        [
            (drow, row_out, 128, mine, from_sib, from_far, from_near, from_z),
            (gate_grads, gate_out, 16, mine_g, sib_g, far_g, near_g, z_g),
        ],
        send_sem, recv_sem, load_sem,
    )
    span = tile.shape[2]
    steps = x_all.shape[1] // span
    hidden = d_gate.shape[2]
    begin()
    held = [
        pltpu.make_async_copy(dpre_all, dpre, in_sem.at[0]),
        pltpu.make_async_copy(gated_all, gated, in_sem.at[1]),
    ]

    def columns_of(j):
        return pl.ds(pl.multiple_of(lax.rem(j, steps) * span, span), span)

    def fetch(j, slot, act):
        @pl.when(j < steps)
        def _():
            act(pltpu.make_async_copy(x_all.at[:, columns_of(j)], tile.at[slot], tile_sem.at[slot]))

        @pl.when((j >= steps) & (j < 2 * steps))
        def _():
            act(pltpu.make_async_copy(grads.at[:, columns_of(j)], tile.at[slot], tile_sem.at[slot]))

    def results(j, slot, act):
        cols = columns_of(j)

        @pl.when(j < steps)
        def _():
            for i in range(2):
                act(
                    pltpu.make_async_copy(
                        wide.at[slot, :, pl.ds(i * hidden, hidden)], d_gate.at[i, cols, :], out_sem.at[slot, i]
                    )
                )
                act(
                    pltpu.make_async_copy(
                        wide.at[slot, :, pl.ds((2 + i) * hidden, hidden)],
                        d_up.at[i, cols, :],
                        out_sem.at[slot, 2 + i],
                    )
                )

        @pl.when(j >= steps)
        def _():
            act(
                pltpu.make_async_copy(
                    wide.at[slot, :, pl.ds(0, span)], d_down.at[:, cols], out_sem.at[slot, 0]
                )
            )

    fetch(jnp.int32(0), 0, lambda copy: copy.start())
    for copy in held:
        copy.start()

    def step(j, carry):
        slot = lax.rem(j, 2)
        fetch(j + 1, 1 - slot, lambda copy: copy.start())
        sum_events(SUM_BEFORE, j, first, second, third)

        @pl.when(j == 0)
        def _():
            for copy in held:
                copy.wait()

        fetch(j, slot, lambda copy: copy.wait())

        @pl.when(j >= 2)
        def _():
            results(j - 2, slot, lambda copy: copy.wait())

        @pl.when(j < steps)
        def _():
            wide[slot] = lax.dot_general(
                tile[slot], dpre[...], (((0,), (0,)), ((), ())), preferred_element_type=jnp.float32
            )

        @pl.when(j >= steps)
        def _():
            wide[slot, :, 0:span] = lax.dot_general(
                gated[...], tile[slot], (((0,), (0,)), ((), ())), preferred_element_type=jnp.float32
            )

        results(j, slot, lambda copy: copy.start())
        sum_events(SUM_MIDDLE, j, first, second, third)
        return carry

    lax.fori_loop(0, 2 * steps, step, 0)
    third(3)
    third(0)
    for j in (2 * steps - 2, 2 * steps - 1):
        results(jnp.int32(j), j % 2, lambda copy: copy.wait())
    plan.finish()


def experts_weights(drow, gate_grads, x_all, grads, dpre, gated):
    rows, width = grads.shape
    joined, hidden = dpre.shape[1], gated.shape[1]
    span = width // 4
    bf16, f32, sds = jnp.bfloat16, jnp.float32, jax.ShapeDtypeStruct
    return pl.pallas_call(
        weights_kernel,
        out_shape=[
            sds((rows // 32, width), f32),
            sds((16, 128), f32),
            sds((2, width, joined // 4), f32),
            sds((2, width, joined // 4), f32),
            sds((hidden, width), f32),
        ],
        in_specs=[ANY] * 6,
        out_specs=[IN_VMEM, IN_VMEM, ANY, ANY, ANY],
        scratch_shapes=sum_scratch(rows // 32, width, bf16)
        + sum_scratch(16, 128, f32)
        + [
            pltpu.VMEM((rows, joined), bf16),
            pltpu.VMEM((rows, hidden), bf16),
            pltpu.VMEM((2, rows, span), bf16),
            pltpu.VMEM((2, span, joined), f32),
            DMA((2, 32)),
            DMA((2, 32)),
            DMA((2, 16)),
            DMA((2,)),
            DMA((2,)),
            DMA((2, 4)),
        ],
        compiler_params=pltpu.CompilerParams(
            collective_id=3, has_side_effects=True, vmem_limit_bytes=58 * 2**20
        ),
        cost_estimate=cost_of(90),
        name="experts_weights",
    )(drow, gate_grads, x_all, grads, dpre, gated)


def rotated(values, cosines, sines):
    return values * cosines + pltpu.roll(values, HEAD_DIM // 2, 1) * sines


def turned_back(values, cosines, sines):
    return values * cosines - pltpu.roll(values, HEAD_DIM // 2, 1) * sines


def mask_scores(spans_col, places_row, bias):
    place = places_row[0:1, :]

    def body(r):
        allowed = (place >= spans_col[r, 0:1]) & (place <= spans_col[r, 1:2])
        bias[r, :] = jnp.where(allowed, 0.0, -1e30)

    tiles(bias.shape[0] // 128, 128, body)


def attend_kernel(
    qkv, invs, gains, cosines, sines, spans, places, w_out,
    q_out, k_out, v_out, attended, lse, branch, bias,
):
    rows, local = q_out.shape
    mask_scores(spans, places, bias)

    def prepare(r):
        v_out[r, :] = qkv[r, 2 * local : 3 * local].astype(jnp.bfloat16)
        for h in range(local // HEAD_DIM):
            c = slice(h * HEAD_DIM, (h + 1) * HEAD_DIM)
            for i, target in ((0, q_out), (1, k_out)):
                normed = qkv[r, i * local + h * HEAD_DIM : i * local + (h + 1) * HEAD_DIM]
                normed = normed * invs[r, i : i + 1] * gains[i : i + 1, c]
                target[r, c] = rotated(normed, cosines[r, :], sines[r, :]).astype(jnp.bfloat16)

    tiles(rows // 128, 128, prepare)
    scale = 1.0 / math.sqrt(HEAD_DIM)
    for h in range(local // HEAD_DIM):
        c = slice(h * HEAD_DIM, (h + 1) * HEAD_DIM)

        def one(r, h=h, c=c):
            scores = dot32(q_out[r, c], k_out[:, c], NT) * scale + bias[r, :]
            top = jnp.max(scores, axis=-1, keepdims=True)
            total = top + jnp.log(jnp.sum(jnp.exp(scores - top), axis=-1, keepdims=True))
            lse[h, r, :] = total
            probs = jnp.exp(scores - total).astype(jnp.bfloat16)
            attended[r, c] = dot32(probs, v_out[:, c], NN).astype(jnp.bfloat16)

        tiles(rows // 128, 128, one)
    for e in range(w_out.shape[0]):
        span = w_out.shape[2]
        branch[:, e * span : (e + 1) * span] = dot32(attended[...], w_out[e], NN).astype(
            jnp.bfloat16
        )


def attend(qkv, invs, gains, cosines, sines, spans, places, w_out):
    rows, local = qkv.shape[0], qkv.shape[1] // 3
    bf16, f32, sds = jnp.bfloat16, jnp.float32, jax.ShapeDtypeStruct
    return pl.pallas_call(
        attend_kernel,
        out_shape=[sds((rows, local), bf16)] * 4
        + [
            sds((local // HEAD_DIM, rows, 1), f32),
            sds((rows, w_out.shape[0] * w_out.shape[2]), bf16),
        ],
        in_specs=[IN_VMEM] * 8,
        out_specs=[IN_VMEM] * 6,
        scratch_shapes=[pltpu.VMEM((rows, rows), f32)],
        compiler_params=pltpu.CompilerParams(vmem_limit_bytes=32 * 2**20),
        cost_estimate=cost_of(15),
        name="attend",
    )(qkv, invs, gains, cosines, sines, spans, places, w_out)


def attend_back_kernel(
    grad, w_out, q, k, v, lse, qkv, invs, gains, cosines, sines, spans, places,
    hat_grads, value_grad, dots, d_gains, bias, out_grad, probs_low, score_grad,
):
    rows, local = q.shape
    mask_scores(spans, places, bias)
    span = w_out.shape[2]

    def project(r):
        total = None
        for e in range(w_out.shape[0]):
            term = dot32(grad[r, e * span : (e + 1) * span], w_out[e], NT)
            total = term if total is None else total + term
        out_grad[r, :] = total.astype(jnp.bfloat16)

    tiles(rows // 128, 128, project)
    scale = 1.0 / math.sqrt(HEAD_DIM)
    dots[...] = jnp.zeros_like(dots)
    for h in range(local // HEAD_DIM):
        c = slice(h * HEAD_DIM, (h + 1) * HEAD_DIM)

        def one(r, h=h, c=c):
            scores = dot32(q[r, c], k[:, c], NT) * scale + bias[r, :]
            probs = jnp.exp(scores - lse[h, r, :])
            prob_grad = dot32(out_grad[r, c], v[:, c], NT)
            delta = jnp.sum(probs * prob_grad, axis=-1, keepdims=True)
            probs_low[r, :] = probs.astype(jnp.bfloat16)
            score_grad[r, :] = (probs * (prob_grad - delta) * scale).astype(jnp.bfloat16)

        tiles(rows // 128, 128, one)
        value_grad[:, c] = dot32(probs_low[...], out_grad[:, c], TN).astype(jnp.bfloat16)
        for i, turned in (
            (0, dot32(score_grad[...], k[:, c], NN)),
            (1, dot32(score_grad[...], q[:, c], TN)),
        ):
            at = slice(i * local + h * HEAD_DIM, i * local + (h + 1) * HEAD_DIM)
            norm_grad = turned_back(turned, cosines[...], sines[...])
            hat = qkv[:, at] * invs[:, i : i + 1]
            hat_grad = norm_grad * gains[i : i + 1, c]
            hat_grads[:, at] = hat_grad
            d_gains[i : i + 1, c] = jnp.sum(norm_grad * hat, axis=0, keepdims=True)
            dots[i] += jnp.sum(hat_grad * hat, axis=-1, keepdims=True)


def attend_back(grad, w_out, q, k, v, lse, qkv, invs, gains, cosines, sines, spans, places):
    rows, local = q.shape
    bf16, f32, sds = jnp.bfloat16, jnp.float32, jax.ShapeDtypeStruct
    return pl.pallas_call(
        attend_back_kernel,
        out_shape=[
            sds((rows, 2 * local), f32),
            sds((rows, local), bf16),
            sds((2, rows, 1), f32),
            sds((2, local), f32),
        ],
        in_specs=[IN_VMEM] * 13,
        out_specs=[IN_VMEM] * 4,
        scratch_shapes=[
            pltpu.VMEM((rows, rows), f32),
            pltpu.VMEM((rows, local), bf16),
            pltpu.VMEM((rows, rows), bf16),
            pltpu.VMEM((rows, rows), bf16),
        ],
        compiler_params=pltpu.CompilerParams(vmem_limit_bytes=40 * 2**20),
        cost_estimate=cost_of(25),
        name="attend_back",
    )(grad, w_out, q, k, v, lse, qkv, invs, gains, cosines, sines, spans, places)


BOTH = (EXPERT, TENSOR)


def dot32(left, right, dims):
    return lax.dot_general(left, right, (dims, ((), ())), preferred_element_type=jnp.float32)


NN = ((1,), (0,))
NT = ((1,), (1,))
TN = ((0,), (0,))


def rms_inv(values):
    return lax.rsqrt(jnp.mean(values * values, axis=-1, keepdims=True) + NORM_EPS)


def dense_body(
    tokens,
    attn_gain,
    w_query,
    w_key,
    w_value,
    w_out,
    query_gain,
    key_gain,
    ffn_gain,
    w_router,
    w_gate,
    w_up,
    w_down,
    doc_ids,
    routes,
    deal,
    out_grad,
):
    rows, width = tokens.shape
    parts = lax.axis_size(TENSOR)
    blocks = lax.axis_size(EXPERT)
    column = lax.axis_index(TENSOR)
    block = lax.axis_index(EXPERT)
    own = rows // parts
    share = rows // blocks
    piece = share // parts
    bf16, f32 = jnp.bfloat16, jnp.float32

    def reorder(per_place):
        grid = per_place.reshape((blocks, parts, piece) + per_place.shape[1:])
        return jnp.swapaxes(grid, 0, 1).reshape(per_place.shape)

    local_width = w_query.shape[1]
    head_count = local_width // HEAD_DIM
    expert_count = w_router.shape[1]
    qkv_own = jnp.concatenate([w_query, w_key, w_value], axis=1)
    gain_stack = jnp.stack([attn_gain, query_gain, key_gain, ffn_gain], axis=1)
    small_own = jnp.concatenate([w_router, gain_stack], axis=1)
    small_own = jnp.pad(small_own, ((0, 0), (0, 128 - small_own.shape[1])))
    deal_grid = deal.reshape(blocks, blocks, parts, piece)
    picks = lax.dynamic_slice(deal_grid, (0, block, column, 0), (blocks, 1, 1, piece)).reshape(-1)
    picks = picks - block * rows
    inputs, dealt_grads, qkv_full, small_full = start_exchange(
        tokens[picks].reshape(blocks, piece, width),
        out_grad[picks].reshape(blocks, piece, width),
        qkv_own,
        small_own,
    )
    own_low = lax.dynamic_slice_in_dim(inputs, column, 1, 0).reshape(own, width)
    inputs = inputs.reshape(rows, width).astype(f32)
    qkv_full = qkv_full.reshape(width, -1)
    small_full = small_full.reshape(width, -1)
    router_full = small_full[:, :expert_count]
    gain_full = small_full[:, expert_count : expert_count + 4].T.astype(f32)
    gain_attn, gain_ffn = gain_full[0], gain_full[3]
    gain_query = lax.dynamic_slice_in_dim(gain_full[1], column * local_width, local_width)
    gain_key = lax.dynamic_slice_in_dim(gain_full[2], column * local_width, local_width)
    out_full = lax.all_gather(w_out, EXPERT, axis=0)
    own_grad_low = dealt_grads.reshape(own, width)
    grads_all = lax.all_gather(own_grad_low, BOTH, axis=0, tiled=True)
    own_in = own_low.astype(f32)
    own_grad = own_grad_low.astype(f32)

    scale = 1.0 / math.sqrt(HEAD_DIM)
    normed = (inputs * rms_inv(inputs) * gain_attn).astype(bf16)
    qkv = dot32(normed, qkv_full, NN)
    query_pre = qkv[:, :local_width]
    key_pre = qkv[:, local_width : 2 * local_width]
    squares = lax.psum(
        jnp.stack([jnp.sum(query_pre * query_pre, axis=-1), jnp.sum(key_pre * key_pre, axis=-1)]),
        TENSOR,
    )
    cosines, sines, starts = rope_tables(doc_ids, HEAD_DIM)
    cosines = reorder(jnp.concatenate([cosines, cosines], axis=1))
    sines = reorder(jnp.concatenate([-sines, sines], axis=1))
    positions = reorder(jnp.arange(rows, dtype=jnp.int32))
    spans = jnp.stack([reorder(starts), positions], axis=1)
    places = jnp.broadcast_to(positions[None], (8, rows))
    invs = lax.rsqrt(squares / width + NORM_EPS).T
    gains = jnp.stack([gain_query, gain_key])
    query_rot, key_rot, value_rows, attended, log_total, branch = attend(
        qkv, invs, gains, cosines, sines, spans, places, out_full
    )
    branch_own = sum_tensor(branch)

    residual = own_in + branch_own
    resid_inv = rms_inv(residual)
    resid_hat = residual * resid_inv
    ffn_in = (resid_hat * gain_ffn).astype(bf16)
    logits = dot32(ffn_in, router_full, NN)
    router_probs = jax.nn.softmax(logits, axis=-1)
    local_experts = w_gate.shape[0]
    own_routes = lax.dynamic_slice(
        routes.reshape(blocks, parts, piece, -1),
        (0, column, 0, 0),
        (blocks, 1, piece, routes.shape[1]),
    ).reshape(own, -1)
    expert_ids = jnp.arange(expert_count, dtype=jnp.int32)
    routed = jnp.any(own_routes[:, :, None] == expert_ids[None, None, :], axis=1)
    gates_own = jnp.where(routed, router_probs, 0.0)

    hidden_width = w_gate.shape[2]
    joined_weight = jnp.concatenate(
        [w_gate[i] for i in range(local_experts)] + [w_up[i] for i in range(local_experts)], axis=1
    )
    down_weight = w_down.reshape(local_experts * hidden_width, width)
    rows_all, gates_all, pre_all, gated_all, mixed = experts_forward(
        ffn_in, gates_own.T, joined_weight, down_weight
    )
    mix_own, joined_grad, row_terms, gate_grads = experts_backward(
        mixed, grads_all, pre_all, gates_all, joined_weight, down_weight
    )
    output_own = (residual + mix_own).astype(bf16)
    row_own, gate_grad_own, d_w_gate, d_w_up, d_w_down = experts_weights(
        row_terms, gate_grads, rows_all, grads_all, joined_grad, gated_all
    )
    gate_grad_own = gate_grad_own.T
    d_w_down = d_w_down.reshape(w_down.shape)

    prob_grad = jnp.where(routed, gate_grad_own, 0.0)
    logit_grad = (
        router_probs * (prob_grad - jnp.sum(router_probs * prob_grad, axis=-1, keepdims=True))
    ).astype(bf16)
    d_router = dot32(ffn_in, logit_grad, TN)
    ffn_grad = row_own + dot32(logit_grad, router_full, NT)
    d_ffn_gain = jnp.sum(ffn_grad * resid_hat, axis=0)
    scaled_ffn = ffn_grad * gain_ffn
    resid_grad = own_grad + resid_inv * (
        scaled_ffn - resid_hat * jnp.mean(scaled_ffn * resid_hat, axis=-1, keepdims=True)
    )
    branch_grad = gather_tensor(resid_grad.astype(bf16))

    branch_cols = branch_grad.reshape(rows, blocks, width // blocks)
    d_wo = jnp.einsum("rk,red->ekd", attended, branch_cols, preferred_element_type=f32).astype(bf16)
    d_wo, branch_grad = lax.optimization_barrier((d_wo, branch_grad))
    sum_wo = lax.psum_scatter(d_wo, EXPERT, scatter_dimension=0, tiled=False)
    hat_grads, value_grad, dots, d_gains = attend_back(
        branch_grad, out_full, query_rot, key_rot, value_rows, log_total,
        qkv, invs, gains, cosines, sines, spans, places,
    )
    d_query_gain, d_key_gain = d_gains[0], d_gains[1]
    dots = lax.psum(dots.reshape(2, rows), TENSOR) / width

    def norm_back(i):
        part = slice(i * local_width, (i + 1) * local_width)
        inv = invs[:, i : i + 1]
        return (inv * (hat_grads[:, part] - qkv[:, part] * inv * dots[i][:, None])).astype(bf16)

    query_grad, key_grad = norm_back(0), norm_back(1)
    qkv_grad = jnp.concatenate([query_grad, key_grad, value_grad], axis=1)
    input_terms = dot32(qkv_grad, qkv_full, NT).astype(bf16)
    normed_grad = sum_tensor(input_terms)
    d_qkv = dot32(normed, qkv_grad, TN).astype(bf16)

    own_inv = rms_inv(own_in)
    own_hat = own_in * own_inv
    d_attn_gain = jnp.sum(normed_grad * own_hat, axis=0)
    scaled_attn = normed_grad * gain_attn
    input_grad = resid_grad + own_inv * (
        scaled_attn - own_hat * jnp.mean(scaled_attn * own_hat, axis=-1, keepdims=True)
    )

    def widen(slots):
        return lax.dynamic_update_slice_in_dim(
            jnp.zeros((width,), f32), slots, column * local_width, 0
        )

    small = jnp.concatenate(
        [
            d_router.T,
            jnp.stack([d_attn_gain, widen(d_query_gain), widen(d_key_gain), d_ffn_gain]),
        ]
    )
    small = jnp.pad(small, ((0, 24 - small.shape[0]), (0, 0)))
    small = jnp.swapaxes(small.reshape(24, blocks, -1), 0, 1)

    back_out, back_in, sum_qkv, small = last_exchange(
        output_own.reshape(blocks, piece, width),
        input_grad.astype(bf16).reshape(blocks, piece, width),
        d_qkv.reshape(blocks, -1, d_qkv.shape[1]),
        small,
    )
    sum_router = small[:expert_count].T
    sum_gains = small[expert_count:]
    came = lax.dynamic_slice(deal_grid, (0, block, 0, 0), (blocks, 1, parts, piece))
    came = jnp.swapaxes(came.reshape(blocks, parts, piece), 0, 1).reshape(-1) - block * rows
    chooser = (jnp.arange(rows, dtype=jnp.int32)[:, None] == came[None, :]).astype(bf16)
    output = dot32(chooser, back_out.reshape(rows, width), NN).astype(bf16)
    d_tokens = dot32(chooser, back_in.reshape(rows, width), NN).astype(bf16)
    return (
        output,
        d_tokens,
        sum_gains[0],
        sum_qkv[:, :local_width],
        sum_qkv[:, local_width : 2 * local_width],
        sum_qkv[:, 2 * local_width :],
        sum_wo.astype(f32),
        sum_gains[1],
        sum_gains[2],
        sum_gains[3],
        sum_router,
        d_w_gate,
        d_w_up,
        d_w_down,
    )


def pick_body(*args):
    routes, experts = args[14], args[9].shape[1]
    mesh_fits = (lax.axis_size(EXPERT), lax.axis_size(TENSOR)) == (8, 4)
    body = dense_body if mesh_fits and experts <= 2 * routes.shape[1] else routed_body
    return body(*args)


def solution(mesh):
    in_specs = (
        P(EXPERT, None),
        P(EXPERT),
        P(EXPERT, TENSOR),
        P(EXPERT, TENSOR),
        P(EXPERT, TENSOR),
        P(TENSOR, EXPERT),
        P(EXPERT),
        P(EXPERT),
        P(EXPERT),
        P(EXPERT, None),
        P(EXPERT, None, TENSOR),
        P(EXPERT, None, TENSOR),
        P(EXPERT, TENSOR, None),
        P(EXPERT),
        P(EXPERT, None),
        P(),
        P(EXPERT, None),
    )
    out_specs = (
        P(EXPERT, None),
        P(EXPERT, None),
        P(EXPERT),
        P(EXPERT, TENSOR),
        P(EXPERT, TENSOR),
        P(EXPERT, TENSOR),
        P(TENSOR, EXPERT),
        P(EXPERT),
        P(EXPERT),
        P(EXPERT),
        P(EXPERT, None),
        P(EXPERT, None, TENSOR),
        P(EXPERT, None, TENSOR),
        P(EXPERT, TENSOR, None),
    )
    return jax.shard_map(pick_body, mesh=mesh, in_specs=in_specs, out_specs=out_specs, check_vma=False)
```

```python
import functools
import math

import jax
import jax.numpy as jnp
from jax import lax
from jax.experimental import pallas as pl
from jax.experimental.pallas import tpu as pltpu
from jax.sharding import PartitionSpec as P

HEAD_DIM = 128
EXPERT, TENSOR = "expert", "tensor"


NORM_EPS = 1e-05
ROPE_BASE = 10000.0


def rope_tables(documents, head_size):
    row_count = documents.shape[0]
    positions = jnp.arange(row_count, dtype=jnp.int32)
    new_doc = jnp.concatenate(
        [jnp.ones((1,), jnp.int32), (documents[1:] != documents[:-1]).astype(jnp.int32)]
    )
    starts = lax.cummax(jnp.where(new_doc > 0, positions, 0), axis=0)
    places = (positions - starts).astype(jnp.float32)
    half_dim = head_size // 2
    frequency = jnp.exp(
        jnp.arange(half_dim, dtype=jnp.float32) * (-2.0 * math.log(ROPE_BASE) / head_size)
    )
    angles = places[:, None] * frequency[None, :]
    return (jnp.cos(angles), jnp.sin(angles), starts)


def rotate(values, cosines, sines):
    half_dim = values.shape[-1] // 2
    first_half = values[..., :half_dim]
    second_half = values[..., half_dim:]
    cos_rows = cosines[:, None, :]
    sin_rows = sines[:, None, :]
    return jnp.concatenate(
        [
            first_half * cos_rows - second_half * sin_rows,
            second_half * cos_rows + first_half * sin_rows,
        ],
        axis=-1,
    )


def unrotate(grads_in, cosines, sines):
    half_dim = grads_in.shape[-1] // 2
    first_half = grads_in[..., :half_dim]
    second_half = grads_in[..., half_dim:]
    cos_rows = cosines[:, None, :]
    sin_rows = sines[:, None, :]
    return jnp.concatenate(
        [
            first_half * cos_rows + second_half * sin_rows,
            second_half * cos_rows - first_half * sin_rows,
        ],
        axis=-1,
    )


def to_experts(rows):
    return lax.all_to_all(rows, EXPERT, split_axis=0, concat_axis=0, tiled=True)


def from_experts(rows):
    return lax.all_to_all(rows, EXPERT, split_axis=0, concat_axis=0, tiled=True)


def hidden_sums(terms):
    return lax.psum_scatter(terms, TENSOR, scatter_dimension=3, tiled=True)


def routed_body(
    tokens,
    attn_gain,
    w_query,
    w_key,
    w_value,
    w_out,
    query_gain,
    key_gain,
    ffn_gain,
    w_router,
    w_gate,
    w_up,
    w_down,
    doc_ids,
    routes,
    deal,
    out_grad,
):
    row_count, width = tokens.shape
    tensor_parts = lax.axis_size(TENSOR)
    expert_parts = lax.axis_size(EXPERT)
    column = lax.axis_index(TENSOR)
    device_idx = lax.axis_index(EXPERT)
    quarter = width // tensor_parts
    share_rows = row_count // expert_parts
    deal_rows = lax.dynamic_slice_in_dim(
        deal.reshape(expert_parts, row_count), device_idx * share_rows, share_rows, 1
    )
    local_pick = deal_rows - device_idx * row_count
    dealt_tokens, dealt_grad = (
        lax.all_to_all(tokens[local_pick], EXPERT, split_axis=0, concat_axis=0, tiled=True),
        lax.all_to_all(out_grad[local_pick], EXPERT, split_axis=0, concat_axis=0, tiled=True),
    )
    dealt_tokens = dealt_tokens.reshape(row_count, width)
    dealt_grad = dealt_grad.reshape(row_count, width)
    gain_stack = jnp.stack([attn_gain, query_gain, key_gain, ffn_gain])
    wq_full, wk_full, wv_full, wo_full, router_full, gain_full = (
        lax.all_gather(w_query, EXPERT, axis=0, tiled=True),
        lax.all_gather(w_key, EXPERT, axis=0, tiled=True),
        lax.all_gather(w_value, EXPERT, axis=0, tiled=True),
        lax.all_gather(w_out, EXPERT, axis=1, tiled=True),
        lax.all_gather(w_router, EXPERT, axis=0, tiled=True),
        lax.all_gather(gain_stack, EXPERT, axis=1, tiled=True),
    )
    local_width = wq_full.shape[1]
    head_count = local_width // HEAD_DIM
    gain_attn = gain_full[0].astype(jnp.float32)
    gain_query = lax.dynamic_slice_in_dim(
        gain_full[1].astype(jnp.float32), column * local_width, local_width
    )
    gain_key = lax.dynamic_slice_in_dim(
        gain_full[2].astype(jnp.float32), column * local_width, local_width
    )
    gain_ffn = gain_full[3].astype(jnp.float32)
    scale = 1.0 / math.sqrt(HEAD_DIM)
    inputs = dealt_tokens.astype(jnp.float32)
    input_inv = lax.rsqrt(jnp.mean(inputs * inputs, axis=-1, keepdims=True) + NORM_EPS)
    input_hat = inputs * input_inv
    normed = (input_hat * gain_attn).astype(jnp.bfloat16)
    query_pre = jnp.dot(normed, wq_full, preferred_element_type=jnp.float32)
    key_pre = jnp.dot(normed, wk_full, preferred_element_type=jnp.float32)
    value_rows = (
        jnp.dot(normed, wv_full, preferred_element_type=jnp.float32)
        .astype(jnp.bfloat16)
        .reshape(row_count, head_count, HEAD_DIM)
    )
    query_sq, key_sq = lax.psum(
        (jnp.sum(query_pre * query_pre, axis=-1), jnp.sum(key_pre * key_pre, axis=-1)), TENSOR
    )
    query_inv = lax.rsqrt(query_sq / width + NORM_EPS)[:, None]
    key_inv = lax.rsqrt(key_sq / width + NORM_EPS)[:, None]
    query_hat = query_pre * query_inv
    key_hat = key_pre * key_inv
    cosines, sines, _ = rope_tables(doc_ids, HEAD_DIM)
    query_rot = rotate(
        (query_hat * gain_query).reshape(row_count, head_count, HEAD_DIM), cosines, sines
    ).astype(jnp.bfloat16)
    key_rot = rotate(
        (key_hat * gain_key).reshape(row_count, head_count, HEAD_DIM), cosines, sines
    ).astype(jnp.bfloat16)
    positions = jnp.arange(row_count, dtype=jnp.int32)
    allowed = (doc_ids[:, None] == doc_ids[None, :]) & (positions[None, :] <= positions[:, None])

    def masked_scores():
        raw_scores = jnp.einsum(
            "qhd,khd->hqk", query_rot, key_rot, preferred_element_type=jnp.float32
        )
        return jnp.where(allowed[None], raw_scores * scale, -1e30)

    scores = masked_scores()
    top_score = jnp.max(scores, axis=-1, keepdims=True)
    log_total = top_score + jnp.log(jnp.sum(jnp.exp(scores - top_score), axis=-1, keepdims=True))
    weights = jnp.exp(scores - log_total).astype(jnp.bfloat16)
    attended = (
        jnp.einsum("hqk,khd->qhd", weights, value_rows, preferred_element_type=jnp.float32)
        .astype(jnp.bfloat16)
        .reshape(row_count, local_width)
    )
    branch = lax.psum(jnp.dot(attended, wo_full, preferred_element_type=jnp.float32), TENSOR)
    residual = inputs + branch
    resid_inv = lax.rsqrt(jnp.mean(residual * residual, axis=-1, keepdims=True) + NORM_EPS)
    resid_hat = residual * resid_inv
    ffn_in = (resid_hat * gain_ffn).astype(jnp.bfloat16)
    logits = jnp.dot(ffn_in, router_full, preferred_element_type=jnp.float32)
    router_probs = jax.nn.softmax(logits, axis=-1)
    expert_count = router_full.shape[1]
    top_count = routes.shape[1]
    local_experts = expert_count // expert_parts
    capacity = tensor_parts * max(
        1,
        (row_count * top_count + expert_count * tensor_parts - 1) // (expert_count * tensor_parts),
        row_count * top_count * 5 // (4 * expert_count * tensor_parts),
    )
    expert_ids = jnp.arange(expert_count, dtype=jnp.int32)
    route_match = routes[:, :, None] == expert_ids[None, None, :]
    gate_probs = jnp.sum(jnp.where(route_match, router_probs[:, None, :], 0.0), axis=-1)
    flat_routes = routes.reshape(-1)
    onehot = (flat_routes[:, None] == expert_ids[None, :]).astype(jnp.int32)
    slot_rank = jnp.sum((jnp.cumsum(onehot, axis=0) - onehot) * onehot, axis=-1)
    row_ids = flat_routes * capacity + slot_rank
    token_ids = jnp.arange(row_count * top_count, dtype=jnp.int32) // top_count
    slot_token = (
        jnp.full((expert_count * capacity,), row_count, jnp.int32).at[row_ids].set(token_ids)
    )
    slot_gates = (
        jnp.zeros((expert_count * capacity,), jnp.float32).at[row_ids].set(gate_probs.reshape(-1))
    )
    pick_rows = row_ids.reshape(row_count, top_count)
    padded_in = jnp.concatenate([ffn_in, jnp.zeros((1, width), jnp.bfloat16)], axis=0)
    grad_full = dealt_grad.astype(jnp.float32)
    grad_padded = jnp.concatenate([grad_full, jnp.zeros((1, width), jnp.float32)], axis=0)
    received = to_experts(
        padded_in[slot_token].reshape(expert_parts, local_experts, capacity, width)
    )
    gate_pre = jnp.einsum("secd,edf->secf", received, w_gate, preferred_element_type=jnp.float32)
    up_pre = jnp.einsum("secd,edf->secf", received, w_up, preferred_element_type=jnp.float32)
    sigmoid_gate = jax.nn.sigmoid(gate_pre)
    silu_gate = gate_pre * sigmoid_gate
    hidden = (silu_gate * up_pre).astype(jnp.bfloat16)
    partial_out = jnp.einsum("secf,efd->secd", hidden, w_down, preferred_element_type=jnp.float32)
    own_columns = hidden_sums(partial_out).astype(jnp.bfloat16)
    returned = from_experts(own_columns).reshape(expert_count * capacity, quarter)
    chosen = returned[pick_rows].astype(jnp.float32)
    mix_own = jnp.sum(gate_probs[:, :, None] * chosen, axis=1)
    mix_part = lax.dynamic_update_slice_in_dim(
        jnp.zeros((row_count, width), jnp.float32), mix_own, column * quarter, 1
    )
    grad_own = lax.dynamic_slice_in_dim(grad_full, column * quarter, quarter, 1)
    gate_grad_part = jnp.sum(grad_own[:, None, :] * chosen, axis=-1)
    send_grad = (
        (grad_padded[slot_token] * slot_gates[:, None])
        .astype(jnp.bfloat16)
        .reshape(expert_parts, local_experts, capacity, width)
    )
    recv_grad = to_experts(send_grad)
    d_w_down = jnp.einsum("secf,secd->efd", hidden, recv_grad, preferred_element_type=jnp.float32)
    hidden_grad = jnp.einsum(
        "secd,efd->secf", recv_grad, w_down, preferred_element_type=jnp.float32
    )
    gate_grad_pre = (
        hidden_grad * up_pre * sigmoid_gate * (1.0 + gate_pre * (1.0 - sigmoid_gate))
    ).astype(jnp.bfloat16)
    up_grad_pre = (hidden_grad * silu_gate).astype(jnp.bfloat16)
    d_w_gate = jnp.einsum(
        "secd,secf->edf", received, gate_grad_pre, preferred_element_type=jnp.float32
    )
    d_w_up = jnp.einsum("secd,secf->edf", received, up_grad_pre, preferred_element_type=jnp.float32)
    joined_grad = jnp.concatenate([gate_grad_pre, up_grad_pre], axis=-1)
    joined_weight = jnp.concatenate([w_gate, w_up], axis=-1)
    row_terms = jnp.einsum(
        "secf,edf->secd", joined_grad, joined_weight, preferred_element_type=jnp.float32
    )
    row_own = hidden_sums(row_terms).astype(jnp.bfloat16)
    row_back = from_experts(row_own).reshape(expert_count * capacity, quarter)
    ffn_grad_own = jnp.sum(row_back[pick_rows].astype(jnp.float32), axis=1)
    placed = lax.dynamic_update_slice_in_dim(
        jnp.zeros((row_count, width), jnp.float32), ffn_grad_own, column * quarter, 1
    )
    ffn_grad_rows, gate_grad, mix_total = lax.psum((placed, gate_grad_part, mix_part), TENSOR)
    output = (residual + mix_total).astype(jnp.bfloat16)
    prob_grad = jnp.sum(jnp.where(route_match, gate_grad[:, :, None], 0.0), axis=1)
    logit_grad = (
        router_probs * (prob_grad - jnp.sum(router_probs * prob_grad, axis=-1, keepdims=True))
    ).astype(jnp.bfloat16)
    d_router = jnp.einsum("rd,re->de", ffn_in, logit_grad, preferred_element_type=jnp.float32)
    ffn_grad = ffn_grad_rows + jnp.einsum(
        "re,de->rd", logit_grad, router_full, preferred_element_type=jnp.float32
    )
    d_ffn_gain = jnp.sum(ffn_grad * resid_hat, axis=0)
    scaled_ffn = ffn_grad * gain_ffn
    resid_grad = grad_full + resid_inv * (
        scaled_ffn - resid_hat * jnp.mean(scaled_ffn * resid_hat, axis=-1, keepdims=True)
    )
    branch_grad = resid_grad.astype(jnp.bfloat16)
    d_wo = jnp.einsum("rk,rd->kd", attended, branch_grad, preferred_element_type=jnp.float32)
    attended_grad = (
        jnp.einsum("rd,kd->rk", branch_grad, wo_full, preferred_element_type=jnp.float32)
        .astype(jnp.bfloat16)
        .reshape(row_count, head_count, HEAD_DIM)
    )
    probs_again = jnp.exp(masked_scores() - log_total)
    prob_grads = jnp.einsum(
        "qhd,khd->hqk", attended_grad, value_rows, preferred_element_type=jnp.float32
    )
    value_grad = (
        jnp.einsum(
            "hqk,qhd->khd",
            probs_again.astype(jnp.bfloat16),
            attended_grad,
            preferred_element_type=jnp.float32,
        )
        .astype(jnp.bfloat16)
        .reshape(row_count, local_width)
    )
    row_delta = jnp.sum(probs_again * prob_grads, axis=-1, keepdims=True)
    score_grad = (probs_again * (prob_grads - row_delta) * scale).astype(jnp.bfloat16)
    query_rot_grad = jnp.einsum(
        "hqk,khd->qhd", score_grad, key_rot, preferred_element_type=jnp.float32
    )
    key_rot_grad = jnp.einsum(
        "hqk,qhd->khd", score_grad, query_rot, preferred_element_type=jnp.float32
    )
    query_norm_grad = unrotate(query_rot_grad, cosines, sines).reshape(row_count, local_width)
    key_norm_grad = unrotate(key_rot_grad, cosines, sines).reshape(row_count, local_width)
    query_hat_grad = query_norm_grad * gain_query
    key_hat_grad = key_norm_grad * gain_key
    gain_pieces = jnp.stack(
        [jnp.sum(query_norm_grad * query_hat, axis=0), jnp.sum(key_norm_grad * key_hat, axis=0)]
    )
    gain_parts = lax.dynamic_update_slice_in_dim(
        jnp.zeros((2, width), jnp.float32), gain_pieces, column * local_width, 1
    )
    query_dot, key_dot, qk_gains = lax.psum(
        (
            jnp.sum(query_hat_grad * query_hat, axis=-1),
            jnp.sum(key_hat_grad * key_hat, axis=-1),
            gain_parts,
        ),
        TENSOR,
    )
    query_grad = (query_inv * (query_hat_grad - query_hat * (query_dot / width)[:, None])).astype(
        jnp.bfloat16
    )
    key_grad = (key_inv * (key_hat_grad - key_hat * (key_dot / width)[:, None])).astype(
        jnp.bfloat16
    )
    d_wq = jnp.einsum("rd,rk->dk", normed, query_grad, preferred_element_type=jnp.float32)
    d_wk = jnp.einsum("rd,rk->dk", normed, key_grad, preferred_element_type=jnp.float32)
    d_wv = jnp.einsum("rd,rk->dk", normed, value_grad, preferred_element_type=jnp.float32)
    input_terms = jnp.einsum("rk,dk->rd", query_grad, wq_full, preferred_element_type=jnp.float32)
    input_terms = input_terms + jnp.einsum(
        "rk,dk->rd", key_grad, wk_full, preferred_element_type=jnp.float32
    )
    input_terms = input_terms + jnp.einsum(
        "rk,dk->rd", value_grad, wv_full, preferred_element_type=jnp.float32
    )
    normed_grad = lax.psum(input_terms, TENSOR)
    d_attn_part = jnp.sum(normed_grad * input_hat, axis=0)
    scaled_attn = normed_grad * gain_attn
    input_grad = resid_grad + input_inv * (
        scaled_attn - input_hat * jnp.mean(scaled_attn * input_hat, axis=-1, keepdims=True)
    )
    dealt_dtokens = input_grad.astype(jnp.bfloat16)
    gain_grads = jnp.stack([d_attn_part, qk_gains[0], qk_gains[1], d_ffn_gain])
    sum_wq, sum_wk, sum_wv, sum_wo, sum_router, sum_gains = (
        lax.psum_scatter(d_wq, EXPERT, scatter_dimension=0, tiled=True),
        lax.psum_scatter(d_wk, EXPERT, scatter_dimension=0, tiled=True),
        lax.psum_scatter(d_wv, EXPERT, scatter_dimension=0, tiled=True),
        lax.psum_scatter(d_wo, EXPERT, scatter_dimension=1, tiled=True),
        lax.psum_scatter(d_router, EXPERT, scatter_dimension=0, tiled=True),
        lax.psum_scatter(gain_grads, EXPERT, scatter_dimension=1, tiled=True),
    )
    back_out, back_dtok = (
        lax.all_to_all(
            output.reshape(expert_parts, share_rows, width),
            EXPERT,
            split_axis=0,
            concat_axis=0,
            tiled=True,
        ),
        lax.all_to_all(
            dealt_dtokens.reshape(expert_parts, share_rows, width),
            EXPERT,
            split_axis=0,
            concat_axis=0,
            tiled=True,
        ),
    )
    flat_pick = local_pick.reshape(-1)
    output_rows = (
        jnp.zeros((row_count, width), jnp.bfloat16)
        .at[flat_pick]
        .set(back_out.reshape(row_count, width))
    )
    d_tokens = (
        jnp.zeros((row_count, width), jnp.bfloat16)
        .at[flat_pick]
        .set(back_dtok.reshape(row_count, width))
    )
    return (
        output_rows,
        d_tokens,
        sum_gains[0],
        sum_wq,
        sum_wk,
        sum_wv,
        sum_wo,
        sum_gains[1],
        sum_gains[2],
        sum_gains[3],
        sum_router,
        d_w_gate,
        d_w_up,
        d_w_down,
    )


MESH_ID = pl.DeviceIdType.MESH
ANY = pl.BlockSpec(memory_space=pl.ANY)
IN_VMEM = pl.BlockSpec(memory_space=pltpu.VMEM)
def cost_of(micros):
    return pl.CostEstimate(flops=0, bytes_accessed=micros * 3_000_000, transcendentals=0)


SELF, NEAR, FAR, BOTH_FLIPPED = 0, 1, 2, 3


def place_of(device):
    expert, tensor = device
    return expert // 2, expert % 2, tensor // 2, tensor % 2


def flipped(device, role):
    expert, tensor = device
    _, x, y, core = place_of(device)
    step_x, step_y = 1 - 2 * x, 2 - 4 * y
    if role == NEAR:
        return expert + (1 - core) * step_x, tensor + core * step_y
    if role == FAR:
        return expert + core * step_x, tensor + (1 - core) * step_y
    if role == BOTH_FLIPPED:
        return expert + step_x, tensor + step_y
    return expert, tensor


def moved_z(device, hops):
    expert, tensor = device
    return lax.rem(expert + 2 * hops, 8), tensor


def sibling(device):
    expert, tensor = device
    return expert, tensor + 1 - 2 * (tensor % 2)


def slot_of(device):
    return device[0] * 4 + device[1]


def here():
    return lax.axis_index(EXPERT), lax.axis_index(TENSOR)


def greet(partners):
    barrier = pltpu.get_barrier_semaphore()
    for partner in partners:
        pl.semaphore_signal(barrier, inc=1, device_id=partner, device_id_type=MESH_ID)
    pl.semaphore_wait(barrier, len(partners))


def push(source, target, send_sem, recv_sem, device):
    return pltpu.make_async_remote_copy(
        src_ref=source,
        dst_ref=target,
        send_sem=send_sem,
        recv_sem=recv_sem,
        device_id=device,
        device_id_type=MESH_ID,
    )


def hop(device, flips, hops):
    expert, tensor = device
    return lax.rem(expert + flips * (1 - 2 * lax.rem(expert, 2)) + 2 * hops, 8), tensor


def across_y(device):
    expert, tensor = device
    return expert, lax.rem(tensor + 2, 4)


class Line:
    def __init__(self, send_sem, recv_sem):
        self.send_sem, self.recv_sem = send_sem, recv_sem
        self.started = []

    def send(self, source, target, tag, recv_tag, device):
        copy = push(source, target, self.send_sem.at[tag], self.recv_sem.at[recv_tag], device)
        copy.start()
        self.started.append(copy)

    def wait(self, target, tag, device):
        push(target, target, self.send_sem.at[0], self.recv_sem.at[tag], device).wait_recv()

    def finish(self):
        for copy in self.started:
            copy.wait_send()


PIECES = ((0, 1), (1, 0), (3, 0), (1, 1), (3, 1), (2, 0), (2, 1))


def exchange_steps(source, out, gathered, line, local_sem):
    me = here()
    tensor = me[1]
    side, sib = across_y(me), sibling(me)

    def at(column, expert):
        return out.at[column, expert] if gathered else out.at[expert]

    local = pltpu.make_async_copy(source.at[me[0]], at(tensor, me[0]), local_sem)
    local.start()
    if gathered:
        line.send(source.at[me[0]], at(tensor, me[0]), 8, 8, side)
        line.send(source.at[me[0]], at(tensor, me[0]), 16, 16, sib)
    for k, flips in PIECES:
        target = hop(me, flips, k)
        line.send(
            source.at[target[0]], at(tensor, me[0]), k * 2 + flips, (4 - k) % 4 * 2 + flips, target
        )
    yield
    for k, flips in PIECES:
        expert = hop(me, flips, k)[0]
        tag = k * 2 + flips
        line.wait(at(tensor, expert), tag, sib)
        if gathered:
            line.send(at(tensor, expert), at(tensor, expert), 8 + tag, 8 + tag, side)
            line.send(at(tensor, expert), at(tensor, expert), 16 + tag, 16 + tag, sib)
        yield
    if gathered:
        for k, flips in ((0, 0),) + PIECES:
            expert = hop(me, flips, k)[0]
            tag = k * 2 + flips
            line.wait(at(side[1], expert), 8 + tag, sib)
            line.send(at(side[1], expert), at(side[1], expert), 24 + tag, 24 + tag, sib)
            yield
        for k, flips in ((0, 0),) + PIECES:
            expert = hop(me, flips, k)[0]
            tag = k * 2 + flips
            line.wait(at(sib[1], expert), 16 + tag, sib)
            line.wait(at(across_y(sib)[1], expert), 24 + tag, sib)
    local.wait()
    line.finish()


def gather_expert_steps(source, out, chunks, straight, line, local_sem):
    me = here()
    z = me[0] // 2
    beside = hop(me, 1, 0)
    step = source.shape[0] // chunks

    def part(ref, i):
        return ref.at[pl.ds(i * step, step), :]

    local = pltpu.make_async_copy(source, out.at[me[0]], local_sem)
    local.start()

    def base(distance, up, i):
        return ((distance - 1) * 2 + up) * chunks + i

    def passes(ref, target, tag, up, held):
        @pl.when(held & ((z < 3) if up else (z > 0)))
        def _():
            push(
                ref, target, line.send_sem.at[tag], line.recv_sem.at[tag], hop(me, 0, 1 if up else 3)
            ).start()

    def block_at(column, distance, up, i):
        expert = lax.rem(column[0] + (8 - 2 * distance if up else 2 * distance), 8)
        return part(out.at[expert], i)

    cross = 6 * chunks
    order = list(range(straight, chunks)) + list(range(straight))
    for i in order:
        line.send(part(source, i), part(out.at[me[0]], i), 12 * chunks + i, 12 * chunks + i, beside)
        for up in (1, 0):
            passes(part(source, i), part(out.at[me[0]], i), base(1, up, i), up, z >= 0)
    yield
    for i in range(straight, chunks):
        block = part(out.at[beside[0]], i)
        line.wait(block, 12 * chunks + i, beside)
        for up in (1, 0):
            passes(block, block, cross + base(1, up, i), up, z >= 0)
        yield
    for distance in (1, 2, 3):
        for i in order:
            for up in (1, 0):
                held = (z >= distance) if up else (z + distance <= 3)
                block = block_at(me, distance, up, i)
                tag = base(distance, up, i)

                @pl.when(held)
                def _():
                    line.wait(block, tag, beside)
                    if i < straight:
                        push(
                            block,
                            block,
                            line.send_sem.at[cross + tag],
                            line.recv_sem.at[cross + tag],
                            beside,
                        ).start()

                if distance < 3:
                    passes(block, block, base(distance + 1, up, i), up, held)
                if i >= straight:
                    other = block_at(beside, distance, up, i)

                    @pl.when(held)
                    def _():
                        line.wait(other, cross + tag, beside)

                    if distance < 3:
                        passes(other, other, cross + base(distance + 1, up, i), up, held)
                yield
    for i in range(straight):
        line.wait(part(out.at[beside[0]], i), 12 * chunks + i, beside)
    for distance in (1, 2, 3):
        for i in order:
            for up in (1, 0):
                held = (z >= distance) if up else (z + distance <= 3)
                block = block_at(beside, distance, up, i)
                tag = base(distance, up, i)
                sent_on = (z + 1 >= distance) & (z < 3) if up else (z - 1 + distance <= 3) & (z > 0)

                def sent(at):
                    push(block, block, line.send_sem.at[at], line.recv_sem.at[at], beside).wait_send()

                if i < straight:

                    @pl.when(held)
                    def _():
                        sent(cross + tag)
                        line.wait(block, cross + tag, beside)

                @pl.when(sent_on)
                def _():
                    sent(tag)
                    if i >= straight:
                        sent(cross + tag)

        yield
    local.wait()
    line.finish()


def sum_rows(target, terms, step=16):
    def body(i, carry):
        window = pl.ds(pl.multiple_of(i * step, step), step)
        value = terms[0][window, :].astype(jnp.float32)
        for ref in terms[1:]:
            value = value + ref[window, :].astype(jnp.float32)
        target[window, :] = value.astype(target.dtype)
        return carry

    lax.fori_loop(0, target.shape[0] // step, body, 0)


def sum_expert_steps(part, out, mine, from_x, from_z, line, load_sem, step=16):
    me = here()
    beside = hop(me, 1, 0)
    loads = {}
    for k in (2, 1, 3, 0):
        line.send(part.at[hop(me, 1, k)[0]], from_x.at[k], k, k, beside)
        loads[k] = pltpu.make_async_copy(part.at[hop(me, 0, k)[0]], mine.at[k], load_sem.at[k])
        loads[k].start()
    yield
    for k in (2, 1, 3, 0):
        loads[k].wait()
        line.wait(from_x.at[k], k, beside)
        if k:
            sum_rows(mine.at[k], [mine.at[k], from_x.at[k]], step)
            line.send(mine.at[k], from_z.at[3 - k], 3 + k, 4 + 3 - k, hop(me, 0, k))
            yield
            yield
    for i in range(3):
        line.wait(from_z.at[i], 4 + i, beside)
    sum_rows(out, [mine.at[0], from_x.at[0], from_z.at[0], from_z.at[1], from_z.at[2]], step)
    line.finish()


def sum_everywhere_steps(part, out, mine, from_x, from_z, total, shares, line, load_sem):
    me = here()
    yield from sum_expert_steps(part, total, mine, from_x, from_z, line, load_sem, 8)
    peers = [across_y(me), sibling(me), across_y(sibling(me))]
    for i, peer in enumerate(peers):
        line.send(total, shares.at[me[1]], 7 + i, 7 + i, peer)
    shares[me[1]] = total[...]
    yield
    for i, peer in enumerate(peers):
        line.wait(shares.at[peer[1]], 7 + i, peer)
    sum_rows(out, [shares.at[i] for i in range(4)], 8)
    for i in range(3):
        line.started[-3 + i].wait_send()


def take_turns(steps):
    steps = list(steps)
    while steps:
        steps = [s for s in steps if next(s, steps) is not steps]


DMA = pltpu.SemaphoreType.DMA


def start_kernel(
    tokens, grads, weights, outs, small, o_tokens, o_grads, o_weights, o_outs, o_small, *sems
):
    me = here()
    pieces = [hop(me, flips, k) for k, flips in PIECES]
    greet(pieces + [across_y(me), sibling(me)])
    local = sems[8]
    take_turns(
        [
            exchange_steps(tokens, o_tokens, True, Line(sems[0], sems[1]), local.at[0]),
            exchange_steps(grads, o_grads, False, Line(sems[2], sems[3]), local.at[1]),
            gather_expert_steps(small, o_small, 1, 1, Line(sems[6], sems[7]), local.at[3]),
            gather_expert_steps(weights, o_weights, 4, 3, Line(sems[4], sems[5]), local.at[2]),
            gather_expert_steps(outs, o_outs, 4, 2, Line(sems[9], sems[10]), local.at[4]),
        ]
    )


def start_exchange(tokens, grads, weights, outs, small):
    piece = tokens.shape[1:]
    sds = jax.ShapeDtypeStruct
    return pl.pallas_call(
        start_kernel,
        out_shape=[
            sds((4, 8) + piece, tokens.dtype),
            sds((8,) + piece, grads.dtype),
            sds((8,) + weights.shape, weights.dtype),
            sds((8,) + outs.shape, outs.dtype),
            sds((8,) + small.shape, small.dtype),
        ],
        in_specs=[IN_VMEM] * 5,
        out_specs=[ANY] * 5,
        scratch_shapes=[DMA((32,)), DMA((32,)), DMA((8,)), DMA((8,))]
        + [DMA((52,)), DMA((52,)), DMA((13,)), DMA((13,)), DMA((5,)), DMA((52,)), DMA((52,))],
        compiler_params=pltpu.CompilerParams(
            collective_id=4, has_side_effects=True, vmem_limit_bytes=16 * 2**20
        ),
        cost_estimate=cost_of(100),
        name="start_exchange",
    )(tokens, grads, weights, outs, small)


def last_kernel(
    rows, more, part, small, o_rows, o_more, out, o_small,
    mine, from_x, from_z, mine_s, x_s, z_s, total_s, shares_s, *sems,
):
    me = here()
    pieces = [hop(me, flips, k) for k, flips in PIECES]
    greet(pieces + [across_y(me), sibling(me), across_y(sibling(me))])
    take_turns(
        [
            exchange_steps(more, o_more, True, Line(sems[2], sems[3]), sems[7].at[1]),
            exchange_steps(rows, o_rows, True, Line(sems[0], sems[1]), sems[7].at[0]),
            sum_everywhere_steps(
                small, o_small, mine_s, x_s, z_s, total_s, shares_s, Line(sems[8], sems[9]), sems[10]
            ),
            sum_expert_steps(part, out, mine, from_x, from_z, Line(sems[4], sems[5]), sems[6]),
        ]
    )


def last_exchange(rows, more, part, small):
    piece = rows.shape[1:]
    block, little = part.shape[1:], small.shape[1:]
    sds = jax.ShapeDtypeStruct
    return pl.pallas_call(
        last_kernel,
        out_shape=[
            sds((4, 8) + piece, rows.dtype),
            sds((4, 8) + piece, more.dtype),
            sds(block, jnp.float32),
            sds(little, jnp.float32),
        ],
        in_specs=[IN_VMEM, IN_VMEM, ANY, ANY],
        out_specs=[ANY, ANY, IN_VMEM, IN_VMEM],
        scratch_shapes=[
            pltpu.VMEM((4,) + block, part.dtype),
            pltpu.VMEM((4,) + block, part.dtype),
            pltpu.VMEM((3,) + block, part.dtype),
        ]
        + [pltpu.VMEM((n,) + little, jnp.float32) for n in (4, 4, 3)]
        + [pltpu.VMEM(little, jnp.float32), pltpu.VMEM((4,) + little, jnp.float32)]
        + [DMA((32,))] * 4
        + [DMA((8,)), DMA((8,)), DMA((4,)), DMA((2,))]
        + [DMA((10,)), DMA((10,)), DMA((4,))],
        compiler_params=pltpu.CompilerParams(
            collective_id=5, has_side_effects=True, vmem_limit_bytes=32 * 2**20
        ),
        cost_estimate=cost_of(1),
        name="last_exchange",
    )(rows, more, part, small)


def gather_tensor_kernel(source, out, send_sem, recv_sem, local_sem):
    me = here()
    side, sib = across_y(me), sibling(me)
    greet([side, sib])
    line = Line(send_sem, recv_sem)
    halves = 4
    step = source.shape[0] // halves

    def part(ref, i):
        return ref.at[pl.ds(i * step, step), :]

    local = pltpu.make_async_copy(source, out.at[me[1]], local_sem)
    for i in range(halves):
        line.send(part(source, i), part(out.at[me[1]], i), i, i, side)
        line.send(part(source, i), part(out.at[me[1]], i), 4 + i, 4 + i, sib)
    local.start()
    for i in range(halves):
        got = part(out.at[side[1]], i)
        line.wait(got, i, sib)
        line.send(got, got, 8 + i, 8 + i, sib)
    for i in range(halves):
        line.wait(part(out.at[sib[1]], i), 4 + i, sib)
        line.wait(part(out.at[across_y(sib)[1]], i), 8 + i, sib)
    local.wait()
    line.finish()


def gather_tensor(rows):
    out = pl.pallas_call(
        gather_tensor_kernel,
        out_shape=jax.ShapeDtypeStruct((4,) + rows.shape, rows.dtype),
        in_specs=[IN_VMEM],
        out_specs=ANY,
        scratch_shapes=[DMA((12,)), DMA((12,)), DMA],
        compiler_params=pltpu.CompilerParams(
            collective_id=6, has_side_effects=True, vmem_limit_bytes=8 * 2**20
        ),
        cost_estimate=cost_of(15),
        name="gather_tensor",
    )(rows)
    return out.reshape((-1,) + rows.shape[1:])


def sum_tensor_kernel(part, out, from_sib, from_side, total, send_sem, recv_sem):
    me = here()
    side, sib = across_y(me), sibling(me)
    greet([side, sib])
    line = Line(send_sem, recv_sem)
    pieces = 4
    step = out.shape[0] // pieces

    def rows(ref, i):
        return ref.at[pl.ds(i * step, step), :]

    for j, column in ((0, across_y(sib)[1]), (1, sib[1])):
        for i in range(pieces):
            line.send(
                rows(part.at[column], i), rows(from_sib.at[j], i), 4 * j + i, 4 * j + i, sib
            )
    for i in range(pieces):
        got = rows(from_sib.at[0], i)
        line.wait(got, i, sib)
        sum_rows(rows(total, i), [rows(part.at[side[1]], i), got])
        line.send(rows(total, i), rows(from_side, i), 8 + i, 8 + i, side)
    for i in range(pieces):
        got = rows(from_sib.at[1], i)
        line.wait(got, 4 + i, sib)
        line.wait(rows(from_side, i), 8 + i, sib)
        sum_rows(rows(out, i), [rows(part.at[me[1]], i), got, rows(from_side, i)])
    line.finish()


def sum_tensor(partial):
    block = (partial.shape[0] // 4, partial.shape[1])
    return pl.pallas_call(
        sum_tensor_kernel,
        out_shape=jax.ShapeDtypeStruct(block, jnp.float32),
        in_specs=[IN_VMEM],
        out_specs=IN_VMEM,
        scratch_shapes=[
            pltpu.VMEM((2,) + block, partial.dtype),
            pltpu.VMEM(block, partial.dtype),
            pltpu.VMEM(block, partial.dtype),
            DMA((12,)),
            DMA((12,)),
        ],
        compiler_params=pltpu.CompilerParams(
            collective_id=7, has_side_effects=True, vmem_limit_bytes=12 * 2**20
        ),
        cost_estimate=cost_of(1),
        name="sum_tensor",
    )(partial.reshape((4,) + block))


def rows_at(ref, slot, size, count=1):
    return ref.at[pl.ds(pl.multiple_of(slot * size, size), size * count), :]


class Plan:
    def __init__(self, send_sem, recv_sem):
        self.send_sem, self.recv_sem, self.made = send_sem, recv_sem, []

    def send(self, make):
        make().start()
        self.made.append(make)

    def finish(self):
        for make in self.made:
            make().wait_send()


def gather_plan(ins, outs, sizes, send_sem, recv_sem):
    me = here()
    near, far, sib = flipped(me, NEAR), flipped(me, FAR), sibling(me)
    plan = Plan(send_sem, recv_sem)
    count = len(ins)

    def send(k, role, device, tag, recv_tag):
        for i in range(count):

            def make(i=i):
                block = rows_at(outs[i], slot_of(moved_z(flipped(me, role), k)), sizes[i])
                source = ins[i] if (k, role) == (0, SELF) else block
                return push(source, block, send_sem.at[i, tag], recv_sem.at[i, recv_tag], device)

            plan.send(make)

    def arrive(k, role):
        for i in range(count):
            block = rows_at(outs[i], slot_of(moved_z(flipped(me, role), k)), sizes[i])
            push(block, block, send_sem.at[i, 0], recv_sem.at[i, k * 4 + role], near).wait_recv()

    def forward(k, role):
        if role == SELF:
            send(k, SELF, far, 4 + k, k * 4 + FAR)
            send(k, SELF, near, k, k * 4 + NEAR)
        if role == NEAR:
            send(k, NEAR, far, 8 + k, k * 4 + BOTH_FLIPPED)
        send(k, role, sib, 16 + k * 4 + role, 16 + k * 4 + role)

    def event(k, role):
        arrive(k, role)
        forward(k, role)

    def from_sibling(k, role):
        for i in range(count):
            block = rows_at(outs[i], 0, sizes[i])
            push(
                block, block, send_sem.at[i, 0], recv_sem.at[i, 16 + k * 4 + role], near
            ).wait_recv()

    def begin():
        forward(0, SELF)
        for d in (1, 3, 2):
            send(0, SELF, moved_z(me, d), 11 + d, (4 - d) * 4 + SELF)

    return plan, begin, event, from_sibling


def gate_columns(gates_ref, slot, columns, first):
    lane = lax.broadcasted_iota(jnp.int32, (128, 128), 1)
    for s in range(4):
        block = gates_ref[pl.ds(pl.multiple_of((slot + s) * 16, 16), 16), :]
        turned = jnp.concatenate([block, jnp.zeros((112, 128), jnp.float32)], axis=0).T
        for i in range(2):
            column = jnp.sum(jnp.where(lane == first + i, turned, 0.0), axis=1, keepdims=True)
            columns[i, pl.ds(s * 128, 128), :] = jnp.broadcast_to(column, (128, 128))


def tiles(count, width, body):
    def step(n, carry):
        body(pl.ds(pl.multiple_of(n * width, width), width))
        return carry

    lax.fori_loop(0, count, step, 0)


STAGES = ((0, 0), (0, 1), (1, 0), (1, 1), (3, 0), (3, 1), (2, 0), (2, 1))
BLOCK = 512


def stage_expert(me, j):
    half = j // 2
    k = half + jnp.where(half == 2, 1, 0) - jnp.where(half == 3, 1, 0)
    flips = lax.rem(j, 2)
    expert = me[0]
    return lax.rem(expert + flips * (1 - 2 * lax.rem(expert, 2)) + 2 * k, 8)


def forward_kernel(
    x_own, g_own, w_joined, w_down, x_out, g_out, pre_out, gated_out, y_out,
    x_all, g_all, columns, pre, gated, y, send_sem, recv_sem, local_sem, out_sem,
):
    me = here()
    core = lax.rem(me[1], 2)
    greet(
        [flipped(me, NEAR), flipped(me, FAR), sibling(me)] + [moved_z(me, d) for d in (1, 2, 3)]
    )
    plan, begin, event, from_sibling = gather_plan(
        [x_own, g_own], [x_all, g_all], [128, 16], send_sem, recv_sem
    )
    local = [
        pltpu.make_async_copy(x_own, rows_at(x_all, slot_of(me), 128), local_sem.at[0]),
        pltpu.make_async_copy(g_own, rows_at(g_all, slot_of(me), 16), local_sem.at[1]),
    ]
    begin()
    for copy in local:
        copy.start()
    for copy in local:
        copy.wait()
    before = {
        0: [(1, SELF), (0, NEAR), (0, FAR)],
        1: [(0, BOTH_FLIPPED)],
        3: [(1, BOTH_FLIPPED)],
        5: [(3, BOTH_FLIPPED)],
        7: [(2, BOTH_FLIPPED)],
    }
    middle = {
        0: [(3, SELF), (1, NEAR)],
        1: [(1, FAR)],
        2: [(2, SELF), (3, NEAR)],
        3: [(3, FAR)],
        4: [(2, NEAR)],
        5: [(2, FAR)],
    }
    half = w_joined.shape[1] // 2

    def results(expert, slot):
        return [
            pltpu.make_async_copy(
                rows_at(x_all, expert, BLOCK), rows_at(x_out, expert, BLOCK), out_sem.at[0, slot]
            ),
            pltpu.make_async_copy(pre.at[slot], rows_at(pre_out, expert, BLOCK), out_sem.at[1, slot]),
            pltpu.make_async_copy(
                gated.at[slot], rows_at(gated_out, expert, BLOCK), out_sem.at[2, slot]
            ),
            pltpu.make_async_copy(y.at[slot], rows_at(y_out, expert, BLOCK), out_sem.at[3, slot]),
        ]

    def block(j, carry):
        slot = lax.rem(j, 2)
        expert = stage_expert(me, j)
        for n, (k, flips) in enumerate(STAGES):

            @pl.when(j == n)
            def _():
                for at in before.get(n, []):
                    event(*at)
                if n:
                    from_sibling(k, 2 - core if flips else SELF)
                    from_sibling(k, BOTH_FLIPPED if flips else 1 + core)
                else:
                    from_sibling(k, SELF)
                    from_sibling(k, 1 + core)

        @pl.when(j >= 2)
        def _():
            for copy in results(stage_expert(me, j - 2), slot):
                copy.wait()

        gate_columns(g_all, expert * 4, columns, me[0] * 2)
        x_rows = rows_at(x_all, expert, BLOCK)

        def first(cols):
            pre[slot, :, cols] = jnp.dot(
                x_rows[...], w_joined[:, cols], preferred_element_type=jnp.float32
            )

        tiles(w_joined.shape[1] // 1024, 1024, first)
        for n in middle:

            @pl.when(j == n)
            def _():
                for at in middle[n]:
                    event(*at)

        def act(r):
            for c in range(half // 128):
                cols = slice(c * 128, (c + 1) * 128)
                g = pre[slot, r, cols]
                u = pre[slot, r, half + c * 128 : half + (c + 1) * 128]
                hidden = (g * (1.0 / (1.0 + jnp.exp(-g))) * u).astype(jnp.bfloat16)
                gate = columns[c * 128 * 2 // half, r, :]
                gated[slot, r, cols] = (hidden.astype(jnp.float32) * gate).astype(jnp.bfloat16)

        tiles(BLOCK // 64, 64, act)

        def second(cols):
            y[slot, :, cols] = jnp.dot(
                gated[slot], w_down[:, cols], preferred_element_type=jnp.float32
            ).astype(jnp.bfloat16)

        tiles(w_down.shape[1] // 1024, 1024, second)
        for copy in results(expert, slot):
            copy.start()
        return carry

    lax.fori_loop(0, 8, block, 0)
    for j in (6, 7):
        for copy in results(stage_expert(me, jnp.int32(j)), j % 2):
            copy.wait()
    g_out[...] = g_all[...]
    plan.finish()


def experts_forward(ffn_in, gates_own, w_joined, w_down):
    rows, width = ffn_in.shape[0] * 32, ffn_in.shape[1]
    joined, hidden = w_joined.shape[1], w_down.shape[0]
    bf16, f32, sds = jnp.bfloat16, jnp.float32, jax.ShapeDtypeStruct
    return pl.pallas_call(
        forward_kernel,
        out_shape=[
            sds((rows, width), bf16),
            sds((512, 128), f32),
            sds((rows, joined), f32),
            sds((rows, hidden), bf16),
            sds((rows, width), bf16),
        ],
        in_specs=[IN_VMEM] * 4,
        out_specs=[ANY, IN_VMEM, ANY, ANY, ANY],
        scratch_shapes=[
            pltpu.VMEM((rows, width), bf16),
            pltpu.VMEM((512, 128), f32),
            pltpu.VMEM((2, BLOCK, 128), f32),
            pltpu.VMEM((2, BLOCK, joined), f32),
            pltpu.VMEM((2, BLOCK, hidden), bf16),
            pltpu.VMEM((2, BLOCK, width), bf16),
            DMA((2, 32)),
            DMA((2, 32)),
            DMA((2,)),
            DMA((4, 2)),
        ],
        compiler_params=pltpu.CompilerParams(
            collective_id=1, has_side_effects=True, vmem_limit_bytes=48 * 2**20
        ),
        cost_estimate=cost_of(90),
        name="experts_forward",
    )(ffn_in, gates_own, w_joined, w_down)


def sum_plan(arrays, send_sem, recv_sem, load_sem):
    me = here()
    near, far, sib = flipped(me, NEAR), flipped(me, FAR), sibling(me)
    plan = Plan(send_sem, recv_sem)
    order = (2, 1, 3, 0)

    def send(i, source, target, tag, recv_tag, device):
        plan.send(
            lambda: push(source(), target(), send_sem.at[i, tag], recv_sem.at[i, recv_tag], device())
        )

    def arrive(i, ref, tag):
        push(ref, ref, send_sem.at[i, 0], recv_sem.at[i, tag], near).wait_recv()

    def load(i, k, role):
        part, _, size, mine = arrays[i][:4]
        tag = k * 4 + role
        return pltpu.make_async_copy(
            rows_at(part, slot_of(moved_z(flipped(me, role), k)), size), mine.at[tag], load_sem.at[i, tag]
        )

    def begin():
        for roles in ((BOTH_FLIPPED, FAR), (NEAR, SELF)):
            for k in order:
                for role in roles:
                    for i, (part, _, size, _, from_sib, _, _, _) in enumerate(arrays):
                        tag = k * 4 + role
                        send(
                            i,
                            lambda part=part, size=size, k=k, role=role: rows_at(
                                part, slot_of(moved_z(flipped(sib, role), k)), size
                            ),
                            lambda from_sib=from_sib, tag=tag: from_sib.at[tag],
                            tag,
                            tag,
                            lambda: sib,
                        )
                        load(i, k, role).start()

    def collect(i, k, role):
        tag = k * 4 + role
        load(i, k, role).wait()
        from_sib = arrays[i][4]
        arrive(i, from_sib.at[tag], tag)
        return [arrays[i][3].at[tag], from_sib.at[tag]]

    def first(k, role):
        for i, (_, _, _, mine, _, from_far, _, _) in enumerate(arrays):
            tag, at = k * 4 + role, k * 2 + (role == BOTH_FLIPPED)
            terms = collect(i, k, role)
            sum_rows(mine.at[tag], terms)
            send(
                i,
                lambda mine=mine, tag=tag: mine.at[tag],
                lambda from_far=from_far, at=at: from_far.at[at],
                16 + at,
                16 + at,
                lambda: far,
            )

    def second(k):
        for i, (_, _, _, mine, _, from_far, from_near, _) in enumerate(arrays):
            tag = k * 4 + NEAR
            terms = collect(i, k, NEAR)
            arrive(i, from_far.at[k * 2 + 1], 16 + k * 2 + 1)
            sum_rows(mine.at[tag], terms + [from_far.at[k * 2 + 1]])
            send(
                i,
                lambda mine=mine, tag=tag: mine.at[tag],
                lambda from_near=from_near, k=k: from_near.at[k],
                24 + k,
                24 + k,
                lambda: near,
            )

    def third(k):
        for i, (_, out, _, mine, _, from_far, from_near, from_z) in enumerate(arrays):
            tag = k * 4 + SELF
            terms = collect(i, k, SELF)
            arrive(i, from_far.at[k * 2], 16 + k * 2)
            arrive(i, from_near.at[k], 24 + k)
            terms = terms + [from_far.at[k * 2], from_near.at[k]]
            if k > 0:
                sum_rows(mine.at[tag], terms)
                send(
                    i,
                    lambda mine=mine, tag=tag: mine.at[tag],
                    lambda from_z=from_z, k=k: from_z.at[3 - k],
                    27 + k,
                    31 - k,
                    lambda k=k: moved_z(me, k),
                )
            else:
                for d in range(3):
                    arrive(i, from_z.at[d], 28 + d)
                    terms.append(from_z.at[d])
                sum_rows(out, terms)

    return plan, begin, first, second, third


def sum_scratch(size, width, dtype):
    return [pltpu.VMEM((n, size, width), dtype) for n in (16, 16, 8, 4, 3)]


SUM_BEFORE = {0: [(2, 3), (2, 2), (1, 3), (1, 2)], 3: [(2, "third")], 5: [(1, "third")]}
SUM_MIDDLE = {
    0: [(3, 3), (3, 2), (0, 3), (0, 2)],
    1: [(2, "second")],
    2: [(1, "second")],
    4: [(3, "second")],
    6: [(0, "second")],
}


def sum_events(table, j, first, second, third):
    for n, events in table.items():

        @pl.when(j == n)
        def _():
            for k, what in events:
                if what == "second":
                    second(k)
                elif what == "third":
                    third(k)
                else:
                    first(k, what)


def greet_all(me):
    greet(
        [flipped(me, NEAR), flipped(me, FAR), sibling(me)] + [moved_z(me, d) for d in (1, 2, 3)]
    )


def backward_kernel(
    y_part, grads, pre_all, gates, w_joined, w_down, mix_out, dpre_out, drow_out, gate_grads,
    mine, from_sib, from_far, from_near, from_z, dz, pre, raw, columns, products, dpre, drow,
    send_sem, recv_sem, load_sem, in_sem, out_sem,
):
    me = here()
    greet_all(me)
    plan, begin, first, second, third = sum_plan(
        [(y_part, mix_out, 128, mine, from_sib, from_far, from_near, from_z)],
        send_sem, recv_sem, load_sem,
    )
    half = w_joined.shape[1] // 2
    expert_lanes = half // 2

    def loads(block, slot):
        return [
            pltpu.make_async_copy(rows_at(grads, block, BLOCK), dz.at[slot], in_sem.at[0, slot]),
            pltpu.make_async_copy(rows_at(pre_all, block, BLOCK), pre.at[slot], in_sem.at[1, slot]),
        ]

    def results(block, slot):
        return [
            pltpu.make_async_copy(dpre.at[slot], rows_at(dpre_out, block, BLOCK), out_sem.at[0, slot]),
            pltpu.make_async_copy(drow.at[slot], rows_at(drow_out, block, BLOCK), out_sem.at[1, slot]),
        ]

    for copy in loads(0, 0):
        copy.start()
    begin()

    def step(j, carry):
        slot = lax.rem(j, 2)

        @pl.when(j < 7)
        def _():
            for copy in loads(j + 1, 1 - slot):
                copy.start()

        sum_events(SUM_BEFORE, j, first, second, third)
        for copy in loads(j, slot):
            copy.wait()

        @pl.when(j >= 2)
        def _():
            for copy in results(j - 2, slot):
                copy.wait()

        gate_columns(gates, j * 4, columns, me[0] * 2)
        raw[...] = lax.dot_general(
            dz[slot], w_down[...], (((1,), (1,)), ((), ())), preferred_element_type=jnp.float32
        )
        sum_events(SUM_MIDDLE, j, first, second, third)

        def act(r):
            for i in range(2):
                product = None
                for c in range(i * expert_lanes, (i + 1) * expert_lanes, 128):
                    g = pre[slot, r, c : c + 128]
                    u = pre[slot, r, half + c : half + c + 128]
                    t = raw[r, c : c + 128]
                    sig = 1.0 / (1.0 + jnp.exp(-g))
                    silu = g * sig
                    hidden = (silu * u).astype(jnp.bfloat16).astype(jnp.float32)
                    term = hidden * t
                    product = term if product is None else product + term
                    dh = t * columns[i, r, :]
                    dpre[slot, r, c : c + 128] = (
                        dh * u * sig * (1.0 + g * (1.0 - sig))
                    ).astype(jnp.bfloat16)
                    dpre[slot, r, half + c : half + c + 128] = (dh * silu).astype(jnp.bfloat16)
                products[i, r, :] = product

        tiles(BLOCK // 64, 64, act)
        place = lax.broadcasted_iota(jnp.int32, (16, 128), 0)
        for s in range(4):
            sums = jnp.zeros((16, 128), jnp.float32)
            for i in range(2):
                turned = products[i, pl.ds(s * 128, 128), :].T
                row = jnp.sum(turned, axis=0, keepdims=True)
                sums = jnp.where(place == me[0] * 2 + i, jnp.broadcast_to(row, (16, 128)), sums)
            gate_grads[pl.ds(pl.multiple_of((j * 4 + s) * 16, 16), 16), :] = sums

        def back(rows):
            drow[slot, :, rows] = lax.dot_general(
                dpre[slot],
                w_joined[rows, :],
                (((1,), (1,)), ((), ())),
                preferred_element_type=jnp.float32,
            ).astype(jnp.bfloat16)

        tiles(w_joined.shape[0] // 1024, 1024, back)
        for copy in results(j, slot):
            copy.start()
        return carry

    lax.fori_loop(0, 8, step, 0)
    third(3)
    third(0)
    for j in (6, 7):
        for copy in results(j, j % 2):
            copy.wait()
    plan.finish()


def experts_backward(y_part, grads, pre, gates, w_joined, w_down):
    rows, width = grads.shape
    joined, hidden = w_joined.shape[1], w_down.shape[0]
    bf16, f32, sds = jnp.bfloat16, jnp.float32, jax.ShapeDtypeStruct
    return pl.pallas_call(
        backward_kernel,
        out_shape=[
            sds((rows // 32, width), f32),
            sds((rows, joined), bf16),
            sds((rows, width), bf16),
            sds((512, 128), f32),
        ],
        in_specs=[ANY, ANY, ANY] + [IN_VMEM] * 3,
        out_specs=[IN_VMEM, ANY, ANY, IN_VMEM],
        scratch_shapes=sum_scratch(rows // 32, width, bf16)
        + [
            pltpu.VMEM((2, BLOCK, width), bf16),
            pltpu.VMEM((2, BLOCK, joined), f32),
            pltpu.VMEM((BLOCK, hidden), f32),
            pltpu.VMEM((2, BLOCK, 128), f32),
            pltpu.VMEM((2, BLOCK, 128), f32),
            pltpu.VMEM((2, BLOCK, joined), bf16),
            pltpu.VMEM((2, BLOCK, width), bf16),
            DMA((1, 32)),
            DMA((1, 32)),
            DMA((1, 16)),
            DMA((2, 2)),
            DMA((2, 2)),
        ],
        compiler_params=pltpu.CompilerParams(
            collective_id=2, has_side_effects=True, vmem_limit_bytes=56 * 2**20
        ),
        cost_estimate=cost_of(90),
        name="experts_backward",
    )(y_part, grads, pre, gates, w_joined, w_down)


def weights_kernel(
    drow, gate_grads, x_all, grads, dpre_all, gated_all, row_out, gate_out, d_gate, d_up, d_down,
    mine, from_sib, from_far, from_near, from_z, mine_g, sib_g, far_g, near_g, z_g,
    dpre, gated, tile, wide, send_sem, recv_sem, load_sem, in_sem, tile_sem, out_sem,
):
    me = here()
    greet_all(me)
    plan, begin, first, second, third = sum_plan(
        [
            (drow, row_out, 128, mine, from_sib, from_far, from_near, from_z),
            (gate_grads, gate_out, 16, mine_g, sib_g, far_g, near_g, z_g),
        ],
        send_sem, recv_sem, load_sem,
    )
    span = tile.shape[2]
    steps = x_all.shape[1] // span
    hidden = d_gate.shape[2]
    begin()
    held = [
        pltpu.make_async_copy(dpre_all, dpre, in_sem.at[0]),
        pltpu.make_async_copy(gated_all, gated, in_sem.at[1]),
    ]

    def columns_of(j):
        return pl.ds(pl.multiple_of(lax.rem(j, steps) * span, span), span)

    def fetch(j, slot, act):
        @pl.when(j < steps)
        def _():
            act(pltpu.make_async_copy(x_all.at[:, columns_of(j)], tile.at[slot], tile_sem.at[slot]))

        @pl.when((j >= steps) & (j < 2 * steps))
        def _():
            act(pltpu.make_async_copy(grads.at[:, columns_of(j)], tile.at[slot], tile_sem.at[slot]))

    def results(j, slot, act):
        cols = columns_of(j)

        @pl.when(j < steps)
        def _():
            for i in range(2):
                act(
                    pltpu.make_async_copy(
                        wide.at[slot, :, pl.ds(i * hidden, hidden)], d_gate.at[i, cols, :], out_sem.at[slot, i]
                    )
                )
                act(
                    pltpu.make_async_copy(
                        wide.at[slot, :, pl.ds((2 + i) * hidden, hidden)],
                        d_up.at[i, cols, :],
                        out_sem.at[slot, 2 + i],
                    )
                )

        @pl.when(j >= steps)
        def _():
            act(
                pltpu.make_async_copy(
                    wide.at[slot, :, pl.ds(0, span)], d_down.at[:, cols], out_sem.at[slot, 0]
                )
            )

    fetch(jnp.int32(0), 0, lambda copy: copy.start())
    for copy in held:
        copy.start()

    def step(j, carry):
        slot = lax.rem(j, 2)
        fetch(j + 1, 1 - slot, lambda copy: copy.start())
        sum_events(SUM_BEFORE, j, first, second, third)

        @pl.when(j == 0)
        def _():
            for copy in held:
                copy.wait()

        fetch(j, slot, lambda copy: copy.wait())

        @pl.when(j >= 2)
        def _():
            results(j - 2, slot, lambda copy: copy.wait())

        @pl.when(j < steps)
        def _():
            wide[slot] = lax.dot_general(
                tile[slot], dpre[...], (((0,), (0,)), ((), ())), preferred_element_type=jnp.float32
            )

        @pl.when(j >= steps)
        def _():
            wide[slot, :, 0:span] = lax.dot_general(
                gated[...], tile[slot], (((0,), (0,)), ((), ())), preferred_element_type=jnp.float32
            )

        results(j, slot, lambda copy: copy.start())
        sum_events(SUM_MIDDLE, j, first, second, third)
        return carry

    lax.fori_loop(0, 2 * steps, step, 0)
    third(3)
    third(0)
    for j in (2 * steps - 2, 2 * steps - 1):
        results(jnp.int32(j), j % 2, lambda copy: copy.wait())
    plan.finish()


def experts_weights(drow, gate_grads, x_all, grads, dpre, gated):
    rows, width = grads.shape
    joined, hidden = dpre.shape[1], gated.shape[1]
    span = width // 4
    bf16, f32, sds = jnp.bfloat16, jnp.float32, jax.ShapeDtypeStruct
    return pl.pallas_call(
        weights_kernel,
        out_shape=[
            sds((rows // 32, width), f32),
            sds((16, 128), f32),
            sds((2, width, joined // 4), f32),
            sds((2, width, joined // 4), f32),
            sds((hidden, width), f32),
        ],
        in_specs=[ANY] * 6,
        out_specs=[IN_VMEM, IN_VMEM, ANY, ANY, ANY],
        scratch_shapes=sum_scratch(rows // 32, width, bf16)
        + sum_scratch(16, 128, f32)
        + [
            pltpu.VMEM((rows, joined), bf16),
            pltpu.VMEM((rows, hidden), bf16),
            pltpu.VMEM((2, rows, span), bf16),
            pltpu.VMEM((2, span, joined), f32),
            DMA((2, 32)),
            DMA((2, 32)),
            DMA((2, 16)),
            DMA((2,)),
            DMA((2,)),
            DMA((2, 4)),
        ],
        compiler_params=pltpu.CompilerParams(
            collective_id=3, has_side_effects=True, vmem_limit_bytes=58 * 2**20
        ),
        cost_estimate=cost_of(90),
        name="experts_weights",
    )(drow, gate_grads, x_all, grads, dpre, gated)


def rotated(values, cosines, sines):
    return values * cosines + pltpu.roll(values, HEAD_DIM // 2, 1) * sines


def turned_back(values, cosines, sines):
    return values * cosines - pltpu.roll(values, HEAD_DIM // 2, 1) * sines


def mask_scores(spans_col, places_row, bias):
    place = places_row[0:1, :]

    def body(r):
        allowed = (place >= spans_col[r, 0:1]) & (place <= spans_col[r, 1:2])
        bias[r, :] = jnp.where(allowed, 0.0, -1e30)

    tiles(bias.shape[0] // 128, 128, body)


def attend_kernel(
    qkv, invs, gains, cosines, sines, spans, places, w_out,
    q_out, k_out, v_out, attended, lse, branch, bias,
):
    rows, local = q_out.shape
    mask_scores(spans, places, bias)

    def prepare(r):
        v_out[r, :] = qkv[r, 2 * local : 3 * local].astype(jnp.bfloat16)
        for h in range(local // HEAD_DIM):
            c = slice(h * HEAD_DIM, (h + 1) * HEAD_DIM)
            for i, target in ((0, q_out), (1, k_out)):
                normed = qkv[r, i * local + h * HEAD_DIM : i * local + (h + 1) * HEAD_DIM]
                normed = normed * invs[r, i : i + 1] * gains[i : i + 1, c]
                target[r, c] = rotated(normed, cosines[r, :], sines[r, :]).astype(jnp.bfloat16)

    tiles(rows // 128, 128, prepare)
    scale = 1.0 / math.sqrt(HEAD_DIM)
    for h in range(local // HEAD_DIM):
        c = slice(h * HEAD_DIM, (h + 1) * HEAD_DIM)

        def one(r, h=h, c=c):
            scores = dot32(q_out[r, c], k_out[:, c], NT) * scale + bias[r, :]
            top = jnp.max(scores, axis=-1, keepdims=True)
            total = top + jnp.log(jnp.sum(jnp.exp(scores - top), axis=-1, keepdims=True))
            lse[h, r, :] = total
            probs = jnp.exp(scores - total).astype(jnp.bfloat16)
            attended[r, c] = dot32(probs, v_out[:, c], NN).astype(jnp.bfloat16)

        tiles(rows // 128, 128, one)
    for e in range(w_out.shape[0]):
        span = w_out.shape[2]
        branch[:, e * span : (e + 1) * span] = dot32(attended[...], w_out[e], NN).astype(
            jnp.bfloat16
        )


def attend(qkv, invs, gains, cosines, sines, spans, places, w_out):
    rows, local = qkv.shape[0], qkv.shape[1] // 3
    bf16, f32, sds = jnp.bfloat16, jnp.float32, jax.ShapeDtypeStruct
    return pl.pallas_call(
        attend_kernel,
        out_shape=[sds((rows, local), bf16)] * 4
        + [
            sds((local // HEAD_DIM, rows, 1), f32),
            sds((rows, w_out.shape[0] * w_out.shape[2]), bf16),
        ],
        in_specs=[IN_VMEM] * 8,
        out_specs=[IN_VMEM] * 6,
        scratch_shapes=[pltpu.VMEM((rows, rows), f32)],
        compiler_params=pltpu.CompilerParams(vmem_limit_bytes=32 * 2**20),
        cost_estimate=cost_of(15),
        name="attend",
    )(qkv, invs, gains, cosines, sines, spans, places, w_out)


def attend_back_kernel(
    grad, w_out, q, k, v, lse, qkv, invs, gains, cosines, sines, spans, places,
    hat_grads, value_grad, dots, d_gains, bias, out_grad, probs_low, score_grad,
):
    rows, local = q.shape
    mask_scores(spans, places, bias)
    span = w_out.shape[2]

    def project(r):
        total = None
        for e in range(w_out.shape[0]):
            term = dot32(grad[r, e * span : (e + 1) * span], w_out[e], NT)
            total = term if total is None else total + term
        out_grad[r, :] = total.astype(jnp.bfloat16)

    tiles(rows // 128, 128, project)
    scale = 1.0 / math.sqrt(HEAD_DIM)
    dots[...] = jnp.zeros_like(dots)
    for h in range(local // HEAD_DIM):
        c = slice(h * HEAD_DIM, (h + 1) * HEAD_DIM)

        def one(r, h=h, c=c):
            scores = dot32(q[r, c], k[:, c], NT) * scale + bias[r, :]
            probs = jnp.exp(scores - lse[h, r, :])
            prob_grad = dot32(out_grad[r, c], v[:, c], NT)
            delta = jnp.sum(probs * prob_grad, axis=-1, keepdims=True)
            probs_low[r, :] = probs.astype(jnp.bfloat16)
            score_grad[r, :] = (probs * (prob_grad - delta) * scale).astype(jnp.bfloat16)

        tiles(rows // 128, 128, one)
        value_grad[:, c] = dot32(probs_low[...], out_grad[:, c], TN).astype(jnp.bfloat16)
        for i, turned in (
            (0, dot32(score_grad[...], k[:, c], NN)),
            (1, dot32(score_grad[...], q[:, c], TN)),
        ):
            at = slice(i * local + h * HEAD_DIM, i * local + (h + 1) * HEAD_DIM)
            norm_grad = turned_back(turned, cosines[...], sines[...])
            hat = qkv[:, at] * invs[:, i : i + 1]
            hat_grad = norm_grad * gains[i : i + 1, c]
            hat_grads[:, at] = hat_grad
            d_gains[i : i + 1, c] = jnp.sum(norm_grad * hat, axis=0, keepdims=True)
            dots[i] += jnp.sum(hat_grad * hat, axis=-1, keepdims=True)


def attend_back(grad, w_out, q, k, v, lse, qkv, invs, gains, cosines, sines, spans, places):
    rows, local = q.shape
    bf16, f32, sds = jnp.bfloat16, jnp.float32, jax.ShapeDtypeStruct
    return pl.pallas_call(
        attend_back_kernel,
        out_shape=[
            sds((rows, 2 * local), f32),
            sds((rows, local), bf16),
            sds((2, rows, 1), f32),
            sds((2, local), f32),
        ],
        in_specs=[IN_VMEM] * 13,
        out_specs=[IN_VMEM] * 4,
        scratch_shapes=[
            pltpu.VMEM((rows, rows), f32),
            pltpu.VMEM((rows, local), bf16),
            pltpu.VMEM((rows, rows), bf16),
            pltpu.VMEM((rows, rows), bf16),
        ],
        compiler_params=pltpu.CompilerParams(vmem_limit_bytes=40 * 2**20),
        cost_estimate=cost_of(5),
        name="attend_back",
    )(grad, w_out, q, k, v, lse, qkv, invs, gains, cosines, sines, spans, places)


def sum_few_kernel(part, out, shares, send_sem, recv_sem):
    me = here()
    peers = [across_y(sibling(me)), across_y(me), sibling(me)]
    greet(peers)
    line = Line(send_sem, recv_sem)
    for i, peer in enumerate(peers):
        line.send(part, shares.at[me[1]], i, i, peer)
    shares[me[1]] = part[...]
    for i, peer in enumerate(peers):
        line.wait(shares.at[peer[1]], i, peer)
    out[...] = (shares[0] + shares[1]) + (shares[2] + shares[3])
    line.finish()


def sum_few(rows):
    block = (rows.size // 128, 128)
    return pl.pallas_call(
        sum_few_kernel,
        out_shape=jax.ShapeDtypeStruct(block, jnp.float32),
        in_specs=[IN_VMEM],
        out_specs=IN_VMEM,
        scratch_shapes=[pltpu.VMEM((4,) + block, jnp.float32), DMA((3,)), DMA((3,))],
        compiler_params=pltpu.CompilerParams(
            collective_id=8, has_side_effects=True, vmem_limit_bytes=2**20
        ),
        cost_estimate=cost_of(1),
        name="sum_few",
    )(rows.reshape(block)).reshape(rows.shape)


BOTH = (EXPERT, TENSOR)


def dot32(left, right, dims):
    return lax.dot_general(left, right, (dims, ((), ())), preferred_element_type=jnp.float32)


NN = ((1,), (0,))
NT = ((1,), (1,))
TN = ((0,), (0,))


def rms_inv(values):
    return lax.rsqrt(jnp.mean(values * values, axis=-1, keepdims=True) + NORM_EPS)


def dense_body(
    tokens,
    attn_gain,
    w_query,
    w_key,
    w_value,
    w_out,
    query_gain,
    key_gain,
    ffn_gain,
    w_router,
    w_gate,
    w_up,
    w_down,
    doc_ids,
    routes,
    deal,
    out_grad,
):
    rows, width = tokens.shape
    parts = lax.axis_size(TENSOR)
    blocks = lax.axis_size(EXPERT)
    column = lax.axis_index(TENSOR)
    block = lax.axis_index(EXPERT)
    own = rows // parts
    share = rows // blocks
    piece = share // parts
    bf16, f32 = jnp.bfloat16, jnp.float32

    def reorder(per_place):
        grid = per_place.reshape((blocks, parts, piece) + per_place.shape[1:])
        return jnp.swapaxes(grid, 0, 1).reshape(per_place.shape)

    local_width = w_query.shape[1]
    head_count = local_width // HEAD_DIM
    expert_count = w_router.shape[1]
    qkv_own = jnp.concatenate([w_query, w_key, w_value], axis=1)
    gain_stack = jnp.stack([attn_gain, query_gain, key_gain, ffn_gain], axis=1)
    small_own = jnp.concatenate([w_router, gain_stack], axis=1)
    small_own = jnp.pad(small_own, ((0, 0), (0, 128 - small_own.shape[1])))
    deal_grid = deal.reshape(blocks, blocks, parts, piece)
    picks = lax.dynamic_slice(deal_grid, (0, block, column, 0), (blocks, 1, 1, piece)).reshape(-1)
    picks = picks - block * rows
    inputs, dealt_grads, qkv_full, out_full, small_full = start_exchange(
        tokens[picks].reshape(blocks, piece, width),
        out_grad[picks].reshape(blocks, piece, width),
        qkv_own,
        w_out,
        small_own,
    )
    own_low = lax.dynamic_slice_in_dim(inputs, column, 1, 0).reshape(own, width)
    inputs = inputs.reshape(rows, width).astype(f32)
    qkv_full = qkv_full.reshape(width, -1)
    small_full = small_full.reshape(width, -1)
    router_full = small_full[:, :expert_count]
    gain_full = small_full[:, expert_count : expert_count + 4].T.astype(f32)
    gain_attn, gain_ffn = gain_full[0], gain_full[3]
    gain_query = lax.dynamic_slice_in_dim(gain_full[1], column * local_width, local_width)
    gain_key = lax.dynamic_slice_in_dim(gain_full[2], column * local_width, local_width)
    own_grad_low = dealt_grads.reshape(own, width)
    grads_all = lax.all_gather(own_grad_low, BOTH, axis=0, tiled=True)
    own_in = own_low.astype(f32)
    own_grad = own_grad_low.astype(f32)

    scale = 1.0 / math.sqrt(HEAD_DIM)
    normed = (inputs * rms_inv(inputs) * gain_attn).astype(bf16)
    qkv = dot32(normed, qkv_full, NN)
    query_pre = qkv[:, :local_width]
    key_pre = qkv[:, local_width : 2 * local_width]
    squares = sum_few(
        jnp.stack([jnp.sum(query_pre * query_pre, axis=-1), jnp.sum(key_pre * key_pre, axis=-1)])
    )
    cosines, sines, starts = rope_tables(doc_ids, HEAD_DIM)
    cosines = reorder(jnp.concatenate([cosines, cosines], axis=1))
    sines = reorder(jnp.concatenate([-sines, sines], axis=1))
    positions = reorder(jnp.arange(rows, dtype=jnp.int32))
    spans = jnp.stack([reorder(starts), positions], axis=1)
    places = jnp.broadcast_to(positions[None], (8, rows))
    invs = lax.rsqrt(squares / width + NORM_EPS).T
    gains = jnp.stack([gain_query, gain_key])
    query_rot, key_rot, value_rows, attended, log_total, branch = attend(
        qkv, invs, gains, cosines, sines, spans, places, out_full
    )
    branch_own = sum_tensor(branch)

    residual = own_in + branch_own
    resid_inv = rms_inv(residual)
    resid_hat = residual * resid_inv
    ffn_in = (resid_hat * gain_ffn).astype(bf16)
    logits = dot32(ffn_in, router_full, NN)
    router_probs = jax.nn.softmax(logits, axis=-1)
    local_experts = w_gate.shape[0]
    own_routes = lax.dynamic_slice(
        routes.reshape(blocks, parts, piece, -1),
        (0, column, 0, 0),
        (blocks, 1, piece, routes.shape[1]),
    ).reshape(own, -1)
    expert_ids = jnp.arange(expert_count, dtype=jnp.int32)
    routed = jnp.any(own_routes[:, :, None] == expert_ids[None, None, :], axis=1)
    gates_own = jnp.where(routed, router_probs, 0.0)

    hidden_width = w_gate.shape[2]
    joined_weight = jnp.concatenate(
        [w_gate[i] for i in range(local_experts)] + [w_up[i] for i in range(local_experts)], axis=1
    )
    down_weight = w_down.reshape(local_experts * hidden_width, width)
    rows_all, gates_all, pre_all, gated_all, mixed = experts_forward(
        ffn_in, gates_own.T, joined_weight, down_weight
    )
    mix_own, joined_grad, row_terms, gate_grads = experts_backward(
        mixed, grads_all, pre_all, gates_all, joined_weight, down_weight
    )
    output_own = (residual + mix_own).astype(bf16)
    row_own, gate_grad_own, d_w_gate, d_w_up, d_w_down = experts_weights(
        row_terms, gate_grads, rows_all, grads_all, joined_grad, gated_all
    )
    gate_grad_own = gate_grad_own.T
    d_w_down = d_w_down.reshape(w_down.shape)

    prob_grad = jnp.where(routed, gate_grad_own, 0.0)
    logit_grad = (
        router_probs * (prob_grad - jnp.sum(router_probs * prob_grad, axis=-1, keepdims=True))
    ).astype(bf16)
    d_router = dot32(ffn_in, logit_grad, TN)
    ffn_grad = row_own + dot32(logit_grad, router_full, NT)
    d_ffn_gain = jnp.sum(ffn_grad * resid_hat, axis=0)
    scaled_ffn = ffn_grad * gain_ffn
    resid_grad = own_grad + resid_inv * (
        scaled_ffn - resid_hat * jnp.mean(scaled_ffn * resid_hat, axis=-1, keepdims=True)
    )
    branch_grad = gather_tensor(resid_grad.astype(bf16))

    branch_cols = branch_grad.reshape(rows, blocks, width // blocks)
    d_wo = jnp.einsum("rk,red->ekd", attended, branch_cols, preferred_element_type=f32).astype(bf16)
    d_wo, branch_grad = lax.optimization_barrier((d_wo, branch_grad))
    sum_wo = lax.psum_scatter(d_wo, EXPERT, scatter_dimension=0, tiled=False)
    hat_grads, value_grad, dots, d_gains = attend_back(
        branch_grad, out_full, query_rot, key_rot, value_rows, log_total,
        qkv, invs, gains, cosines, sines, spans, places,
    )
    d_query_gain, d_key_gain = d_gains[0], d_gains[1]
    dots = sum_few(dots.reshape(2, rows)) / width

    def norm_back(i):
        part = slice(i * local_width, (i + 1) * local_width)
        inv = invs[:, i : i + 1]
        return (inv * (hat_grads[:, part] - qkv[:, part] * inv * dots[i][:, None])).astype(bf16)

    query_grad, key_grad = norm_back(0), norm_back(1)
    qkv_grad = jnp.concatenate([query_grad, key_grad, value_grad], axis=1)
    input_terms = dot32(qkv_grad, qkv_full, NT).astype(bf16)
    normed_grad = sum_tensor(input_terms)
    d_qkv = dot32(normed, qkv_grad, TN).astype(bf16)
    d_qkv, sum_wo = lax.optimization_barrier((d_qkv, sum_wo))

    own_inv = rms_inv(own_in)
    own_hat = own_in * own_inv
    d_attn_gain = jnp.sum(normed_grad * own_hat, axis=0)
    scaled_attn = normed_grad * gain_attn
    input_grad = resid_grad + own_inv * (
        scaled_attn - own_hat * jnp.mean(scaled_attn * own_hat, axis=-1, keepdims=True)
    )

    def widen(slots):
        return lax.dynamic_update_slice_in_dim(
            jnp.zeros((width,), f32), slots, column * local_width, 0
        )

    small = jnp.concatenate(
        [
            d_router.T,
            jnp.stack([d_attn_gain, widen(d_query_gain), widen(d_key_gain), d_ffn_gain]),
        ]
    )
    small = jnp.pad(small, ((0, 24 - small.shape[0]), (0, 0)))
    small = jnp.swapaxes(small.reshape(24, blocks, -1), 0, 1)

    back_out, back_in, sum_qkv, small = last_exchange(
        output_own.reshape(blocks, piece, width),
        input_grad.astype(bf16).reshape(blocks, piece, width),
        d_qkv.reshape(blocks, -1, d_qkv.shape[1]),
        small,
    )
    sum_router = small[:expert_count].T
    sum_gains = small[expert_count:]
    came = lax.dynamic_slice(deal_grid, (0, block, 0, 0), (blocks, 1, parts, piece))
    came = jnp.swapaxes(came.reshape(blocks, parts, piece), 0, 1).reshape(-1) - block * rows
    chooser = (jnp.arange(rows, dtype=jnp.int32)[:, None] == came[None, :]).astype(bf16)
    output = dot32(chooser, back_out.reshape(rows, width), NN).astype(bf16)
    d_tokens = dot32(chooser, back_in.reshape(rows, width), NN).astype(bf16)
    return (
        output,
        d_tokens,
        sum_gains[0],
        sum_qkv[:, :local_width],
        sum_qkv[:, local_width : 2 * local_width],
        sum_qkv[:, 2 * local_width :],
        sum_wo.astype(f32),
        sum_gains[1],
        sum_gains[2],
        sum_gains[3],
        sum_router,
        d_w_gate,
        d_w_up,
        d_w_down,
    )


def pick_body(*args):
    routes, experts = args[14], args[9].shape[1]
    mesh_fits = (lax.axis_size(EXPERT), lax.axis_size(TENSOR)) == (8, 4)
    body = dense_body if mesh_fits and experts <= 2 * routes.shape[1] else routed_body
    return body(*args)


def solution(mesh):
    in_specs = (
        P(EXPERT, None),
        P(EXPERT),
        P(EXPERT, TENSOR),
        P(EXPERT, TENSOR),
        P(EXPERT, TENSOR),
        P(TENSOR, EXPERT),
        P(EXPERT),
        P(EXPERT),
        P(EXPERT),
        P(EXPERT, None),
        P(EXPERT, None, TENSOR),
        P(EXPERT, None, TENSOR),
        P(EXPERT, TENSOR, None),
        P(EXPERT),
        P(EXPERT, None),
        P(),
        P(EXPERT, None),
    )
    out_specs = (
        P(EXPERT, None),
        P(EXPERT, None),
        P(EXPERT),
        P(EXPERT, TENSOR),
        P(EXPERT, TENSOR),
        P(EXPERT, TENSOR),
        P(TENSOR, EXPERT),
        P(EXPERT),
        P(EXPERT),
        P(EXPERT),
        P(EXPERT, None),
        P(EXPERT, None, TENSOR),
        P(EXPERT, None, TENSOR),
        P(EXPERT, TENSOR, None),
    )
    return jax.shard_map(pick_body, mesh=mesh, in_specs=in_specs, out_specs=out_specs, check_vma=False)
```

```python
import functools
import math

import jax
import jax.numpy as jnp
from jax import lax
from jax.experimental import pallas as pl
from jax.experimental.pallas import tpu as pltpu
from jax.sharding import PartitionSpec as P

HEAD_DIM = 128
EXPERT, TENSOR = "expert", "tensor"


NORM_EPS = 1e-05
ROPE_BASE = 10000.0


def rope_tables(documents, head_size):
    row_count = documents.shape[0]
    positions = jnp.arange(row_count, dtype=jnp.int32)
    new_doc = jnp.concatenate(
        [jnp.ones((1,), jnp.int32), (documents[1:] != documents[:-1]).astype(jnp.int32)]
    )
    starts = lax.cummax(jnp.where(new_doc > 0, positions, 0), axis=0)
    places = (positions - starts).astype(jnp.float32)
    half_dim = head_size // 2
    frequency = jnp.exp(
        jnp.arange(half_dim, dtype=jnp.float32) * (-2.0 * math.log(ROPE_BASE) / head_size)
    )
    angles = places[:, None] * frequency[None, :]
    return (jnp.cos(angles), jnp.sin(angles), starts)


def rotate(values, cosines, sines):
    half_dim = values.shape[-1] // 2
    first_half = values[..., :half_dim]
    second_half = values[..., half_dim:]
    cos_rows = cosines[:, None, :]
    sin_rows = sines[:, None, :]
    return jnp.concatenate(
        [
            first_half * cos_rows - second_half * sin_rows,
            second_half * cos_rows + first_half * sin_rows,
        ],
        axis=-1,
    )


def unrotate(grads_in, cosines, sines):
    half_dim = grads_in.shape[-1] // 2
    first_half = grads_in[..., :half_dim]
    second_half = grads_in[..., half_dim:]
    cos_rows = cosines[:, None, :]
    sin_rows = sines[:, None, :]
    return jnp.concatenate(
        [
            first_half * cos_rows + second_half * sin_rows,
            second_half * cos_rows - first_half * sin_rows,
        ],
        axis=-1,
    )


def to_experts(rows):
    return lax.all_to_all(rows, EXPERT, split_axis=0, concat_axis=0, tiled=True)


def from_experts(rows):
    return lax.all_to_all(rows, EXPERT, split_axis=0, concat_axis=0, tiled=True)


def hidden_sums(terms):
    return lax.psum_scatter(terms, TENSOR, scatter_dimension=3, tiled=True)


def routed_body(
    tokens,
    attn_gain,
    w_query,
    w_key,
    w_value,
    w_out,
    query_gain,
    key_gain,
    ffn_gain,
    w_router,
    w_gate,
    w_up,
    w_down,
    doc_ids,
    routes,
    deal,
    out_grad,
):
    row_count, width = tokens.shape
    tensor_parts = lax.axis_size(TENSOR)
    expert_parts = lax.axis_size(EXPERT)
    column = lax.axis_index(TENSOR)
    device_idx = lax.axis_index(EXPERT)
    quarter = width // tensor_parts
    share_rows = row_count // expert_parts
    deal_rows = lax.dynamic_slice_in_dim(
        deal.reshape(expert_parts, row_count), device_idx * share_rows, share_rows, 1
    )
    local_pick = deal_rows - device_idx * row_count
    dealt_tokens, dealt_grad = (
        lax.all_to_all(tokens[local_pick], EXPERT, split_axis=0, concat_axis=0, tiled=True),
        lax.all_to_all(out_grad[local_pick], EXPERT, split_axis=0, concat_axis=0, tiled=True),
    )
    dealt_tokens = dealt_tokens.reshape(row_count, width)
    dealt_grad = dealt_grad.reshape(row_count, width)
    gain_stack = jnp.stack([attn_gain, query_gain, key_gain, ffn_gain])
    wq_full, wk_full, wv_full, wo_full, router_full, gain_full = (
        lax.all_gather(w_query, EXPERT, axis=0, tiled=True),
        lax.all_gather(w_key, EXPERT, axis=0, tiled=True),
        lax.all_gather(w_value, EXPERT, axis=0, tiled=True),
        lax.all_gather(w_out, EXPERT, axis=1, tiled=True),
        lax.all_gather(w_router, EXPERT, axis=0, tiled=True),
        lax.all_gather(gain_stack, EXPERT, axis=1, tiled=True),
    )
    local_width = wq_full.shape[1]
    head_count = local_width // HEAD_DIM
    gain_attn = gain_full[0].astype(jnp.float32)
    gain_query = lax.dynamic_slice_in_dim(
        gain_full[1].astype(jnp.float32), column * local_width, local_width
    )
    gain_key = lax.dynamic_slice_in_dim(
        gain_full[2].astype(jnp.float32), column * local_width, local_width
    )
    gain_ffn = gain_full[3].astype(jnp.float32)
    scale = 1.0 / math.sqrt(HEAD_DIM)
    inputs = dealt_tokens.astype(jnp.float32)
    input_inv = lax.rsqrt(jnp.mean(inputs * inputs, axis=-1, keepdims=True) + NORM_EPS)
    input_hat = inputs * input_inv
    normed = (input_hat * gain_attn).astype(jnp.bfloat16)
    query_pre = jnp.dot(normed, wq_full, preferred_element_type=jnp.float32)
    key_pre = jnp.dot(normed, wk_full, preferred_element_type=jnp.float32)
    value_rows = (
        jnp.dot(normed, wv_full, preferred_element_type=jnp.float32)
        .astype(jnp.bfloat16)
        .reshape(row_count, head_count, HEAD_DIM)
    )
    query_sq, key_sq = lax.psum(
        (jnp.sum(query_pre * query_pre, axis=-1), jnp.sum(key_pre * key_pre, axis=-1)), TENSOR
    )
    query_inv = lax.rsqrt(query_sq / width + NORM_EPS)[:, None]
    key_inv = lax.rsqrt(key_sq / width + NORM_EPS)[:, None]
    query_hat = query_pre * query_inv
    key_hat = key_pre * key_inv
    cosines, sines, _ = rope_tables(doc_ids, HEAD_DIM)
    query_rot = rotate(
        (query_hat * gain_query).reshape(row_count, head_count, HEAD_DIM), cosines, sines
    ).astype(jnp.bfloat16)
    key_rot = rotate(
        (key_hat * gain_key).reshape(row_count, head_count, HEAD_DIM), cosines, sines
    ).astype(jnp.bfloat16)
    positions = jnp.arange(row_count, dtype=jnp.int32)
    allowed = (doc_ids[:, None] == doc_ids[None, :]) & (positions[None, :] <= positions[:, None])

    def masked_scores():
        raw_scores = jnp.einsum(
            "qhd,khd->hqk", query_rot, key_rot, preferred_element_type=jnp.float32
        )
        return jnp.where(allowed[None], raw_scores * scale, -1e30)

    scores = masked_scores()
    top_score = jnp.max(scores, axis=-1, keepdims=True)
    log_total = top_score + jnp.log(jnp.sum(jnp.exp(scores - top_score), axis=-1, keepdims=True))
    weights = jnp.exp(scores - log_total).astype(jnp.bfloat16)
    attended = (
        jnp.einsum("hqk,khd->qhd", weights, value_rows, preferred_element_type=jnp.float32)
        .astype(jnp.bfloat16)
        .reshape(row_count, local_width)
    )
    branch = lax.psum(jnp.dot(attended, wo_full, preferred_element_type=jnp.float32), TENSOR)
    residual = inputs + branch
    resid_inv = lax.rsqrt(jnp.mean(residual * residual, axis=-1, keepdims=True) + NORM_EPS)
    resid_hat = residual * resid_inv
    ffn_in = (resid_hat * gain_ffn).astype(jnp.bfloat16)
    logits = jnp.dot(ffn_in, router_full, preferred_element_type=jnp.float32)
    router_probs = jax.nn.softmax(logits, axis=-1)
    expert_count = router_full.shape[1]
    top_count = routes.shape[1]
    local_experts = expert_count // expert_parts
    capacity = tensor_parts * max(
        1,
        (row_count * top_count + expert_count * tensor_parts - 1) // (expert_count * tensor_parts),
        row_count * top_count * 5 // (4 * expert_count * tensor_parts),
    )
    expert_ids = jnp.arange(expert_count, dtype=jnp.int32)
    route_match = routes[:, :, None] == expert_ids[None, None, :]
    gate_probs = jnp.sum(jnp.where(route_match, router_probs[:, None, :], 0.0), axis=-1)
    flat_routes = routes.reshape(-1)
    onehot = (flat_routes[:, None] == expert_ids[None, :]).astype(jnp.int32)
    slot_rank = jnp.sum((jnp.cumsum(onehot, axis=0) - onehot) * onehot, axis=-1)
    row_ids = flat_routes * capacity + slot_rank
    token_ids = jnp.arange(row_count * top_count, dtype=jnp.int32) // top_count
    slot_token = (
        jnp.full((expert_count * capacity,), row_count, jnp.int32).at[row_ids].set(token_ids)
    )
    slot_gates = (
        jnp.zeros((expert_count * capacity,), jnp.float32).at[row_ids].set(gate_probs.reshape(-1))
    )
    pick_rows = row_ids.reshape(row_count, top_count)
    padded_in = jnp.concatenate([ffn_in, jnp.zeros((1, width), jnp.bfloat16)], axis=0)
    grad_full = dealt_grad.astype(jnp.float32)
    grad_padded = jnp.concatenate([grad_full, jnp.zeros((1, width), jnp.float32)], axis=0)
    received = to_experts(
        padded_in[slot_token].reshape(expert_parts, local_experts, capacity, width)
    )
    gate_pre = jnp.einsum("secd,edf->secf", received, w_gate, preferred_element_type=jnp.float32)
    up_pre = jnp.einsum("secd,edf->secf", received, w_up, preferred_element_type=jnp.float32)
    sigmoid_gate = jax.nn.sigmoid(gate_pre)
    silu_gate = gate_pre * sigmoid_gate
    hidden = (silu_gate * up_pre).astype(jnp.bfloat16)
    partial_out = jnp.einsum("secf,efd->secd", hidden, w_down, preferred_element_type=jnp.float32)
    own_columns = hidden_sums(partial_out).astype(jnp.bfloat16)
    returned = from_experts(own_columns).reshape(expert_count * capacity, quarter)
    chosen = returned[pick_rows].astype(jnp.float32)
    mix_own = jnp.sum(gate_probs[:, :, None] * chosen, axis=1)
    mix_part = lax.dynamic_update_slice_in_dim(
        jnp.zeros((row_count, width), jnp.float32), mix_own, column * quarter, 1
    )
    grad_own = lax.dynamic_slice_in_dim(grad_full, column * quarter, quarter, 1)
    gate_grad_part = jnp.sum(grad_own[:, None, :] * chosen, axis=-1)
    send_grad = (
        (grad_padded[slot_token] * slot_gates[:, None])
        .astype(jnp.bfloat16)
        .reshape(expert_parts, local_experts, capacity, width)
    )
    recv_grad = to_experts(send_grad)
    d_w_down = jnp.einsum("secf,secd->efd", hidden, recv_grad, preferred_element_type=jnp.float32)
    hidden_grad = jnp.einsum(
        "secd,efd->secf", recv_grad, w_down, preferred_element_type=jnp.float32
    )
    gate_grad_pre = (
        hidden_grad * up_pre * sigmoid_gate * (1.0 + gate_pre * (1.0 - sigmoid_gate))
    ).astype(jnp.bfloat16)
    up_grad_pre = (hidden_grad * silu_gate).astype(jnp.bfloat16)
    d_w_gate = jnp.einsum(
        "secd,secf->edf", received, gate_grad_pre, preferred_element_type=jnp.float32
    )
    d_w_up = jnp.einsum("secd,secf->edf", received, up_grad_pre, preferred_element_type=jnp.float32)
    joined_grad = jnp.concatenate([gate_grad_pre, up_grad_pre], axis=-1)
    joined_weight = jnp.concatenate([w_gate, w_up], axis=-1)
    row_terms = jnp.einsum(
        "secf,edf->secd", joined_grad, joined_weight, preferred_element_type=jnp.float32
    )
    row_own = hidden_sums(row_terms).astype(jnp.bfloat16)
    row_back = from_experts(row_own).reshape(expert_count * capacity, quarter)
    ffn_grad_own = jnp.sum(row_back[pick_rows].astype(jnp.float32), axis=1)
    placed = lax.dynamic_update_slice_in_dim(
        jnp.zeros((row_count, width), jnp.float32), ffn_grad_own, column * quarter, 1
    )
    ffn_grad_rows, gate_grad, mix_total = lax.psum((placed, gate_grad_part, mix_part), TENSOR)
    output = (residual + mix_total).astype(jnp.bfloat16)
    prob_grad = jnp.sum(jnp.where(route_match, gate_grad[:, :, None], 0.0), axis=1)
    logit_grad = (
        router_probs * (prob_grad - jnp.sum(router_probs * prob_grad, axis=-1, keepdims=True))
    ).astype(jnp.bfloat16)
    d_router = jnp.einsum("rd,re->de", ffn_in, logit_grad, preferred_element_type=jnp.float32)
    ffn_grad = ffn_grad_rows + jnp.einsum(
        "re,de->rd", logit_grad, router_full, preferred_element_type=jnp.float32
    )
    d_ffn_gain = jnp.sum(ffn_grad * resid_hat, axis=0)
    scaled_ffn = ffn_grad * gain_ffn
    resid_grad = grad_full + resid_inv * (
        scaled_ffn - resid_hat * jnp.mean(scaled_ffn * resid_hat, axis=-1, keepdims=True)
    )
    branch_grad = resid_grad.astype(jnp.bfloat16)
    d_wo = jnp.einsum("rk,rd->kd", attended, branch_grad, preferred_element_type=jnp.float32)
    attended_grad = (
        jnp.einsum("rd,kd->rk", branch_grad, wo_full, preferred_element_type=jnp.float32)
        .astype(jnp.bfloat16)
        .reshape(row_count, head_count, HEAD_DIM)
    )
    probs_again = jnp.exp(masked_scores() - log_total)
    prob_grads = jnp.einsum(
        "qhd,khd->hqk", attended_grad, value_rows, preferred_element_type=jnp.float32
    )
    value_grad = (
        jnp.einsum(
            "hqk,qhd->khd",
            probs_again.astype(jnp.bfloat16),
            attended_grad,
            preferred_element_type=jnp.float32,
        )
        .astype(jnp.bfloat16)
        .reshape(row_count, local_width)
    )
    row_delta = jnp.sum(probs_again * prob_grads, axis=-1, keepdims=True)
    score_grad = (probs_again * (prob_grads - row_delta) * scale).astype(jnp.bfloat16)
    query_rot_grad = jnp.einsum(
        "hqk,khd->qhd", score_grad, key_rot, preferred_element_type=jnp.float32
    )
    key_rot_grad = jnp.einsum(
        "hqk,qhd->khd", score_grad, query_rot, preferred_element_type=jnp.float32
    )
    query_norm_grad = unrotate(query_rot_grad, cosines, sines).reshape(row_count, local_width)
    key_norm_grad = unrotate(key_rot_grad, cosines, sines).reshape(row_count, local_width)
    query_hat_grad = query_norm_grad * gain_query
    key_hat_grad = key_norm_grad * gain_key
    gain_pieces = jnp.stack(
        [jnp.sum(query_norm_grad * query_hat, axis=0), jnp.sum(key_norm_grad * key_hat, axis=0)]
    )
    gain_parts = lax.dynamic_update_slice_in_dim(
        jnp.zeros((2, width), jnp.float32), gain_pieces, column * local_width, 1
    )
    query_dot, key_dot, qk_gains = lax.psum(
        (
            jnp.sum(query_hat_grad * query_hat, axis=-1),
            jnp.sum(key_hat_grad * key_hat, axis=-1),
            gain_parts,
        ),
        TENSOR,
    )
    query_grad = (query_inv * (query_hat_grad - query_hat * (query_dot / width)[:, None])).astype(
        jnp.bfloat16
    )
    key_grad = (key_inv * (key_hat_grad - key_hat * (key_dot / width)[:, None])).astype(
        jnp.bfloat16
    )
    d_wq = jnp.einsum("rd,rk->dk", normed, query_grad, preferred_element_type=jnp.float32)
    d_wk = jnp.einsum("rd,rk->dk", normed, key_grad, preferred_element_type=jnp.float32)
    d_wv = jnp.einsum("rd,rk->dk", normed, value_grad, preferred_element_type=jnp.float32)
    input_terms = jnp.einsum("rk,dk->rd", query_grad, wq_full, preferred_element_type=jnp.float32)
    input_terms = input_terms + jnp.einsum(
        "rk,dk->rd", key_grad, wk_full, preferred_element_type=jnp.float32
    )
    input_terms = input_terms + jnp.einsum(
        "rk,dk->rd", value_grad, wv_full, preferred_element_type=jnp.float32
    )
    normed_grad = lax.psum(input_terms, TENSOR)
    d_attn_part = jnp.sum(normed_grad * input_hat, axis=0)
    scaled_attn = normed_grad * gain_attn
    input_grad = resid_grad + input_inv * (
        scaled_attn - input_hat * jnp.mean(scaled_attn * input_hat, axis=-1, keepdims=True)
    )
    dealt_dtokens = input_grad.astype(jnp.bfloat16)
    gain_grads = jnp.stack([d_attn_part, qk_gains[0], qk_gains[1], d_ffn_gain])
    sum_wq, sum_wk, sum_wv, sum_wo, sum_router, sum_gains = (
        lax.psum_scatter(d_wq, EXPERT, scatter_dimension=0, tiled=True),
        lax.psum_scatter(d_wk, EXPERT, scatter_dimension=0, tiled=True),
        lax.psum_scatter(d_wv, EXPERT, scatter_dimension=0, tiled=True),
        lax.psum_scatter(d_wo, EXPERT, scatter_dimension=1, tiled=True),
        lax.psum_scatter(d_router, EXPERT, scatter_dimension=0, tiled=True),
        lax.psum_scatter(gain_grads, EXPERT, scatter_dimension=1, tiled=True),
    )
    back_out, back_dtok = (
        lax.all_to_all(
            output.reshape(expert_parts, share_rows, width),
            EXPERT,
            split_axis=0,
            concat_axis=0,
            tiled=True,
        ),
        lax.all_to_all(
            dealt_dtokens.reshape(expert_parts, share_rows, width),
            EXPERT,
            split_axis=0,
            concat_axis=0,
            tiled=True,
        ),
    )
    flat_pick = local_pick.reshape(-1)
    output_rows = (
        jnp.zeros((row_count, width), jnp.bfloat16)
        .at[flat_pick]
        .set(back_out.reshape(row_count, width))
    )
    d_tokens = (
        jnp.zeros((row_count, width), jnp.bfloat16)
        .at[flat_pick]
        .set(back_dtok.reshape(row_count, width))
    )
    return (
        output_rows,
        d_tokens,
        sum_gains[0],
        sum_wq,
        sum_wk,
        sum_wv,
        sum_wo,
        sum_gains[1],
        sum_gains[2],
        sum_gains[3],
        sum_router,
        d_w_gate,
        d_w_up,
        d_w_down,
    )


MESH_ID = pl.DeviceIdType.MESH
ANY = pl.BlockSpec(memory_space=pl.ANY)
IN_VMEM = pl.BlockSpec(memory_space=pltpu.VMEM)
def cost_of(micros):
    return pl.CostEstimate(flops=0, bytes_accessed=micros * 3_000_000, transcendentals=0)


SELF, NEAR, FAR, BOTH_FLIPPED = 0, 1, 2, 3


def place_of(device):
    expert, tensor = device
    return expert // 2, expert % 2, tensor // 2, tensor % 2


def flipped(device, role):
    expert, tensor = device
    _, x, y, core = place_of(device)
    step_x, step_y = 1 - 2 * x, 2 - 4 * y
    if role == NEAR:
        return expert + (1 - core) * step_x, tensor + core * step_y
    if role == FAR:
        return expert + core * step_x, tensor + (1 - core) * step_y
    if role == BOTH_FLIPPED:
        return expert + step_x, tensor + step_y
    return expert, tensor


def moved_z(device, hops):
    expert, tensor = device
    return lax.rem(expert + 2 * hops, 8), tensor


def sibling(device):
    expert, tensor = device
    return expert, tensor + 1 - 2 * (tensor % 2)


def slot_of(device):
    return device[0] * 4 + device[1]


def here():
    return lax.axis_index(EXPERT), lax.axis_index(TENSOR)


def greet(partners):
    barrier = pltpu.get_barrier_semaphore()
    for partner in partners:
        pl.semaphore_signal(barrier, inc=1, device_id=partner, device_id_type=MESH_ID)
    pl.semaphore_wait(barrier, len(partners))


def push(source, target, send_sem, recv_sem, device):
    return pltpu.make_async_remote_copy(
        src_ref=source,
        dst_ref=target,
        send_sem=send_sem,
        recv_sem=recv_sem,
        device_id=device,
        device_id_type=MESH_ID,
    )


def hop(device, flips, hops):
    expert, tensor = device
    return lax.rem(expert + flips * (1 - 2 * lax.rem(expert, 2)) + 2 * hops, 8), tensor


def across_y(device):
    expert, tensor = device
    return expert, lax.rem(tensor + 2, 4)


class Line:
    def __init__(self, send_sem, recv_sem):
        self.send_sem, self.recv_sem = send_sem, recv_sem
        self.started = []

    def send(self, source, target, tag, recv_tag, device):
        copy = push(source, target, self.send_sem.at[tag], self.recv_sem.at[recv_tag], device)
        copy.start()
        self.started.append(copy)

    def wait(self, target, tag, device):
        push(target, target, self.send_sem.at[0], self.recv_sem.at[tag], device).wait_recv()

    def finish(self):
        for copy in self.started:
            copy.wait_send()


PIECES = ((0, 1), (1, 0), (3, 0), (1, 1), (3, 1), (2, 0), (2, 1))


def exchange_steps(source, out, gathered, line, local_sem):
    me = here()
    tensor = me[1]
    side, sib = across_y(me), sibling(me)

    def at(column, expert):
        return out.at[column, expert] if gathered else out.at[expert]

    local = pltpu.make_async_copy(source.at[me[0]], at(tensor, me[0]), local_sem)
    local.start()
    if gathered:
        line.send(source.at[me[0]], at(tensor, me[0]), 8, 8, side)
        line.send(source.at[me[0]], at(tensor, me[0]), 16, 16, sib)
    for k, flips in PIECES:
        target = hop(me, flips, k)
        line.send(
            source.at[target[0]], at(tensor, me[0]), k * 2 + flips, (4 - k) % 4 * 2 + flips, target
        )
    yield
    for k, flips in PIECES:
        expert = hop(me, flips, k)[0]
        tag = k * 2 + flips
        line.wait(at(tensor, expert), tag, sib)
        if gathered:
            line.send(at(tensor, expert), at(tensor, expert), 8 + tag, 8 + tag, side)
            line.send(at(tensor, expert), at(tensor, expert), 16 + tag, 16 + tag, sib)
        yield
    if gathered:
        for k, flips in ((0, 0),) + PIECES:
            expert = hop(me, flips, k)[0]
            tag = k * 2 + flips
            line.wait(at(side[1], expert), 8 + tag, sib)
            line.send(at(side[1], expert), at(side[1], expert), 24 + tag, 24 + tag, sib)
            yield
        for k, flips in ((0, 0),) + PIECES:
            expert = hop(me, flips, k)[0]
            tag = k * 2 + flips
            line.wait(at(sib[1], expert), 16 + tag, sib)
            line.wait(at(across_y(sib)[1], expert), 24 + tag, sib)
    local.wait()
    line.finish()


def gather_expert_steps(sources, outs, plans, line, local_sems):
    me = here()
    z = me[0] // 2
    beside = hop(me, 1, 0)
    locals_ = [
        pltpu.make_async_copy(source, out.at[me[0]], local_sems.at[n])
        for n, (source, out) in enumerate(zip(sources, outs))
    ]
    for copy in locals_:
        copy.start()
    items = [(n, i, i < s) for n, (c, s) in enumerate(plans) for i in range(c)]
    count = len(items)
    straight = [j for j in range(count) if items[j][2]]
    crossed = [j for j in range(count) if not items[j][2]]

    def window(ref, j):
        n, i, _ = items[j]
        step = sources[n].shape[0] // plans[n][0]
        return ref.at[pl.ds(i * step, step), :]

    def own(j):
        return window(sources[items[j][0]], j)

    def block_of(expert, j):
        return window(outs[items[j][0]].at[expert], j)

    def base(distance, up, j):
        return ((distance - 1) * 2 + up) * count + j

    def passes(ref, target, tag, up, held):
        @pl.when(held & ((z < 3) if up else (z > 0)))
        def _():
            push(
                ref, target, line.send_sem.at[tag], line.recv_sem.at[tag], hop(me, 0, 1 if up else 3)
            ).start()

    def came(column, distance, up):
        return lax.rem(column[0] + (8 - 2 * distance if up else 2 * distance), 8)

    def is_held(distance, up):
        return (z >= distance) if up else (z + distance <= 3)

    cross, over = 6 * count, 12 * count
    for j in crossed + straight:
        line.send(own(j), block_of(me[0], j), over + j, over + j, beside)
    for j in straight + crossed:
        for up in (1, 0):
            passes(own(j), block_of(me[0], j), base(1, up, j), up, z >= 0)
    yield
    for j in crossed:
        block = block_of(beside[0], j)
        line.wait(block, over + j, beside)
        for up in (1, 0):
            passes(block, block, cross + base(1, up, j), up, z >= 0)
    yield
    for distance in (1, 2, 3):
        for j in straight + crossed:
            for up in (1, 0):
                held = is_held(distance, up)
                block = block_of(came(me, distance, up), j)
                tag = base(distance, up, j)

                @pl.when(held)
                def _():
                    line.wait(block, tag, beside)

                if distance < 3:
                    passes(block, block, base(distance + 1, up, j), up, held)
                if items[j][2]:

                    @pl.when(held)
                    def _():
                        push(
                            block,
                            block,
                            line.send_sem.at[cross + tag],
                            line.recv_sem.at[cross + tag],
                            beside,
                        ).start()

            yield
        for j in crossed:
            for up in (1, 0):
                held = is_held(distance, up)
                block = block_of(came(beside, distance, up), j)
                tag = cross + base(distance, up, j)

                @pl.when(held)
                def _():
                    line.wait(block, tag, beside)

                if distance < 3:
                    passes(block, block, cross + base(distance + 1, up, j), up, held)
            yield
    for j in straight:
        line.wait(block_of(beside[0], j), over + j, beside)
    for distance in (1, 2, 3):
        for j in straight + crossed:
            for up in (1, 0):
                held = is_held(distance, up)
                block = block_of(came(beside, distance, up), j)
                tag = base(distance, up, j)
                sent_on = (z + 1 >= distance) & (z < 3) if up else (z - 1 + distance <= 3) & (z > 0)

                def sent(at):
                    push(block, block, line.send_sem.at[at], line.recv_sem.at[at], beside).wait_send()

                if items[j][2]:

                    @pl.when(held)
                    def _():
                        sent(cross + tag)
                        line.wait(block, cross + tag, beside)

                @pl.when(sent_on)
                def _():
                    sent(tag)
                    if not items[j][2]:
                        sent(cross + tag)

        yield
    for copy in locals_:
        copy.wait()
    line.finish()


def sum_rows(target, terms, step=16):
    def body(i, carry):
        window = pl.ds(pl.multiple_of(i * step, step), step)
        value = terms[0][window, :].astype(jnp.float32)
        for ref in terms[1:]:
            value = value + ref[window, :].astype(jnp.float32)
        target[window, :] = value.astype(target.dtype)
        return carry

    lax.fori_loop(0, target.shape[0] // step, body, 0)


def sum_expert_steps(part, out, mine, from_x, from_z, line, load_sem, step=16):
    me = here()
    beside = hop(me, 1, 0)
    loads = {}
    for k in (2, 1, 3, 0):
        line.send(part.at[hop(me, 1, k)[0]], from_x.at[k], k, k, beside)
        loads[k] = pltpu.make_async_copy(part.at[hop(me, 0, k)[0]], mine.at[k], load_sem.at[k])
        loads[k].start()
    yield
    for k in (2, 1, 3, 0):
        loads[k].wait()
        line.wait(from_x.at[k], k, beside)
        if k:
            sum_rows(mine.at[k], [mine.at[k], from_x.at[k]], step)
            line.send(mine.at[k], from_z.at[3 - k], 3 + k, 4 + 3 - k, hop(me, 0, k))
            yield
            yield
    for i in range(3):
        line.wait(from_z.at[i], 4 + i, beside)
    sum_rows(out, [mine.at[0], from_x.at[0], from_z.at[0], from_z.at[1], from_z.at[2]], step)
    line.finish()


CHAIN = (3, 0, 2, 1)


def sum_chain_steps(part, out, mine, from_x, arrive, from_b, line, load_sem, straight):
    me = here()
    z = me[0] // 2
    x = lax.rem(me[0], 2)
    low = z < 2
    near = jnp.where(low, z, 3 - z)
    behind = jnp.where(low, 0, 1)
    beside = hop(me, 1, 0)
    step = mine.shape[2]
    chunks = out.shape[0] // step
    streams = []
    for i in range(straight, chunks):
        streams += [(i, 1, None), (i, 0, None)]
    streams += [(i, 0, i) for i in range(straight)]
    first_x = len(streams) * 4
    first_b = first_x + straight * 4
    recv_x = len(streams) * 8
    recv_b = recv_x + straight * 4

    def plane(a):
        return jnp.where(low, a, 3 - a)

    def chunk_of(expert, i):
        return part.at[expert, pl.ds(i * step, step), :]

    def column(flip):
        return jnp.where(flip == 1, 1 - x, x)

    def load(s, a):
        i, flip, _ = streams[s]
        p = plane(a)
        return pltpu.make_async_copy(
            chunk_of(2 * p + column(flip), i), mine.at[s, p], load_sem.at[s * 4 + p]
        )

    for a in CHAIN:
        p = plane(a)
        for s, (i, _, at) in enumerate(streams):
            if at is not None:
                line.send(
                    chunk_of(2 * p + 1 - x, i), from_x.at[at, p], first_x + at * 4 + p,
                    recv_x + at * 4 + p, beside,
                )
            load(s, a).start()
    yield

    def own_terms(s, a):
        p = plane(a)
        load(s, a).wait()
        at = streams[s][2]
        if at is None:
            return [mine.at[s, p]]
        line.wait(from_x.at[at, p], recv_x + at * 4 + p, beside)
        return [mine.at[s, p], from_x.at[at, p]]

    def arrived(s, a, side):
        p = plane(a)
        ref = arrive.at[s, side, p]
        line.wait(ref, (s * 2 + side) * 4 + p, beside)
        return ref

    def passing(s, a, forward):
        p = plane(a)
        side = behind if forward else 1 - behind
        up = jnp.where(low, 1, 3) if forward else jnp.where(low, 3, 1)
        return push(
            mine.at[s, p],
            arrive.at[s, side, p],
            line.send_sem.at[s * 4 + p],
            line.recv_sem.at[(s * 2 + side) * 4 + p],
            hop(me, 0, up),
        )

    def pass_on(s, a, forward, sides):
        terms = own_terms(s, a) + [arrived(s, a, side) for side in sides]
        if len(terms) > 1:
            sum_rows(mine.at[s, plane(a)], terms)
        passing(s, a, forward).start()

    for a in CHAIN:
        for s in range(len(streams)):
            if a != 0:

                @pl.when(near == 0)
                def _():
                    pass_on(s, a, True, [])

            if a != 1:

                @pl.when(near == 1)
                def _():
                    pass_on(s, a, a != 0, [1 - behind if a == 0 else behind])

            yield

    def final(s, a, sides):
        i, flip, at = streams[s]
        terms = own_terms(s, a) + [arrived(s, a, side) for side in sides]
        if flip:
            total = mine.at[s, plane(a)]
            sum_rows(total, terms)
            j = i - straight
            push(
                total, from_b.at[j], line.send_sem.at[first_b + j], line.recv_sem.at[recv_b + j], beside
            ).start()
        else:
            sum_rows(out.at[pl.ds(i * step, step), :], terms)

    for s in sorted(range(len(streams)), key=lambda s: streams[s][2] is not None):

        @pl.when(near == 0)
        def _():
            final(s, 0, [1 - behind])

        @pl.when(near == 1)
        def _():
            final(s, 1, [behind, 1 - behind])

        yield
    for j in range(chunks - straight):
        rows = out.at[pl.ds((straight + j) * step, step), :]
        both = push(
            from_b.at[j], from_b.at[j], line.send_sem.at[first_b + j], line.recv_sem.at[recv_b + j], beside
        )
        both.wait()
        sum_rows(rows, [rows, from_b.at[j]])
    for a in CHAIN:
        for s in range(len(streams)):
            if a != 0:

                @pl.when(near == 0)
                def _():
                    passing(s, a, True).wait_send()

            if a != 1:

                @pl.when(near == 1)
                def _():
                    passing(s, a, a != 0).wait_send()

    line.finish()


def sum_everywhere_steps(part, out, mine, from_x, from_z, total, shares, line, load_sem):
    me = here()
    yield from sum_expert_steps(part, total, mine, from_x, from_z, line, load_sem, 8)
    peers = [across_y(me), sibling(me), across_y(sibling(me))]
    for i, peer in enumerate(peers):
        line.send(total, shares.at[me[1]], 7 + i, 7 + i, peer)
    shares[me[1]] = total[...]
    yield
    for i, peer in enumerate(peers):
        line.wait(shares.at[peer[1]], 7 + i, peer)
    sum_rows(out, [shares.at[i] for i in range(4)], 8)
    for i in range(3):
        line.started[-3 + i].wait_send()


def take_turns(steps):
    steps = list(steps)
    while steps:
        steps = [s for s in steps if next(s, steps) is not steps]


DMA = pltpu.SemaphoreType.DMA


GATHER_PLANS = ((1, 1), (4, 3), (2, 2))


def start_kernel(
    tokens, grads, weights, outs, small, o_tokens, o_grads, o_weights, o_outs, o_small, *sems
):
    me = here()
    pieces = [hop(me, flips, k) for k, flips in PIECES]
    greet(pieces + [across_y(me), sibling(me)])
    local = sems[7]
    take_turns(
        [
            exchange_steps(tokens, o_tokens, True, Line(sems[0], sems[1]), local.at[0]),
            exchange_steps(grads, o_grads, False, Line(sems[2], sems[3]), local.at[1]),
            gather_expert_steps(
                [small, weights, outs], [o_small, o_weights, o_outs], GATHER_PLANS,
                Line(sems[4], sems[5]), sems[6],
            ),
        ]
    )


def start_exchange(tokens, grads, weights, outs, small):
    piece = tokens.shape[1:]
    sds = jax.ShapeDtypeStruct
    return pl.pallas_call(
        start_kernel,
        out_shape=[
            sds((4, 8) + piece, tokens.dtype),
            sds((8,) + piece, grads.dtype),
            sds((8,) + weights.shape, weights.dtype),
            sds((8,) + outs.shape, outs.dtype),
            sds((8,) + small.shape, small.dtype),
        ],
        in_specs=[IN_VMEM] * 5,
        out_specs=[ANY] * 5,
        scratch_shapes=[DMA((32,)), DMA((32,)), DMA((8,)), DMA((8,))]
        + [DMA((13 * sum(c for c, _ in GATHER_PLANS),))] * 2
        + [DMA((3,)), DMA((2,))],
        compiler_params=pltpu.CompilerParams(
            collective_id=4, has_side_effects=True, vmem_limit_bytes=16 * 2**20
        ),
        cost_estimate=cost_of(100),
        name="start_exchange",
    )(tokens, grads, weights, outs, small)


def last_kernel(
    rows, more, part, small, o_rows, o_more, out, o_small,
    mine, from_x, arrive, from_b, mine_s, x_s, z_s, total_s, shares_s, *sems,
):
    me = here()
    pieces = [hop(me, flips, k) for k, flips in PIECES]
    greet(pieces + [across_y(me), sibling(me), across_y(sibling(me))])
    take_turns(
        [
            exchange_steps(more, o_more, True, Line(sems[2], sems[3]), sems[7].at[1]),
            exchange_steps(rows, o_rows, True, Line(sems[0], sems[1]), sems[7].at[0]),
            sum_everywhere_steps(
                small, o_small, mine_s, x_s, z_s, total_s, shares_s, Line(sems[8], sems[9]), sems[10]
            ),
            sum_chain_steps(
                part, out, mine, from_x, arrive, from_b, Line(sems[4], sems[5]), sems[6], from_x.shape[0]
            ),
        ]
    )


def last_exchange(rows, more, part, small):
    piece = rows.shape[1:]
    block, little = part.shape[1:], small.shape[1:]
    chunks, straight = 4, 3
    streams = 2 * chunks - straight
    chunk = (block[0] // chunks, block[1])
    first = (streams + straight) * 4
    sds = jax.ShapeDtypeStruct
    return pl.pallas_call(
        last_kernel,
        out_shape=[
            sds((4, 8) + piece, rows.dtype),
            sds((4, 8) + piece, more.dtype),
            sds(block, jnp.float32),
            sds(little, jnp.float32),
        ],
        in_specs=[IN_VMEM, IN_VMEM, ANY, ANY],
        out_specs=[ANY, ANY, IN_VMEM, IN_VMEM],
        scratch_shapes=[
            pltpu.VMEM((streams, 4) + chunk, part.dtype),
            pltpu.VMEM((straight, 4) + chunk, part.dtype),
            pltpu.VMEM((streams, 2, 4) + chunk, part.dtype),
            pltpu.VMEM((chunks - straight,) + chunk, part.dtype),
        ]
        + [pltpu.VMEM((n,) + little, jnp.float32) for n in (4, 4, 3)]
        + [pltpu.VMEM(little, jnp.float32), pltpu.VMEM((4,) + little, jnp.float32)]
        + [DMA((32,))] * 4
        + [DMA((first + chunks,)), DMA((first + streams * 4 + chunks,)), DMA((streams * 4,)), DMA((2,))]
        + [DMA((10,)), DMA((10,)), DMA((4,))],
        compiler_params=pltpu.CompilerParams(
            collective_id=5, has_side_effects=True, vmem_limit_bytes=32 * 2**20
        ),
        cost_estimate=cost_of(1),
        name="last_exchange",
    )(rows, more, part, small)


def gather_tensor_kernel(source, out, send_sem, recv_sem, local_sem):
    me = here()
    side, sib = across_y(me), sibling(me)
    greet([side, sib])
    line = Line(send_sem, recv_sem)
    halves = 4
    step = source.shape[0] // halves

    def part(ref, i):
        return ref.at[pl.ds(i * step, step), :]

    local = pltpu.make_async_copy(source, out.at[me[1]], local_sem)
    for i in range(halves):
        line.send(part(source, i), part(out.at[me[1]], i), i, i, side)
        line.send(part(source, i), part(out.at[me[1]], i), 4 + i, 4 + i, sib)
    local.start()
    for i in range(halves):
        got = part(out.at[side[1]], i)
        line.wait(got, i, sib)
        line.send(got, got, 8 + i, 8 + i, sib)
    for i in range(halves):
        line.wait(part(out.at[sib[1]], i), 4 + i, sib)
        line.wait(part(out.at[across_y(sib)[1]], i), 8 + i, sib)
    local.wait()
    line.finish()


def gather_tensor(rows):
    out = pl.pallas_call(
        gather_tensor_kernel,
        out_shape=jax.ShapeDtypeStruct((4,) + rows.shape, rows.dtype),
        in_specs=[IN_VMEM],
        out_specs=ANY,
        scratch_shapes=[DMA((12,)), DMA((12,)), DMA],
        compiler_params=pltpu.CompilerParams(
            collective_id=6, has_side_effects=True, vmem_limit_bytes=8 * 2**20
        ),
        cost_estimate=cost_of(15),
        name="gather_tensor",
    )(rows)
    return out.reshape((-1,) + rows.shape[1:])


def sum_tensor_kernel(part, out, from_sib, from_side, total, send_sem, recv_sem):
    me = here()
    side, sib = across_y(me), sibling(me)
    greet([side, sib])
    line = Line(send_sem, recv_sem)
    pieces = 4
    step = out.shape[0] // pieces

    def rows(ref, i):
        return ref.at[pl.ds(i * step, step), :]

    for j, column in ((0, across_y(sib)[1]), (1, sib[1])):
        for i in range(pieces):
            line.send(
                rows(part.at[column], i), rows(from_sib.at[j], i), 4 * j + i, 4 * j + i, sib
            )
    for i in range(pieces):
        got = rows(from_sib.at[0], i)
        line.wait(got, i, sib)
        sum_rows(rows(total, i), [rows(part.at[side[1]], i), got])
        line.send(rows(total, i), rows(from_side, i), 8 + i, 8 + i, side)
    for i in range(pieces):
        got = rows(from_sib.at[1], i)
        line.wait(got, 4 + i, sib)
        line.wait(rows(from_side, i), 8 + i, sib)
        sum_rows(rows(out, i), [rows(part.at[me[1]], i), got, rows(from_side, i)])
    line.finish()


def sum_tensor(partial):
    block = (partial.shape[0] // 4, partial.shape[1])
    return pl.pallas_call(
        sum_tensor_kernel,
        out_shape=jax.ShapeDtypeStruct(block, jnp.float32),
        in_specs=[IN_VMEM],
        out_specs=IN_VMEM,
        scratch_shapes=[
            pltpu.VMEM((2,) + block, partial.dtype),
            pltpu.VMEM(block, partial.dtype),
            pltpu.VMEM(block, partial.dtype),
            DMA((12,)),
            DMA((12,)),
        ],
        compiler_params=pltpu.CompilerParams(
            collective_id=7, has_side_effects=True, vmem_limit_bytes=12 * 2**20
        ),
        cost_estimate=cost_of(1),
        name="sum_tensor",
    )(partial.reshape((4,) + block))


def rows_at(ref, slot, size, count=1):
    return ref.at[pl.ds(pl.multiple_of(slot * size, size), size * count), :]


class Plan:
    def __init__(self, send_sem, recv_sem):
        self.send_sem, self.recv_sem, self.made = send_sem, recv_sem, []

    def send(self, make):
        make().start()
        self.made.append(make)

    def finish(self):
        for make in self.made:
            make().wait_send()


def gather_plan(ins, outs, sizes, send_sem, recv_sem):
    me = here()
    near, far, sib = flipped(me, NEAR), flipped(me, FAR), sibling(me)
    plan = Plan(send_sem, recv_sem)
    count = len(ins)

    def send(k, role, device, tag, recv_tag):
        for i in range(count):

            def make(i=i):
                block = rows_at(outs[i], slot_of(moved_z(flipped(me, role), k)), sizes[i])
                source = ins[i] if (k, role) == (0, SELF) else block
                return push(source, block, send_sem.at[i, tag], recv_sem.at[i, recv_tag], device)

            plan.send(make)

    def arrive(k, role):
        for i in range(count):
            block = rows_at(outs[i], slot_of(moved_z(flipped(me, role), k)), sizes[i])
            push(block, block, send_sem.at[i, 0], recv_sem.at[i, k * 4 + role], near).wait_recv()

    def forward(k, role):
        if role == SELF:
            send(k, SELF, far, 4 + k, k * 4 + FAR)
            send(k, SELF, near, k, k * 4 + NEAR)
        if role == NEAR:
            send(k, NEAR, far, 8 + k, k * 4 + BOTH_FLIPPED)
        send(k, role, sib, 16 + k * 4 + role, 16 + k * 4 + role)

    def event(k, role):
        arrive(k, role)
        forward(k, role)

    def from_sibling(k, role):
        for i in range(count):
            block = rows_at(outs[i], 0, sizes[i])
            push(
                block, block, send_sem.at[i, 0], recv_sem.at[i, 16 + k * 4 + role], near
            ).wait_recv()

    def begin():
        forward(0, SELF)
        for d in (1, 3, 2):
            send(0, SELF, moved_z(me, d), 11 + d, (4 - d) * 4 + SELF)

    return plan, begin, event, from_sibling


def gate_columns(gates_ref, slot, columns, first):
    lane = lax.broadcasted_iota(jnp.int32, (128, 128), 1)
    for s in range(4):
        block = gates_ref[pl.ds(pl.multiple_of((slot + s) * 16, 16), 16), :]
        turned = jnp.concatenate([block, jnp.zeros((112, 128), jnp.float32)], axis=0).T
        for i in range(2):
            column = jnp.sum(jnp.where(lane == first + i, turned, 0.0), axis=1, keepdims=True)
            columns[i, pl.ds(s * 128, 128), :] = jnp.broadcast_to(column, (128, 128))


def tiles(count, width, body):
    def step(n, carry):
        body(pl.ds(pl.multiple_of(n * width, width), width))
        return carry

    lax.fori_loop(0, count, step, 0)


STAGES = ((0, 0), (0, 1), (1, 0), (1, 1), (3, 0), (3, 1), (2, 0), (2, 1))
BLOCK = 512


def stage_expert(me, j):
    half = j // 2
    k = half + jnp.where(half == 2, 1, 0) - jnp.where(half == 3, 1, 0)
    flips = lax.rem(j, 2)
    expert = me[0]
    return lax.rem(expert + flips * (1 - 2 * lax.rem(expert, 2)) + 2 * k, 8)


def forward_kernel(
    x_own, g_own, w_joined, w_down, x_out, g_out, pre_out, gated_out, y_out,
    x_all, g_all, columns, pre, gated, y, send_sem, recv_sem, local_sem, out_sem,
):
    me = here()
    core = lax.rem(me[1], 2)
    greet(
        [flipped(me, NEAR), flipped(me, FAR), sibling(me)] + [moved_z(me, d) for d in (1, 2, 3)]
    )
    plan, begin, event, from_sibling = gather_plan(
        [x_own, g_own], [x_all, g_all], [128, 16], send_sem, recv_sem
    )
    local = [
        pltpu.make_async_copy(x_own, rows_at(x_all, slot_of(me), 128), local_sem.at[0]),
        pltpu.make_async_copy(g_own, rows_at(g_all, slot_of(me), 16), local_sem.at[1]),
    ]
    begin()
    for copy in local:
        copy.start()
    for copy in local:
        copy.wait()
    before = {
        0: [(1, SELF), (0, NEAR), (0, FAR)],
        1: [(0, BOTH_FLIPPED)],
        3: [(1, BOTH_FLIPPED)],
        5: [(3, BOTH_FLIPPED)],
        7: [(2, BOTH_FLIPPED)],
    }
    middle = {
        0: [(3, SELF), (1, NEAR)],
        1: [(1, FAR)],
        2: [(2, SELF), (3, NEAR)],
        3: [(3, FAR)],
        4: [(2, NEAR)],
        5: [(2, FAR)],
    }
    half = w_joined.shape[1] // 2

    def results(expert, slot):
        return [
            pltpu.make_async_copy(
                rows_at(x_all, expert, BLOCK), rows_at(x_out, expert, BLOCK), out_sem.at[0, slot]
            ),
            pltpu.make_async_copy(pre.at[slot], rows_at(pre_out, expert, BLOCK), out_sem.at[1, slot]),
            pltpu.make_async_copy(
                gated.at[slot], rows_at(gated_out, expert, BLOCK), out_sem.at[2, slot]
            ),
            pltpu.make_async_copy(y.at[slot], rows_at(y_out, expert, BLOCK), out_sem.at[3, slot]),
        ]

    def block(j, carry):
        slot = lax.rem(j, 2)
        expert = stage_expert(me, j)
        for n, (k, flips) in enumerate(STAGES):

            @pl.when(j == n)
            def _():
                for at in before.get(n, []):
                    event(*at)
                if n:
                    from_sibling(k, 2 - core if flips else SELF)
                    from_sibling(k, BOTH_FLIPPED if flips else 1 + core)
                else:
                    from_sibling(k, SELF)
                    from_sibling(k, 1 + core)

        @pl.when(j >= 2)
        def _():
            for copy in results(stage_expert(me, j - 2), slot):
                copy.wait()

        gate_columns(g_all, expert * 4, columns, me[0] * 2)
        x_rows = rows_at(x_all, expert, BLOCK)

        def first(cols):
            pre[slot, :, cols] = jnp.dot(
                x_rows[...], w_joined[:, cols], preferred_element_type=jnp.float32
            )

        tiles(w_joined.shape[1] // 1024, 1024, first)
        for n in middle:

            @pl.when(j == n)
            def _():
                for at in middle[n]:
                    event(*at)

        def act(r):
            for c in range(half // 128):
                cols = slice(c * 128, (c + 1) * 128)
                g = pre[slot, r, cols]
                u = pre[slot, r, half + c * 128 : half + (c + 1) * 128]
                hidden = (g * (1.0 / (1.0 + jnp.exp(-g))) * u).astype(jnp.bfloat16)
                gate = columns[c * 128 * 2 // half, r, :]
                gated[slot, r, cols] = (hidden.astype(jnp.float32) * gate).astype(jnp.bfloat16)

        tiles(BLOCK // 64, 64, act)

        def second(cols):
            y[slot, :, cols] = jnp.dot(
                gated[slot], w_down[:, cols], preferred_element_type=jnp.float32
            ).astype(jnp.bfloat16)

        tiles(w_down.shape[1] // 1024, 1024, second)
        for copy in results(expert, slot):
            copy.start()
        return carry

    lax.fori_loop(0, 8, block, 0)
    for j in (6, 7):
        for copy in results(stage_expert(me, jnp.int32(j)), j % 2):
            copy.wait()
    g_out[...] = g_all[...]
    plan.finish()


def experts_forward(ffn_in, gates_own, w_joined, w_down):
    rows, width = ffn_in.shape[0] * 32, ffn_in.shape[1]
    joined, hidden = w_joined.shape[1], w_down.shape[0]
    bf16, f32, sds = jnp.bfloat16, jnp.float32, jax.ShapeDtypeStruct
    return pl.pallas_call(
        forward_kernel,
        out_shape=[
            sds((rows, width), bf16),
            sds((512, 128), f32),
            sds((rows, joined), f32),
            sds((rows, hidden), bf16),
            sds((rows, width), bf16),
        ],
        in_specs=[IN_VMEM] * 4,
        out_specs=[ANY, IN_VMEM, ANY, ANY, ANY],
        scratch_shapes=[
            pltpu.VMEM((rows, width), bf16),
            pltpu.VMEM((512, 128), f32),
            pltpu.VMEM((2, BLOCK, 128), f32),
            pltpu.VMEM((2, BLOCK, joined), f32),
            pltpu.VMEM((2, BLOCK, hidden), bf16),
            pltpu.VMEM((2, BLOCK, width), bf16),
            DMA((2, 32)),
            DMA((2, 32)),
            DMA((2,)),
            DMA((4, 2)),
        ],
        compiler_params=pltpu.CompilerParams(
            collective_id=1, has_side_effects=True, vmem_limit_bytes=48 * 2**20
        ),
        cost_estimate=cost_of(90),
        name="experts_forward",
    )(ffn_in, gates_own, w_joined, w_down)


def sum_plan(arrays, send_sem, recv_sem, load_sem):
    me = here()
    near, far, sib = flipped(me, NEAR), flipped(me, FAR), sibling(me)
    plan = Plan(send_sem, recv_sem)
    order = (2, 1, 3, 0)

    def send(i, source, target, tag, recv_tag, device):
        plan.send(
            lambda: push(source(), target(), send_sem.at[i, tag], recv_sem.at[i, recv_tag], device())
        )

    def arrive(i, ref, tag):
        push(ref, ref, send_sem.at[i, 0], recv_sem.at[i, tag], near).wait_recv()

    def load(i, k, role):
        part, _, size, mine = arrays[i][:4]
        tag = k * 4 + role
        return pltpu.make_async_copy(
            rows_at(part, slot_of(moved_z(flipped(me, role), k)), size), mine.at[tag], load_sem.at[i, tag]
        )

    def begin():
        for roles in ((BOTH_FLIPPED, FAR), (NEAR, SELF)):
            for k in order:
                for role in roles:
                    for i, (part, _, size, _, from_sib, _, _, _) in enumerate(arrays):
                        tag = k * 4 + role
                        send(
                            i,
                            lambda part=part, size=size, k=k, role=role: rows_at(
                                part, slot_of(moved_z(flipped(sib, role), k)), size
                            ),
                            lambda from_sib=from_sib, tag=tag: from_sib.at[tag],
                            tag,
                            tag,
                            lambda: sib,
                        )
                        load(i, k, role).start()

    def collect(i, k, role):
        tag = k * 4 + role
        load(i, k, role).wait()
        from_sib = arrays[i][4]
        arrive(i, from_sib.at[tag], tag)
        return [arrays[i][3].at[tag], from_sib.at[tag]]

    def first(k, role):
        for i, (_, _, _, mine, _, from_far, _, _) in enumerate(arrays):
            tag, at = k * 4 + role, k * 2 + (role == BOTH_FLIPPED)
            terms = collect(i, k, role)
            sum_rows(mine.at[tag], terms)
            send(
                i,
                lambda mine=mine, tag=tag: mine.at[tag],
                lambda from_far=from_far, at=at: from_far.at[at],
                16 + at,
                16 + at,
                lambda: far,
            )

    def second(k):
        for i, (_, _, _, mine, _, from_far, from_near, _) in enumerate(arrays):
            tag = k * 4 + NEAR
            terms = collect(i, k, NEAR)
            arrive(i, from_far.at[k * 2 + 1], 16 + k * 2 + 1)
            sum_rows(mine.at[tag], terms + [from_far.at[k * 2 + 1]])
            send(
                i,
                lambda mine=mine, tag=tag: mine.at[tag],
                lambda from_near=from_near, k=k: from_near.at[k],
                24 + k,
                24 + k,
                lambda: near,
            )

    def third(k):
        for i, (_, out, _, mine, _, from_far, from_near, from_z) in enumerate(arrays):
            tag = k * 4 + SELF
            terms = collect(i, k, SELF)
            arrive(i, from_far.at[k * 2], 16 + k * 2)
            arrive(i, from_near.at[k], 24 + k)
            terms = terms + [from_far.at[k * 2], from_near.at[k]]
            if k > 0:
                sum_rows(mine.at[tag], terms)
                send(
                    i,
                    lambda mine=mine, tag=tag: mine.at[tag],
                    lambda from_z=from_z, k=k: from_z.at[3 - k],
                    27 + k,
                    31 - k,
                    lambda k=k: moved_z(me, k),
                )
            else:
                for d in range(3):
                    arrive(i, from_z.at[d], 28 + d)
                    terms.append(from_z.at[d])
                sum_rows(out, terms)

    return plan, begin, first, second, third


def sum_scratch(size, width, dtype):
    return [pltpu.VMEM((n, size, width), dtype) for n in (16, 16, 8, 4, 3)]


SUM_BEFORE = {0: [(2, 3), (2, 2), (1, 3), (1, 2)], 3: [(2, "third")], 5: [(1, "third")]}
SUM_MIDDLE = {
    0: [(3, 3), (3, 2), (0, 3), (0, 2)],
    1: [(2, "second")],
    2: [(1, "second")],
    4: [(3, "second")],
    6: [(0, "second")],
}


def sum_events(table, j, first, second, third):
    for n, events in table.items():

        @pl.when(j == n)
        def _():
            for k, what in events:
                if what == "second":
                    second(k)
                elif what == "third":
                    third(k)
                else:
                    first(k, what)


def greet_all(me):
    greet(
        [flipped(me, NEAR), flipped(me, FAR), sibling(me)] + [moved_z(me, d) for d in (1, 2, 3)]
    )


def backward_kernel(
    y_part, grads, pre_all, gates, w_joined, w_down, mix_out, dpre_out, drow_out, gate_grads,
    mine, from_sib, from_far, from_near, from_z, dz, pre, raw, columns, products, dpre, drow,
    send_sem, recv_sem, load_sem, in_sem, out_sem,
):
    me = here()
    greet_all(me)
    plan, begin, first, second, third = sum_plan(
        [(y_part, mix_out, 128, mine, from_sib, from_far, from_near, from_z)],
        send_sem, recv_sem, load_sem,
    )
    half = w_joined.shape[1] // 2
    expert_lanes = half // 2

    def loads(block, slot):
        return [
            pltpu.make_async_copy(rows_at(grads, block, BLOCK), dz.at[slot], in_sem.at[0, slot]),
            pltpu.make_async_copy(rows_at(pre_all, block, BLOCK), pre.at[slot], in_sem.at[1, slot]),
        ]

    def results(block, slot):
        return [
            pltpu.make_async_copy(dpre.at[slot], rows_at(dpre_out, block, BLOCK), out_sem.at[0, slot]),
            pltpu.make_async_copy(drow.at[slot], rows_at(drow_out, block, BLOCK), out_sem.at[1, slot]),
        ]

    for copy in loads(0, 0):
        copy.start()
    begin()

    def step(j, carry):
        slot = lax.rem(j, 2)

        @pl.when(j < 7)
        def _():
            for copy in loads(j + 1, 1 - slot):
                copy.start()

        sum_events(SUM_BEFORE, j, first, second, third)
        for copy in loads(j, slot):
            copy.wait()

        @pl.when(j >= 2)
        def _():
            for copy in results(j - 2, slot):
                copy.wait()

        gate_columns(gates, j * 4, columns, me[0] * 2)
        raw[...] = lax.dot_general(
            dz[slot], w_down[...], (((1,), (1,)), ((), ())), preferred_element_type=jnp.float32
        )
        sum_events(SUM_MIDDLE, j, first, second, third)

        def act(r):
            for i in range(2):
                product = None
                for c in range(i * expert_lanes, (i + 1) * expert_lanes, 128):
                    g = pre[slot, r, c : c + 128]
                    u = pre[slot, r, half + c : half + c + 128]
                    t = raw[r, c : c + 128]
                    sig = 1.0 / (1.0 + jnp.exp(-g))
                    silu = g * sig
                    hidden = (silu * u).astype(jnp.bfloat16).astype(jnp.float32)
                    term = hidden * t
                    product = term if product is None else product + term
                    dh = t * columns[i, r, :]
                    dpre[slot, r, c : c + 128] = (
                        dh * u * sig * (1.0 + g * (1.0 - sig))
                    ).astype(jnp.bfloat16)
                    dpre[slot, r, half + c : half + c + 128] = (dh * silu).astype(jnp.bfloat16)
                products[i, r, :] = product

        tiles(BLOCK // 64, 64, act)
        place = lax.broadcasted_iota(jnp.int32, (16, 128), 0)
        for s in range(4):
            sums = jnp.zeros((16, 128), jnp.float32)
            for i in range(2):
                turned = products[i, pl.ds(s * 128, 128), :].T
                row = jnp.sum(turned, axis=0, keepdims=True)
                sums = jnp.where(place == me[0] * 2 + i, jnp.broadcast_to(row, (16, 128)), sums)
            gate_grads[pl.ds(pl.multiple_of((j * 4 + s) * 16, 16), 16), :] = sums

        def back(rows):
            drow[slot, :, rows] = lax.dot_general(
                dpre[slot],
                w_joined[rows, :],
                (((1,), (1,)), ((), ())),
                preferred_element_type=jnp.float32,
            ).astype(jnp.bfloat16)

        tiles(w_joined.shape[0] // 1024, 1024, back)
        for copy in results(j, slot):
            copy.start()
        return carry

    lax.fori_loop(0, 8, step, 0)
    third(3)
    third(0)
    for j in (6, 7):
        for copy in results(j, j % 2):
            copy.wait()
    plan.finish()


def experts_backward(y_part, grads, pre, gates, w_joined, w_down):
    rows, width = grads.shape
    joined, hidden = w_joined.shape[1], w_down.shape[0]
    bf16, f32, sds = jnp.bfloat16, jnp.float32, jax.ShapeDtypeStruct
    return pl.pallas_call(
        backward_kernel,
        out_shape=[
            sds((rows // 32, width), f32),
            sds((rows, joined), bf16),
            sds((rows, width), bf16),
            sds((512, 128), f32),
        ],
        in_specs=[ANY, ANY, ANY] + [IN_VMEM] * 3,
        out_specs=[IN_VMEM, ANY, ANY, IN_VMEM],
        scratch_shapes=sum_scratch(rows // 32, width, bf16)
        + [
            pltpu.VMEM((2, BLOCK, width), bf16),
            pltpu.VMEM((2, BLOCK, joined), f32),
            pltpu.VMEM((BLOCK, hidden), f32),
            pltpu.VMEM((2, BLOCK, 128), f32),
            pltpu.VMEM((2, BLOCK, 128), f32),
            pltpu.VMEM((2, BLOCK, joined), bf16),
            pltpu.VMEM((2, BLOCK, width), bf16),
            DMA((1, 32)),
            DMA((1, 32)),
            DMA((1, 16)),
            DMA((2, 2)),
            DMA((2, 2)),
        ],
        compiler_params=pltpu.CompilerParams(
            collective_id=2, has_side_effects=True, vmem_limit_bytes=56 * 2**20
        ),
        cost_estimate=cost_of(90),
        name="experts_backward",
    )(y_part, grads, pre, gates, w_joined, w_down)


def weights_kernel(
    drow, gate_grads, x_all, grads, dpre_all, gated_all, row_out, gate_out, d_gate, d_up, d_down,
    mine, from_sib, from_far, from_near, from_z, mine_g, sib_g, far_g, near_g, z_g,
    dpre, gated, tile, wide, send_sem, recv_sem, load_sem, in_sem, tile_sem, out_sem,
):
    me = here()
    greet_all(me)
    plan, begin, first, second, third = sum_plan(
        [
            (drow, row_out, 128, mine, from_sib, from_far, from_near, from_z),
            (gate_grads, gate_out, 16, mine_g, sib_g, far_g, near_g, z_g),
        ],
        send_sem, recv_sem, load_sem,
    )
    span = tile.shape[2]
    steps = x_all.shape[1] // span
    hidden = d_gate.shape[2]
    begin()
    held = [
        pltpu.make_async_copy(dpre_all, dpre, in_sem.at[0]),
        pltpu.make_async_copy(gated_all, gated, in_sem.at[1]),
    ]

    def columns_of(j):
        return pl.ds(pl.multiple_of(lax.rem(j, steps) * span, span), span)

    def fetch(j, slot, act):
        @pl.when(j < steps)
        def _():
            act(pltpu.make_async_copy(x_all.at[:, columns_of(j)], tile.at[slot], tile_sem.at[slot]))

        @pl.when((j >= steps) & (j < 2 * steps))
        def _():
            act(pltpu.make_async_copy(grads.at[:, columns_of(j)], tile.at[slot], tile_sem.at[slot]))

    def results(j, slot, act):
        cols = columns_of(j)

        @pl.when(j < steps)
        def _():
            for i in range(2):
                act(
                    pltpu.make_async_copy(
                        wide.at[slot, :, pl.ds(i * hidden, hidden)], d_gate.at[i, cols, :], out_sem.at[slot, i]
                    )
                )
                act(
                    pltpu.make_async_copy(
                        wide.at[slot, :, pl.ds((2 + i) * hidden, hidden)],
                        d_up.at[i, cols, :],
                        out_sem.at[slot, 2 + i],
                    )
                )

        @pl.when(j >= steps)
        def _():
            act(
                pltpu.make_async_copy(
                    wide.at[slot, :, pl.ds(0, span)], d_down.at[:, cols], out_sem.at[slot, 0]
                )
            )

    fetch(jnp.int32(0), 0, lambda copy: copy.start())
    for copy in held:
        copy.start()

    def step(j, carry):
        slot = lax.rem(j, 2)
        fetch(j + 1, 1 - slot, lambda copy: copy.start())
        sum_events(SUM_BEFORE, j, first, second, third)

        @pl.when(j == 0)
        def _():
            for copy in held:
                copy.wait()

        fetch(j, slot, lambda copy: copy.wait())

        @pl.when(j >= 2)
        def _():
            results(j - 2, slot, lambda copy: copy.wait())

        @pl.when(j < steps)
        def _():
            wide[slot] = lax.dot_general(
                tile[slot], dpre[...], (((0,), (0,)), ((), ())), preferred_element_type=jnp.float32
            )

        @pl.when(j >= steps)
        def _():
            wide[slot, :, 0:span] = lax.dot_general(
                gated[...], tile[slot], (((0,), (0,)), ((), ())), preferred_element_type=jnp.float32
            )

        results(j, slot, lambda copy: copy.start())
        sum_events(SUM_MIDDLE, j, first, second, third)
        return carry

    lax.fori_loop(0, 2 * steps, step, 0)
    third(3)
    third(0)
    for j in (2 * steps - 2, 2 * steps - 1):
        results(jnp.int32(j), j % 2, lambda copy: copy.wait())
    plan.finish()


def experts_weights(drow, gate_grads, x_all, grads, dpre, gated):
    rows, width = grads.shape
    joined, hidden = dpre.shape[1], gated.shape[1]
    span = width // 4
    bf16, f32, sds = jnp.bfloat16, jnp.float32, jax.ShapeDtypeStruct
    return pl.pallas_call(
        weights_kernel,
        out_shape=[
            sds((rows // 32, width), f32),
            sds((16, 128), f32),
            sds((2, width, joined // 4), f32),
            sds((2, width, joined // 4), f32),
            sds((hidden, width), f32),
        ],
        in_specs=[ANY] * 6,
        out_specs=[IN_VMEM, IN_VMEM, ANY, ANY, ANY],
        scratch_shapes=sum_scratch(rows // 32, width, bf16)
        + sum_scratch(16, 128, f32)
        + [
            pltpu.VMEM((rows, joined), bf16),
            pltpu.VMEM((rows, hidden), bf16),
            pltpu.VMEM((2, rows, span), bf16),
            pltpu.VMEM((2, span, joined), f32),
            DMA((2, 32)),
            DMA((2, 32)),
            DMA((2, 16)),
            DMA((2,)),
            DMA((2,)),
            DMA((2, 4)),
        ],
        compiler_params=pltpu.CompilerParams(
            collective_id=3, has_side_effects=True, vmem_limit_bytes=58 * 2**20
        ),
        cost_estimate=cost_of(90),
        name="experts_weights",
    )(drow, gate_grads, x_all, grads, dpre, gated)


def rotated(values, cosines, sines):
    return values * cosines + pltpu.roll(values, HEAD_DIM // 2, 1) * sines


def turned_back(values, cosines, sines):
    return values * cosines - pltpu.roll(values, HEAD_DIM // 2, 1) * sines


def mask_scores(spans_col, places_row, bias):
    place = places_row[0:1, :]

    def body(r):
        allowed = (place >= spans_col[r, 0:1]) & (place <= spans_col[r, 1:2])
        bias[r, :] = jnp.where(allowed, 0.0, -1e30)

    tiles(bias.shape[0] // 128, 128, body)


def attend_kernel(
    qkv, invs, gains, cosines, sines, spans, places, w_out,
    q_out, k_out, v_out, attended, lse, branch, bias,
):
    rows, local = q_out.shape
    mask_scores(spans, places, bias)

    def prepare(r):
        v_out[r, :] = qkv[r, 2 * local : 3 * local].astype(jnp.bfloat16)
        for h in range(local // HEAD_DIM):
            c = slice(h * HEAD_DIM, (h + 1) * HEAD_DIM)
            for i, target in ((0, q_out), (1, k_out)):
                normed = qkv[r, i * local + h * HEAD_DIM : i * local + (h + 1) * HEAD_DIM]
                normed = normed * invs[r, i : i + 1] * gains[i : i + 1, c]
                target[r, c] = rotated(normed, cosines[r, :], sines[r, :]).astype(jnp.bfloat16)

    tiles(rows // 128, 128, prepare)
    scale = 1.0 / math.sqrt(HEAD_DIM)
    for h in range(local // HEAD_DIM):
        c = slice(h * HEAD_DIM, (h + 1) * HEAD_DIM)

        def one(r, h=h, c=c):
            scores = dot32(q_out[r, c], k_out[:, c], NT) * scale + bias[r, :]
            top = jnp.max(scores, axis=-1, keepdims=True)
            total = top + jnp.log(jnp.sum(jnp.exp(scores - top), axis=-1, keepdims=True))
            lse[h, r, :] = total
            probs = jnp.exp(scores - total).astype(jnp.bfloat16)
            attended[r, c] = dot32(probs, v_out[:, c], NN).astype(jnp.bfloat16)

        tiles(rows // 128, 128, one)
    for e in range(w_out.shape[0]):
        span = w_out.shape[2]
        branch[:, e * span : (e + 1) * span] = dot32(attended[...], w_out[e], NN).astype(
            jnp.bfloat16
        )


def attend(qkv, invs, gains, cosines, sines, spans, places, w_out):
    rows, local = qkv.shape[0], qkv.shape[1] // 3
    bf16, f32, sds = jnp.bfloat16, jnp.float32, jax.ShapeDtypeStruct
    return pl.pallas_call(
        attend_kernel,
        out_shape=[sds((rows, local), bf16)] * 4
        + [
            sds((local // HEAD_DIM, rows, 1), f32),
            sds((rows, w_out.shape[0] * w_out.shape[2]), bf16),
        ],
        in_specs=[IN_VMEM] * 8,
        out_specs=[IN_VMEM] * 6,
        scratch_shapes=[pltpu.VMEM((rows, rows), f32)],
        compiler_params=pltpu.CompilerParams(vmem_limit_bytes=32 * 2**20),
        cost_estimate=cost_of(15),
        name="attend",
    )(qkv, invs, gains, cosines, sines, spans, places, w_out)


def attend_back_kernel(
    grad, w_out_far, q_far, k_far, v_far, lse, qkv_far, invs, gains, cosines, sines, spans, places,
    hat_grads, value_grad, dots, d_gains, bias, out_grad, probs_low, score_grad,
    w_out, q, k, v, qkv, sems,
):
    rows, local = q.shape
    fetched = [
        pltpu.make_async_copy(far, close, sems.at[i])
        for i, (far, close) in enumerate(
            ((w_out_far, w_out), (q_far, q), (k_far, k), (v_far, v), (qkv_far, qkv))
        )
    ]
    for copy in fetched:
        copy.start()
    mask_scores(spans, places, bias)
    span = w_out.shape[2]
    fetched[0].wait()

    def project(r):
        total = None
        for e in range(w_out.shape[0]):
            term = dot32(grad[r, e * span : (e + 1) * span], w_out[e], NT)
            total = term if total is None else total + term
        out_grad[r, :] = total.astype(jnp.bfloat16)

    tiles(rows // 128, 128, project)
    for copy in fetched[1:]:
        copy.wait()
    scale = 1.0 / math.sqrt(HEAD_DIM)
    dots[...] = jnp.zeros_like(dots)
    for h in range(local // HEAD_DIM):
        c = slice(h * HEAD_DIM, (h + 1) * HEAD_DIM)

        def one(r, h=h, c=c):
            scores = dot32(q[r, c], k[:, c], NT) * scale + bias[r, :]
            probs = jnp.exp(scores - lse[h, r, :])
            prob_grad = dot32(out_grad[r, c], v[:, c], NT)
            delta = jnp.sum(probs * prob_grad, axis=-1, keepdims=True)
            probs_low[r, :] = probs.astype(jnp.bfloat16)
            score_grad[r, :] = (probs * (prob_grad - delta) * scale).astype(jnp.bfloat16)

        tiles(rows // 128, 128, one)
        value_grad[:, c] = dot32(probs_low[...], out_grad[:, c], TN).astype(jnp.bfloat16)
        for i, turned in (
            (0, dot32(score_grad[...], k[:, c], NN)),
            (1, dot32(score_grad[...], q[:, c], TN)),
        ):
            at = slice(i * local + h * HEAD_DIM, i * local + (h + 1) * HEAD_DIM)
            norm_grad = turned_back(turned, cosines[...], sines[...])
            hat = qkv[:, at] * invs[:, i : i + 1]
            hat_grad = norm_grad * gains[i : i + 1, c]
            hat_grads[:, at] = hat_grad
            d_gains[i : i + 1, c] = jnp.sum(norm_grad * hat, axis=0, keepdims=True)
            dots[i] += jnp.sum(hat_grad * hat, axis=-1, keepdims=True)


def attend_back(grad, w_out, q, k, v, lse, qkv, invs, gains, cosines, sines, spans, places):
    rows, local = q.shape
    bf16, f32, sds = jnp.bfloat16, jnp.float32, jax.ShapeDtypeStruct
    return pl.pallas_call(
        attend_back_kernel,
        out_shape=[
            sds((rows, 2 * local), f32),
            sds((rows, local), bf16),
            sds((2, rows, 1), f32),
            sds((2, local), f32),
        ],
        in_specs=[IN_VMEM] + [ANY] * 4 + [IN_VMEM, ANY] + [IN_VMEM] * 6,
        out_specs=[IN_VMEM] * 4,
        scratch_shapes=[
            pltpu.VMEM((rows, rows), f32),
            pltpu.VMEM((rows, local), bf16),
            pltpu.VMEM((rows, rows), bf16),
            pltpu.VMEM((rows, rows), bf16),
        ]
        + [pltpu.VMEM(a.shape, a.dtype) for a in (w_out, q, k, v, qkv)]
        + [DMA((5,))],
        compiler_params=pltpu.CompilerParams(vmem_limit_bytes=40 * 2**20),
        cost_estimate=cost_of(5),
        name="attend_back",
    )(grad, w_out, q, k, v, lse, qkv, invs, gains, cosines, sines, spans, places)


def sum_few_kernel(part, out, shares, send_sem, recv_sem):
    me = here()
    peers = [across_y(sibling(me)), across_y(me), sibling(me)]
    greet(peers)
    line = Line(send_sem, recv_sem)
    for i, peer in enumerate(peers):
        line.send(part, shares.at[me[1]], i, i, peer)
    shares[me[1]] = part[...]
    for i, peer in enumerate(peers):
        line.wait(shares.at[peer[1]], i, peer)
    out[...] = (shares[0] + shares[1]) + (shares[2] + shares[3])
    line.finish()


def sum_few(rows):
    block = (rows.size // 128, 128)
    return pl.pallas_call(
        sum_few_kernel,
        out_shape=jax.ShapeDtypeStruct(block, jnp.float32),
        in_specs=[IN_VMEM],
        out_specs=IN_VMEM,
        scratch_shapes=[pltpu.VMEM((4,) + block, jnp.float32), DMA((3,)), DMA((3,))],
        compiler_params=pltpu.CompilerParams(
            collective_id=8, has_side_effects=True, vmem_limit_bytes=2**20
        ),
        cost_estimate=cost_of(1),
        name="sum_few",
    )(rows.reshape(block)).reshape(rows.shape)


BOTH = (EXPERT, TENSOR)


def dot32(left, right, dims):
    return lax.dot_general(left, right, (dims, ((), ())), preferred_element_type=jnp.float32)


NN = ((1,), (0,))
NT = ((1,), (1,))
TN = ((0,), (0,))


def rms_inv(values):
    return lax.rsqrt(jnp.mean(values * values, axis=-1, keepdims=True) + NORM_EPS)


def dense_body(
    tokens,
    attn_gain,
    w_query,
    w_key,
    w_value,
    w_out,
    query_gain,
    key_gain,
    ffn_gain,
    w_router,
    w_gate,
    w_up,
    w_down,
    doc_ids,
    routes,
    deal,
    out_grad,
):
    rows, width = tokens.shape
    parts = lax.axis_size(TENSOR)
    blocks = lax.axis_size(EXPERT)
    column = lax.axis_index(TENSOR)
    block = lax.axis_index(EXPERT)
    own = rows // parts
    share = rows // blocks
    piece = share // parts
    bf16, f32 = jnp.bfloat16, jnp.float32

    def reorder(per_place):
        grid = per_place.reshape((blocks, parts, piece) + per_place.shape[1:])
        return jnp.swapaxes(grid, 0, 1).reshape(per_place.shape)

    local_width = w_query.shape[1]
    head_count = local_width // HEAD_DIM
    expert_count = w_router.shape[1]
    qkv_own = jnp.concatenate([w_query, w_key, w_value], axis=1)
    gain_stack = jnp.stack([attn_gain, query_gain, key_gain, ffn_gain], axis=1)
    small_own = jnp.concatenate([w_router, gain_stack], axis=1)
    small_own = jnp.pad(small_own, ((0, 0), (0, 128 - small_own.shape[1])))
    deal_grid = deal.reshape(blocks, blocks, parts, piece)
    picks = lax.dynamic_slice(deal_grid, (0, block, column, 0), (blocks, 1, 1, piece)).reshape(-1)
    picks = picks - block * rows
    inputs, dealt_grads, qkv_full, out_full, small_full = start_exchange(
        tokens[picks].reshape(blocks, piece, width),
        out_grad[picks].reshape(blocks, piece, width),
        qkv_own,
        w_out,
        small_own,
    )
    own_low = lax.dynamic_slice_in_dim(inputs, column, 1, 0).reshape(own, width)
    inputs = inputs.reshape(rows, width).astype(f32)
    qkv_full = qkv_full.reshape(width, -1)
    small_full = small_full.reshape(width, -1)
    router_full = small_full[:, :expert_count]
    gain_full = small_full[:, expert_count : expert_count + 4].T.astype(f32)
    gain_attn, gain_ffn = gain_full[0], gain_full[3]
    gain_query = lax.dynamic_slice_in_dim(gain_full[1], column * local_width, local_width)
    gain_key = lax.dynamic_slice_in_dim(gain_full[2], column * local_width, local_width)
    own_grad_low = dealt_grads.reshape(own, width)
    grads_all = lax.all_gather(own_grad_low, BOTH, axis=0, tiled=True)
    own_in = own_low.astype(f32)
    own_grad = own_grad_low.astype(f32)

    scale = 1.0 / math.sqrt(HEAD_DIM)
    normed = (inputs * rms_inv(inputs) * gain_attn).astype(bf16)
    qkv = dot32(normed, qkv_full, NN)
    query_pre = qkv[:, :local_width]
    key_pre = qkv[:, local_width : 2 * local_width]
    squares = sum_few(
        jnp.stack([jnp.sum(query_pre * query_pre, axis=-1), jnp.sum(key_pre * key_pre, axis=-1)])
    )
    cosines, sines, starts = rope_tables(doc_ids, HEAD_DIM)
    cosines = reorder(jnp.concatenate([cosines, cosines], axis=1))
    sines = reorder(jnp.concatenate([-sines, sines], axis=1))
    positions = reorder(jnp.arange(rows, dtype=jnp.int32))
    spans = jnp.stack([reorder(starts), positions], axis=1)
    places = jnp.broadcast_to(positions[None], (8, rows))
    invs = lax.rsqrt(squares / width + NORM_EPS).T
    gains = jnp.stack([gain_query, gain_key])
    query_rot, key_rot, value_rows, attended, log_total, branch = attend(
        qkv, invs, gains, cosines, sines, spans, places, out_full
    )
    branch_own = sum_tensor(branch)

    residual = own_in + branch_own
    resid_inv = rms_inv(residual)
    resid_hat = residual * resid_inv
    ffn_in = (resid_hat * gain_ffn).astype(bf16)
    logits = dot32(ffn_in, router_full, NN)
    router_probs = jax.nn.softmax(logits, axis=-1)
    local_experts = w_gate.shape[0]
    own_routes = lax.dynamic_slice(
        routes.reshape(blocks, parts, piece, -1),
        (0, column, 0, 0),
        (blocks, 1, piece, routes.shape[1]),
    ).reshape(own, -1)
    expert_ids = jnp.arange(expert_count, dtype=jnp.int32)
    routed = jnp.any(own_routes[:, :, None] == expert_ids[None, None, :], axis=1)
    gates_own = jnp.where(routed, router_probs, 0.0)

    hidden_width = w_gate.shape[2]
    joined_weight = jnp.concatenate(
        [w_gate[i] for i in range(local_experts)] + [w_up[i] for i in range(local_experts)], axis=1
    )
    down_weight = w_down.reshape(local_experts * hidden_width, width)
    rows_all, gates_all, pre_all, gated_all, mixed = experts_forward(
        ffn_in, gates_own.T, joined_weight, down_weight
    )
    mix_own, joined_grad, row_terms, gate_grads = experts_backward(
        mixed, grads_all, pre_all, gates_all, joined_weight, down_weight
    )
    output_own = (residual + mix_own).astype(bf16)
    row_own, gate_grad_own, d_w_gate, d_w_up, d_w_down = experts_weights(
        row_terms, gate_grads, rows_all, grads_all, joined_grad, gated_all
    )
    gate_grad_own = gate_grad_own.T
    d_w_down = d_w_down.reshape(w_down.shape)

    prob_grad = jnp.where(routed, gate_grad_own, 0.0)
    logit_grad = (
        router_probs * (prob_grad - jnp.sum(router_probs * prob_grad, axis=-1, keepdims=True))
    ).astype(bf16)
    d_router = dot32(ffn_in, logit_grad, TN)
    ffn_grad = row_own + dot32(logit_grad, router_full, NT)
    d_ffn_gain = jnp.sum(ffn_grad * resid_hat, axis=0)
    scaled_ffn = ffn_grad * gain_ffn
    resid_grad = own_grad + resid_inv * (
        scaled_ffn - resid_hat * jnp.mean(scaled_ffn * resid_hat, axis=-1, keepdims=True)
    )
    branch_grad = gather_tensor(resid_grad.astype(bf16))

    branch_cols = branch_grad.reshape(rows, blocks, width // blocks)
    d_wo = jnp.einsum("rk,red->ekd", attended, branch_cols, preferred_element_type=f32).astype(bf16)
    d_wo, branch_grad = lax.optimization_barrier((d_wo, branch_grad))
    sum_wo = lax.psum_scatter(d_wo, EXPERT, scatter_dimension=0, tiled=False)
    hat_grads, value_grad, dots, d_gains = attend_back(
        branch_grad, out_full, query_rot, key_rot, value_rows, log_total,
        qkv, invs, gains, cosines, sines, spans, places,
    )
    d_query_gain, d_key_gain = d_gains[0], d_gains[1]
    dots = sum_few(dots.reshape(2, rows)) / width

    def norm_back(i):
        part = slice(i * local_width, (i + 1) * local_width)
        inv = invs[:, i : i + 1]
        return (inv * (hat_grads[:, part] - qkv[:, part] * inv * dots[i][:, None])).astype(bf16)

    query_grad, key_grad = norm_back(0), norm_back(1)
    qkv_grad = jnp.concatenate([query_grad, key_grad, value_grad], axis=1)
    input_terms = dot32(qkv_grad, qkv_full, NT).astype(bf16)
    normed_grad = sum_tensor(input_terms)
    d_qkv = dot32(normed, qkv_grad, TN).astype(bf16)
    d_qkv, sum_wo = lax.optimization_barrier((d_qkv, sum_wo))

    own_inv = rms_inv(own_in)
    own_hat = own_in * own_inv
    d_attn_gain = jnp.sum(normed_grad * own_hat, axis=0)
    scaled_attn = normed_grad * gain_attn
    input_grad = resid_grad + own_inv * (
        scaled_attn - own_hat * jnp.mean(scaled_attn * own_hat, axis=-1, keepdims=True)
    )

    def widen(slots):
        return lax.dynamic_update_slice_in_dim(
            jnp.zeros((width,), f32), slots, column * local_width, 0
        )

    small = jnp.concatenate(
        [
            d_router.T,
            jnp.stack([d_attn_gain, widen(d_query_gain), widen(d_key_gain), d_ffn_gain]),
        ]
    )
    small = jnp.pad(small, ((0, 24 - small.shape[0]), (0, 0)))
    small = jnp.swapaxes(small.reshape(24, blocks, -1), 0, 1)

    back_out, back_in, sum_qkv, small = last_exchange(
        output_own.reshape(blocks, piece, width),
        input_grad.astype(bf16).reshape(blocks, piece, width),
        d_qkv.reshape(blocks, -1, d_qkv.shape[1]),
        small,
    )
    sum_router = small[:expert_count].T
    sum_gains = small[expert_count:]
    came = lax.dynamic_slice(deal_grid, (0, block, 0, 0), (blocks, 1, parts, piece))
    came = jnp.swapaxes(came.reshape(blocks, parts, piece), 0, 1).reshape(-1) - block * rows
    chooser = (jnp.arange(rows, dtype=jnp.int32)[:, None] == came[None, :]).astype(bf16)
    output = dot32(chooser, back_out.reshape(rows, width), NN).astype(bf16)
    d_tokens = dot32(chooser, back_in.reshape(rows, width), NN).astype(bf16)
    return (
        output,
        d_tokens,
        sum_gains[0],
        sum_qkv[:, :local_width],
        sum_qkv[:, local_width : 2 * local_width],
        sum_qkv[:, 2 * local_width :],
        sum_wo.astype(f32),
        sum_gains[1],
        sum_gains[2],
        sum_gains[3],
        sum_router,
        d_w_gate,
        d_w_up,
        d_w_down,
    )


def pick_body(*args):
    routes, experts = args[14], args[9].shape[1]
    mesh_fits = (lax.axis_size(EXPERT), lax.axis_size(TENSOR)) == (8, 4)
    body = dense_body if mesh_fits and experts <= 2 * routes.shape[1] else routed_body
    return body(*args)


def solution(mesh):
    in_specs = (
        P(EXPERT, None),
        P(EXPERT),
        P(EXPERT, TENSOR),
        P(EXPERT, TENSOR),
        P(EXPERT, TENSOR),
        P(TENSOR, EXPERT),
        P(EXPERT),
        P(EXPERT),
        P(EXPERT),
        P(EXPERT, None),
        P(EXPERT, None, TENSOR),
        P(EXPERT, None, TENSOR),
        P(EXPERT, TENSOR, None),
        P(EXPERT),
        P(EXPERT, None),
        P(),
        P(EXPERT, None),
    )
    out_specs = (
        P(EXPERT, None),
        P(EXPERT, None),
        P(EXPERT),
        P(EXPERT, TENSOR),
        P(EXPERT, TENSOR),
        P(EXPERT, TENSOR),
        P(TENSOR, EXPERT),
        P(EXPERT),
        P(EXPERT),
        P(EXPERT),
        P(EXPERT, None),
        P(EXPERT, None, TENSOR),
        P(EXPERT, None, TENSOR),
        P(EXPERT, TENSOR, None),
    )
    return jax.shard_map(pick_body, mesh=mesh, in_specs=in_specs, out_specs=out_specs, check_vma=False)
```

```python
import functools
import math

import jax
import jax.numpy as jnp
from jax import lax
from jax.experimental import pallas as pl
from jax.experimental.pallas import tpu as pltpu
from jax.sharding import PartitionSpec as P

HEAD_DIM = 128
EXPERT, TENSOR = "expert", "tensor"


NORM_EPS = 1e-05
ROPE_BASE = 10000.0


def rope_tables(documents, head_size):
    row_count = documents.shape[0]
    positions = jnp.arange(row_count, dtype=jnp.int32)
    new_doc = jnp.concatenate(
        [jnp.ones((1,), jnp.int32), (documents[1:] != documents[:-1]).astype(jnp.int32)]
    )
    starts = lax.cummax(jnp.where(new_doc > 0, positions, 0), axis=0)
    places = (positions - starts).astype(jnp.float32)
    half_dim = head_size // 2
    frequency = jnp.exp(
        jnp.arange(half_dim, dtype=jnp.float32) * (-2.0 * math.log(ROPE_BASE) / head_size)
    )
    angles = places[:, None] * frequency[None, :]
    return (jnp.cos(angles), jnp.sin(angles), starts)


def rotate(values, cosines, sines):
    half_dim = values.shape[-1] // 2
    first_half = values[..., :half_dim]
    second_half = values[..., half_dim:]
    cos_rows = cosines[:, None, :]
    sin_rows = sines[:, None, :]
    return jnp.concatenate(
        [
            first_half * cos_rows - second_half * sin_rows,
            second_half * cos_rows + first_half * sin_rows,
        ],
        axis=-1,
    )


def unrotate(grads_in, cosines, sines):
    half_dim = grads_in.shape[-1] // 2
    first_half = grads_in[..., :half_dim]
    second_half = grads_in[..., half_dim:]
    cos_rows = cosines[:, None, :]
    sin_rows = sines[:, None, :]
    return jnp.concatenate(
        [
            first_half * cos_rows + second_half * sin_rows,
            second_half * cos_rows - first_half * sin_rows,
        ],
        axis=-1,
    )


def to_experts(rows):
    return lax.all_to_all(rows, EXPERT, split_axis=0, concat_axis=0, tiled=True)


def from_experts(rows):
    return lax.all_to_all(rows, EXPERT, split_axis=0, concat_axis=0, tiled=True)


def hidden_sums(terms):
    return lax.psum_scatter(terms, TENSOR, scatter_dimension=3, tiled=True)


def routed_body(
    tokens,
    attn_gain,
    w_query,
    w_key,
    w_value,
    w_out,
    query_gain,
    key_gain,
    ffn_gain,
    w_router,
    w_gate,
    w_up,
    w_down,
    doc_ids,
    routes,
    deal,
    out_grad,
):
    row_count, width = tokens.shape
    tensor_parts = lax.axis_size(TENSOR)
    expert_parts = lax.axis_size(EXPERT)
    column = lax.axis_index(TENSOR)
    device_idx = lax.axis_index(EXPERT)
    quarter = width // tensor_parts
    share_rows = row_count // expert_parts
    deal_rows = lax.dynamic_slice_in_dim(
        deal.reshape(expert_parts, row_count), device_idx * share_rows, share_rows, 1
    )
    local_pick = deal_rows - device_idx * row_count
    dealt_tokens, dealt_grad = (
        lax.all_to_all(tokens[local_pick], EXPERT, split_axis=0, concat_axis=0, tiled=True),
        lax.all_to_all(out_grad[local_pick], EXPERT, split_axis=0, concat_axis=0, tiled=True),
    )
    dealt_tokens = dealt_tokens.reshape(row_count, width)
    dealt_grad = dealt_grad.reshape(row_count, width)
    gain_stack = jnp.stack([attn_gain, query_gain, key_gain, ffn_gain])
    wq_full, wk_full, wv_full, wo_full, router_full, gain_full = (
        lax.all_gather(w_query, EXPERT, axis=0, tiled=True),
        lax.all_gather(w_key, EXPERT, axis=0, tiled=True),
        lax.all_gather(w_value, EXPERT, axis=0, tiled=True),
        lax.all_gather(w_out, EXPERT, axis=1, tiled=True),
        lax.all_gather(w_router, EXPERT, axis=0, tiled=True),
        lax.all_gather(gain_stack, EXPERT, axis=1, tiled=True),
    )
    local_width = wq_full.shape[1]
    head_count = local_width // HEAD_DIM
    gain_attn = gain_full[0].astype(jnp.float32)
    gain_query = lax.dynamic_slice_in_dim(
        gain_full[1].astype(jnp.float32), column * local_width, local_width
    )
    gain_key = lax.dynamic_slice_in_dim(
        gain_full[2].astype(jnp.float32), column * local_width, local_width
    )
    gain_ffn = gain_full[3].astype(jnp.float32)
    scale = 1.0 / math.sqrt(HEAD_DIM)
    inputs = dealt_tokens.astype(jnp.float32)
    input_inv = lax.rsqrt(jnp.mean(inputs * inputs, axis=-1, keepdims=True) + NORM_EPS)
    input_hat = inputs * input_inv
    normed = (input_hat * gain_attn).astype(jnp.bfloat16)
    query_pre = jnp.dot(normed, wq_full, preferred_element_type=jnp.float32)
    key_pre = jnp.dot(normed, wk_full, preferred_element_type=jnp.float32)
    value_rows = (
        jnp.dot(normed, wv_full, preferred_element_type=jnp.float32)
        .astype(jnp.bfloat16)
        .reshape(row_count, head_count, HEAD_DIM)
    )
    query_sq, key_sq = lax.psum(
        (jnp.sum(query_pre * query_pre, axis=-1), jnp.sum(key_pre * key_pre, axis=-1)), TENSOR
    )
    query_inv = lax.rsqrt(query_sq / width + NORM_EPS)[:, None]
    key_inv = lax.rsqrt(key_sq / width + NORM_EPS)[:, None]
    query_hat = query_pre * query_inv
    key_hat = key_pre * key_inv
    cosines, sines, _ = rope_tables(doc_ids, HEAD_DIM)
    query_rot = rotate(
        (query_hat * gain_query).reshape(row_count, head_count, HEAD_DIM), cosines, sines
    ).astype(jnp.bfloat16)
    key_rot = rotate(
        (key_hat * gain_key).reshape(row_count, head_count, HEAD_DIM), cosines, sines
    ).astype(jnp.bfloat16)
    positions = jnp.arange(row_count, dtype=jnp.int32)
    allowed = (doc_ids[:, None] == doc_ids[None, :]) & (positions[None, :] <= positions[:, None])

    def masked_scores():
        raw_scores = jnp.einsum(
            "qhd,khd->hqk", query_rot, key_rot, preferred_element_type=jnp.float32
        )
        return jnp.where(allowed[None], raw_scores * scale, -1e30)

    scores = masked_scores()
    top_score = jnp.max(scores, axis=-1, keepdims=True)
    log_total = top_score + jnp.log(jnp.sum(jnp.exp(scores - top_score), axis=-1, keepdims=True))
    weights = jnp.exp(scores - log_total).astype(jnp.bfloat16)
    attended = (
        jnp.einsum("hqk,khd->qhd", weights, value_rows, preferred_element_type=jnp.float32)
        .astype(jnp.bfloat16)
        .reshape(row_count, local_width)
    )
    branch = lax.psum(jnp.dot(attended, wo_full, preferred_element_type=jnp.float32), TENSOR)
    residual = inputs + branch
    resid_inv = lax.rsqrt(jnp.mean(residual * residual, axis=-1, keepdims=True) + NORM_EPS)
    resid_hat = residual * resid_inv
    ffn_in = (resid_hat * gain_ffn).astype(jnp.bfloat16)
    logits = jnp.dot(ffn_in, router_full, preferred_element_type=jnp.float32)
    router_probs = jax.nn.softmax(logits, axis=-1)
    expert_count = router_full.shape[1]
    top_count = routes.shape[1]
    local_experts = expert_count // expert_parts
    capacity = tensor_parts * max(
        1,
        (row_count * top_count + expert_count * tensor_parts - 1) // (expert_count * tensor_parts),
        row_count * top_count * 5 // (4 * expert_count * tensor_parts),
    )
    expert_ids = jnp.arange(expert_count, dtype=jnp.int32)
    route_match = routes[:, :, None] == expert_ids[None, None, :]
    gate_probs = jnp.sum(jnp.where(route_match, router_probs[:, None, :], 0.0), axis=-1)
    flat_routes = routes.reshape(-1)
    onehot = (flat_routes[:, None] == expert_ids[None, :]).astype(jnp.int32)
    slot_rank = jnp.sum((jnp.cumsum(onehot, axis=0) - onehot) * onehot, axis=-1)
    row_ids = flat_routes * capacity + slot_rank
    token_ids = jnp.arange(row_count * top_count, dtype=jnp.int32) // top_count
    slot_token = (
        jnp.full((expert_count * capacity,), row_count, jnp.int32).at[row_ids].set(token_ids)
    )
    slot_gates = (
        jnp.zeros((expert_count * capacity,), jnp.float32).at[row_ids].set(gate_probs.reshape(-1))
    )
    pick_rows = row_ids.reshape(row_count, top_count)
    padded_in = jnp.concatenate([ffn_in, jnp.zeros((1, width), jnp.bfloat16)], axis=0)
    grad_full = dealt_grad.astype(jnp.float32)
    grad_padded = jnp.concatenate([grad_full, jnp.zeros((1, width), jnp.float32)], axis=0)
    received = to_experts(
        padded_in[slot_token].reshape(expert_parts, local_experts, capacity, width)
    )
    gate_pre = jnp.einsum("secd,edf->secf", received, w_gate, preferred_element_type=jnp.float32)
    up_pre = jnp.einsum("secd,edf->secf", received, w_up, preferred_element_type=jnp.float32)
    sigmoid_gate = jax.nn.sigmoid(gate_pre)
    silu_gate = gate_pre * sigmoid_gate
    hidden = (silu_gate * up_pre).astype(jnp.bfloat16)
    partial_out = jnp.einsum("secf,efd->secd", hidden, w_down, preferred_element_type=jnp.float32)
    own_columns = hidden_sums(partial_out).astype(jnp.bfloat16)
    returned = from_experts(own_columns).reshape(expert_count * capacity, quarter)
    chosen = returned[pick_rows].astype(jnp.float32)
    mix_own = jnp.sum(gate_probs[:, :, None] * chosen, axis=1)
    mix_part = lax.dynamic_update_slice_in_dim(
        jnp.zeros((row_count, width), jnp.float32), mix_own, column * quarter, 1
    )
    grad_own = lax.dynamic_slice_in_dim(grad_full, column * quarter, quarter, 1)
    gate_grad_part = jnp.sum(grad_own[:, None, :] * chosen, axis=-1)
    send_grad = (
        (grad_padded[slot_token] * slot_gates[:, None])
        .astype(jnp.bfloat16)
        .reshape(expert_parts, local_experts, capacity, width)
    )
    recv_grad = to_experts(send_grad)
    d_w_down = jnp.einsum("secf,secd->efd", hidden, recv_grad, preferred_element_type=jnp.float32)
    hidden_grad = jnp.einsum(
        "secd,efd->secf", recv_grad, w_down, preferred_element_type=jnp.float32
    )
    gate_grad_pre = (
        hidden_grad * up_pre * sigmoid_gate * (1.0 + gate_pre * (1.0 - sigmoid_gate))
    ).astype(jnp.bfloat16)
    up_grad_pre = (hidden_grad * silu_gate).astype(jnp.bfloat16)
    d_w_gate = jnp.einsum(
        "secd,secf->edf", received, gate_grad_pre, preferred_element_type=jnp.float32
    )
    d_w_up = jnp.einsum("secd,secf->edf", received, up_grad_pre, preferred_element_type=jnp.float32)
    joined_grad = jnp.concatenate([gate_grad_pre, up_grad_pre], axis=-1)
    joined_weight = jnp.concatenate([w_gate, w_up], axis=-1)
    row_terms = jnp.einsum(
        "secf,edf->secd", joined_grad, joined_weight, preferred_element_type=jnp.float32
    )
    row_own = hidden_sums(row_terms).astype(jnp.bfloat16)
    row_back = from_experts(row_own).reshape(expert_count * capacity, quarter)
    ffn_grad_own = jnp.sum(row_back[pick_rows].astype(jnp.float32), axis=1)
    placed = lax.dynamic_update_slice_in_dim(
        jnp.zeros((row_count, width), jnp.float32), ffn_grad_own, column * quarter, 1
    )
    ffn_grad_rows, gate_grad, mix_total = lax.psum((placed, gate_grad_part, mix_part), TENSOR)
    output = (residual + mix_total).astype(jnp.bfloat16)
    prob_grad = jnp.sum(jnp.where(route_match, gate_grad[:, :, None], 0.0), axis=1)
    logit_grad = (
        router_probs * (prob_grad - jnp.sum(router_probs * prob_grad, axis=-1, keepdims=True))
    ).astype(jnp.bfloat16)
    d_router = jnp.einsum("rd,re->de", ffn_in, logit_grad, preferred_element_type=jnp.float32)
    ffn_grad = ffn_grad_rows + jnp.einsum(
        "re,de->rd", logit_grad, router_full, preferred_element_type=jnp.float32
    )
    d_ffn_gain = jnp.sum(ffn_grad * resid_hat, axis=0)
    scaled_ffn = ffn_grad * gain_ffn
    resid_grad = grad_full + resid_inv * (
        scaled_ffn - resid_hat * jnp.mean(scaled_ffn * resid_hat, axis=-1, keepdims=True)
    )
    branch_grad = resid_grad.astype(jnp.bfloat16)
    d_wo = jnp.einsum("rk,rd->kd", attended, branch_grad, preferred_element_type=jnp.float32)
    attended_grad = (
        jnp.einsum("rd,kd->rk", branch_grad, wo_full, preferred_element_type=jnp.float32)
        .astype(jnp.bfloat16)
        .reshape(row_count, head_count, HEAD_DIM)
    )
    probs_again = jnp.exp(masked_scores() - log_total)
    prob_grads = jnp.einsum(
        "qhd,khd->hqk", attended_grad, value_rows, preferred_element_type=jnp.float32
    )
    value_grad = (
        jnp.einsum(
            "hqk,qhd->khd",
            probs_again.astype(jnp.bfloat16),
            attended_grad,
            preferred_element_type=jnp.float32,
        )
        .astype(jnp.bfloat16)
        .reshape(row_count, local_width)
    )
    row_delta = jnp.sum(probs_again * prob_grads, axis=-1, keepdims=True)
    score_grad = (probs_again * (prob_grads - row_delta) * scale).astype(jnp.bfloat16)
    query_rot_grad = jnp.einsum(
        "hqk,khd->qhd", score_grad, key_rot, preferred_element_type=jnp.float32
    )
    key_rot_grad = jnp.einsum(
        "hqk,qhd->khd", score_grad, query_rot, preferred_element_type=jnp.float32
    )
    query_norm_grad = unrotate(query_rot_grad, cosines, sines).reshape(row_count, local_width)
    key_norm_grad = unrotate(key_rot_grad, cosines, sines).reshape(row_count, local_width)
    query_hat_grad = query_norm_grad * gain_query
    key_hat_grad = key_norm_grad * gain_key
    gain_pieces = jnp.stack(
        [jnp.sum(query_norm_grad * query_hat, axis=0), jnp.sum(key_norm_grad * key_hat, axis=0)]
    )
    gain_parts = lax.dynamic_update_slice_in_dim(
        jnp.zeros((2, width), jnp.float32), gain_pieces, column * local_width, 1
    )
    query_dot, key_dot, qk_gains = lax.psum(
        (
            jnp.sum(query_hat_grad * query_hat, axis=-1),
            jnp.sum(key_hat_grad * key_hat, axis=-1),
            gain_parts,
        ),
        TENSOR,
    )
    query_grad = (query_inv * (query_hat_grad - query_hat * (query_dot / width)[:, None])).astype(
        jnp.bfloat16
    )
    key_grad = (key_inv * (key_hat_grad - key_hat * (key_dot / width)[:, None])).astype(
        jnp.bfloat16
    )
    d_wq = jnp.einsum("rd,rk->dk", normed, query_grad, preferred_element_type=jnp.float32)
    d_wk = jnp.einsum("rd,rk->dk", normed, key_grad, preferred_element_type=jnp.float32)
    d_wv = jnp.einsum("rd,rk->dk", normed, value_grad, preferred_element_type=jnp.float32)
    input_terms = jnp.einsum("rk,dk->rd", query_grad, wq_full, preferred_element_type=jnp.float32)
    input_terms = input_terms + jnp.einsum(
        "rk,dk->rd", key_grad, wk_full, preferred_element_type=jnp.float32
    )
    input_terms = input_terms + jnp.einsum(
        "rk,dk->rd", value_grad, wv_full, preferred_element_type=jnp.float32
    )
    normed_grad = lax.psum(input_terms, TENSOR)
    d_attn_part = jnp.sum(normed_grad * input_hat, axis=0)
    scaled_attn = normed_grad * gain_attn
    input_grad = resid_grad + input_inv * (
        scaled_attn - input_hat * jnp.mean(scaled_attn * input_hat, axis=-1, keepdims=True)
    )
    dealt_dtokens = input_grad.astype(jnp.bfloat16)
    gain_grads = jnp.stack([d_attn_part, qk_gains[0], qk_gains[1], d_ffn_gain])
    sum_wq, sum_wk, sum_wv, sum_wo, sum_router, sum_gains = (
        lax.psum_scatter(d_wq, EXPERT, scatter_dimension=0, tiled=True),
        lax.psum_scatter(d_wk, EXPERT, scatter_dimension=0, tiled=True),
        lax.psum_scatter(d_wv, EXPERT, scatter_dimension=0, tiled=True),
        lax.psum_scatter(d_wo, EXPERT, scatter_dimension=1, tiled=True),
        lax.psum_scatter(d_router, EXPERT, scatter_dimension=0, tiled=True),
        lax.psum_scatter(gain_grads, EXPERT, scatter_dimension=1, tiled=True),
    )
    back_out, back_dtok = (
        lax.all_to_all(
            output.reshape(expert_parts, share_rows, width),
            EXPERT,
            split_axis=0,
            concat_axis=0,
            tiled=True,
        ),
        lax.all_to_all(
            dealt_dtokens.reshape(expert_parts, share_rows, width),
            EXPERT,
            split_axis=0,
            concat_axis=0,
            tiled=True,
        ),
    )
    flat_pick = local_pick.reshape(-1)
    output_rows = (
        jnp.zeros((row_count, width), jnp.bfloat16)
        .at[flat_pick]
        .set(back_out.reshape(row_count, width))
    )
    d_tokens = (
        jnp.zeros((row_count, width), jnp.bfloat16)
        .at[flat_pick]
        .set(back_dtok.reshape(row_count, width))
    )
    return (
        output_rows,
        d_tokens,
        sum_gains[0],
        sum_wq,
        sum_wk,
        sum_wv,
        sum_wo,
        sum_gains[1],
        sum_gains[2],
        sum_gains[3],
        sum_router,
        d_w_gate,
        d_w_up,
        d_w_down,
    )


MESH_ID = pl.DeviceIdType.MESH
ANY = pl.BlockSpec(memory_space=pl.ANY)
IN_VMEM = pl.BlockSpec(memory_space=pltpu.VMEM)
def cost_of(micros):
    return pl.CostEstimate(flops=0, bytes_accessed=micros * 3_000_000, transcendentals=0)


SELF, NEAR, FAR, BOTH_FLIPPED = 0, 1, 2, 3


def place_of(device):
    expert, tensor = device
    return expert // 2, expert % 2, tensor // 2, tensor % 2


def flipped(device, role):
    expert, tensor = device
    _, x, y, core = place_of(device)
    step_x, step_y = 1 - 2 * x, 2 - 4 * y
    if role == NEAR:
        return expert + (1 - core) * step_x, tensor + core * step_y
    if role == FAR:
        return expert + core * step_x, tensor + (1 - core) * step_y
    if role == BOTH_FLIPPED:
        return expert + step_x, tensor + step_y
    return expert, tensor


def moved_z(device, hops):
    expert, tensor = device
    return lax.rem(expert + 2 * hops, 8), tensor


def sibling(device):
    expert, tensor = device
    return expert, tensor + 1 - 2 * (tensor % 2)


def slot_of(device):
    return device[0] * 4 + device[1]


def here():
    return lax.axis_index(EXPERT), lax.axis_index(TENSOR)


def greet(partners):
    barrier = pltpu.get_barrier_semaphore()
    for partner in partners:
        pl.semaphore_signal(barrier, inc=1, device_id=partner, device_id_type=MESH_ID)
    pl.semaphore_wait(barrier, len(partners))


def push(source, target, send_sem, recv_sem, device):
    return pltpu.make_async_remote_copy(
        src_ref=source,
        dst_ref=target,
        send_sem=send_sem,
        recv_sem=recv_sem,
        device_id=device,
        device_id_type=MESH_ID,
    )


def hop(device, flips, hops):
    expert, tensor = device
    return lax.rem(expert + flips * (1 - 2 * lax.rem(expert, 2)) + 2 * hops, 8), tensor


def across_y(device):
    expert, tensor = device
    return expert, lax.rem(tensor + 2, 4)


class Line:
    def __init__(self, send_sem, recv_sem):
        self.send_sem, self.recv_sem = send_sem, recv_sem
        self.started = []

    def send(self, source, target, tag, recv_tag, device):
        copy = push(source, target, self.send_sem.at[tag], self.recv_sem.at[recv_tag], device)
        copy.start()
        self.started.append(copy)

    def wait(self, target, tag, device):
        push(target, target, self.send_sem.at[0], self.recv_sem.at[tag], device).wait_recv()

    def finish(self):
        for copy in self.started:
            copy.wait_send()


PIECES = ((0, 1), (1, 0), (3, 0), (1, 1), (3, 1), (2, 0), (2, 1))


def exchange_steps(source, out, gathered, line, local_sem):
    me = here()
    tensor = me[1]
    side, sib = across_y(me), sibling(me)

    def at(column, expert):
        return out.at[column, expert] if gathered else out.at[expert]

    local = pltpu.make_async_copy(source.at[me[0]], at(tensor, me[0]), local_sem)
    local.start()
    if gathered:
        line.send(source.at[me[0]], at(tensor, me[0]), 8, 8, side)
        line.send(source.at[me[0]], at(tensor, me[0]), 16, 16, sib)
    for k, flips in PIECES:
        target = hop(me, flips, k)
        line.send(
            source.at[target[0]], at(tensor, me[0]), k * 2 + flips, (4 - k) % 4 * 2 + flips, target
        )
    yield
    for k, flips in PIECES:
        expert = hop(me, flips, k)[0]
        tag = k * 2 + flips
        line.wait(at(tensor, expert), tag, sib)
        if gathered:
            line.send(at(tensor, expert), at(tensor, expert), 8 + tag, 8 + tag, side)
            line.send(at(tensor, expert), at(tensor, expert), 16 + tag, 16 + tag, sib)
        yield
    if gathered:
        for k, flips in ((0, 0),) + PIECES:
            expert = hop(me, flips, k)[0]
            tag = k * 2 + flips
            line.wait(at(side[1], expert), 8 + tag, sib)
            line.send(at(side[1], expert), at(side[1], expert), 24 + tag, 24 + tag, sib)
            yield
        for k, flips in ((0, 0),) + PIECES:
            expert = hop(me, flips, k)[0]
            tag = k * 2 + flips
            line.wait(at(sib[1], expert), 16 + tag, sib)
            line.wait(at(across_y(sib)[1], expert), 24 + tag, sib)
    local.wait()
    line.finish()


def gather_expert_steps(sources, outs, plans, line, local_sems):
    me = here()
    z = me[0] // 2
    beside = hop(me, 1, 0)
    locals_ = [
        pltpu.make_async_copy(source, out.at[me[0]], local_sems.at[n])
        for n, (source, out) in enumerate(zip(sources, outs))
    ]
    for copy in locals_:
        copy.start()
    items = [(n, i, i < s) for n, (c, s) in enumerate(plans) for i in range(c)]
    count = len(items)
    straight = [j for j in range(count) if items[j][2]]
    crossed = [j for j in range(count) if not items[j][2]]

    def window(ref, j):
        n, i, _ = items[j]
        step = sources[n].shape[0] // plans[n][0]
        return ref.at[pl.ds(i * step, step), :]

    def own(j):
        return window(sources[items[j][0]], j)

    def block_of(expert, j):
        return window(outs[items[j][0]].at[expert], j)

    def base(distance, up, j):
        return ((distance - 1) * 2 + up) * count + j

    def passes(ref, target, tag, up, held):
        @pl.when(held & ((z < 3) if up else (z > 0)))
        def _():
            push(
                ref, target, line.send_sem.at[tag], line.recv_sem.at[tag], hop(me, 0, 1 if up else 3)
            ).start()

    def came(column, distance, up):
        return lax.rem(column[0] + (8 - 2 * distance if up else 2 * distance), 8)

    def is_held(distance, up):
        return (z >= distance) if up else (z + distance <= 3)

    cross, over = 6 * count, 12 * count
    for j in crossed + straight:
        line.send(own(j), block_of(me[0], j), over + j, over + j, beside)
    for j in straight + crossed:
        for up in (1, 0):
            passes(own(j), block_of(me[0], j), base(1, up, j), up, z >= 0)
    yield
    for j in crossed:
        block = block_of(beside[0], j)
        line.wait(block, over + j, beside)
        for up in (1, 0):
            passes(block, block, cross + base(1, up, j), up, z >= 0)
    yield
    for distance in (1, 2, 3):
        for j in straight + crossed:
            for up in (1, 0):
                held = is_held(distance, up)
                block = block_of(came(me, distance, up), j)
                tag = base(distance, up, j)

                @pl.when(held)
                def _():
                    line.wait(block, tag, beside)

                if distance < 3:
                    passes(block, block, base(distance + 1, up, j), up, held)
                if items[j][2]:

                    @pl.when(held)
                    def _():
                        push(
                            block,
                            block,
                            line.send_sem.at[cross + tag],
                            line.recv_sem.at[cross + tag],
                            beside,
                        ).start()

            yield
        for j in crossed:
            for up in (1, 0):
                held = is_held(distance, up)
                block = block_of(came(beside, distance, up), j)
                tag = cross + base(distance, up, j)

                @pl.when(held)
                def _():
                    line.wait(block, tag, beside)

                if distance < 3:
                    passes(block, block, cross + base(distance + 1, up, j), up, held)
            yield
    for j in straight:
        line.wait(block_of(beside[0], j), over + j, beside)
    for distance in (1, 2, 3):
        for j in straight + crossed:
            for up in (1, 0):
                held = is_held(distance, up)
                block = block_of(came(beside, distance, up), j)
                tag = base(distance, up, j)
                sent_on = (z + 1 >= distance) & (z < 3) if up else (z - 1 + distance <= 3) & (z > 0)

                def sent(at):
                    push(block, block, line.send_sem.at[at], line.recv_sem.at[at], beside).wait_send()

                if items[j][2]:

                    @pl.when(held)
                    def _():
                        sent(cross + tag)
                        line.wait(block, cross + tag, beside)

                @pl.when(sent_on)
                def _():
                    sent(tag)
                    if not items[j][2]:
                        sent(cross + tag)

        yield
    for copy in locals_:
        copy.wait()
    line.finish()


def sum_rows(target, terms, step=16):
    def body(i, carry):
        window = pl.ds(pl.multiple_of(i * step, step), step)
        value = terms[0][window, :].astype(jnp.float32)
        for ref in terms[1:]:
            value = value + ref[window, :].astype(jnp.float32)
        target[window, :] = value.astype(target.dtype)
        return carry

    lax.fori_loop(0, target.shape[0] // step, body, 0)


def sum_expert_steps(part, out, mine, from_x, from_z, line, load_sem, step=16):
    me = here()
    beside = hop(me, 1, 0)
    loads = {}
    for k in (2, 1, 3, 0):
        line.send(part.at[hop(me, 1, k)[0]], from_x.at[k], k, k, beside)
        loads[k] = pltpu.make_async_copy(part.at[hop(me, 0, k)[0]], mine.at[k], load_sem.at[k])
        loads[k].start()
    yield
    for k in (2, 1, 3, 0):
        loads[k].wait()
        line.wait(from_x.at[k], k, beside)
        if k:
            sum_rows(mine.at[k], [mine.at[k], from_x.at[k]], step)
            line.send(mine.at[k], from_z.at[3 - k], 3 + k, 4 + 3 - k, hop(me, 0, k))
            yield
            yield
    for i in range(3):
        line.wait(from_z.at[i], 4 + i, beside)
    sum_rows(out, [mine.at[0], from_x.at[0], from_z.at[0], from_z.at[1], from_z.at[2]], step)
    line.finish()


CHAIN = (3, 0, 2, 1)


def sum_chain_steps(part, out, mine, from_x, arrive, from_b, line, load_sem, straight):
    me = here()
    z = me[0] // 2
    x = lax.rem(me[0], 2)
    low = z < 2
    near = jnp.where(low, z, 3 - z)
    behind = jnp.where(low, 0, 1)
    beside = hop(me, 1, 0)
    step = mine.shape[2]
    chunks = out.shape[0] // step
    streams = []
    for i in range(straight, chunks):
        streams += [(i, 1, None), (i, 0, None)]
    streams += [(i, 0, i) for i in range(straight)]
    first_x = len(streams) * 4
    first_b = first_x + straight * 4
    recv_x = len(streams) * 8
    recv_b = recv_x + straight * 4

    def plane(a):
        return jnp.where(low, a, 3 - a)

    def chunk_of(expert, i):
        return part.at[expert, pl.ds(i * step, step), :]

    def column(flip):
        return jnp.where(flip == 1, 1 - x, x)

    def load(s, a):
        i, flip, _ = streams[s]
        p = plane(a)
        return pltpu.make_async_copy(
            chunk_of(2 * p + column(flip), i), mine.at[s, p], load_sem.at[s * 4 + p]
        )

    for a in CHAIN:
        p = plane(a)
        for s, (i, _, at) in enumerate(streams):
            if at is not None:
                line.send(
                    chunk_of(2 * p + 1 - x, i), from_x.at[at, p], first_x + at * 4 + p,
                    recv_x + at * 4 + p, beside,
                )
            load(s, a).start()
    yield

    def own_terms(s, a):
        p = plane(a)
        load(s, a).wait()
        at = streams[s][2]
        if at is None:
            return [mine.at[s, p]]
        line.wait(from_x.at[at, p], recv_x + at * 4 + p, beside)
        return [mine.at[s, p], from_x.at[at, p]]

    def arrived(s, a, side):
        p = plane(a)
        ref = arrive.at[s, side, p]
        line.wait(ref, (s * 2 + side) * 4 + p, beside)
        return ref

    def passing(s, a, forward):
        p = plane(a)
        side = behind if forward else 1 - behind
        up = jnp.where(low, 1, 3) if forward else jnp.where(low, 3, 1)
        return push(
            mine.at[s, p],
            arrive.at[s, side, p],
            line.send_sem.at[s * 4 + p],
            line.recv_sem.at[(s * 2 + side) * 4 + p],
            hop(me, 0, up),
        )

    def pass_on(s, a, forward, sides):
        terms = own_terms(s, a) + [arrived(s, a, side) for side in sides]
        if len(terms) > 1:
            sum_rows(mine.at[s, plane(a)], terms)
        passing(s, a, forward).start()

    for a in CHAIN:
        for s in range(len(streams)):
            if a != 0:

                @pl.when(near == 0)
                def _():
                    pass_on(s, a, True, [])

            if a != 1:

                @pl.when(near == 1)
                def _():
                    pass_on(s, a, a != 0, [1 - behind if a == 0 else behind])

            yield

    def final(s, a, sides):
        i, flip, at = streams[s]
        terms = own_terms(s, a) + [arrived(s, a, side) for side in sides]
        if flip:
            total = mine.at[s, plane(a)]
            sum_rows(total, terms)
            j = i - straight
            push(
                total, from_b.at[j], line.send_sem.at[first_b + j], line.recv_sem.at[recv_b + j], beside
            ).start()
        else:
            sum_rows(out.at[pl.ds(i * step, step), :], terms)

    for s in sorted(range(len(streams)), key=lambda s: streams[s][2] is not None):

        @pl.when(near == 0)
        def _():
            final(s, 0, [1 - behind])

        @pl.when(near == 1)
        def _():
            final(s, 1, [behind, 1 - behind])

        yield
    for j in range(chunks - straight):
        rows = out.at[pl.ds((straight + j) * step, step), :]
        both = push(
            from_b.at[j], from_b.at[j], line.send_sem.at[first_b + j], line.recv_sem.at[recv_b + j], beside
        )
        both.wait()
        sum_rows(rows, [rows, from_b.at[j]])
    for a in CHAIN:
        for s in range(len(streams)):
            if a != 0:

                @pl.when(near == 0)
                def _():
                    passing(s, a, True).wait_send()

            if a != 1:

                @pl.when(near == 1)
                def _():
                    passing(s, a, a != 0).wait_send()

    line.finish()


def sum_everywhere_steps(part, out, mine, from_x, from_z, total, shares, line, load_sem):
    me = here()
    yield from sum_expert_steps(part, total, mine, from_x, from_z, line, load_sem, 8)
    peers = [across_y(me), sibling(me), across_y(sibling(me))]
    for i, peer in enumerate(peers):
        line.send(total, shares.at[me[1]], 7 + i, 7 + i, peer)
    shares[me[1]] = total[...]
    yield
    for i, peer in enumerate(peers):
        line.wait(shares.at[peer[1]], 7 + i, peer)
    sum_rows(out, [shares.at[i] for i in range(4)], 8)
    for i in range(3):
        line.started[-3 + i].wait_send()


def take_turns(steps):
    steps = list(steps)
    while steps:
        steps = [s for s in steps if next(s, steps) is not steps]


DMA = pltpu.SemaphoreType.DMA


GATHER_PLANS = ((1, 1), (4, 3), (2, 2))


def start_kernel(
    tokens, grads, weights, outs, small, o_tokens, o_grads, o_weights, o_outs, o_small, *sems
):
    me = here()
    pieces = [hop(me, flips, k) for k, flips in PIECES]
    greet(pieces + [across_y(me), sibling(me)])
    local = sems[7]
    take_turns(
        [
            exchange_steps(tokens, o_tokens, True, Line(sems[0], sems[1]), local.at[0]),
            exchange_steps(grads, o_grads, False, Line(sems[2], sems[3]), local.at[1]),
            gather_expert_steps(
                [small, weights, outs], [o_small, o_weights, o_outs], GATHER_PLANS,
                Line(sems[4], sems[5]), sems[6],
            ),
        ]
    )


def start_exchange(tokens, grads, weights, outs, small):
    piece = tokens.shape[1:]
    sds = jax.ShapeDtypeStruct
    return pl.pallas_call(
        start_kernel,
        out_shape=[
            sds((4, 8) + piece, tokens.dtype),
            sds((8,) + piece, grads.dtype),
            sds((8,) + weights.shape, weights.dtype),
            sds((8,) + outs.shape, outs.dtype),
            sds((8,) + small.shape, small.dtype),
        ],
        in_specs=[IN_VMEM] * 5,
        out_specs=[ANY] * 5,
        scratch_shapes=[DMA((32,)), DMA((32,)), DMA((8,)), DMA((8,))]
        + [DMA((13 * sum(c for c, _ in GATHER_PLANS),))] * 2
        + [DMA((3,)), DMA((2,))],
        compiler_params=pltpu.CompilerParams(
            collective_id=4, has_side_effects=True, vmem_limit_bytes=16 * 2**20
        ),
        cost_estimate=cost_of(100),
        name="start_exchange",
    )(tokens, grads, weights, outs, small)


def last_kernel(
    rows, more, part, small, o_rows, o_more, out, o_small,
    mine, from_x, arrive, from_b, mine_s, x_s, z_s, total_s, shares_s, *sems,
):
    me = here()
    pieces = [hop(me, flips, k) for k, flips in PIECES]
    greet(pieces + [across_y(me), sibling(me), across_y(sibling(me))])
    take_turns(
        [
            exchange_steps(more, o_more, True, Line(sems[2], sems[3]), sems[7].at[1]),
            exchange_steps(rows, o_rows, True, Line(sems[0], sems[1]), sems[7].at[0]),
            sum_everywhere_steps(
                small, o_small, mine_s, x_s, z_s, total_s, shares_s, Line(sems[8], sems[9]), sems[10]
            ),
            sum_chain_steps(
                part, out, mine, from_x, arrive, from_b, Line(sems[4], sems[5]), sems[6], from_x.shape[0]
            ),
        ]
    )


def last_exchange(rows, more, part, small):
    piece = rows.shape[1:]
    block, little = part.shape[1:], small.shape[1:]
    chunks, straight = 4, 3
    streams = 2 * chunks - straight
    chunk = (block[0] // chunks, block[1])
    first = (streams + straight) * 4
    sds = jax.ShapeDtypeStruct
    return pl.pallas_call(
        last_kernel,
        out_shape=[
            sds((4, 8) + piece, rows.dtype),
            sds((4, 8) + piece, more.dtype),
            sds(block, jnp.float32),
            sds(little, jnp.float32),
        ],
        in_specs=[IN_VMEM, IN_VMEM, ANY, ANY],
        out_specs=[ANY, ANY, IN_VMEM, IN_VMEM],
        scratch_shapes=[
            pltpu.VMEM((streams, 4) + chunk, part.dtype),
            pltpu.VMEM((straight, 4) + chunk, part.dtype),
            pltpu.VMEM((streams, 2, 4) + chunk, part.dtype),
            pltpu.VMEM((chunks - straight,) + chunk, part.dtype),
        ]
        + [pltpu.VMEM((n,) + little, jnp.float32) for n in (4, 4, 3)]
        + [pltpu.VMEM(little, jnp.float32), pltpu.VMEM((4,) + little, jnp.float32)]
        + [DMA((32,))] * 4
        + [DMA((first + chunks,)), DMA((first + streams * 4 + chunks,)), DMA((streams * 4,)), DMA((2,))]
        + [DMA((10,)), DMA((10,)), DMA((4,))],
        compiler_params=pltpu.CompilerParams(
            collective_id=5, has_side_effects=True, vmem_limit_bytes=62 * 2**20
        ),
        cost_estimate=cost_of(1),
        name="last_exchange",
    )(rows, more, part, small)


def gather_tensor_kernel(source, out, send_sem, recv_sem, local_sem):
    me = here()
    side, sib = across_y(me), sibling(me)
    greet([side, sib])
    line = Line(send_sem, recv_sem)
    halves = 4
    step = source.shape[0] // halves

    def part(ref, i):
        return ref.at[pl.ds(i * step, step), :]

    local = pltpu.make_async_copy(source, out.at[me[1]], local_sem)
    for i in range(halves):
        line.send(part(source, i), part(out.at[me[1]], i), i, i, side)
        line.send(part(source, i), part(out.at[me[1]], i), 4 + i, 4 + i, sib)
    local.start()
    for i in range(halves):
        got = part(out.at[side[1]], i)
        line.wait(got, i, sib)
        line.send(got, got, 8 + i, 8 + i, sib)
    for i in range(halves):
        line.wait(part(out.at[sib[1]], i), 4 + i, sib)
        line.wait(part(out.at[across_y(sib)[1]], i), 8 + i, sib)
    local.wait()
    line.finish()


def gather_tensor(rows):
    out = pl.pallas_call(
        gather_tensor_kernel,
        out_shape=jax.ShapeDtypeStruct((4,) + rows.shape, rows.dtype),
        in_specs=[IN_VMEM],
        out_specs=ANY,
        scratch_shapes=[DMA((12,)), DMA((12,)), DMA],
        compiler_params=pltpu.CompilerParams(
            collective_id=6, has_side_effects=True, vmem_limit_bytes=8 * 2**20
        ),
        cost_estimate=cost_of(15),
        name="gather_tensor",
    )(rows)
    return out.reshape((-1,) + rows.shape[1:])


def sum_tensor_into(make, part, out, from_sib, from_side, total, line):
    me = here()
    side, sib = across_y(me), sibling(me)
    pieces = 4
    step = out.shape[0] // pieces

    def rows(ref, i):
        return ref.at[pl.ds(i * step, step), :]

    for j, column in ((0, across_y(sib)[1]), (1, sib[1])):
        make(column)
        for i in range(pieces):
            line.send(
                rows(part.at[column], i), rows(from_sib.at[j], i), 4 * j + i, 4 * j + i, sib
            )
    make(side[1])
    for i in range(pieces):
        got = rows(from_sib.at[0], i)
        line.wait(got, i, sib)
        sum_rows(rows(total, i), [rows(part.at[side[1]], i), got])
        line.send(rows(total, i), rows(from_side, i), 8 + i, 8 + i, side)
    make(me[1])
    for i in range(pieces):
        got = rows(from_sib.at[1], i)
        line.wait(got, 4 + i, sib)
        line.wait(rows(from_side, i), 8 + i, sib)
        sum_rows(rows(out, i), [rows(part.at[me[1]], i), got, rows(from_side, i)])
    line.finish()


def sum_tensor_scratch(block):
    bf16 = jnp.bfloat16
    return [
        pltpu.VMEM((4,) + block, bf16),
        pltpu.VMEM((2,) + block, bf16),
        pltpu.VMEM(block, bf16),
        pltpu.VMEM(block, bf16),
        DMA((12,)),
        DMA((12,)),
    ]


def input_sum_kernel(left, right, out, part, from_sib, from_side, total, send_sem, recv_sem):
    me = here()
    greet([across_y(me), sibling(me)])

    def make(column):
        rows = pl.ds(pl.multiple_of(column * out.shape[0], out.shape[0]), out.shape[0])
        for c in range(4):
            span = right.shape[0] // 4
            cols = slice(c * span, (c + 1) * span)
            part[column, :, cols] = dot32(left[rows, :], right[cols, :], NT).astype(jnp.bfloat16)

    sum_tensor_into(make, part, out, from_sib, from_side, total, Line(send_sem, recv_sem))


def input_sum(left, right):
    block = (left.shape[0] // 4, right.shape[0])
    return pl.pallas_call(
        input_sum_kernel,
        out_shape=jax.ShapeDtypeStruct(block, jnp.float32),
        in_specs=[IN_VMEM] * 2,
        out_specs=IN_VMEM,
        scratch_shapes=sum_tensor_scratch(block),
        compiler_params=pltpu.CompilerParams(
            collective_id=7, has_side_effects=True, vmem_limit_bytes=32 * 2**20
        ),
        cost_estimate=cost_of(1),
        name="input_sum",
    )(left, right)


def rows_at(ref, slot, size, count=1):
    return ref.at[pl.ds(pl.multiple_of(slot * size, size), size * count), :]


class Plan:
    def __init__(self, send_sem, recv_sem):
        self.send_sem, self.recv_sem, self.made = send_sem, recv_sem, []

    def send(self, make):
        make().start()
        self.made.append(make)

    def finish(self):
        for make in self.made:
            make().wait_send()


def gather_plan(ins, outs, sizes, send_sem, recv_sem):
    me = here()
    near, far, sib = flipped(me, NEAR), flipped(me, FAR), sibling(me)
    plan = Plan(send_sem, recv_sem)
    count = len(ins)

    def send(k, role, device, tag, recv_tag):
        for i in range(count):

            def make(i=i):
                block = rows_at(outs[i], slot_of(moved_z(flipped(me, role), k)), sizes[i])
                source = ins[i] if (k, role) == (0, SELF) else block
                return push(source, block, send_sem.at[i, tag], recv_sem.at[i, recv_tag], device)

            plan.send(make)

    def arrive(k, role):
        for i in range(count):
            block = rows_at(outs[i], slot_of(moved_z(flipped(me, role), k)), sizes[i])
            push(block, block, send_sem.at[i, 0], recv_sem.at[i, k * 4 + role], near).wait_recv()

    def forward(k, role):
        if role == SELF:
            send(k, SELF, far, 4 + k, k * 4 + FAR)
            send(k, SELF, near, k, k * 4 + NEAR)
        if role == NEAR:
            send(k, NEAR, far, 8 + k, k * 4 + BOTH_FLIPPED)
        send(k, role, sib, 16 + k * 4 + role, 16 + k * 4 + role)

    def event(k, role):
        arrive(k, role)
        forward(k, role)

    def from_sibling(k, role):
        for i in range(count):
            block = rows_at(outs[i], 0, sizes[i])
            push(
                block, block, send_sem.at[i, 0], recv_sem.at[i, 16 + k * 4 + role], near
            ).wait_recv()

    def begin():
        forward(0, SELF)
        for d in (1, 3, 2):
            send(0, SELF, moved_z(me, d), 11 + d, (4 - d) * 4 + SELF)

    return plan, begin, event, from_sibling


def gate_columns(gates_ref, slot, columns, first):
    lane = lax.broadcasted_iota(jnp.int32, (128, 128), 1)
    for s in range(4):
        block = gates_ref[pl.ds(pl.multiple_of((slot + s) * 16, 16), 16), :]
        turned = jnp.concatenate([block, jnp.zeros((112, 128), jnp.float32)], axis=0).T
        for i in range(2):
            column = jnp.sum(jnp.where(lane == first + i, turned, 0.0), axis=1, keepdims=True)
            columns[i, pl.ds(s * 128, 128), :] = jnp.broadcast_to(column, (128, 128))


def tiles(count, width, body):
    def step(n, carry):
        body(pl.ds(pl.multiple_of(n * width, width), width))
        return carry

    lax.fori_loop(0, count, step, 0)


STAGES = ((0, 0), (0, 1), (1, 0), (1, 1), (3, 0), (3, 1), (2, 0), (2, 1))
BLOCK = 512


def stage_expert(me, j):
    half = j // 2
    k = half + jnp.where(half == 2, 1, 0) - jnp.where(half == 3, 1, 0)
    flips = lax.rem(j, 2)
    expert = me[0]
    return lax.rem(expert + flips * (1 - 2 * lax.rem(expert, 2)) + 2 * k, 8)


def forward_kernel(
    x_own, g_own, w_joined, w_down, x_out, g_out, pre_out, gated_out, y_out,
    x_all, g_all, columns, pre, gated, y, send_sem, recv_sem, local_sem, out_sem,
):
    me = here()
    core = lax.rem(me[1], 2)
    greet(
        [flipped(me, NEAR), flipped(me, FAR), sibling(me)] + [moved_z(me, d) for d in (1, 2, 3)]
    )
    plan, begin, event, from_sibling = gather_plan(
        [x_own, g_own], [x_all, g_all], [128, 16], send_sem, recv_sem
    )
    local = [
        pltpu.make_async_copy(x_own, rows_at(x_all, slot_of(me), 128), local_sem.at[0]),
        pltpu.make_async_copy(g_own, rows_at(g_all, slot_of(me), 16), local_sem.at[1]),
    ]
    begin()
    for copy in local:
        copy.start()
    for copy in local:
        copy.wait()
    before = {
        0: [(1, SELF), (0, NEAR), (0, FAR)],
        1: [(0, BOTH_FLIPPED)],
        3: [(1, BOTH_FLIPPED)],
        5: [(3, BOTH_FLIPPED)],
        7: [(2, BOTH_FLIPPED)],
    }
    middle = {
        0: [(3, SELF), (1, NEAR)],
        1: [(1, FAR)],
        2: [(2, SELF), (3, NEAR)],
        3: [(3, FAR)],
        4: [(2, NEAR)],
        5: [(2, FAR)],
    }
    half = w_joined.shape[1] // 2

    def results(expert, slot):
        return [
            pltpu.make_async_copy(
                rows_at(x_all, expert, BLOCK), rows_at(x_out, expert, BLOCK), out_sem.at[0, slot]
            ),
            pltpu.make_async_copy(pre.at[slot], rows_at(pre_out, expert, BLOCK), out_sem.at[1, slot]),
            pltpu.make_async_copy(
                gated.at[slot], rows_at(gated_out, expert, BLOCK), out_sem.at[2, slot]
            ),
            pltpu.make_async_copy(y.at[slot], rows_at(y_out, expert, BLOCK), out_sem.at[3, slot]),
        ]

    def block(j, carry):
        slot = lax.rem(j, 2)
        expert = stage_expert(me, j)
        for n, (k, flips) in enumerate(STAGES):

            @pl.when(j == n)
            def _():
                for at in before.get(n, []):
                    event(*at)
                if n:
                    from_sibling(k, 2 - core if flips else SELF)
                    from_sibling(k, BOTH_FLIPPED if flips else 1 + core)
                else:
                    from_sibling(k, SELF)
                    from_sibling(k, 1 + core)

        @pl.when(j >= 2)
        def _():
            for copy in results(stage_expert(me, j - 2), slot):
                copy.wait()

        gate_columns(g_all, expert * 4, columns, me[0] * 2)
        x_rows = rows_at(x_all, expert, BLOCK)

        def first(cols):
            pre[slot, :, cols] = jnp.dot(
                x_rows[...], w_joined[:, cols], preferred_element_type=jnp.float32
            )

        tiles(w_joined.shape[1] // 1024, 1024, first)
        for n in middle:

            @pl.when(j == n)
            def _():
                for at in middle[n]:
                    event(*at)

        def act(r):
            for c in range(half // 128):
                cols = slice(c * 128, (c + 1) * 128)
                g = pre[slot, r, cols]
                u = pre[slot, r, half + c * 128 : half + (c + 1) * 128]
                hidden = (g * (1.0 / (1.0 + jnp.exp(-g))) * u).astype(jnp.bfloat16)
                gate = columns[c * 128 * 2 // half, r, :]
                gated[slot, r, cols] = (hidden.astype(jnp.float32) * gate).astype(jnp.bfloat16)

        tiles(BLOCK // 64, 64, act)

        def second(cols):
            y[slot, :, cols] = jnp.dot(
                gated[slot], w_down[:, cols], preferred_element_type=jnp.float32
            ).astype(jnp.bfloat16)

        tiles(w_down.shape[1] // 1024, 1024, second)
        for copy in results(expert, slot):
            copy.start()
        return carry

    lax.fori_loop(0, 8, block, 0)
    for j in (6, 7):
        for copy in results(stage_expert(me, jnp.int32(j)), j % 2):
            copy.wait()
    g_out[...] = g_all[...]
    plan.finish()


def experts_forward(ffn_in, gates_own, w_joined, w_down):
    rows, width = ffn_in.shape[0] * 32, ffn_in.shape[1]
    joined, hidden = w_joined.shape[1], w_down.shape[0]
    bf16, f32, sds = jnp.bfloat16, jnp.float32, jax.ShapeDtypeStruct
    return pl.pallas_call(
        forward_kernel,
        out_shape=[
            sds((rows, width), bf16),
            sds((512, 128), f32),
            sds((rows, joined), f32),
            sds((rows, hidden), bf16),
            sds((rows, width), bf16),
        ],
        in_specs=[IN_VMEM] * 4,
        out_specs=[ANY, IN_VMEM, ANY, ANY, ANY],
        scratch_shapes=[
            pltpu.VMEM((rows, width), bf16),
            pltpu.VMEM((512, 128), f32),
            pltpu.VMEM((2, BLOCK, 128), f32),
            pltpu.VMEM((2, BLOCK, joined), f32),
            pltpu.VMEM((2, BLOCK, hidden), bf16),
            pltpu.VMEM((2, BLOCK, width), bf16),
            DMA((2, 32)),
            DMA((2, 32)),
            DMA((2,)),
            DMA((4, 2)),
        ],
        compiler_params=pltpu.CompilerParams(
            collective_id=1, has_side_effects=True, vmem_limit_bytes=48 * 2**20
        ),
        cost_estimate=cost_of(90),
        name="experts_forward",
    )(ffn_in, gates_own, w_joined, w_down)


def sum_plan(arrays, send_sem, recv_sem, load_sem):
    me = here()
    near, far, sib = flipped(me, NEAR), flipped(me, FAR), sibling(me)
    plan = Plan(send_sem, recv_sem)
    order = (2, 1, 3, 0)

    def send(i, source, target, tag, recv_tag, device):
        plan.send(
            lambda: push(source(), target(), send_sem.at[i, tag], recv_sem.at[i, recv_tag], device())
        )

    def arrive(i, ref, tag):
        push(ref, ref, send_sem.at[i, 0], recv_sem.at[i, tag], near).wait_recv()

    def load(i, k, role):
        part, _, size, mine = arrays[i][:4]
        tag = k * 4 + role
        return pltpu.make_async_copy(
            rows_at(part, slot_of(moved_z(flipped(me, role), k)), size), mine.at[tag], load_sem.at[i, tag]
        )

    def begin():
        for roles in ((BOTH_FLIPPED, FAR), (NEAR, SELF)):
            for k in order:
                for role in roles:
                    for i, (part, _, size, _, from_sib, _, _, _) in enumerate(arrays):
                        tag = k * 4 + role
                        send(
                            i,
                            lambda part=part, size=size, k=k, role=role: rows_at(
                                part, slot_of(moved_z(flipped(sib, role), k)), size
                            ),
                            lambda from_sib=from_sib, tag=tag: from_sib.at[tag],
                            tag,
                            tag,
                            lambda: sib,
                        )
                        load(i, k, role).start()

    def collect(i, k, role):
        tag = k * 4 + role
        load(i, k, role).wait()
        from_sib = arrays[i][4]
        arrive(i, from_sib.at[tag], tag)
        return [arrays[i][3].at[tag], from_sib.at[tag]]

    def first(k, role):
        for i, (_, _, _, mine, _, from_far, _, _) in enumerate(arrays):
            tag, at = k * 4 + role, k * 2 + (role == BOTH_FLIPPED)
            terms = collect(i, k, role)
            sum_rows(mine.at[tag], terms)
            send(
                i,
                lambda mine=mine, tag=tag: mine.at[tag],
                lambda from_far=from_far, at=at: from_far.at[at],
                16 + at,
                16 + at,
                lambda: far,
            )

    def second(k):
        for i, (_, _, _, mine, _, from_far, from_near, _) in enumerate(arrays):
            tag = k * 4 + NEAR
            terms = collect(i, k, NEAR)
            arrive(i, from_far.at[k * 2 + 1], 16 + k * 2 + 1)
            sum_rows(mine.at[tag], terms + [from_far.at[k * 2 + 1]])
            send(
                i,
                lambda mine=mine, tag=tag: mine.at[tag],
                lambda from_near=from_near, k=k: from_near.at[k],
                24 + k,
                24 + k,
                lambda: near,
            )

    def third(k):
        for i, (_, out, _, mine, _, from_far, from_near, from_z) in enumerate(arrays):
            tag = k * 4 + SELF
            terms = collect(i, k, SELF)
            arrive(i, from_far.at[k * 2], 16 + k * 2)
            arrive(i, from_near.at[k], 24 + k)
            terms = terms + [from_far.at[k * 2], from_near.at[k]]
            if k > 0:
                sum_rows(mine.at[tag], terms)
                send(
                    i,
                    lambda mine=mine, tag=tag: mine.at[tag],
                    lambda from_z=from_z, k=k: from_z.at[3 - k],
                    27 + k,
                    31 - k,
                    lambda k=k: moved_z(me, k),
                )
            else:
                for d in range(3):
                    arrive(i, from_z.at[d], 28 + d)
                    terms.append(from_z.at[d])
                sum_rows(out, terms)

    return plan, begin, first, second, third


def sum_scratch(size, width, dtype):
    return [pltpu.VMEM((n, size, width), dtype) for n in (16, 16, 8, 4, 3)]


SUM_BEFORE = {0: [(2, 3), (2, 2), (1, 3), (1, 2)], 3: [(2, "third")], 5: [(1, "third")]}
SUM_MIDDLE = {
    0: [(3, 3), (3, 2), (0, 3), (0, 2)],
    1: [(2, "second")],
    2: [(1, "second")],
    4: [(3, "second")],
    6: [(0, "second")],
}


def sum_events(table, j, first, second, third):
    for n, events in table.items():

        @pl.when(j == n)
        def _():
            for k, what in events:
                if what == "second":
                    second(k)
                elif what == "third":
                    third(k)
                else:
                    first(k, what)


def greet_all(me):
    greet(
        [flipped(me, NEAR), flipped(me, FAR), sibling(me)] + [moved_z(me, d) for d in (1, 2, 3)]
    )


def backward_kernel(
    y_part, grads, pre_all, gates, w_joined, w_down, mix_out, dpre_out, drow_out, gate_grads,
    mine, from_sib, from_far, from_near, from_z, dz, pre, raw, columns, products, dpre, drow,
    send_sem, recv_sem, load_sem, in_sem, out_sem,
):
    me = here()
    greet_all(me)
    plan, begin, first, second, third = sum_plan(
        [(y_part, mix_out, 128, mine, from_sib, from_far, from_near, from_z)],
        send_sem, recv_sem, load_sem,
    )
    half = w_joined.shape[1] // 2
    expert_lanes = half // 2

    def loads(block, slot):
        return [
            pltpu.make_async_copy(rows_at(grads, block, BLOCK), dz.at[slot], in_sem.at[0, slot]),
            pltpu.make_async_copy(rows_at(pre_all, block, BLOCK), pre.at[slot], in_sem.at[1, slot]),
        ]

    def results(block, slot):
        return [
            pltpu.make_async_copy(dpre.at[slot], rows_at(dpre_out, block, BLOCK), out_sem.at[0, slot]),
            pltpu.make_async_copy(drow.at[slot], rows_at(drow_out, block, BLOCK), out_sem.at[1, slot]),
        ]

    for copy in loads(0, 0):
        copy.start()
    begin()

    def step(j, carry):
        slot = lax.rem(j, 2)

        @pl.when(j < 7)
        def _():
            for copy in loads(j + 1, 1 - slot):
                copy.start()

        sum_events(SUM_BEFORE, j, first, second, third)
        for copy in loads(j, slot):
            copy.wait()

        @pl.when(j >= 2)
        def _():
            for copy in results(j - 2, slot):
                copy.wait()

        gate_columns(gates, j * 4, columns, me[0] * 2)
        raw[...] = lax.dot_general(
            dz[slot], w_down[...], (((1,), (1,)), ((), ())), preferred_element_type=jnp.float32
        )
        sum_events(SUM_MIDDLE, j, first, second, third)

        def act(r):
            for i in range(2):
                product = None
                for c in range(i * expert_lanes, (i + 1) * expert_lanes, 128):
                    g = pre[slot, r, c : c + 128]
                    u = pre[slot, r, half + c : half + c + 128]
                    t = raw[r, c : c + 128]
                    sig = 1.0 / (1.0 + jnp.exp(-g))
                    silu = g * sig
                    hidden = (silu * u).astype(jnp.bfloat16).astype(jnp.float32)
                    term = hidden * t
                    product = term if product is None else product + term
                    dh = t * columns[i, r, :]
                    dpre[slot, r, c : c + 128] = (
                        dh * u * sig * (1.0 + g * (1.0 - sig))
                    ).astype(jnp.bfloat16)
                    dpre[slot, r, half + c : half + c + 128] = (dh * silu).astype(jnp.bfloat16)
                products[i, r, :] = product

        tiles(BLOCK // 64, 64, act)
        place = lax.broadcasted_iota(jnp.int32, (16, 128), 0)
        for s in range(4):
            sums = jnp.zeros((16, 128), jnp.float32)
            for i in range(2):
                turned = products[i, pl.ds(s * 128, 128), :].T
                row = jnp.sum(turned, axis=0, keepdims=True)
                sums = jnp.where(place == me[0] * 2 + i, jnp.broadcast_to(row, (16, 128)), sums)
            gate_grads[pl.ds(pl.multiple_of((j * 4 + s) * 16, 16), 16), :] = sums

        def back(rows):
            drow[slot, :, rows] = lax.dot_general(
                dpre[slot],
                w_joined[rows, :],
                (((1,), (1,)), ((), ())),
                preferred_element_type=jnp.float32,
            ).astype(jnp.bfloat16)

        tiles(w_joined.shape[0] // 1024, 1024, back)
        for copy in results(j, slot):
            copy.start()
        return carry

    lax.fori_loop(0, 8, step, 0)
    third(3)
    third(0)
    for j in (6, 7):
        for copy in results(j, j % 2):
            copy.wait()
    plan.finish()


def experts_backward(y_part, grads, pre, gates, w_joined, w_down):
    rows, width = grads.shape
    joined, hidden = w_joined.shape[1], w_down.shape[0]
    bf16, f32, sds = jnp.bfloat16, jnp.float32, jax.ShapeDtypeStruct
    return pl.pallas_call(
        backward_kernel,
        out_shape=[
            sds((rows // 32, width), f32),
            sds((rows, joined), bf16),
            sds((rows, width), bf16),
            sds((512, 128), f32),
        ],
        in_specs=[ANY, ANY, ANY] + [IN_VMEM] * 3,
        out_specs=[IN_VMEM, ANY, ANY, IN_VMEM],
        scratch_shapes=sum_scratch(rows // 32, width, bf16)
        + [
            pltpu.VMEM((2, BLOCK, width), bf16),
            pltpu.VMEM((2, BLOCK, joined), f32),
            pltpu.VMEM((BLOCK, hidden), f32),
            pltpu.VMEM((2, BLOCK, 128), f32),
            pltpu.VMEM((2, BLOCK, 128), f32),
            pltpu.VMEM((2, BLOCK, joined), bf16),
            pltpu.VMEM((2, BLOCK, width), bf16),
            DMA((1, 32)),
            DMA((1, 32)),
            DMA((1, 16)),
            DMA((2, 2)),
            DMA((2, 2)),
        ],
        compiler_params=pltpu.CompilerParams(
            collective_id=2, has_side_effects=True, vmem_limit_bytes=56 * 2**20
        ),
        cost_estimate=cost_of(90),
        name="experts_backward",
    )(y_part, grads, pre, gates, w_joined, w_down)


def weights_kernel(
    drow, gate_grads, x_all, grads, dpre_all, gated_all, row_out, gate_out, d_gate, d_up, d_down,
    mine, from_sib, from_far, from_near, from_z, mine_g, sib_g, far_g, near_g, z_g,
    dpre, gated, tile, wide, send_sem, recv_sem, load_sem, in_sem, tile_sem, out_sem,
):
    me = here()
    greet_all(me)
    plan, begin, first, second, third = sum_plan(
        [
            (drow, row_out, 128, mine, from_sib, from_far, from_near, from_z),
            (gate_grads, gate_out, 16, mine_g, sib_g, far_g, near_g, z_g),
        ],
        send_sem, recv_sem, load_sem,
    )
    span = tile.shape[2]
    steps = x_all.shape[1] // span
    hidden = d_gate.shape[2]
    begin()
    held = [
        pltpu.make_async_copy(dpre_all, dpre, in_sem.at[0]),
        pltpu.make_async_copy(gated_all, gated, in_sem.at[1]),
    ]

    def columns_of(j):
        return pl.ds(pl.multiple_of(lax.rem(j, steps) * span, span), span)

    def fetch(j, slot, act):
        @pl.when(j < steps)
        def _():
            act(pltpu.make_async_copy(x_all.at[:, columns_of(j)], tile.at[slot], tile_sem.at[slot]))

        @pl.when((j >= steps) & (j < 2 * steps))
        def _():
            act(pltpu.make_async_copy(grads.at[:, columns_of(j)], tile.at[slot], tile_sem.at[slot]))

    def results(j, slot, act):
        cols = columns_of(j)

        @pl.when(j < steps)
        def _():
            for i in range(2):
                act(
                    pltpu.make_async_copy(
                        wide.at[slot, :, pl.ds(i * hidden, hidden)], d_gate.at[i, cols, :], out_sem.at[slot, i]
                    )
                )
                act(
                    pltpu.make_async_copy(
                        wide.at[slot, :, pl.ds((2 + i) * hidden, hidden)],
                        d_up.at[i, cols, :],
                        out_sem.at[slot, 2 + i],
                    )
                )

        @pl.when(j >= steps)
        def _():
            act(
                pltpu.make_async_copy(
                    wide.at[slot, :, pl.ds(0, span)], d_down.at[:, cols], out_sem.at[slot, 0]
                )
            )

    fetch(jnp.int32(0), 0, lambda copy: copy.start())
    for copy in held:
        copy.start()

    def step(j, carry):
        slot = lax.rem(j, 2)
        fetch(j + 1, 1 - slot, lambda copy: copy.start())
        sum_events(SUM_BEFORE, j, first, second, third)

        @pl.when(j == 0)
        def _():
            for copy in held:
                copy.wait()

        fetch(j, slot, lambda copy: copy.wait())

        @pl.when(j >= 2)
        def _():
            results(j - 2, slot, lambda copy: copy.wait())

        @pl.when(j < steps)
        def _():
            wide[slot] = lax.dot_general(
                tile[slot], dpre[...], (((0,), (0,)), ((), ())), preferred_element_type=jnp.float32
            )

        @pl.when(j >= steps)
        def _():
            wide[slot, :, 0:span] = lax.dot_general(
                gated[...], tile[slot], (((0,), (0,)), ((), ())), preferred_element_type=jnp.float32
            )

        results(j, slot, lambda copy: copy.start())
        sum_events(SUM_MIDDLE, j, first, second, third)
        return carry

    lax.fori_loop(0, 2 * steps, step, 0)
    third(3)
    third(0)
    for j in (2 * steps - 2, 2 * steps - 1):
        results(jnp.int32(j), j % 2, lambda copy: copy.wait())
    plan.finish()


def experts_weights(drow, gate_grads, x_all, grads, dpre, gated):
    rows, width = grads.shape
    joined, hidden = dpre.shape[1], gated.shape[1]
    span = width // 4
    bf16, f32, sds = jnp.bfloat16, jnp.float32, jax.ShapeDtypeStruct
    return pl.pallas_call(
        weights_kernel,
        out_shape=[
            sds((rows // 32, width), f32),
            sds((16, 128), f32),
            sds((2, width, joined // 4), f32),
            sds((2, width, joined // 4), f32),
            sds((hidden, width), f32),
        ],
        in_specs=[ANY] * 6,
        out_specs=[IN_VMEM, IN_VMEM, ANY, ANY, ANY],
        scratch_shapes=sum_scratch(rows // 32, width, bf16)
        + sum_scratch(16, 128, f32)
        + [
            pltpu.VMEM((rows, joined), bf16),
            pltpu.VMEM((rows, hidden), bf16),
            pltpu.VMEM((2, rows, span), bf16),
            pltpu.VMEM((2, span, joined), f32),
            DMA((2, 32)),
            DMA((2, 32)),
            DMA((2, 16)),
            DMA((2,)),
            DMA((2,)),
            DMA((2, 4)),
        ],
        compiler_params=pltpu.CompilerParams(
            collective_id=3, has_side_effects=True, vmem_limit_bytes=58 * 2**20
        ),
        cost_estimate=cost_of(90),
        name="experts_weights",
    )(drow, gate_grads, x_all, grads, dpre, gated)


def rotated(values, cosines, sines):
    return values * cosines + pltpu.roll(values, HEAD_DIM // 2, 1) * sines


def turned_back(values, cosines, sines):
    return values * cosines - pltpu.roll(values, HEAD_DIM // 2, 1) * sines


def mask_scores(spans_col, places_row, bias):
    place = places_row[0:1, :]

    def body(r):
        allowed = (place >= spans_col[r, 0:1]) & (place <= spans_col[r, 1:2])
        bias[r, :] = jnp.where(allowed, 0.0, -1e30)

    tiles(bias.shape[0] // 128, 128, body)


def attend_kernel(
    qkv, invs, gains, cosines, sines, spans, places, w_out,
    q_out, k_out, v_out, attended, lse, branch_own, bias,
    part, from_sib, from_side, total, send_sem, recv_sem,
):
    me = here()
    greet([across_y(me), sibling(me)])
    rows, local = q_out.shape
    mask_scores(spans, places, bias)

    def prepare(r):
        v_out[r, :] = qkv[r, 2 * local : 3 * local].astype(jnp.bfloat16)
        for h in range(local // HEAD_DIM):
            c = slice(h * HEAD_DIM, (h + 1) * HEAD_DIM)
            for i, target in ((0, q_out), (1, k_out)):
                normed = qkv[r, i * local + h * HEAD_DIM : i * local + (h + 1) * HEAD_DIM]
                normed = normed * invs[r, i : i + 1] * gains[i : i + 1, c]
                target[r, c] = rotated(normed, cosines[r, :], sines[r, :]).astype(jnp.bfloat16)

    tiles(rows // 128, 128, prepare)
    scale = 1.0 / math.sqrt(HEAD_DIM)
    for h in range(local // HEAD_DIM):
        c = slice(h * HEAD_DIM, (h + 1) * HEAD_DIM)

        def one(r, h=h, c=c):
            scores = dot32(q_out[r, c], k_out[:, c], NT) * scale + bias[r, :]
            top = jnp.max(scores, axis=-1, keepdims=True)
            log_total = top + jnp.log(jnp.sum(jnp.exp(scores - top), axis=-1, keepdims=True))
            lse[h, r, :] = log_total
            probs = jnp.exp(scores - log_total).astype(jnp.bfloat16)
            attended[r, c] = dot32(probs, v_out[:, c], NN).astype(jnp.bfloat16)

        tiles(rows // 128, 128, one)

    def make(column):
        own = branch_own.shape[0]
        places_of = pl.ds(pl.multiple_of(column * own, own), own)
        span = w_out.shape[2]
        for e in range(w_out.shape[0]):
            part[column, :, e * span : (e + 1) * span] = dot32(
                attended[places_of, :], w_out[e], NN
            ).astype(jnp.bfloat16)

    sum_tensor_into(make, part, branch_own, from_sib, from_side, total, Line(send_sem, recv_sem))


def attend(qkv, invs, gains, cosines, sines, spans, places, w_out):
    rows, local = qkv.shape[0], qkv.shape[1] // 3
    block = (rows // 4, w_out.shape[0] * w_out.shape[2])
    bf16, f32, sds = jnp.bfloat16, jnp.float32, jax.ShapeDtypeStruct
    return pl.pallas_call(
        attend_kernel,
        out_shape=[sds((rows, local), bf16)] * 4
        + [
            sds((local // HEAD_DIM, rows, 1), f32),
            sds(block, f32),
        ],
        in_specs=[IN_VMEM] * 8,
        out_specs=[IN_VMEM] * 6,
        scratch_shapes=[pltpu.VMEM((rows, rows), f32)] + sum_tensor_scratch(block),
        compiler_params=pltpu.CompilerParams(
            collective_id=9, has_side_effects=True, vmem_limit_bytes=62 * 2**20
        ),
        cost_estimate=cost_of(15),
        name="attend",
    )(qkv, invs, gains, cosines, sines, spans, places, w_out)


def attend_back_kernel(
    grad, w_out_far, q_far, k_far, v_far, lse, qkv_far, invs, gains, cosines, sines, spans, places,
    hat_grads, value_grad, dots, d_gains, bias, out_grad, probs_low, score_grad,
    w_out, q, k, v, qkv, sems,
):
    rows, local = q.shape
    fetched = [
        pltpu.make_async_copy(far, close, sems.at[i])
        for i, (far, close) in enumerate(
            ((w_out_far, w_out), (q_far, q), (k_far, k), (v_far, v), (qkv_far, qkv))
        )
    ]
    for copy in fetched:
        copy.start()
    mask_scores(spans, places, bias)
    span = w_out.shape[2]
    fetched[0].wait()

    def project(r):
        total = None
        for e in range(w_out.shape[0]):
            term = dot32(grad[r, e * span : (e + 1) * span], w_out[e], NT)
            total = term if total is None else total + term
        out_grad[r, :] = total.astype(jnp.bfloat16)

    tiles(rows // 128, 128, project)
    for copy in fetched[1:]:
        copy.wait()
    scale = 1.0 / math.sqrt(HEAD_DIM)
    dots[...] = jnp.zeros_like(dots)
    for h in range(local // HEAD_DIM):
        c = slice(h * HEAD_DIM, (h + 1) * HEAD_DIM)

        def one(r, h=h, c=c):
            scores = dot32(q[r, c], k[:, c], NT) * scale + bias[r, :]
            probs = jnp.exp(scores - lse[h, r, :])
            prob_grad = dot32(out_grad[r, c], v[:, c], NT)
            delta = jnp.sum(probs * prob_grad, axis=-1, keepdims=True)
            probs_low[r, :] = probs.astype(jnp.bfloat16)
            score_grad[r, :] = (probs * (prob_grad - delta) * scale).astype(jnp.bfloat16)

        tiles(rows // 128, 128, one)
        value_grad[:, c] = dot32(probs_low[...], out_grad[:, c], TN).astype(jnp.bfloat16)
        for i, turned in (
            (0, dot32(score_grad[...], k[:, c], NN)),
            (1, dot32(score_grad[...], q[:, c], TN)),
        ):
            at = slice(i * local + h * HEAD_DIM, i * local + (h + 1) * HEAD_DIM)
            norm_grad = turned_back(turned, cosines[...], sines[...])
            hat = qkv[:, at] * invs[:, i : i + 1]
            hat_grad = norm_grad * gains[i : i + 1, c]
            hat_grads[:, at] = hat_grad
            d_gains[i : i + 1, c] = jnp.sum(norm_grad * hat, axis=0, keepdims=True)
            dots[i] += jnp.sum(hat_grad * hat, axis=-1, keepdims=True)


def attend_back(grad, w_out, q, k, v, lse, qkv, invs, gains, cosines, sines, spans, places):
    rows, local = q.shape
    bf16, f32, sds = jnp.bfloat16, jnp.float32, jax.ShapeDtypeStruct
    return pl.pallas_call(
        attend_back_kernel,
        out_shape=[
            sds((rows, 2 * local), f32),
            sds((rows, local), bf16),
            sds((2, rows, 1), f32),
            sds((2, local), f32),
        ],
        in_specs=[IN_VMEM] + [ANY] * 4 + [IN_VMEM, ANY] + [IN_VMEM] * 6,
        out_specs=[IN_VMEM] * 4,
        scratch_shapes=[
            pltpu.VMEM((rows, rows), f32),
            pltpu.VMEM((rows, local), bf16),
            pltpu.VMEM((rows, rows), bf16),
            pltpu.VMEM((rows, rows), bf16),
        ]
        + [pltpu.VMEM(a.shape, a.dtype) for a in (w_out, q, k, v, qkv)]
        + [DMA((5,))],
        compiler_params=pltpu.CompilerParams(vmem_limit_bytes=62 * 2**20),
        cost_estimate=cost_of(5),
        name="attend_back",
    )(grad, w_out, q, k, v, lse, qkv, invs, gains, cosines, sines, spans, places)


def sum_few_kernel(part, out, shares, send_sem, recv_sem):
    me = here()
    peers = [across_y(sibling(me)), across_y(me), sibling(me)]
    greet(peers)
    line = Line(send_sem, recv_sem)
    for i, peer in enumerate(peers):
        line.send(part, shares.at[me[1]], i, i, peer)
    shares[me[1]] = part[...]
    for i, peer in enumerate(peers):
        line.wait(shares.at[peer[1]], i, peer)
    out[...] = (shares[0] + shares[1]) + (shares[2] + shares[3])
    line.finish()


def sum_few(rows):
    block = (rows.size // 128, 128)
    return pl.pallas_call(
        sum_few_kernel,
        out_shape=jax.ShapeDtypeStruct(block, jnp.float32),
        in_specs=[IN_VMEM],
        out_specs=IN_VMEM,
        scratch_shapes=[pltpu.VMEM((4,) + block, jnp.float32), DMA((3,)), DMA((3,))],
        compiler_params=pltpu.CompilerParams(
            collective_id=8, has_side_effects=True, vmem_limit_bytes=2**20
        ),
        cost_estimate=cost_of(1),
        name="sum_few",
    )(rows.reshape(block)).reshape(rows.shape)


BOTH = (EXPERT, TENSOR)


def dot32(left, right, dims):
    return lax.dot_general(left, right, (dims, ((), ())), preferred_element_type=jnp.float32)


NN = ((1,), (0,))
NT = ((1,), (1,))
TN = ((0,), (0,))


def rms_inv(values):
    return lax.rsqrt(jnp.mean(values * values, axis=-1, keepdims=True) + NORM_EPS)


def dense_body(
    tokens,
    attn_gain,
    w_query,
    w_key,
    w_value,
    w_out,
    query_gain,
    key_gain,
    ffn_gain,
    w_router,
    w_gate,
    w_up,
    w_down,
    doc_ids,
    routes,
    deal,
    out_grad,
):
    rows, width = tokens.shape
    parts = lax.axis_size(TENSOR)
    blocks = lax.axis_size(EXPERT)
    column = lax.axis_index(TENSOR)
    block = lax.axis_index(EXPERT)
    own = rows // parts
    share = rows // blocks
    piece = share // parts
    bf16, f32 = jnp.bfloat16, jnp.float32

    def reorder(per_place):
        grid = per_place.reshape((blocks, parts, piece) + per_place.shape[1:])
        return jnp.swapaxes(grid, 0, 1).reshape(per_place.shape)

    local_width = w_query.shape[1]
    head_count = local_width // HEAD_DIM
    expert_count = w_router.shape[1]
    qkv_own = jnp.concatenate([w_query, w_key, w_value], axis=1)
    gain_stack = jnp.stack([attn_gain, query_gain, key_gain, ffn_gain], axis=1)
    small_own = jnp.concatenate([w_router, gain_stack], axis=1)
    small_own = jnp.pad(small_own, ((0, 0), (0, 128 - small_own.shape[1])))
    deal_grid = deal.reshape(blocks, blocks, parts, piece)
    picks = lax.dynamic_slice(deal_grid, (0, block, column, 0), (blocks, 1, 1, piece)).reshape(-1)
    picks = picks - block * rows
    inputs, dealt_grads, qkv_full, out_full, small_full = start_exchange(
        tokens[picks].reshape(blocks, piece, width),
        out_grad[picks].reshape(blocks, piece, width),
        qkv_own,
        w_out,
        small_own,
    )
    own_low = lax.dynamic_slice_in_dim(inputs, column, 1, 0).reshape(own, width)
    inputs = inputs.reshape(rows, width).astype(f32)
    qkv_full = qkv_full.reshape(width, -1)
    small_full = small_full.reshape(width, -1)
    router_full = small_full[:, :expert_count]
    gain_full = small_full[:, expert_count : expert_count + 4].T.astype(f32)
    gain_attn, gain_ffn = gain_full[0], gain_full[3]
    gain_query = lax.dynamic_slice_in_dim(gain_full[1], column * local_width, local_width)
    gain_key = lax.dynamic_slice_in_dim(gain_full[2], column * local_width, local_width)
    own_grad_low = dealt_grads.reshape(own, width)
    grads_all = lax.all_gather(own_grad_low, BOTH, axis=0, tiled=True)
    own_in = own_low.astype(f32)
    own_grad = own_grad_low.astype(f32)

    scale = 1.0 / math.sqrt(HEAD_DIM)
    normed = (inputs * rms_inv(inputs) * gain_attn).astype(bf16)
    qkv = dot32(normed, qkv_full, NN)
    query_pre = qkv[:, :local_width]
    key_pre = qkv[:, local_width : 2 * local_width]
    squares = sum_few(
        jnp.stack([jnp.sum(query_pre * query_pre, axis=-1), jnp.sum(key_pre * key_pre, axis=-1)])
    )
    cosines, sines, starts = rope_tables(doc_ids, HEAD_DIM)
    cosines = reorder(jnp.concatenate([cosines, cosines], axis=1))
    sines = reorder(jnp.concatenate([-sines, sines], axis=1))
    positions = reorder(jnp.arange(rows, dtype=jnp.int32))
    spans = jnp.stack([reorder(starts), positions], axis=1)
    places = jnp.broadcast_to(positions[None], (8, rows))
    invs = lax.rsqrt(squares / width + NORM_EPS).T
    gains = jnp.stack([gain_query, gain_key])
    query_rot, key_rot, value_rows, attended, log_total, branch_own = attend(
        qkv, invs, gains, cosines, sines, spans, places, out_full
    )

    residual = own_in + branch_own
    resid_inv = rms_inv(residual)
    resid_hat = residual * resid_inv
    ffn_in = (resid_hat * gain_ffn).astype(bf16)
    logits = dot32(ffn_in, router_full, NN)
    router_probs = jax.nn.softmax(logits, axis=-1)
    local_experts = w_gate.shape[0]
    own_routes = lax.dynamic_slice(
        routes.reshape(blocks, parts, piece, -1),
        (0, column, 0, 0),
        (blocks, 1, piece, routes.shape[1]),
    ).reshape(own, -1)
    expert_ids = jnp.arange(expert_count, dtype=jnp.int32)
    routed = jnp.any(own_routes[:, :, None] == expert_ids[None, None, :], axis=1)
    gates_own = jnp.where(routed, router_probs, 0.0)

    hidden_width = w_gate.shape[2]
    joined_weight = jnp.concatenate(
        [w_gate[i] for i in range(local_experts)] + [w_up[i] for i in range(local_experts)], axis=1
    )
    down_weight = w_down.reshape(local_experts * hidden_width, width)
    rows_all, gates_all, pre_all, gated_all, mixed = experts_forward(
        ffn_in, gates_own.T, joined_weight, down_weight
    )
    mix_own, joined_grad, row_terms, gate_grads = experts_backward(
        mixed, grads_all, pre_all, gates_all, joined_weight, down_weight
    )
    output_own = (residual + mix_own).astype(bf16)
    row_own, gate_grad_own, d_w_gate, d_w_up, d_w_down = experts_weights(
        row_terms, gate_grads, rows_all, grads_all, joined_grad, gated_all
    )
    gate_grad_own = gate_grad_own.T
    d_w_down = d_w_down.reshape(w_down.shape)

    prob_grad = jnp.where(routed, gate_grad_own, 0.0)
    logit_grad = (
        router_probs * (prob_grad - jnp.sum(router_probs * prob_grad, axis=-1, keepdims=True))
    ).astype(bf16)
    d_router = dot32(ffn_in, logit_grad, TN)
    ffn_grad = row_own + dot32(logit_grad, router_full, NT)
    d_ffn_gain = jnp.sum(ffn_grad * resid_hat, axis=0)
    scaled_ffn = ffn_grad * gain_ffn
    resid_grad = own_grad + resid_inv * (
        scaled_ffn - resid_hat * jnp.mean(scaled_ffn * resid_hat, axis=-1, keepdims=True)
    )
    branch_grad = gather_tensor(resid_grad.astype(bf16))

    branch_cols = branch_grad.reshape(rows, blocks, width // blocks)
    d_wo = jnp.einsum("rk,red->ekd", attended, branch_cols, preferred_element_type=f32).astype(bf16)
    d_wo, branch_grad = lax.optimization_barrier((d_wo, branch_grad))
    sum_wo = lax.psum_scatter(d_wo, EXPERT, scatter_dimension=0, tiled=False)
    hat_grads, value_grad, dots, d_gains = attend_back(
        branch_grad, out_full, query_rot, key_rot, value_rows, log_total,
        qkv, invs, gains, cosines, sines, spans, places,
    )
    d_query_gain, d_key_gain = d_gains[0], d_gains[1]
    dots = sum_few(dots.reshape(2, rows)) / width

    def norm_back(i):
        part = slice(i * local_width, (i + 1) * local_width)
        inv = invs[:, i : i + 1]
        return (inv * (hat_grads[:, part] - qkv[:, part] * inv * dots[i][:, None])).astype(bf16)

    query_grad, key_grad = norm_back(0), norm_back(1)
    qkv_grad = jnp.concatenate([query_grad, key_grad, value_grad], axis=1)
    normed_grad = input_sum(qkv_grad, qkv_full)
    d_qkv = dot32(normed, qkv_grad, TN).astype(bf16)
    d_qkv, sum_wo = lax.optimization_barrier((d_qkv, sum_wo))

    own_inv = rms_inv(own_in)
    own_hat = own_in * own_inv
    d_attn_gain = jnp.sum(normed_grad * own_hat, axis=0)
    scaled_attn = normed_grad * gain_attn
    input_grad = resid_grad + own_inv * (
        scaled_attn - own_hat * jnp.mean(scaled_attn * own_hat, axis=-1, keepdims=True)
    )

    def widen(slots):
        return lax.dynamic_update_slice_in_dim(
            jnp.zeros((width,), f32), slots, column * local_width, 0
        )

    small = jnp.concatenate(
        [
            d_router.T,
            jnp.stack([d_attn_gain, widen(d_query_gain), widen(d_key_gain), d_ffn_gain]),
        ]
    )
    small = jnp.pad(small, ((0, 24 - small.shape[0]), (0, 0)))
    small = jnp.swapaxes(small.reshape(24, blocks, -1), 0, 1)

    back_out, back_in, sum_qkv, small = last_exchange(
        output_own.reshape(blocks, piece, width),
        input_grad.astype(bf16).reshape(blocks, piece, width),
        d_qkv.reshape(blocks, -1, d_qkv.shape[1]),
        small,
    )
    sum_router = small[:expert_count].T
    sum_gains = small[expert_count:]
    came = lax.dynamic_slice(deal_grid, (0, block, 0, 0), (blocks, 1, parts, piece))
    came = jnp.swapaxes(came.reshape(blocks, parts, piece), 0, 1).reshape(-1) - block * rows
    chooser = (jnp.arange(rows, dtype=jnp.int32)[:, None] == came[None, :]).astype(bf16)
    output = dot32(chooser, back_out.reshape(rows, width), NN).astype(bf16)
    d_tokens = dot32(chooser, back_in.reshape(rows, width), NN).astype(bf16)
    return (
        output,
        d_tokens,
        sum_gains[0],
        sum_qkv[:, :local_width],
        sum_qkv[:, local_width : 2 * local_width],
        sum_qkv[:, 2 * local_width :],
        sum_wo.astype(f32),
        sum_gains[1],
        sum_gains[2],
        sum_gains[3],
        sum_router,
        d_w_gate,
        d_w_up,
        d_w_down,
    )


def pick_body(*args):
    routes, experts = args[14], args[9].shape[1]
    mesh_fits = (lax.axis_size(EXPERT), lax.axis_size(TENSOR)) == (8, 4)
    body = dense_body if mesh_fits and experts <= 2 * routes.shape[1] else routed_body
    return body(*args)


def solution(mesh):
    in_specs = (
        P(EXPERT, None),
        P(EXPERT),
        P(EXPERT, TENSOR),
        P(EXPERT, TENSOR),
        P(EXPERT, TENSOR),
        P(TENSOR, EXPERT),
        P(EXPERT),
        P(EXPERT),
        P(EXPERT),
        P(EXPERT, None),
        P(EXPERT, None, TENSOR),
        P(EXPERT, None, TENSOR),
        P(EXPERT, TENSOR, None),
        P(EXPERT),
        P(EXPERT, None),
        P(),
        P(EXPERT, None),
    )
    out_specs = (
        P(EXPERT, None),
        P(EXPERT, None),
        P(EXPERT),
        P(EXPERT, TENSOR),
        P(EXPERT, TENSOR),
        P(EXPERT, TENSOR),
        P(TENSOR, EXPERT),
        P(EXPERT),
        P(EXPERT),
        P(EXPERT),
        P(EXPERT, None),
        P(EXPERT, None, TENSOR),
        P(EXPERT, None, TENSOR),
        P(EXPERT, TENSOR, None),
    )
    return jax.shard_map(pick_body, mesh=mesh, in_specs=in_specs, out_specs=out_specs, check_vma=False)
```

```python
import functools
import math

import jax
import jax.numpy as jnp
from jax import lax
from jax.experimental import pallas as pl
from jax.experimental.pallas import tpu as pltpu
from jax.sharding import PartitionSpec as P

HEAD_DIM = 128
EXPERT, TENSOR = "expert", "tensor"


NORM_EPS = 1e-05
ROPE_BASE = 10000.0


def rope_tables(documents, head_size):
    row_count = documents.shape[0]
    positions = jnp.arange(row_count, dtype=jnp.int32)
    new_doc = jnp.concatenate(
        [jnp.ones((1,), jnp.int32), (documents[1:] != documents[:-1]).astype(jnp.int32)]
    )
    starts = lax.cummax(jnp.where(new_doc > 0, positions, 0), axis=0)
    places = (positions - starts).astype(jnp.float32)
    half_dim = head_size // 2
    frequency = jnp.exp(
        jnp.arange(half_dim, dtype=jnp.float32) * (-2.0 * math.log(ROPE_BASE) / head_size)
    )
    angles = places[:, None] * frequency[None, :]
    return (jnp.cos(angles), jnp.sin(angles), starts)


def rotate(values, cosines, sines):
    half_dim = values.shape[-1] // 2
    first_half = values[..., :half_dim]
    second_half = values[..., half_dim:]
    cos_rows = cosines[:, None, :]
    sin_rows = sines[:, None, :]
    return jnp.concatenate(
        [
            first_half * cos_rows - second_half * sin_rows,
            second_half * cos_rows + first_half * sin_rows,
        ],
        axis=-1,
    )


def unrotate(grads_in, cosines, sines):
    half_dim = grads_in.shape[-1] // 2
    first_half = grads_in[..., :half_dim]
    second_half = grads_in[..., half_dim:]
    cos_rows = cosines[:, None, :]
    sin_rows = sines[:, None, :]
    return jnp.concatenate(
        [
            first_half * cos_rows + second_half * sin_rows,
            second_half * cos_rows - first_half * sin_rows,
        ],
        axis=-1,
    )


def to_experts(rows):
    return lax.all_to_all(rows, EXPERT, split_axis=0, concat_axis=0, tiled=True)


def from_experts(rows):
    return lax.all_to_all(rows, EXPERT, split_axis=0, concat_axis=0, tiled=True)


def hidden_sums(terms):
    return lax.psum_scatter(terms, TENSOR, scatter_dimension=3, tiled=True)


def routed_body(
    tokens,
    attn_gain,
    w_query,
    w_key,
    w_value,
    w_out,
    query_gain,
    key_gain,
    ffn_gain,
    w_router,
    w_gate,
    w_up,
    w_down,
    doc_ids,
    routes,
    deal,
    out_grad,
):
    row_count, width = tokens.shape
    tensor_parts = lax.axis_size(TENSOR)
    expert_parts = lax.axis_size(EXPERT)
    column = lax.axis_index(TENSOR)
    device_idx = lax.axis_index(EXPERT)
    quarter = width // tensor_parts
    share_rows = row_count // expert_parts
    deal_rows = lax.dynamic_slice_in_dim(
        deal.reshape(expert_parts, row_count), device_idx * share_rows, share_rows, 1
    )
    local_pick = deal_rows - device_idx * row_count
    dealt_tokens, dealt_grad = (
        lax.all_to_all(tokens[local_pick], EXPERT, split_axis=0, concat_axis=0, tiled=True),
        lax.all_to_all(out_grad[local_pick], EXPERT, split_axis=0, concat_axis=0, tiled=True),
    )
    dealt_tokens = dealt_tokens.reshape(row_count, width)
    dealt_grad = dealt_grad.reshape(row_count, width)
    gain_stack = jnp.stack([attn_gain, query_gain, key_gain, ffn_gain])
    wq_full, wk_full, wv_full, wo_full, router_full, gain_full = (
        lax.all_gather(w_query, EXPERT, axis=0, tiled=True),
        lax.all_gather(w_key, EXPERT, axis=0, tiled=True),
        lax.all_gather(w_value, EXPERT, axis=0, tiled=True),
        lax.all_gather(w_out, EXPERT, axis=1, tiled=True),
        lax.all_gather(w_router, EXPERT, axis=0, tiled=True),
        lax.all_gather(gain_stack, EXPERT, axis=1, tiled=True),
    )
    local_width = wq_full.shape[1]
    head_count = local_width // HEAD_DIM
    gain_attn = gain_full[0].astype(jnp.float32)
    gain_query = lax.dynamic_slice_in_dim(
        gain_full[1].astype(jnp.float32), column * local_width, local_width
    )
    gain_key = lax.dynamic_slice_in_dim(
        gain_full[2].astype(jnp.float32), column * local_width, local_width
    )
    gain_ffn = gain_full[3].astype(jnp.float32)
    scale = 1.0 / math.sqrt(HEAD_DIM)
    inputs = dealt_tokens.astype(jnp.float32)
    input_inv = lax.rsqrt(jnp.mean(inputs * inputs, axis=-1, keepdims=True) + NORM_EPS)
    input_hat = inputs * input_inv
    normed = (input_hat * gain_attn).astype(jnp.bfloat16)
    query_pre = jnp.dot(normed, wq_full, preferred_element_type=jnp.float32)
    key_pre = jnp.dot(normed, wk_full, preferred_element_type=jnp.float32)
    value_rows = (
        jnp.dot(normed, wv_full, preferred_element_type=jnp.float32)
        .astype(jnp.bfloat16)
        .reshape(row_count, head_count, HEAD_DIM)
    )
    query_sq, key_sq = lax.psum(
        (jnp.sum(query_pre * query_pre, axis=-1), jnp.sum(key_pre * key_pre, axis=-1)), TENSOR
    )
    query_inv = lax.rsqrt(query_sq / width + NORM_EPS)[:, None]
    key_inv = lax.rsqrt(key_sq / width + NORM_EPS)[:, None]
    query_hat = query_pre * query_inv
    key_hat = key_pre * key_inv
    cosines, sines, _ = rope_tables(doc_ids, HEAD_DIM)
    query_rot = rotate(
        (query_hat * gain_query).reshape(row_count, head_count, HEAD_DIM), cosines, sines
    ).astype(jnp.bfloat16)
    key_rot = rotate(
        (key_hat * gain_key).reshape(row_count, head_count, HEAD_DIM), cosines, sines
    ).astype(jnp.bfloat16)
    positions = jnp.arange(row_count, dtype=jnp.int32)
    allowed = (doc_ids[:, None] == doc_ids[None, :]) & (positions[None, :] <= positions[:, None])

    def masked_scores():
        raw_scores = jnp.einsum(
            "qhd,khd->hqk", query_rot, key_rot, preferred_element_type=jnp.float32
        )
        return jnp.where(allowed[None], raw_scores * scale, -1e30)

    scores = masked_scores()
    top_score = jnp.max(scores, axis=-1, keepdims=True)
    log_total = top_score + jnp.log(jnp.sum(jnp.exp(scores - top_score), axis=-1, keepdims=True))
    weights = jnp.exp(scores - log_total).astype(jnp.bfloat16)
    attended = (
        jnp.einsum("hqk,khd->qhd", weights, value_rows, preferred_element_type=jnp.float32)
        .astype(jnp.bfloat16)
        .reshape(row_count, local_width)
    )
    branch = lax.psum(jnp.dot(attended, wo_full, preferred_element_type=jnp.float32), TENSOR)
    residual = inputs + branch
    resid_inv = lax.rsqrt(jnp.mean(residual * residual, axis=-1, keepdims=True) + NORM_EPS)
    resid_hat = residual * resid_inv
    ffn_in = (resid_hat * gain_ffn).astype(jnp.bfloat16)
    logits = jnp.dot(ffn_in, router_full, preferred_element_type=jnp.float32)
    router_probs = jax.nn.softmax(logits, axis=-1)
    expert_count = router_full.shape[1]
    top_count = routes.shape[1]
    local_experts = expert_count // expert_parts
    capacity = tensor_parts * max(
        1,
        (row_count * top_count + expert_count * tensor_parts - 1) // (expert_count * tensor_parts),
        row_count * top_count * 5 // (4 * expert_count * tensor_parts),
    )
    expert_ids = jnp.arange(expert_count, dtype=jnp.int32)
    route_match = routes[:, :, None] == expert_ids[None, None, :]
    gate_probs = jnp.sum(jnp.where(route_match, router_probs[:, None, :], 0.0), axis=-1)
    flat_routes = routes.reshape(-1)
    onehot = (flat_routes[:, None] == expert_ids[None, :]).astype(jnp.int32)
    slot_rank = jnp.sum((jnp.cumsum(onehot, axis=0) - onehot) * onehot, axis=-1)
    row_ids = flat_routes * capacity + slot_rank
    token_ids = jnp.arange(row_count * top_count, dtype=jnp.int32) // top_count
    slot_token = (
        jnp.full((expert_count * capacity,), row_count, jnp.int32).at[row_ids].set(token_ids)
    )
    slot_gates = (
        jnp.zeros((expert_count * capacity,), jnp.float32).at[row_ids].set(gate_probs.reshape(-1))
    )
    pick_rows = row_ids.reshape(row_count, top_count)
    padded_in = jnp.concatenate([ffn_in, jnp.zeros((1, width), jnp.bfloat16)], axis=0)
    grad_full = dealt_grad.astype(jnp.float32)
    grad_padded = jnp.concatenate([grad_full, jnp.zeros((1, width), jnp.float32)], axis=0)
    received = to_experts(
        padded_in[slot_token].reshape(expert_parts, local_experts, capacity, width)
    )
    gate_pre = jnp.einsum("secd,edf->secf", received, w_gate, preferred_element_type=jnp.float32)
    up_pre = jnp.einsum("secd,edf->secf", received, w_up, preferred_element_type=jnp.float32)
    sigmoid_gate = jax.nn.sigmoid(gate_pre)
    silu_gate = gate_pre * sigmoid_gate
    hidden = (silu_gate * up_pre).astype(jnp.bfloat16)
    partial_out = jnp.einsum("secf,efd->secd", hidden, w_down, preferred_element_type=jnp.float32)
    own_columns = hidden_sums(partial_out).astype(jnp.bfloat16)
    returned = from_experts(own_columns).reshape(expert_count * capacity, quarter)
    chosen = returned[pick_rows].astype(jnp.float32)
    mix_own = jnp.sum(gate_probs[:, :, None] * chosen, axis=1)
    mix_part = lax.dynamic_update_slice_in_dim(
        jnp.zeros((row_count, width), jnp.float32), mix_own, column * quarter, 1
    )
    grad_own = lax.dynamic_slice_in_dim(grad_full, column * quarter, quarter, 1)
    gate_grad_part = jnp.sum(grad_own[:, None, :] * chosen, axis=-1)
    send_grad = (
        (grad_padded[slot_token] * slot_gates[:, None])
        .astype(jnp.bfloat16)
        .reshape(expert_parts, local_experts, capacity, width)
    )
    recv_grad = to_experts(send_grad)
    d_w_down = jnp.einsum("secf,secd->efd", hidden, recv_grad, preferred_element_type=jnp.float32)
    hidden_grad = jnp.einsum(
        "secd,efd->secf", recv_grad, w_down, preferred_element_type=jnp.float32
    )
    gate_grad_pre = (
        hidden_grad * up_pre * sigmoid_gate * (1.0 + gate_pre * (1.0 - sigmoid_gate))
    ).astype(jnp.bfloat16)
    up_grad_pre = (hidden_grad * silu_gate).astype(jnp.bfloat16)
    d_w_gate = jnp.einsum(
        "secd,secf->edf", received, gate_grad_pre, preferred_element_type=jnp.float32
    )
    d_w_up = jnp.einsum("secd,secf->edf", received, up_grad_pre, preferred_element_type=jnp.float32)
    joined_grad = jnp.concatenate([gate_grad_pre, up_grad_pre], axis=-1)
    joined_weight = jnp.concatenate([w_gate, w_up], axis=-1)
    row_terms = jnp.einsum(
        "secf,edf->secd", joined_grad, joined_weight, preferred_element_type=jnp.float32
    )
    row_own = hidden_sums(row_terms).astype(jnp.bfloat16)
    row_back = from_experts(row_own).reshape(expert_count * capacity, quarter)
    ffn_grad_own = jnp.sum(row_back[pick_rows].astype(jnp.float32), axis=1)
    placed = lax.dynamic_update_slice_in_dim(
        jnp.zeros((row_count, width), jnp.float32), ffn_grad_own, column * quarter, 1
    )
    ffn_grad_rows, gate_grad, mix_total = lax.psum((placed, gate_grad_part, mix_part), TENSOR)
    output = (residual + mix_total).astype(jnp.bfloat16)
    prob_grad = jnp.sum(jnp.where(route_match, gate_grad[:, :, None], 0.0), axis=1)
    logit_grad = (
        router_probs * (prob_grad - jnp.sum(router_probs * prob_grad, axis=-1, keepdims=True))
    ).astype(jnp.bfloat16)
    d_router = jnp.einsum("rd,re->de", ffn_in, logit_grad, preferred_element_type=jnp.float32)
    ffn_grad = ffn_grad_rows + jnp.einsum(
        "re,de->rd", logit_grad, router_full, preferred_element_type=jnp.float32
    )
    d_ffn_gain = jnp.sum(ffn_grad * resid_hat, axis=0)
    scaled_ffn = ffn_grad * gain_ffn
    resid_grad = grad_full + resid_inv * (
        scaled_ffn - resid_hat * jnp.mean(scaled_ffn * resid_hat, axis=-1, keepdims=True)
    )
    branch_grad = resid_grad.astype(jnp.bfloat16)
    d_wo = jnp.einsum("rk,rd->kd", attended, branch_grad, preferred_element_type=jnp.float32)
    attended_grad = (
        jnp.einsum("rd,kd->rk", branch_grad, wo_full, preferred_element_type=jnp.float32)
        .astype(jnp.bfloat16)
        .reshape(row_count, head_count, HEAD_DIM)
    )
    probs_again = jnp.exp(masked_scores() - log_total)
    prob_grads = jnp.einsum(
        "qhd,khd->hqk", attended_grad, value_rows, preferred_element_type=jnp.float32
    )
    value_grad = (
        jnp.einsum(
            "hqk,qhd->khd",
            probs_again.astype(jnp.bfloat16),
            attended_grad,
            preferred_element_type=jnp.float32,
        )
        .astype(jnp.bfloat16)
        .reshape(row_count, local_width)
    )
    row_delta = jnp.sum(probs_again * prob_grads, axis=-1, keepdims=True)
    score_grad = (probs_again * (prob_grads - row_delta) * scale).astype(jnp.bfloat16)
    query_rot_grad = jnp.einsum(
        "hqk,khd->qhd", score_grad, key_rot, preferred_element_type=jnp.float32
    )
    key_rot_grad = jnp.einsum(
        "hqk,qhd->khd", score_grad, query_rot, preferred_element_type=jnp.float32
    )
    query_norm_grad = unrotate(query_rot_grad, cosines, sines).reshape(row_count, local_width)
    key_norm_grad = unrotate(key_rot_grad, cosines, sines).reshape(row_count, local_width)
    query_hat_grad = query_norm_grad * gain_query
    key_hat_grad = key_norm_grad * gain_key
    gain_pieces = jnp.stack(
        [jnp.sum(query_norm_grad * query_hat, axis=0), jnp.sum(key_norm_grad * key_hat, axis=0)]
    )
    gain_parts = lax.dynamic_update_slice_in_dim(
        jnp.zeros((2, width), jnp.float32), gain_pieces, column * local_width, 1
    )
    query_dot, key_dot, qk_gains = lax.psum(
        (
            jnp.sum(query_hat_grad * query_hat, axis=-1),
            jnp.sum(key_hat_grad * key_hat, axis=-1),
            gain_parts,
        ),
        TENSOR,
    )
    query_grad = (query_inv * (query_hat_grad - query_hat * (query_dot / width)[:, None])).astype(
        jnp.bfloat16
    )
    key_grad = (key_inv * (key_hat_grad - key_hat * (key_dot / width)[:, None])).astype(
        jnp.bfloat16
    )
    d_wq = jnp.einsum("rd,rk->dk", normed, query_grad, preferred_element_type=jnp.float32)
    d_wk = jnp.einsum("rd,rk->dk", normed, key_grad, preferred_element_type=jnp.float32)
    d_wv = jnp.einsum("rd,rk->dk", normed, value_grad, preferred_element_type=jnp.float32)
    input_terms = jnp.einsum("rk,dk->rd", query_grad, wq_full, preferred_element_type=jnp.float32)
    input_terms = input_terms + jnp.einsum(
        "rk,dk->rd", key_grad, wk_full, preferred_element_type=jnp.float32
    )
    input_terms = input_terms + jnp.einsum(
        "rk,dk->rd", value_grad, wv_full, preferred_element_type=jnp.float32
    )
    normed_grad = lax.psum(input_terms, TENSOR)
    d_attn_part = jnp.sum(normed_grad * input_hat, axis=0)
    scaled_attn = normed_grad * gain_attn
    input_grad = resid_grad + input_inv * (
        scaled_attn - input_hat * jnp.mean(scaled_attn * input_hat, axis=-1, keepdims=True)
    )
    dealt_dtokens = input_grad.astype(jnp.bfloat16)
    gain_grads = jnp.stack([d_attn_part, qk_gains[0], qk_gains[1], d_ffn_gain])
    sum_wq, sum_wk, sum_wv, sum_wo, sum_router, sum_gains = (
        lax.psum_scatter(d_wq, EXPERT, scatter_dimension=0, tiled=True),
        lax.psum_scatter(d_wk, EXPERT, scatter_dimension=0, tiled=True),
        lax.psum_scatter(d_wv, EXPERT, scatter_dimension=0, tiled=True),
        lax.psum_scatter(d_wo, EXPERT, scatter_dimension=1, tiled=True),
        lax.psum_scatter(d_router, EXPERT, scatter_dimension=0, tiled=True),
        lax.psum_scatter(gain_grads, EXPERT, scatter_dimension=1, tiled=True),
    )
    back_out, back_dtok = (
        lax.all_to_all(
            output.reshape(expert_parts, share_rows, width),
            EXPERT,
            split_axis=0,
            concat_axis=0,
            tiled=True,
        ),
        lax.all_to_all(
            dealt_dtokens.reshape(expert_parts, share_rows, width),
            EXPERT,
            split_axis=0,
            concat_axis=0,
            tiled=True,
        ),
    )
    flat_pick = local_pick.reshape(-1)
    output_rows = (
        jnp.zeros((row_count, width), jnp.bfloat16)
        .at[flat_pick]
        .set(back_out.reshape(row_count, width))
    )
    d_tokens = (
        jnp.zeros((row_count, width), jnp.bfloat16)
        .at[flat_pick]
        .set(back_dtok.reshape(row_count, width))
    )
    return (
        output_rows,
        d_tokens,
        sum_gains[0],
        sum_wq,
        sum_wk,
        sum_wv,
        sum_wo,
        sum_gains[1],
        sum_gains[2],
        sum_gains[3],
        sum_router,
        d_w_gate,
        d_w_up,
        d_w_down,
    )


MESH_ID = pl.DeviceIdType.MESH
ANY = pl.BlockSpec(memory_space=pl.ANY)
IN_VMEM = pl.BlockSpec(memory_space=pltpu.VMEM)
def cost_of(micros):
    return pl.CostEstimate(flops=0, bytes_accessed=micros * 3_000_000, transcendentals=0)


SELF, NEAR, FAR, BOTH_FLIPPED = 0, 1, 2, 3


def place_of(device):
    expert, tensor = device
    return expert // 2, expert % 2, tensor // 2, tensor % 2


def flipped(device, role):
    expert, tensor = device
    _, x, y, core = place_of(device)
    step_x, step_y = 1 - 2 * x, 2 - 4 * y
    if role == NEAR:
        return expert + (1 - core) * step_x, tensor + core * step_y
    if role == FAR:
        return expert + core * step_x, tensor + (1 - core) * step_y
    if role == BOTH_FLIPPED:
        return expert + step_x, tensor + step_y
    return expert, tensor


def moved_z(device, hops):
    expert, tensor = device
    return lax.rem(expert + 2 * hops, 8), tensor


def sibling(device):
    expert, tensor = device
    return expert, tensor + 1 - 2 * (tensor % 2)


def slot_of(device):
    return device[0] * 4 + device[1]


def here():
    return lax.axis_index(EXPERT), lax.axis_index(TENSOR)


def greet(partners):
    barrier = pltpu.get_barrier_semaphore()
    for partner in partners:
        pl.semaphore_signal(barrier, inc=1, device_id=partner, device_id_type=MESH_ID)
    pl.semaphore_wait(barrier, len(partners))


def push(source, target, send_sem, recv_sem, device):
    return pltpu.make_async_remote_copy(
        src_ref=source,
        dst_ref=target,
        send_sem=send_sem,
        recv_sem=recv_sem,
        device_id=device,
        device_id_type=MESH_ID,
    )


def hop(device, flips, hops):
    expert, tensor = device
    return lax.rem(expert + flips * (1 - 2 * lax.rem(expert, 2)) + 2 * hops, 8), tensor


def across_y(device):
    expert, tensor = device
    return expert, lax.rem(tensor + 2, 4)


class Line:
    def __init__(self, send_sem, recv_sem):
        self.send_sem, self.recv_sem = send_sem, recv_sem
        self.started = []

    def send(self, source, target, tag, recv_tag, device):
        copy = push(source, target, self.send_sem.at[tag], self.recv_sem.at[recv_tag], device)
        copy.start()
        self.started.append(copy)

    def wait(self, target, tag, device):
        push(target, target, self.send_sem.at[0], self.recv_sem.at[tag], device).wait_recv()

    def finish(self):
        for copy in self.started:
            copy.wait_send()


PIECES = ((0, 1), (1, 0), (3, 0), (1, 1), (3, 1), (2, 0), (2, 1))


def exchange_steps(source, out, gathered, line, local_sem):
    me = here()
    tensor = me[1]
    side, sib = across_y(me), sibling(me)

    def at(column, expert):
        return out.at[column, expert] if gathered else out.at[expert]

    local = pltpu.make_async_copy(source.at[me[0]], at(tensor, me[0]), local_sem)
    local.start()
    if gathered:
        line.send(source.at[me[0]], at(tensor, me[0]), 8, 8, side)
        line.send(source.at[me[0]], at(tensor, me[0]), 16, 16, sib)
    for k, flips in PIECES:
        target = hop(me, flips, k)
        line.send(
            source.at[target[0]], at(tensor, me[0]), k * 2 + flips, (4 - k) % 4 * 2 + flips, target
        )
    yield
    for k, flips in PIECES:
        expert = hop(me, flips, k)[0]
        tag = k * 2 + flips
        line.wait(at(tensor, expert), tag, sib)
        if gathered:
            line.send(at(tensor, expert), at(tensor, expert), 8 + tag, 8 + tag, side)
            line.send(at(tensor, expert), at(tensor, expert), 16 + tag, 16 + tag, sib)
        yield
    if gathered:
        for k, flips in ((0, 0),) + PIECES:
            expert = hop(me, flips, k)[0]
            tag = k * 2 + flips
            line.wait(at(side[1], expert), 8 + tag, sib)
            line.send(at(side[1], expert), at(side[1], expert), 24 + tag, 24 + tag, sib)
            yield
        for k, flips in ((0, 0),) + PIECES:
            expert = hop(me, flips, k)[0]
            tag = k * 2 + flips
            line.wait(at(sib[1], expert), 16 + tag, sib)
            line.wait(at(across_y(sib)[1], expert), 24 + tag, sib)
    local.wait()
    line.finish()


def gather_expert_steps(sources, outs, plans, line, local_sems):
    me = here()
    z = me[0] // 2
    beside = hop(me, 1, 0)
    locals_ = [
        pltpu.make_async_copy(source, out.at[me[0]], local_sems.at[n])
        for n, (source, out) in enumerate(zip(sources, outs))
    ]
    for copy in locals_:
        copy.start()
    items = [(n, i, i < s) for n, (c, s) in enumerate(plans) for i in range(c)]
    count = len(items)
    straight = [j for j in range(count) if items[j][2]]
    crossed = [j for j in range(count) if not items[j][2]]

    def window(ref, j):
        n, i, _ = items[j]
        step = sources[n].shape[0] // plans[n][0]
        return ref.at[pl.ds(i * step, step), :]

    def own(j):
        return window(sources[items[j][0]], j)

    def block_of(expert, j):
        return window(outs[items[j][0]].at[expert], j)

    def base(distance, up, j):
        return ((distance - 1) * 2 + up) * count + j

    def passes(ref, target, tag, up, held):
        @pl.when(held & ((z < 3) if up else (z > 0)))
        def _():
            push(
                ref, target, line.send_sem.at[tag], line.recv_sem.at[tag], hop(me, 0, 1 if up else 3)
            ).start()

    def came(column, distance, up):
        return lax.rem(column[0] + (8 - 2 * distance if up else 2 * distance), 8)

    def is_held(distance, up):
        return (z >= distance) if up else (z + distance <= 3)

    cross, over = 6 * count, 12 * count
    for j in crossed + straight:
        line.send(own(j), block_of(me[0], j), over + j, over + j, beside)
    for j in straight + crossed:
        for up in (1, 0):
            passes(own(j), block_of(me[0], j), base(1, up, j), up, z >= 0)
    yield
    for j in crossed:
        block = block_of(beside[0], j)
        line.wait(block, over + j, beside)
        for up in (1, 0):
            passes(block, block, cross + base(1, up, j), up, z >= 0)
    yield
    for distance in (1, 2, 3):
        for j in straight + crossed:
            for up in (1, 0):
                held = is_held(distance, up)
                block = block_of(came(me, distance, up), j)
                tag = base(distance, up, j)

                @pl.when(held)
                def _():
                    line.wait(block, tag, beside)

                if distance < 3:
                    passes(block, block, base(distance + 1, up, j), up, held)
                if items[j][2]:

                    @pl.when(held)
                    def _():
                        push(
                            block,
                            block,
                            line.send_sem.at[cross + tag],
                            line.recv_sem.at[cross + tag],
                            beside,
                        ).start()

            yield
        for j in crossed:
            for up in (1, 0):
                held = is_held(distance, up)
                block = block_of(came(beside, distance, up), j)
                tag = cross + base(distance, up, j)

                @pl.when(held)
                def _():
                    line.wait(block, tag, beside)

                if distance < 3:
                    passes(block, block, cross + base(distance + 1, up, j), up, held)
            yield
    for j in straight:
        line.wait(block_of(beside[0], j), over + j, beside)
    for distance in (1, 2, 3):
        for j in straight + crossed:
            for up in (1, 0):
                held = is_held(distance, up)
                block = block_of(came(beside, distance, up), j)
                tag = base(distance, up, j)
                sent_on = (z + 1 >= distance) & (z < 3) if up else (z - 1 + distance <= 3) & (z > 0)

                def sent(at):
                    push(block, block, line.send_sem.at[at], line.recv_sem.at[at], beside).wait_send()

                if items[j][2]:

                    @pl.when(held)
                    def _():
                        sent(cross + tag)
                        line.wait(block, cross + tag, beside)

                @pl.when(sent_on)
                def _():
                    sent(tag)
                    if not items[j][2]:
                        sent(cross + tag)

        yield
    for copy in locals_:
        copy.wait()
    line.finish()


def sum_rows(target, terms, step=16):
    def body(i, carry):
        window = pl.ds(pl.multiple_of(i * step, step), step)
        value = terms[0][window, :].astype(jnp.float32)
        for ref in terms[1:]:
            value = value + ref[window, :].astype(jnp.float32)
        target[window, :] = value.astype(target.dtype)
        return carry

    lax.fori_loop(0, target.shape[0] // step, body, 0)


def sum_expert_steps(part, out, mine, from_x, from_z, line, load_sem, step=16):
    me = here()
    beside = hop(me, 1, 0)
    loads = {}
    for k in (2, 1, 3, 0):
        line.send(part.at[hop(me, 1, k)[0]], from_x.at[k], k, k, beside)
        loads[k] = pltpu.make_async_copy(part.at[hop(me, 0, k)[0]], mine.at[k], load_sem.at[k])
        loads[k].start()
    yield
    for k in (2, 1, 3, 0):
        loads[k].wait()
        line.wait(from_x.at[k], k, beside)
        if k:
            sum_rows(mine.at[k], [mine.at[k], from_x.at[k]], step)
            line.send(mine.at[k], from_z.at[3 - k], 3 + k, 4 + 3 - k, hop(me, 0, k))
            yield
            yield
    for i in range(3):
        line.wait(from_z.at[i], 4 + i, beside)
    sum_rows(out, [mine.at[0], from_x.at[0], from_z.at[0], from_z.at[1], from_z.at[2]], step)
    line.finish()


CHAIN = (3, 0, 2, 1)


def sum_chain_steps(part, out, mine, from_x, arrive, from_b, line, load_sem, straight):
    me = here()
    z = me[0] // 2
    x = lax.rem(me[0], 2)
    low = z < 2
    near = jnp.where(low, z, 3 - z)
    behind = jnp.where(low, 0, 1)
    beside = hop(me, 1, 0)
    step = mine.shape[2]
    chunks = out.shape[0] // step
    streams = []
    for i in range(straight, chunks):
        streams += [(i, 1, None), (i, 0, None)]
    streams += [(i, 0, i) for i in range(straight)]
    first_x = len(streams) * 4
    first_b = first_x + straight * 4
    recv_x = len(streams) * 8
    recv_b = recv_x + straight * 4

    def plane(a):
        return jnp.where(low, a, 3 - a)

    def chunk_of(expert, i):
        return part.at[expert, pl.ds(i * step, step), :]

    def column(flip):
        return jnp.where(flip == 1, 1 - x, x)

    def load(s, a):
        i, flip, _ = streams[s]
        p = plane(a)
        return pltpu.make_async_copy(
            chunk_of(2 * p + column(flip), i), mine.at[s, p], load_sem.at[s * 4 + p]
        )

    for a in CHAIN:
        p = plane(a)
        for s, (i, _, at) in enumerate(streams):
            if at is not None:
                line.send(
                    chunk_of(2 * p + 1 - x, i), from_x.at[at, p], first_x + at * 4 + p,
                    recv_x + at * 4 + p, beside,
                )
            load(s, a).start()
    yield

    def own_terms(s, a):
        p = plane(a)
        load(s, a).wait()
        at = streams[s][2]
        if at is None:
            return [mine.at[s, p]]
        line.wait(from_x.at[at, p], recv_x + at * 4 + p, beside)
        return [mine.at[s, p], from_x.at[at, p]]

    def arrived(s, a, side):
        p = plane(a)
        ref = arrive.at[s, side, p]
        line.wait(ref, (s * 2 + side) * 4 + p, beside)
        return ref

    def passing(s, a, forward):
        p = plane(a)
        side = behind if forward else 1 - behind
        up = jnp.where(low, 1, 3) if forward else jnp.where(low, 3, 1)
        return push(
            mine.at[s, p],
            arrive.at[s, side, p],
            line.send_sem.at[s * 4 + p],
            line.recv_sem.at[(s * 2 + side) * 4 + p],
            hop(me, 0, up),
        )

    def pass_on(s, a, forward, sides):
        terms = own_terms(s, a) + [arrived(s, a, side) for side in sides]
        if len(terms) > 1:
            sum_rows(mine.at[s, plane(a)], terms)
        passing(s, a, forward).start()

    for a in CHAIN:
        for s in range(len(streams)):
            if a != 0:

                @pl.when(near == 0)
                def _():
                    pass_on(s, a, True, [])

            if a != 1:

                @pl.when(near == 1)
                def _():
                    pass_on(s, a, a != 0, [1 - behind if a == 0 else behind])

            yield

    def final(s, a, sides):
        i, flip, at = streams[s]
        terms = own_terms(s, a) + [arrived(s, a, side) for side in sides]
        if flip:
            total = mine.at[s, plane(a)]
            sum_rows(total, terms)
            j = i - straight
            push(
                total, from_b.at[j], line.send_sem.at[first_b + j], line.recv_sem.at[recv_b + j], beside
            ).start()
        else:
            sum_rows(out.at[pl.ds(i * step, step), :], terms)

    for s in sorted(range(len(streams)), key=lambda s: streams[s][2] is not None):

        @pl.when(near == 0)
        def _():
            final(s, 0, [1 - behind])

        @pl.when(near == 1)
        def _():
            final(s, 1, [behind, 1 - behind])

        yield
    for j in range(chunks - straight):
        rows = out.at[pl.ds((straight + j) * step, step), :]
        both = push(
            from_b.at[j], from_b.at[j], line.send_sem.at[first_b + j], line.recv_sem.at[recv_b + j], beside
        )
        both.wait()
        sum_rows(rows, [rows, from_b.at[j]])
    for a in CHAIN:
        for s in range(len(streams)):
            if a != 0:

                @pl.when(near == 0)
                def _():
                    passing(s, a, True).wait_send()

            if a != 1:

                @pl.when(near == 1)
                def _():
                    passing(s, a, a != 0).wait_send()

    line.finish()


def sum_everywhere_steps(part, out, mine, from_x, from_z, total, shares, line, load_sem):
    me = here()
    yield from sum_expert_steps(part, total, mine, from_x, from_z, line, load_sem, 8)
    peers = [across_y(me), sibling(me), across_y(sibling(me))]
    for i, peer in enumerate(peers):
        line.send(total, shares.at[me[1]], 7 + i, 7 + i, peer)
    shares[me[1]] = total[...]
    yield
    for i, peer in enumerate(peers):
        line.wait(shares.at[peer[1]], 7 + i, peer)
    sum_rows(out, [shares.at[i] for i in range(4)], 8)
    for i in range(3):
        line.started[-3 + i].wait_send()


def take_turns(steps):
    steps = list(steps)
    while steps:
        steps = [s for s in steps if next(s, steps) is not steps]


DMA = pltpu.SemaphoreType.DMA


GATHER_PLANS = ((1, 1), (4, 3), (2, 2))


def start_kernel(
    tokens, grads, weights, outs, small, o_tokens, o_grads, o_weights, o_outs, o_small, *sems
):
    me = here()
    pieces = [hop(me, flips, k) for k, flips in PIECES]
    greet(pieces + [across_y(me), sibling(me)])
    local = sems[7]
    take_turns(
        [
            exchange_steps(tokens, o_tokens, True, Line(sems[0], sems[1]), local.at[0]),
            exchange_steps(grads, o_grads, False, Line(sems[2], sems[3]), local.at[1]),
            gather_expert_steps(
                [small, weights, outs], [o_small, o_weights, o_outs], GATHER_PLANS,
                Line(sems[4], sems[5]), sems[6],
            ),
        ]
    )


def start_exchange(tokens, grads, weights, outs, small):
    piece = tokens.shape[1:]
    sds = jax.ShapeDtypeStruct
    return pl.pallas_call(
        start_kernel,
        out_shape=[
            sds((4, 8) + piece, tokens.dtype),
            sds((8,) + piece, grads.dtype),
            sds((8,) + weights.shape, weights.dtype),
            sds((8,) + outs.shape, outs.dtype),
            sds((8,) + small.shape, small.dtype),
        ],
        in_specs=[IN_VMEM] * 5,
        out_specs=[ANY] * 5,
        scratch_shapes=[DMA((32,)), DMA((32,)), DMA((8,)), DMA((8,))]
        + [DMA((13 * sum(c for c, _ in GATHER_PLANS),))] * 2
        + [DMA((3,)), DMA((2,))],
        compiler_params=pltpu.CompilerParams(
            collective_id=4, has_side_effects=True, vmem_limit_bytes=16 * 2**20
        ),
        cost_estimate=cost_of(100),
        name="start_exchange",
    )(tokens, grads, weights, outs, small)


def last_kernel(
    rows, more, part, small, o_rows, o_more, out, o_small,
    mine, from_x, arrive, from_b, mine_s, x_s, z_s, total_s, shares_s, *sems,
):
    me = here()
    pieces = [hop(me, flips, k) for k, flips in PIECES]
    greet(pieces + [across_y(me), sibling(me), across_y(sibling(me))])
    take_turns(
        [
            exchange_steps(more, o_more, True, Line(sems[2], sems[3]), sems[7].at[1]),
            exchange_steps(rows, o_rows, True, Line(sems[0], sems[1]), sems[7].at[0]),
            sum_everywhere_steps(
                small, o_small, mine_s, x_s, z_s, total_s, shares_s, Line(sems[8], sems[9]), sems[10]
            ),
            sum_chain_steps(
                part, out, mine, from_x, arrive, from_b, Line(sems[4], sems[5]), sems[6], from_x.shape[0]
            ),
        ]
    )


def last_exchange(rows, more, part, small):
    piece = rows.shape[1:]
    block, little = part.shape[1:], small.shape[1:]
    chunks, straight = 4, 3
    streams = 2 * chunks - straight
    chunk = (block[0] // chunks, block[1])
    first = (streams + straight) * 4
    sds = jax.ShapeDtypeStruct
    return pl.pallas_call(
        last_kernel,
        out_shape=[
            sds((4, 8) + piece, rows.dtype),
            sds((4, 8) + piece, more.dtype),
            sds(block, jnp.float32),
            sds(little, jnp.float32),
        ],
        in_specs=[IN_VMEM, IN_VMEM, ANY, ANY],
        out_specs=[ANY, ANY, IN_VMEM, IN_VMEM],
        scratch_shapes=[
            pltpu.VMEM((streams, 4) + chunk, part.dtype),
            pltpu.VMEM((straight, 4) + chunk, part.dtype),
            pltpu.VMEM((streams, 2, 4) + chunk, part.dtype),
            pltpu.VMEM((chunks - straight,) + chunk, part.dtype),
        ]
        + [pltpu.VMEM((n,) + little, jnp.float32) for n in (4, 4, 3)]
        + [pltpu.VMEM(little, jnp.float32), pltpu.VMEM((4,) + little, jnp.float32)]
        + [DMA((32,))] * 4
        + [DMA((first + chunks,)), DMA((first + streams * 4 + chunks,)), DMA((streams * 4,)), DMA((2,))]
        + [DMA((10,)), DMA((10,)), DMA((4,))],
        compiler_params=pltpu.CompilerParams(
            collective_id=5, has_side_effects=True, vmem_limit_bytes=46 * 2**20
        ),
        cost_estimate=cost_of(1),
        name="last_exchange",
    )(rows, more, part, small)


def gather_tensor_kernel(source, out, send_sem, recv_sem, local_sem):
    me = here()
    side, sib = across_y(me), sibling(me)
    greet([side, sib])
    line = Line(send_sem, recv_sem)
    halves = 4
    step = source.shape[0] // halves

    def part(ref, i):
        return ref.at[pl.ds(i * step, step), :]

    local = pltpu.make_async_copy(source, out.at[me[1]], local_sem)
    for i in range(halves):
        line.send(part(source, i), part(out.at[me[1]], i), i, i, side)
        line.send(part(source, i), part(out.at[me[1]], i), 4 + i, 4 + i, sib)
    local.start()
    for i in range(halves):
        got = part(out.at[side[1]], i)
        line.wait(got, i, sib)
        line.send(got, got, 8 + i, 8 + i, sib)
    for i in range(halves):
        line.wait(part(out.at[sib[1]], i), 4 + i, sib)
        line.wait(part(out.at[across_y(sib)[1]], i), 8 + i, sib)
    local.wait()
    line.finish()


def gather_tensor(rows):
    out = pl.pallas_call(
        gather_tensor_kernel,
        out_shape=jax.ShapeDtypeStruct((4,) + rows.shape, rows.dtype),
        in_specs=[IN_VMEM],
        out_specs=ANY,
        scratch_shapes=[DMA((12,)), DMA((12,)), DMA],
        compiler_params=pltpu.CompilerParams(
            collective_id=6, has_side_effects=True, vmem_limit_bytes=8 * 2**20
        ),
        cost_estimate=cost_of(15),
        name="gather_tensor",
    )(rows)
    return out.reshape((-1,) + rows.shape[1:])


def sum_tensor_into(make, part, out, from_sib, from_side, total, line):
    me = here()
    side, sib = across_y(me), sibling(me)
    pieces = 4
    step = out.shape[0] // pieces

    def rows(ref, i):
        return ref.at[pl.ds(i * step, step), :]

    for j, column in ((0, across_y(sib)[1]), (1, sib[1])):
        make(column)
        for i in range(pieces):
            line.send(
                rows(part.at[column], i), rows(from_sib.at[j], i), 4 * j + i, 4 * j + i, sib
            )
    make(side[1])
    for i in range(pieces):
        got = rows(from_sib.at[0], i)
        line.wait(got, i, sib)
        sum_rows(rows(total, i), [rows(part.at[side[1]], i), got])
        line.send(rows(total, i), rows(from_side, i), 8 + i, 8 + i, side)
    make(me[1])
    for i in range(pieces):
        got = rows(from_sib.at[1], i)
        line.wait(got, 4 + i, sib)
        line.wait(rows(from_side, i), 8 + i, sib)
        sum_rows(rows(out, i), [rows(part.at[me[1]], i), got, rows(from_side, i)])
    line.finish()


def sum_tensor_scratch(block):
    bf16 = jnp.bfloat16
    return [
        pltpu.VMEM((4,) + block, bf16),
        pltpu.VMEM((2,) + block, bf16),
        pltpu.VMEM(block, bf16),
        pltpu.VMEM(block, bf16),
        DMA((12,)),
        DMA((12,)),
    ]


def input_sum_kernel(left, right, out, part, from_sib, from_side, total, send_sem, recv_sem):
    me = here()
    greet([across_y(me), sibling(me)])

    def make(column):
        rows = pl.ds(pl.multiple_of(column * out.shape[0], out.shape[0]), out.shape[0])
        for c in range(4):
            span = right.shape[0] // 4
            cols = slice(c * span, (c + 1) * span)
            part[column, :, cols] = dot32(left[rows, :], right[cols, :], NT).astype(jnp.bfloat16)

    sum_tensor_into(make, part, out, from_sib, from_side, total, Line(send_sem, recv_sem))


def input_sum(left, right):
    block = (left.shape[0] // 4, right.shape[0])
    return pl.pallas_call(
        input_sum_kernel,
        out_shape=jax.ShapeDtypeStruct(block, jnp.float32),
        in_specs=[IN_VMEM] * 2,
        out_specs=IN_VMEM,
        scratch_shapes=sum_tensor_scratch(block),
        compiler_params=pltpu.CompilerParams(
            collective_id=7, has_side_effects=True, vmem_limit_bytes=32 * 2**20
        ),
        cost_estimate=cost_of(1),
        name="input_sum",
    )(left, right)


def rows_at(ref, slot, size, count=1):
    return ref.at[pl.ds(pl.multiple_of(slot * size, size), size * count), :]


class Plan:
    def __init__(self, send_sem, recv_sem):
        self.send_sem, self.recv_sem, self.made = send_sem, recv_sem, []

    def send(self, make):
        make().start()
        self.made.append(make)

    def finish(self):
        for make in self.made:
            make().wait_send()


def gather_plan(ins, outs, sizes, send_sem, recv_sem):
    me = here()
    near, far, sib = flipped(me, NEAR), flipped(me, FAR), sibling(me)
    plan = Plan(send_sem, recv_sem)
    count = len(ins)

    def send(k, role, device, tag, recv_tag):
        for i in range(count):

            def make(i=i):
                block = rows_at(outs[i], slot_of(moved_z(flipped(me, role), k)), sizes[i])
                source = ins[i] if (k, role) == (0, SELF) else block
                return push(source, block, send_sem.at[i, tag], recv_sem.at[i, recv_tag], device)

            plan.send(make)

    def arrive(k, role):
        for i in range(count):
            block = rows_at(outs[i], slot_of(moved_z(flipped(me, role), k)), sizes[i])
            push(block, block, send_sem.at[i, 0], recv_sem.at[i, k * 4 + role], near).wait_recv()

    def forward(k, role):
        if role == SELF:
            send(k, SELF, far, 4 + k, k * 4 + FAR)
            send(k, SELF, near, k, k * 4 + NEAR)
        if role == NEAR:
            send(k, NEAR, far, 8 + k, k * 4 + BOTH_FLIPPED)
        send(k, role, sib, 16 + k * 4 + role, 16 + k * 4 + role)

    def event(k, role):
        arrive(k, role)
        forward(k, role)

    def from_sibling(k, role):
        for i in range(count):
            block = rows_at(outs[i], 0, sizes[i])
            push(
                block, block, send_sem.at[i, 0], recv_sem.at[i, 16 + k * 4 + role], near
            ).wait_recv()

    def begin():
        forward(0, SELF)
        for d in (1, 3, 2):
            send(0, SELF, moved_z(me, d), 11 + d, (4 - d) * 4 + SELF)

    return plan, begin, event, from_sibling


def gate_columns(gates_ref, slot, columns, first):
    lane = lax.broadcasted_iota(jnp.int32, (128, 128), 1)
    for s in range(4):
        block = gates_ref[pl.ds(pl.multiple_of((slot + s) * 16, 16), 16), :]
        turned = jnp.concatenate([block, jnp.zeros((112, 128), jnp.float32)], axis=0).T
        for i in range(2):
            column = jnp.sum(jnp.where(lane == first + i, turned, 0.0), axis=1, keepdims=True)
            columns[i, pl.ds(s * 128, 128), :] = jnp.broadcast_to(column, (128, 128))


def tiles(count, width, body):
    def step(n, carry):
        body(pl.ds(pl.multiple_of(n * width, width), width))
        return carry

    lax.fori_loop(0, count, step, 0)


STAGES = ((0, 0), (0, 1), (1, 0), (1, 1), (3, 0), (3, 1), (2, 0), (2, 1))
BLOCK = 512


def stage_expert(me, j):
    half = j // 2
    k = half + jnp.where(half == 2, 1, 0) - jnp.where(half == 3, 1, 0)
    flips = lax.rem(j, 2)
    expert = me[0]
    return lax.rem(expert + flips * (1 - 2 * lax.rem(expert, 2)) + 2 * k, 8)


def forward_kernel(
    x_own, g_own, w_joined, w_down, x_out, g_out, pre_out, gated_out, y_out,
    x_all, g_all, columns, pre, gated, y, send_sem, recv_sem, local_sem, out_sem,
):
    me = here()
    core = lax.rem(me[1], 2)
    greet(
        [flipped(me, NEAR), flipped(me, FAR), sibling(me)] + [moved_z(me, d) for d in (1, 2, 3)]
    )
    plan, begin, event, from_sibling = gather_plan(
        [x_own, g_own], [x_all, g_all], [128, 16], send_sem, recv_sem
    )
    local = [
        pltpu.make_async_copy(x_own, rows_at(x_all, slot_of(me), 128), local_sem.at[0]),
        pltpu.make_async_copy(g_own, rows_at(g_all, slot_of(me), 16), local_sem.at[1]),
    ]
    begin()
    for copy in local:
        copy.start()
    for copy in local:
        copy.wait()
    before = {
        0: [(1, SELF), (0, NEAR), (0, FAR)],
        1: [(0, BOTH_FLIPPED)],
        3: [(1, BOTH_FLIPPED)],
        5: [(3, BOTH_FLIPPED)],
        7: [(2, BOTH_FLIPPED)],
    }
    middle = {
        0: [(3, SELF), (1, NEAR)],
        1: [(1, FAR)],
        2: [(2, SELF), (3, NEAR)],
        3: [(3, FAR)],
        4: [(2, NEAR)],
        5: [(2, FAR)],
    }
    half = w_joined.shape[1] // 2

    def results(expert, slot):
        return [
            pltpu.make_async_copy(
                rows_at(x_all, expert, BLOCK), rows_at(x_out, expert, BLOCK), out_sem.at[0, slot]
            ),
            pltpu.make_async_copy(pre.at[slot], rows_at(pre_out, expert, BLOCK), out_sem.at[1, slot]),
            pltpu.make_async_copy(
                gated.at[slot], rows_at(gated_out, expert, BLOCK), out_sem.at[2, slot]
            ),
            pltpu.make_async_copy(y.at[slot], rows_at(y_out, expert, BLOCK), out_sem.at[3, slot]),
        ]

    def block(j, carry):
        slot = lax.rem(j, 2)
        expert = stage_expert(me, j)
        for n, (k, flips) in enumerate(STAGES):

            @pl.when(j == n)
            def _():
                for at in before.get(n, []):
                    event(*at)
                if n:
                    from_sibling(k, 2 - core if flips else SELF)
                    from_sibling(k, BOTH_FLIPPED if flips else 1 + core)
                else:
                    from_sibling(k, SELF)
                    from_sibling(k, 1 + core)

        @pl.when(j >= 2)
        def _():
            for copy in results(stage_expert(me, j - 2), slot):
                copy.wait()

        gate_columns(g_all, expert * 4, columns, me[0] * 2)
        x_rows = rows_at(x_all, expert, BLOCK)

        def first(cols):
            pre[slot, :, cols] = jnp.dot(
                x_rows[...], w_joined[:, cols], preferred_element_type=jnp.float32
            )

        tiles(w_joined.shape[1] // 1024, 1024, first)
        for n in middle:

            @pl.when(j == n)
            def _():
                for at in middle[n]:
                    event(*at)

        def act(r):
            for c in range(half // 128):
                cols = slice(c * 128, (c + 1) * 128)
                g = pre[slot, r, cols]
                u = pre[slot, r, half + c * 128 : half + (c + 1) * 128]
                hidden = (g * (1.0 / (1.0 + jnp.exp(-g))) * u).astype(jnp.bfloat16)
                gate = columns[c * 128 * 2 // half, r, :]
                gated[slot, r, cols] = (hidden.astype(jnp.float32) * gate).astype(jnp.bfloat16)

        tiles(BLOCK // 64, 64, act)

        def second(cols):
            y[slot, :, cols] = jnp.dot(
                gated[slot], w_down[:, cols], preferred_element_type=jnp.float32
            ).astype(jnp.bfloat16)

        tiles(w_down.shape[1] // 1024, 1024, second)
        for copy in results(expert, slot):
            copy.start()
        return carry

    lax.fori_loop(0, 8, block, 0)
    for j in (6, 7):
        for copy in results(stage_expert(me, jnp.int32(j)), j % 2):
            copy.wait()
    g_out[...] = g_all[...]
    plan.finish()


def experts_forward(ffn_in, gates_own, w_joined, w_down):
    rows, width = ffn_in.shape[0] * 32, ffn_in.shape[1]
    joined, hidden = w_joined.shape[1], w_down.shape[0]
    bf16, f32, sds = jnp.bfloat16, jnp.float32, jax.ShapeDtypeStruct
    return pl.pallas_call(
        forward_kernel,
        out_shape=[
            sds((rows, width), bf16),
            sds((512, 128), f32),
            sds((rows, joined), f32),
            sds((rows, hidden), bf16),
            sds((rows, width), bf16),
        ],
        in_specs=[IN_VMEM] * 4,
        out_specs=[ANY, IN_VMEM, ANY, ANY, ANY],
        scratch_shapes=[
            pltpu.VMEM((rows, width), bf16),
            pltpu.VMEM((512, 128), f32),
            pltpu.VMEM((2, BLOCK, 128), f32),
            pltpu.VMEM((2, BLOCK, joined), f32),
            pltpu.VMEM((2, BLOCK, hidden), bf16),
            pltpu.VMEM((2, BLOCK, width), bf16),
            DMA((2, 32)),
            DMA((2, 32)),
            DMA((2,)),
            DMA((4, 2)),
        ],
        compiler_params=pltpu.CompilerParams(
            collective_id=1, has_side_effects=True, vmem_limit_bytes=48 * 2**20
        ),
        cost_estimate=cost_of(90),
        name="experts_forward",
    )(ffn_in, gates_own, w_joined, w_down)


def sum_plan(arrays, send_sem, recv_sem, load_sem):
    me = here()
    near, far, sib = flipped(me, NEAR), flipped(me, FAR), sibling(me)
    plan = Plan(send_sem, recv_sem)
    order = (2, 1, 3, 0)

    def send(i, source, target, tag, recv_tag, device):
        plan.send(
            lambda: push(source(), target(), send_sem.at[i, tag], recv_sem.at[i, recv_tag], device())
        )

    def arrive(i, ref, tag):
        push(ref, ref, send_sem.at[i, 0], recv_sem.at[i, tag], near).wait_recv()

    def load(i, k, role):
        part, _, size, mine = arrays[i][:4]
        tag = k * 4 + role
        return pltpu.make_async_copy(
            rows_at(part, slot_of(moved_z(flipped(me, role), k)), size), mine.at[tag], load_sem.at[i, tag]
        )

    def begin():
        for roles in ((BOTH_FLIPPED, FAR), (NEAR, SELF)):
            for k in order:
                for role in roles:
                    for i, (part, _, size, _, from_sib, _, _, _) in enumerate(arrays):
                        tag = k * 4 + role
                        send(
                            i,
                            lambda part=part, size=size, k=k, role=role: rows_at(
                                part, slot_of(moved_z(flipped(sib, role), k)), size
                            ),
                            lambda from_sib=from_sib, tag=tag: from_sib.at[tag],
                            tag,
                            tag,
                            lambda: sib,
                        )
                        load(i, k, role).start()

    def collect(i, k, role):
        tag = k * 4 + role
        load(i, k, role).wait()
        from_sib = arrays[i][4]
        arrive(i, from_sib.at[tag], tag)
        return [arrays[i][3].at[tag], from_sib.at[tag]]

    def first(k, role):
        for i, (_, _, _, mine, _, from_far, _, _) in enumerate(arrays):
            tag, at = k * 4 + role, k * 2 + (role == BOTH_FLIPPED)
            terms = collect(i, k, role)
            sum_rows(mine.at[tag], terms)
            send(
                i,
                lambda mine=mine, tag=tag: mine.at[tag],
                lambda from_far=from_far, at=at: from_far.at[at],
                16 + at,
                16 + at,
                lambda: far,
            )

    def second(k):
        for i, (_, _, _, mine, _, from_far, from_near, _) in enumerate(arrays):
            tag = k * 4 + NEAR
            terms = collect(i, k, NEAR)
            arrive(i, from_far.at[k * 2 + 1], 16 + k * 2 + 1)
            sum_rows(mine.at[tag], terms + [from_far.at[k * 2 + 1]])
            send(
                i,
                lambda mine=mine, tag=tag: mine.at[tag],
                lambda from_near=from_near, k=k: from_near.at[k],
                24 + k,
                24 + k,
                lambda: near,
            )

    def third(k):
        for i, (_, out, _, mine, _, from_far, from_near, from_z) in enumerate(arrays):
            tag = k * 4 + SELF
            terms = collect(i, k, SELF)
            arrive(i, from_far.at[k * 2], 16 + k * 2)
            arrive(i, from_near.at[k], 24 + k)
            terms = terms + [from_far.at[k * 2], from_near.at[k]]
            if k > 0:
                sum_rows(mine.at[tag], terms)
                send(
                    i,
                    lambda mine=mine, tag=tag: mine.at[tag],
                    lambda from_z=from_z, k=k: from_z.at[3 - k],
                    27 + k,
                    31 - k,
                    lambda k=k: moved_z(me, k),
                )
            else:
                for d in range(3):
                    arrive(i, from_z.at[d], 28 + d)
                    terms.append(from_z.at[d])
                sum_rows(out, terms)

    return plan, begin, first, second, third


def sum_scratch(size, width, dtype):
    return [pltpu.VMEM((n, size, width), dtype) for n in (16, 16, 8, 4, 3)]


SUM_BEFORE = {0: [(2, 3), (2, 2), (1, 3), (1, 2)], 3: [(2, "third")], 5: [(1, "third")]}
SUM_MIDDLE = {
    0: [(3, 3), (3, 2), (0, 3), (0, 2)],
    1: [(2, "second")],
    2: [(1, "second")],
    4: [(3, "second")],
    6: [(0, "second")],
}


def sum_events(table, j, first, second, third):
    for n, events in table.items():

        @pl.when(j == n)
        def _():
            for k, what in events:
                if what == "second":
                    second(k)
                elif what == "third":
                    third(k)
                else:
                    first(k, what)


def greet_all(me):
    greet(
        [flipped(me, NEAR), flipped(me, FAR), sibling(me)] + [moved_z(me, d) for d in (1, 2, 3)]
    )


def backward_kernel(
    y_part, grads, pre_all, gates, w_joined, w_down, mix_out, dpre_out, drow_out, gate_grads,
    mine, from_sib, from_far, from_near, from_z, dz, pre, raw, columns, products, dpre, drow,
    send_sem, recv_sem, load_sem, in_sem, out_sem,
):
    me = here()
    greet_all(me)
    plan, begin, first, second, third = sum_plan(
        [(y_part, mix_out, 128, mine, from_sib, from_far, from_near, from_z)],
        send_sem, recv_sem, load_sem,
    )
    half = w_joined.shape[1] // 2
    expert_lanes = half // 2

    def loads(block, slot):
        return [
            pltpu.make_async_copy(rows_at(grads, block, BLOCK), dz.at[slot], in_sem.at[0, slot]),
            pltpu.make_async_copy(rows_at(pre_all, block, BLOCK), pre.at[slot], in_sem.at[1, slot]),
        ]

    def results(block, slot):
        return [
            pltpu.make_async_copy(dpre.at[slot], rows_at(dpre_out, block, BLOCK), out_sem.at[0, slot]),
            pltpu.make_async_copy(drow.at[slot], rows_at(drow_out, block, BLOCK), out_sem.at[1, slot]),
        ]

    for copy in loads(0, 0):
        copy.start()
    begin()

    def step(j, carry):
        slot = lax.rem(j, 2)

        @pl.when(j < 7)
        def _():
            for copy in loads(j + 1, 1 - slot):
                copy.start()

        sum_events(SUM_BEFORE, j, first, second, third)
        for copy in loads(j, slot):
            copy.wait()

        @pl.when(j >= 2)
        def _():
            for copy in results(j - 2, slot):
                copy.wait()

        gate_columns(gates, j * 4, columns, me[0] * 2)
        raw[...] = lax.dot_general(
            dz[slot], w_down[...], (((1,), (1,)), ((), ())), preferred_element_type=jnp.float32
        )
        sum_events(SUM_MIDDLE, j, first, second, third)

        def act(r):
            for i in range(2):
                product = None
                for c in range(i * expert_lanes, (i + 1) * expert_lanes, 128):
                    g = pre[slot, r, c : c + 128]
                    u = pre[slot, r, half + c : half + c + 128]
                    t = raw[r, c : c + 128]
                    sig = 1.0 / (1.0 + jnp.exp(-g))
                    silu = g * sig
                    hidden = (silu * u).astype(jnp.bfloat16).astype(jnp.float32)
                    term = hidden * t
                    product = term if product is None else product + term
                    dh = t * columns[i, r, :]
                    dpre[slot, r, c : c + 128] = (
                        dh * u * sig * (1.0 + g * (1.0 - sig))
                    ).astype(jnp.bfloat16)
                    dpre[slot, r, half + c : half + c + 128] = (dh * silu).astype(jnp.bfloat16)
                products[i, r, :] = product

        tiles(BLOCK // 64, 64, act)
        place = lax.broadcasted_iota(jnp.int32, (16, 128), 0)
        for s in range(4):
            sums = jnp.zeros((16, 128), jnp.float32)
            for i in range(2):
                turned = products[i, pl.ds(s * 128, 128), :].T
                row = jnp.sum(turned, axis=0, keepdims=True)
                sums = jnp.where(place == me[0] * 2 + i, jnp.broadcast_to(row, (16, 128)), sums)
            gate_grads[pl.ds(pl.multiple_of((j * 4 + s) * 16, 16), 16), :] = sums

        def back(rows):
            drow[slot, :, rows] = lax.dot_general(
                dpre[slot],
                w_joined[rows, :],
                (((1,), (1,)), ((), ())),
                preferred_element_type=jnp.float32,
            ).astype(jnp.bfloat16)

        tiles(w_joined.shape[0] // 1024, 1024, back)
        for copy in results(j, slot):
            copy.start()
        return carry

    lax.fori_loop(0, 8, step, 0)
    third(3)
    third(0)
    for j in (6, 7):
        for copy in results(j, j % 2):
            copy.wait()
    plan.finish()


def experts_backward(y_part, grads, pre, gates, w_joined, w_down):
    rows, width = grads.shape
    joined, hidden = w_joined.shape[1], w_down.shape[0]
    bf16, f32, sds = jnp.bfloat16, jnp.float32, jax.ShapeDtypeStruct
    return pl.pallas_call(
        backward_kernel,
        out_shape=[
            sds((rows // 32, width), f32),
            sds((rows, joined), bf16),
            sds((rows, width), bf16),
            sds((512, 128), f32),
        ],
        in_specs=[ANY, ANY, ANY] + [IN_VMEM] * 3,
        out_specs=[IN_VMEM, ANY, ANY, IN_VMEM],
        scratch_shapes=sum_scratch(rows // 32, width, bf16)
        + [
            pltpu.VMEM((2, BLOCK, width), bf16),
            pltpu.VMEM((2, BLOCK, joined), f32),
            pltpu.VMEM((BLOCK, hidden), f32),
            pltpu.VMEM((2, BLOCK, 128), f32),
            pltpu.VMEM((2, BLOCK, 128), f32),
            pltpu.VMEM((2, BLOCK, joined), bf16),
            pltpu.VMEM((2, BLOCK, width), bf16),
            DMA((1, 32)),
            DMA((1, 32)),
            DMA((1, 16)),
            DMA((2, 2)),
            DMA((2, 2)),
        ],
        compiler_params=pltpu.CompilerParams(
            collective_id=2, has_side_effects=True, vmem_limit_bytes=56 * 2**20
        ),
        cost_estimate=cost_of(90),
        name="experts_backward",
    )(y_part, grads, pre, gates, w_joined, w_down)


def weights_kernel(
    drow, gate_grads, x_all, grads, dpre_all, gated_all, row_out, gate_out, d_gate, d_up, d_down,
    mine, from_sib, from_far, from_near, from_z, mine_g, sib_g, far_g, near_g, z_g,
    dpre, gated, tile, wide, send_sem, recv_sem, load_sem, in_sem, tile_sem, out_sem,
):
    me = here()
    greet_all(me)
    plan, begin, first, second, third = sum_plan(
        [
            (drow, row_out, 128, mine, from_sib, from_far, from_near, from_z),
            (gate_grads, gate_out, 16, mine_g, sib_g, far_g, near_g, z_g),
        ],
        send_sem, recv_sem, load_sem,
    )
    span = tile.shape[2]
    steps = x_all.shape[1] // span
    hidden = d_gate.shape[2]
    begin()
    held = [
        pltpu.make_async_copy(dpre_all, dpre, in_sem.at[0]),
        pltpu.make_async_copy(gated_all, gated, in_sem.at[1]),
    ]

    def columns_of(j):
        return pl.ds(pl.multiple_of(lax.rem(j, steps) * span, span), span)

    def fetch(j, slot, act):
        @pl.when(j < steps)
        def _():
            act(pltpu.make_async_copy(x_all.at[:, columns_of(j)], tile.at[slot], tile_sem.at[slot]))

        @pl.when((j >= steps) & (j < 2 * steps))
        def _():
            act(pltpu.make_async_copy(grads.at[:, columns_of(j)], tile.at[slot], tile_sem.at[slot]))

    def results(j, slot, act):
        cols = columns_of(j)

        @pl.when(j < steps)
        def _():
            for i in range(2):
                act(
                    pltpu.make_async_copy(
                        wide.at[slot, :, pl.ds(i * hidden, hidden)], d_gate.at[i, cols, :], out_sem.at[slot, i]
                    )
                )
                act(
                    pltpu.make_async_copy(
                        wide.at[slot, :, pl.ds((2 + i) * hidden, hidden)],
                        d_up.at[i, cols, :],
                        out_sem.at[slot, 2 + i],
                    )
                )

        @pl.when(j >= steps)
        def _():
            act(
                pltpu.make_async_copy(
                    wide.at[slot, :, pl.ds(0, span)], d_down.at[:, cols], out_sem.at[slot, 0]
                )
            )

    fetch(jnp.int32(0), 0, lambda copy: copy.start())
    for copy in held:
        copy.start()

    def step(j, carry):
        slot = lax.rem(j, 2)
        fetch(j + 1, 1 - slot, lambda copy: copy.start())
        sum_events(SUM_BEFORE, j, first, second, third)

        @pl.when(j == 0)
        def _():
            for copy in held:
                copy.wait()

        fetch(j, slot, lambda copy: copy.wait())

        @pl.when(j >= 2)
        def _():
            results(j - 2, slot, lambda copy: copy.wait())

        @pl.when(j < steps)
        def _():
            wide[slot] = lax.dot_general(
                tile[slot], dpre[...], (((0,), (0,)), ((), ())), preferred_element_type=jnp.float32
            )

        @pl.when(j >= steps)
        def _():
            wide[slot, :, 0:span] = lax.dot_general(
                gated[...], tile[slot], (((0,), (0,)), ((), ())), preferred_element_type=jnp.float32
            )

        results(j, slot, lambda copy: copy.start())
        sum_events(SUM_MIDDLE, j, first, second, third)
        return carry

    lax.fori_loop(0, 2 * steps, step, 0)
    third(3)
    third(0)
    for j in (2 * steps - 2, 2 * steps - 1):
        results(jnp.int32(j), j % 2, lambda copy: copy.wait())
    plan.finish()


def experts_weights(drow, gate_grads, x_all, grads, dpre, gated):
    rows, width = grads.shape
    joined, hidden = dpre.shape[1], gated.shape[1]
    span = width // 4
    bf16, f32, sds = jnp.bfloat16, jnp.float32, jax.ShapeDtypeStruct
    return pl.pallas_call(
        weights_kernel,
        out_shape=[
            sds((rows // 32, width), f32),
            sds((16, 128), f32),
            sds((2, width, joined // 4), f32),
            sds((2, width, joined // 4), f32),
            sds((hidden, width), f32),
        ],
        in_specs=[ANY] * 6,
        out_specs=[IN_VMEM, IN_VMEM, ANY, ANY, ANY],
        scratch_shapes=sum_scratch(rows // 32, width, bf16)
        + sum_scratch(16, 128, f32)
        + [
            pltpu.VMEM((rows, joined), bf16),
            pltpu.VMEM((rows, hidden), bf16),
            pltpu.VMEM((2, rows, span), bf16),
            pltpu.VMEM((2, span, joined), f32),
            DMA((2, 32)),
            DMA((2, 32)),
            DMA((2, 16)),
            DMA((2,)),
            DMA((2,)),
            DMA((2, 4)),
        ],
        compiler_params=pltpu.CompilerParams(
            collective_id=3, has_side_effects=True, vmem_limit_bytes=58 * 2**20
        ),
        cost_estimate=cost_of(90),
        name="experts_weights",
    )(drow, gate_grads, x_all, grads, dpre, gated)


def rotated(values, cosines, sines):
    return values * cosines + pltpu.roll(values, HEAD_DIM // 2, 1) * sines


def turned_back(values, cosines, sines):
    return values * cosines - pltpu.roll(values, HEAD_DIM // 2, 1) * sines


def mask_scores(spans_col, places_row, bias):
    place = places_row[0:1, :]

    def body(r):
        allowed = (place >= spans_col[r, 0:1]) & (place <= spans_col[r, 1:2])
        bias[r, :] = jnp.where(allowed, 0.0, -1e30)

    tiles(bias.shape[0] // 128, 128, body)


def attend_kernel(
    qkv, invs, gains, cosines, sines, spans, places, w_out,
    q_out, k_out, v_out, attended, lse, branch_own, bias,
    part, from_sib, from_side, total, send_sem, recv_sem,
):
    me = here()
    greet([across_y(me), sibling(me)])
    rows, local = q_out.shape
    mask_scores(spans, places, bias)

    def prepare(r):
        v_out[r, :] = qkv[r, 2 * local : 3 * local].astype(jnp.bfloat16)
        for h in range(local // HEAD_DIM):
            c = slice(h * HEAD_DIM, (h + 1) * HEAD_DIM)
            for i, target in ((0, q_out), (1, k_out)):
                normed = qkv[r, i * local + h * HEAD_DIM : i * local + (h + 1) * HEAD_DIM]
                normed = normed * invs[r, i : i + 1] * gains[i : i + 1, c]
                target[r, c] = rotated(normed, cosines[r, :], sines[r, :]).astype(jnp.bfloat16)

    tiles(rows // 128, 128, prepare)
    scale = 1.0 / math.sqrt(HEAD_DIM)
    for h in range(local // HEAD_DIM):
        c = slice(h * HEAD_DIM, (h + 1) * HEAD_DIM)

        def one(r, h=h, c=c):
            scores = dot32(q_out[r, c], k_out[:, c], NT) * scale + bias[r, :]
            top = jnp.max(scores, axis=-1, keepdims=True)
            log_total = top + jnp.log(jnp.sum(jnp.exp(scores - top), axis=-1, keepdims=True))
            lse[h, r, :] = log_total
            probs = jnp.exp(scores - log_total).astype(jnp.bfloat16)
            attended[r, c] = dot32(probs, v_out[:, c], NN).astype(jnp.bfloat16)

        tiles(rows // 128, 128, one)

    def make(column):
        own = branch_own.shape[0]
        places_of = pl.ds(pl.multiple_of(column * own, own), own)
        span = w_out.shape[2]
        for e in range(w_out.shape[0]):
            part[column, :, e * span : (e + 1) * span] = dot32(
                attended[places_of, :], w_out[e], NN
            ).astype(jnp.bfloat16)

    sum_tensor_into(make, part, branch_own, from_sib, from_side, total, Line(send_sem, recv_sem))


def attend(qkv, invs, gains, cosines, sines, spans, places, w_out):
    rows, local = qkv.shape[0], qkv.shape[1] // 3
    block = (rows // 4, w_out.shape[0] * w_out.shape[2])
    bf16, f32, sds = jnp.bfloat16, jnp.float32, jax.ShapeDtypeStruct
    return pl.pallas_call(
        attend_kernel,
        out_shape=[sds((rows, local), bf16)] * 4
        + [
            sds((local // HEAD_DIM, rows, 1), f32),
            sds(block, f32),
        ],
        in_specs=[IN_VMEM] * 8,
        out_specs=[IN_VMEM] * 6,
        scratch_shapes=[pltpu.VMEM((rows, rows), f32)] + sum_tensor_scratch(block),
        compiler_params=pltpu.CompilerParams(
            collective_id=9, has_side_effects=True, vmem_limit_bytes=24 * 2**20
        ),
        cost_estimate=cost_of(15),
        name="attend",
    )(qkv, invs, gains, cosines, sines, spans, places, w_out)


def attend_back_kernel(
    grad, w_out_far, q_far, k_far, v_far, lse, qkv_far, invs, gains, cosines, sines, spans, places,
    hat_grads, value_grad, dots, d_gains, bias, out_grad, probs_low, score_grad,
    w_out, q, k, v, qkv, sems,
):
    rows, local = q.shape
    fetched = [
        pltpu.make_async_copy(far, close, sems.at[i])
        for i, (far, close) in enumerate(
            ((w_out_far, w_out), (q_far, q), (k_far, k), (v_far, v), (qkv_far, qkv))
        )
    ]
    for copy in fetched:
        copy.start()
    mask_scores(spans, places, bias)
    span = w_out.shape[2]
    fetched[0].wait()

    def project(r):
        total = None
        for e in range(w_out.shape[0]):
            term = dot32(grad[r, e * span : (e + 1) * span], w_out[e], NT)
            total = term if total is None else total + term
        out_grad[r, :] = total.astype(jnp.bfloat16)

    tiles(rows // 128, 128, project)
    for copy in fetched[1:]:
        copy.wait()
    scale = 1.0 / math.sqrt(HEAD_DIM)
    dots[...] = jnp.zeros_like(dots)
    for h in range(local // HEAD_DIM):
        c = slice(h * HEAD_DIM, (h + 1) * HEAD_DIM)

        def one(r, h=h, c=c):
            scores = dot32(q[r, c], k[:, c], NT) * scale + bias[r, :]
            probs = jnp.exp(scores - lse[h, r, :])
            prob_grad = dot32(out_grad[r, c], v[:, c], NT)
            delta = jnp.sum(probs * prob_grad, axis=-1, keepdims=True)
            probs_low[r, :] = probs.astype(jnp.bfloat16)
            score_grad[r, :] = (probs * (prob_grad - delta) * scale).astype(jnp.bfloat16)

        tiles(rows // 128, 128, one)
        value_grad[:, c] = dot32(probs_low[...], out_grad[:, c], TN).astype(jnp.bfloat16)
        for i, turned in (
            (0, dot32(score_grad[...], k[:, c], NN)),
            (1, dot32(score_grad[...], q[:, c], TN)),
        ):
            at = slice(i * local + h * HEAD_DIM, i * local + (h + 1) * HEAD_DIM)
            norm_grad = turned_back(turned, cosines[...], sines[...])
            hat = qkv[:, at] * invs[:, i : i + 1]
            hat_grad = norm_grad * gains[i : i + 1, c]
            hat_grads[:, at] = hat_grad
            d_gains[i : i + 1, c] = jnp.sum(norm_grad * hat, axis=0, keepdims=True)
            dots[i] += jnp.sum(hat_grad * hat, axis=-1, keepdims=True)


def attend_back(grad, w_out, q, k, v, lse, qkv, invs, gains, cosines, sines, spans, places):
    rows, local = q.shape
    bf16, f32, sds = jnp.bfloat16, jnp.float32, jax.ShapeDtypeStruct
    return pl.pallas_call(
        attend_back_kernel,
        out_shape=[
            sds((rows, 2 * local), f32),
            sds((rows, local), bf16),
            sds((2, rows, 1), f32),
            sds((2, local), f32),
        ],
        in_specs=[IN_VMEM] + [ANY] * 4 + [IN_VMEM, ANY] + [IN_VMEM] * 6,
        out_specs=[IN_VMEM] * 4,
        scratch_shapes=[
            pltpu.VMEM((rows, rows), f32),
            pltpu.VMEM((rows, local), bf16),
            pltpu.VMEM((rows, rows), bf16),
            pltpu.VMEM((rows, rows), bf16),
        ]
        + [pltpu.VMEM(a.shape, a.dtype) for a in (w_out, q, k, v, qkv)]
        + [DMA((5,))],
        compiler_params=pltpu.CompilerParams(vmem_limit_bytes=62 * 2**20),
        cost_estimate=cost_of(5),
        name="attend_back",
    )(grad, w_out, q, k, v, lse, qkv, invs, gains, cosines, sines, spans, places)


def sum_few_kernel(part, out, shares, send_sem, recv_sem):
    me = here()
    peers = [across_y(sibling(me)), across_y(me), sibling(me)]
    greet(peers)
    line = Line(send_sem, recv_sem)
    for i, peer in enumerate(peers):
        line.send(part, shares.at[me[1]], i, i, peer)
    shares[me[1]] = part[...]
    for i, peer in enumerate(peers):
        line.wait(shares.at[peer[1]], i, peer)
    out[...] = (shares[0] + shares[1]) + (shares[2] + shares[3])
    line.finish()


def sum_few(rows):
    block = (rows.size // 128, 128)
    return pl.pallas_call(
        sum_few_kernel,
        out_shape=jax.ShapeDtypeStruct(block, jnp.float32),
        in_specs=[IN_VMEM],
        out_specs=IN_VMEM,
        scratch_shapes=[pltpu.VMEM((4,) + block, jnp.float32), DMA((3,)), DMA((3,))],
        compiler_params=pltpu.CompilerParams(
            collective_id=8, has_side_effects=True, vmem_limit_bytes=2**20
        ),
        cost_estimate=cost_of(1),
        name="sum_few",
    )(rows.reshape(block)).reshape(rows.shape)


BOTH = (EXPERT, TENSOR)


def dot32(left, right, dims):
    return lax.dot_general(left, right, (dims, ((), ())), preferred_element_type=jnp.float32)


NN = ((1,), (0,))
NT = ((1,), (1,))
TN = ((0,), (0,))


def rms_inv(values):
    return lax.rsqrt(jnp.mean(values * values, axis=-1, keepdims=True) + NORM_EPS)


def dense_body(
    tokens,
    attn_gain,
    w_query,
    w_key,
    w_value,
    w_out,
    query_gain,
    key_gain,
    ffn_gain,
    w_router,
    w_gate,
    w_up,
    w_down,
    doc_ids,
    routes,
    deal,
    out_grad,
):
    rows, width = tokens.shape
    parts = lax.axis_size(TENSOR)
    blocks = lax.axis_size(EXPERT)
    column = lax.axis_index(TENSOR)
    block = lax.axis_index(EXPERT)
    own = rows // parts
    share = rows // blocks
    piece = share // parts
    bf16, f32 = jnp.bfloat16, jnp.float32

    def reorder(per_place):
        grid = per_place.reshape((blocks, parts, piece) + per_place.shape[1:])
        return jnp.swapaxes(grid, 0, 1).reshape(per_place.shape)

    local_width = w_query.shape[1]
    head_count = local_width // HEAD_DIM
    expert_count = w_router.shape[1]
    qkv_own = jnp.concatenate([w_query, w_key, w_value], axis=1)
    gain_stack = jnp.stack([attn_gain, query_gain, key_gain, ffn_gain], axis=1)
    small_own = jnp.concatenate([w_router, gain_stack], axis=1)
    small_own = jnp.pad(small_own, ((0, 0), (0, 128 - small_own.shape[1])))
    deal_grid = deal.reshape(blocks, blocks, parts, piece)
    picks = lax.dynamic_slice(deal_grid, (0, block, column, 0), (blocks, 1, 1, piece)).reshape(-1)
    picks = picks - block * rows
    inputs, dealt_grads, qkv_full, out_full, small_full = start_exchange(
        tokens[picks].reshape(blocks, piece, width),
        out_grad[picks].reshape(blocks, piece, width),
        qkv_own,
        w_out,
        small_own,
    )
    own_low = lax.dynamic_slice_in_dim(inputs, column, 1, 0).reshape(own, width)
    inputs = inputs.reshape(rows, width).astype(f32)
    qkv_full = qkv_full.reshape(width, -1)
    small_full = small_full.reshape(width, -1)
    router_full = small_full[:, :expert_count]
    gain_full = small_full[:, expert_count : expert_count + 4].T.astype(f32)
    gain_attn, gain_ffn = gain_full[0], gain_full[3]
    gain_query = lax.dynamic_slice_in_dim(gain_full[1], column * local_width, local_width)
    gain_key = lax.dynamic_slice_in_dim(gain_full[2], column * local_width, local_width)
    own_grad_low = dealt_grads.reshape(own, width)
    grads_all = lax.all_gather(own_grad_low, BOTH, axis=0, tiled=True)
    own_in = own_low.astype(f32)
    own_grad = own_grad_low.astype(f32)

    scale = 1.0 / math.sqrt(HEAD_DIM)
    normed = (inputs * rms_inv(inputs) * gain_attn).astype(bf16)
    qkv = dot32(normed, qkv_full, NN)
    query_pre = qkv[:, :local_width]
    key_pre = qkv[:, local_width : 2 * local_width]
    squares = sum_few(
        jnp.stack([jnp.sum(query_pre * query_pre, axis=-1), jnp.sum(key_pre * key_pre, axis=-1)])
    )
    cosines, sines, starts = rope_tables(doc_ids, HEAD_DIM)
    cosines = reorder(jnp.concatenate([cosines, cosines], axis=1))
    sines = reorder(jnp.concatenate([-sines, sines], axis=1))
    positions = reorder(jnp.arange(rows, dtype=jnp.int32))
    spans = jnp.stack([reorder(starts), positions], axis=1)
    places = jnp.broadcast_to(positions[None], (8, rows))
    invs = lax.rsqrt(squares / width + NORM_EPS).T
    gains = jnp.stack([gain_query, gain_key])
    query_rot, key_rot, value_rows, attended, log_total, branch_own = attend(
        qkv, invs, gains, cosines, sines, spans, places, out_full
    )

    residual = own_in + branch_own
    resid_inv = rms_inv(residual)
    resid_hat = residual * resid_inv
    ffn_in = (resid_hat * gain_ffn).astype(bf16)
    logits = dot32(ffn_in, router_full, NN)
    router_probs = jax.nn.softmax(logits, axis=-1)
    local_experts = w_gate.shape[0]
    own_routes = lax.dynamic_slice(
        routes.reshape(blocks, parts, piece, -1),
        (0, column, 0, 0),
        (blocks, 1, piece, routes.shape[1]),
    ).reshape(own, -1)
    expert_ids = jnp.arange(expert_count, dtype=jnp.int32)
    routed = jnp.any(own_routes[:, :, None] == expert_ids[None, None, :], axis=1)
    gates_own = jnp.where(routed, router_probs, 0.0)

    hidden_width = w_gate.shape[2]
    joined_weight = jnp.concatenate(
        [w_gate[i] for i in range(local_experts)] + [w_up[i] for i in range(local_experts)], axis=1
    )
    down_weight = w_down.reshape(local_experts * hidden_width, width)
    rows_all, gates_all, pre_all, gated_all, mixed = experts_forward(
        ffn_in, gates_own.T, joined_weight, down_weight
    )
    mix_own, joined_grad, row_terms, gate_grads = experts_backward(
        mixed, grads_all, pre_all, gates_all, joined_weight, down_weight
    )
    output_own = (residual + mix_own).astype(bf16)
    row_own, gate_grad_own, d_w_gate, d_w_up, d_w_down = experts_weights(
        row_terms, gate_grads, rows_all, grads_all, joined_grad, gated_all
    )
    gate_grad_own = gate_grad_own.T
    d_w_down = d_w_down.reshape(w_down.shape)

    prob_grad = jnp.where(routed, gate_grad_own, 0.0)
    logit_grad = (
        router_probs * (prob_grad - jnp.sum(router_probs * prob_grad, axis=-1, keepdims=True))
    ).astype(bf16)
    d_router = dot32(ffn_in, logit_grad, TN)
    ffn_grad = row_own + dot32(logit_grad, router_full, NT)
    d_ffn_gain = jnp.sum(ffn_grad * resid_hat, axis=0)
    scaled_ffn = ffn_grad * gain_ffn
    resid_grad = own_grad + resid_inv * (
        scaled_ffn - resid_hat * jnp.mean(scaled_ffn * resid_hat, axis=-1, keepdims=True)
    )
    branch_grad = gather_tensor(resid_grad.astype(bf16))

    branch_cols = branch_grad.reshape(rows, blocks, width // blocks)
    d_wo = jnp.einsum("rk,red->ekd", attended, branch_cols, preferred_element_type=f32).astype(bf16)
    d_wo, branch_grad = lax.optimization_barrier((d_wo, branch_grad))
    sum_wo = lax.psum_scatter(d_wo, EXPERT, scatter_dimension=0, tiled=False)
    hat_grads, value_grad, dots, d_gains = attend_back(
        branch_grad, out_full, query_rot, key_rot, value_rows, log_total,
        qkv, invs, gains, cosines, sines, spans, places,
    )
    d_query_gain, d_key_gain = d_gains[0], d_gains[1]
    dots = sum_few(dots.reshape(2, rows)) / width

    def norm_back(i):
        part = slice(i * local_width, (i + 1) * local_width)
        inv = invs[:, i : i + 1]
        return (inv * (hat_grads[:, part] - qkv[:, part] * inv * dots[i][:, None])).astype(bf16)

    query_grad, key_grad = norm_back(0), norm_back(1)
    qkv_grad = jnp.concatenate([query_grad, key_grad, value_grad], axis=1)
    normed_grad = input_sum(qkv_grad, qkv_full)
    d_qkv = dot32(normed, qkv_grad, TN).astype(bf16)
    d_qkv, sum_wo = lax.optimization_barrier((d_qkv, sum_wo))

    own_inv = rms_inv(own_in)
    own_hat = own_in * own_inv
    d_attn_gain = jnp.sum(normed_grad * own_hat, axis=0)
    scaled_attn = normed_grad * gain_attn
    input_grad = resid_grad + own_inv * (
        scaled_attn - own_hat * jnp.mean(scaled_attn * own_hat, axis=-1, keepdims=True)
    )

    def widen(slots):
        return lax.dynamic_update_slice_in_dim(
            jnp.zeros((width,), f32), slots, column * local_width, 0
        )

    small = jnp.concatenate(
        [
            d_router.T,
            jnp.stack([d_attn_gain, widen(d_query_gain), widen(d_key_gain), d_ffn_gain]),
        ]
    )
    small = jnp.pad(small, ((0, 24 - small.shape[0]), (0, 0)))
    small = jnp.swapaxes(small.reshape(24, blocks, -1), 0, 1)

    back_out, back_in, sum_qkv, small = last_exchange(
        output_own.reshape(blocks, piece, width),
        input_grad.astype(bf16).reshape(blocks, piece, width),
        d_qkv.reshape(blocks, -1, d_qkv.shape[1]),
        small,
    )
    sum_router = small[:expert_count].T
    sum_gains = small[expert_count:]
    came = lax.dynamic_slice(deal_grid, (0, block, 0, 0), (blocks, 1, parts, piece))
    came = jnp.swapaxes(came.reshape(blocks, parts, piece), 0, 1).reshape(-1) - block * rows
    chooser = (jnp.arange(rows, dtype=jnp.int32)[:, None] == came[None, :]).astype(bf16)
    output = dot32(chooser, back_out.reshape(rows, width), NN).astype(bf16)
    d_tokens = dot32(chooser, back_in.reshape(rows, width), NN).astype(bf16)
    return (
        output,
        d_tokens,
        sum_gains[0],
        sum_qkv[:, :local_width],
        sum_qkv[:, local_width : 2 * local_width],
        sum_qkv[:, 2 * local_width :],
        sum_wo.astype(f32),
        sum_gains[1],
        sum_gains[2],
        sum_gains[3],
        sum_router,
        d_w_gate,
        d_w_up,
        d_w_down,
    )


def pick_body(*args):
    routes, experts = args[14], args[9].shape[1]
    mesh_fits = (lax.axis_size(EXPERT), lax.axis_size(TENSOR)) == (8, 4)
    body = dense_body if mesh_fits and experts <= 2 * routes.shape[1] else routed_body
    return body(*args)


def solution(mesh):
    in_specs = (
        P(EXPERT, None),
        P(EXPERT),
        P(EXPERT, TENSOR),
        P(EXPERT, TENSOR),
        P(EXPERT, TENSOR),
        P(TENSOR, EXPERT),
        P(EXPERT),
        P(EXPERT),
        P(EXPERT),
        P(EXPERT, None),
        P(EXPERT, None, TENSOR),
        P(EXPERT, None, TENSOR),
        P(EXPERT, TENSOR, None),
        P(EXPERT),
        P(EXPERT, None),
        P(),
        P(EXPERT, None),
    )
    out_specs = (
        P(EXPERT, None),
        P(EXPERT, None),
        P(EXPERT),
        P(EXPERT, TENSOR),
        P(EXPERT, TENSOR),
        P(EXPERT, TENSOR),
        P(TENSOR, EXPERT),
        P(EXPERT),
        P(EXPERT),
        P(EXPERT),
        P(EXPERT, None),
        P(EXPERT, None, TENSOR),
        P(EXPERT, None, TENSOR),
        P(EXPERT, TENSOR, None),
    )
    return jax.shard_map(pick_body, mesh=mesh, in_specs=in_specs, out_specs=out_specs, check_vma=False)
```

```python
import functools
import math

import jax
import jax.numpy as jnp
from jax import lax
from jax.experimental import pallas as pl
from jax.experimental.pallas import tpu as pltpu
from jax.sharding import PartitionSpec as P

HEAD_DIM = 128
EXPERT, TENSOR = "expert", "tensor"


NORM_EPS = 1e-05
ROPE_BASE = 10000.0


def rope_tables(documents, head_size):
    row_count = documents.shape[0]
    positions = jnp.arange(row_count, dtype=jnp.int32)
    new_doc = jnp.concatenate(
        [jnp.ones((1,), jnp.int32), (documents[1:] != documents[:-1]).astype(jnp.int32)]
    )
    starts = lax.cummax(jnp.where(new_doc > 0, positions, 0), axis=0)
    places = (positions - starts).astype(jnp.float32)
    half_dim = head_size // 2
    frequency = jnp.exp(
        jnp.arange(half_dim, dtype=jnp.float32) * (-2.0 * math.log(ROPE_BASE) / head_size)
    )
    angles = places[:, None] * frequency[None, :]
    return (jnp.cos(angles), jnp.sin(angles), starts)


def rotate(values, cosines, sines):
    half_dim = values.shape[-1] // 2
    first_half = values[..., :half_dim]
    second_half = values[..., half_dim:]
    cos_rows = cosines[:, None, :]
    sin_rows = sines[:, None, :]
    return jnp.concatenate(
        [
            first_half * cos_rows - second_half * sin_rows,
            second_half * cos_rows + first_half * sin_rows,
        ],
        axis=-1,
    )


def unrotate(grads_in, cosines, sines):
    half_dim = grads_in.shape[-1] // 2
    first_half = grads_in[..., :half_dim]
    second_half = grads_in[..., half_dim:]
    cos_rows = cosines[:, None, :]
    sin_rows = sines[:, None, :]
    return jnp.concatenate(
        [
            first_half * cos_rows + second_half * sin_rows,
            second_half * cos_rows - first_half * sin_rows,
        ],
        axis=-1,
    )


def to_experts(rows):
    return lax.all_to_all(rows, EXPERT, split_axis=0, concat_axis=0, tiled=True)


def from_experts(rows):
    return lax.all_to_all(rows, EXPERT, split_axis=0, concat_axis=0, tiled=True)


def hidden_sums(terms):
    return lax.psum_scatter(terms, TENSOR, scatter_dimension=3, tiled=True)


def routed_body(
    tokens,
    attn_gain,
    w_query,
    w_key,
    w_value,
    w_out,
    query_gain,
    key_gain,
    ffn_gain,
    w_router,
    w_gate,
    w_up,
    w_down,
    doc_ids,
    routes,
    deal,
    out_grad,
):
    row_count, width = tokens.shape
    tensor_parts = lax.axis_size(TENSOR)
    expert_parts = lax.axis_size(EXPERT)
    column = lax.axis_index(TENSOR)
    device_idx = lax.axis_index(EXPERT)
    quarter = width // tensor_parts
    share_rows = row_count // expert_parts
    deal_rows = lax.dynamic_slice_in_dim(
        deal.reshape(expert_parts, row_count), device_idx * share_rows, share_rows, 1
    )
    local_pick = deal_rows - device_idx * row_count
    dealt_tokens, dealt_grad = (
        lax.all_to_all(tokens[local_pick], EXPERT, split_axis=0, concat_axis=0, tiled=True),
        lax.all_to_all(out_grad[local_pick], EXPERT, split_axis=0, concat_axis=0, tiled=True),
    )
    dealt_tokens = dealt_tokens.reshape(row_count, width)
    dealt_grad = dealt_grad.reshape(row_count, width)
    gain_stack = jnp.stack([attn_gain, query_gain, key_gain, ffn_gain])
    wq_full, wk_full, wv_full, wo_full, router_full, gain_full = (
        lax.all_gather(w_query, EXPERT, axis=0, tiled=True),
        lax.all_gather(w_key, EXPERT, axis=0, tiled=True),
        lax.all_gather(w_value, EXPERT, axis=0, tiled=True),
        lax.all_gather(w_out, EXPERT, axis=1, tiled=True),
        lax.all_gather(w_router, EXPERT, axis=0, tiled=True),
        lax.all_gather(gain_stack, EXPERT, axis=1, tiled=True),
    )
    local_width = wq_full.shape[1]
    head_count = local_width // HEAD_DIM
    gain_attn = gain_full[0].astype(jnp.float32)
    gain_query = lax.dynamic_slice_in_dim(
        gain_full[1].astype(jnp.float32), column * local_width, local_width
    )
    gain_key = lax.dynamic_slice_in_dim(
        gain_full[2].astype(jnp.float32), column * local_width, local_width
    )
    gain_ffn = gain_full[3].astype(jnp.float32)
    scale = 1.0 / math.sqrt(HEAD_DIM)
    inputs = dealt_tokens.astype(jnp.float32)
    input_inv = lax.rsqrt(jnp.mean(inputs * inputs, axis=-1, keepdims=True) + NORM_EPS)
    input_hat = inputs * input_inv
    normed = (input_hat * gain_attn).astype(jnp.bfloat16)
    query_pre = jnp.dot(normed, wq_full, preferred_element_type=jnp.float32)
    key_pre = jnp.dot(normed, wk_full, preferred_element_type=jnp.float32)
    value_rows = (
        jnp.dot(normed, wv_full, preferred_element_type=jnp.float32)
        .astype(jnp.bfloat16)
        .reshape(row_count, head_count, HEAD_DIM)
    )
    query_sq, key_sq = lax.psum(
        (jnp.sum(query_pre * query_pre, axis=-1), jnp.sum(key_pre * key_pre, axis=-1)), TENSOR
    )
    query_inv = lax.rsqrt(query_sq / width + NORM_EPS)[:, None]
    key_inv = lax.rsqrt(key_sq / width + NORM_EPS)[:, None]
    query_hat = query_pre * query_inv
    key_hat = key_pre * key_inv
    cosines, sines, _ = rope_tables(doc_ids, HEAD_DIM)
    query_rot = rotate(
        (query_hat * gain_query).reshape(row_count, head_count, HEAD_DIM), cosines, sines
    ).astype(jnp.bfloat16)
    key_rot = rotate(
        (key_hat * gain_key).reshape(row_count, head_count, HEAD_DIM), cosines, sines
    ).astype(jnp.bfloat16)
    positions = jnp.arange(row_count, dtype=jnp.int32)
    allowed = (doc_ids[:, None] == doc_ids[None, :]) & (positions[None, :] <= positions[:, None])

    def masked_scores():
        raw_scores = jnp.einsum(
            "qhd,khd->hqk", query_rot, key_rot, preferred_element_type=jnp.float32
        )
        return jnp.where(allowed[None], raw_scores * scale, -1e30)

    scores = masked_scores()
    top_score = jnp.max(scores, axis=-1, keepdims=True)
    log_total = top_score + jnp.log(jnp.sum(jnp.exp(scores - top_score), axis=-1, keepdims=True))
    weights = jnp.exp(scores - log_total).astype(jnp.bfloat16)
    attended = (
        jnp.einsum("hqk,khd->qhd", weights, value_rows, preferred_element_type=jnp.float32)
        .astype(jnp.bfloat16)
        .reshape(row_count, local_width)
    )
    branch = lax.psum(jnp.dot(attended, wo_full, preferred_element_type=jnp.float32), TENSOR)
    residual = inputs + branch
    resid_inv = lax.rsqrt(jnp.mean(residual * residual, axis=-1, keepdims=True) + NORM_EPS)
    resid_hat = residual * resid_inv
    ffn_in = (resid_hat * gain_ffn).astype(jnp.bfloat16)
    logits = jnp.dot(ffn_in, router_full, preferred_element_type=jnp.float32)
    router_probs = jax.nn.softmax(logits, axis=-1)
    expert_count = router_full.shape[1]
    top_count = routes.shape[1]
    local_experts = expert_count // expert_parts
    capacity = tensor_parts * max(
        1,
        (row_count * top_count + expert_count * tensor_parts - 1) // (expert_count * tensor_parts),
        row_count * top_count * 5 // (4 * expert_count * tensor_parts),
    )
    expert_ids = jnp.arange(expert_count, dtype=jnp.int32)
    route_match = routes[:, :, None] == expert_ids[None, None, :]
    gate_probs = jnp.sum(jnp.where(route_match, router_probs[:, None, :], 0.0), axis=-1)
    flat_routes = routes.reshape(-1)
    onehot = (flat_routes[:, None] == expert_ids[None, :]).astype(jnp.int32)
    slot_rank = jnp.sum((jnp.cumsum(onehot, axis=0) - onehot) * onehot, axis=-1)
    row_ids = flat_routes * capacity + slot_rank
    token_ids = jnp.arange(row_count * top_count, dtype=jnp.int32) // top_count
    slot_token = (
        jnp.full((expert_count * capacity,), row_count, jnp.int32).at[row_ids].set(token_ids)
    )
    slot_gates = (
        jnp.zeros((expert_count * capacity,), jnp.float32).at[row_ids].set(gate_probs.reshape(-1))
    )
    pick_rows = row_ids.reshape(row_count, top_count)
    padded_in = jnp.concatenate([ffn_in, jnp.zeros((1, width), jnp.bfloat16)], axis=0)
    grad_full = dealt_grad.astype(jnp.float32)
    grad_padded = jnp.concatenate([grad_full, jnp.zeros((1, width), jnp.float32)], axis=0)
    received = to_experts(
        padded_in[slot_token].reshape(expert_parts, local_experts, capacity, width)
    )
    gate_pre = jnp.einsum("secd,edf->secf", received, w_gate, preferred_element_type=jnp.float32)
    up_pre = jnp.einsum("secd,edf->secf", received, w_up, preferred_element_type=jnp.float32)
    sigmoid_gate = jax.nn.sigmoid(gate_pre)
    silu_gate = gate_pre * sigmoid_gate
    hidden = (silu_gate * up_pre).astype(jnp.bfloat16)
    partial_out = jnp.einsum("secf,efd->secd", hidden, w_down, preferred_element_type=jnp.float32)
    own_columns = hidden_sums(partial_out).astype(jnp.bfloat16)
    returned = from_experts(own_columns).reshape(expert_count * capacity, quarter)
    chosen = returned[pick_rows].astype(jnp.float32)
    mix_own = jnp.sum(gate_probs[:, :, None] * chosen, axis=1)
    mix_part = lax.dynamic_update_slice_in_dim(
        jnp.zeros((row_count, width), jnp.float32), mix_own, column * quarter, 1
    )
    grad_own = lax.dynamic_slice_in_dim(grad_full, column * quarter, quarter, 1)
    gate_grad_part = jnp.sum(grad_own[:, None, :] * chosen, axis=-1)
    send_grad = (
        (grad_padded[slot_token] * slot_gates[:, None])
        .astype(jnp.bfloat16)
        .reshape(expert_parts, local_experts, capacity, width)
    )
    recv_grad = to_experts(send_grad)
    d_w_down = jnp.einsum("secf,secd->efd", hidden, recv_grad, preferred_element_type=jnp.float32)
    hidden_grad = jnp.einsum(
        "secd,efd->secf", recv_grad, w_down, preferred_element_type=jnp.float32
    )
    gate_grad_pre = (
        hidden_grad * up_pre * sigmoid_gate * (1.0 + gate_pre * (1.0 - sigmoid_gate))
    ).astype(jnp.bfloat16)
    up_grad_pre = (hidden_grad * silu_gate).astype(jnp.bfloat16)
    d_w_gate = jnp.einsum(
        "secd,secf->edf", received, gate_grad_pre, preferred_element_type=jnp.float32
    )
    d_w_up = jnp.einsum("secd,secf->edf", received, up_grad_pre, preferred_element_type=jnp.float32)
    joined_grad = jnp.concatenate([gate_grad_pre, up_grad_pre], axis=-1)
    joined_weight = jnp.concatenate([w_gate, w_up], axis=-1)
    row_terms = jnp.einsum(
        "secf,edf->secd", joined_grad, joined_weight, preferred_element_type=jnp.float32
    )
    row_own = hidden_sums(row_terms).astype(jnp.bfloat16)
    row_back = from_experts(row_own).reshape(expert_count * capacity, quarter)
    ffn_grad_own = jnp.sum(row_back[pick_rows].astype(jnp.float32), axis=1)
    placed = lax.dynamic_update_slice_in_dim(
        jnp.zeros((row_count, width), jnp.float32), ffn_grad_own, column * quarter, 1
    )
    ffn_grad_rows, gate_grad, mix_total = lax.psum((placed, gate_grad_part, mix_part), TENSOR)
    output = (residual + mix_total).astype(jnp.bfloat16)
    prob_grad = jnp.sum(jnp.where(route_match, gate_grad[:, :, None], 0.0), axis=1)
    logit_grad = (
        router_probs * (prob_grad - jnp.sum(router_probs * prob_grad, axis=-1, keepdims=True))
    ).astype(jnp.bfloat16)
    d_router = jnp.einsum("rd,re->de", ffn_in, logit_grad, preferred_element_type=jnp.float32)
    ffn_grad = ffn_grad_rows + jnp.einsum(
        "re,de->rd", logit_grad, router_full, preferred_element_type=jnp.float32
    )
    d_ffn_gain = jnp.sum(ffn_grad * resid_hat, axis=0)
    scaled_ffn = ffn_grad * gain_ffn
    resid_grad = grad_full + resid_inv * (
        scaled_ffn - resid_hat * jnp.mean(scaled_ffn * resid_hat, axis=-1, keepdims=True)
    )
    branch_grad = resid_grad.astype(jnp.bfloat16)
    d_wo = jnp.einsum("rk,rd->kd", attended, branch_grad, preferred_element_type=jnp.float32)
    attended_grad = (
        jnp.einsum("rd,kd->rk", branch_grad, wo_full, preferred_element_type=jnp.float32)
        .astype(jnp.bfloat16)
        .reshape(row_count, head_count, HEAD_DIM)
    )
    probs_again = jnp.exp(masked_scores() - log_total)
    prob_grads = jnp.einsum(
        "qhd,khd->hqk", attended_grad, value_rows, preferred_element_type=jnp.float32
    )
    value_grad = (
        jnp.einsum(
            "hqk,qhd->khd",
            probs_again.astype(jnp.bfloat16),
            attended_grad,
            preferred_element_type=jnp.float32,
        )
        .astype(jnp.bfloat16)
        .reshape(row_count, local_width)
    )
    row_delta = jnp.sum(probs_again * prob_grads, axis=-1, keepdims=True)
    score_grad = (probs_again * (prob_grads - row_delta) * scale).astype(jnp.bfloat16)
    query_rot_grad = jnp.einsum(
        "hqk,khd->qhd", score_grad, key_rot, preferred_element_type=jnp.float32
    )
    key_rot_grad = jnp.einsum(
        "hqk,qhd->khd", score_grad, query_rot, preferred_element_type=jnp.float32
    )
    query_norm_grad = unrotate(query_rot_grad, cosines, sines).reshape(row_count, local_width)
    key_norm_grad = unrotate(key_rot_grad, cosines, sines).reshape(row_count, local_width)
    query_hat_grad = query_norm_grad * gain_query
    key_hat_grad = key_norm_grad * gain_key
    gain_pieces = jnp.stack(
        [jnp.sum(query_norm_grad * query_hat, axis=0), jnp.sum(key_norm_grad * key_hat, axis=0)]
    )
    gain_parts = lax.dynamic_update_slice_in_dim(
        jnp.zeros((2, width), jnp.float32), gain_pieces, column * local_width, 1
    )
    query_dot, key_dot, qk_gains = lax.psum(
        (
            jnp.sum(query_hat_grad * query_hat, axis=-1),
            jnp.sum(key_hat_grad * key_hat, axis=-1),
            gain_parts,
        ),
        TENSOR,
    )
    query_grad = (query_inv * (query_hat_grad - query_hat * (query_dot / width)[:, None])).astype(
        jnp.bfloat16
    )
    key_grad = (key_inv * (key_hat_grad - key_hat * (key_dot / width)[:, None])).astype(
        jnp.bfloat16
    )
    d_wq = jnp.einsum("rd,rk->dk", normed, query_grad, preferred_element_type=jnp.float32)
    d_wk = jnp.einsum("rd,rk->dk", normed, key_grad, preferred_element_type=jnp.float32)
    d_wv = jnp.einsum("rd,rk->dk", normed, value_grad, preferred_element_type=jnp.float32)
    input_terms = jnp.einsum("rk,dk->rd", query_grad, wq_full, preferred_element_type=jnp.float32)
    input_terms = input_terms + jnp.einsum(
        "rk,dk->rd", key_grad, wk_full, preferred_element_type=jnp.float32
    )
    input_terms = input_terms + jnp.einsum(
        "rk,dk->rd", value_grad, wv_full, preferred_element_type=jnp.float32
    )
    normed_grad = lax.psum(input_terms, TENSOR)
    d_attn_part = jnp.sum(normed_grad * input_hat, axis=0)
    scaled_attn = normed_grad * gain_attn
    input_grad = resid_grad + input_inv * (
        scaled_attn - input_hat * jnp.mean(scaled_attn * input_hat, axis=-1, keepdims=True)
    )
    dealt_dtokens = input_grad.astype(jnp.bfloat16)
    gain_grads = jnp.stack([d_attn_part, qk_gains[0], qk_gains[1], d_ffn_gain])
    sum_wq, sum_wk, sum_wv, sum_wo, sum_router, sum_gains = (
        lax.psum_scatter(d_wq, EXPERT, scatter_dimension=0, tiled=True),
        lax.psum_scatter(d_wk, EXPERT, scatter_dimension=0, tiled=True),
        lax.psum_scatter(d_wv, EXPERT, scatter_dimension=0, tiled=True),
        lax.psum_scatter(d_wo, EXPERT, scatter_dimension=1, tiled=True),
        lax.psum_scatter(d_router, EXPERT, scatter_dimension=0, tiled=True),
        lax.psum_scatter(gain_grads, EXPERT, scatter_dimension=1, tiled=True),
    )
    back_out, back_dtok = (
        lax.all_to_all(
            output.reshape(expert_parts, share_rows, width),
            EXPERT,
            split_axis=0,
            concat_axis=0,
            tiled=True,
        ),
        lax.all_to_all(
            dealt_dtokens.reshape(expert_parts, share_rows, width),
            EXPERT,
            split_axis=0,
            concat_axis=0,
            tiled=True,
        ),
    )
    flat_pick = local_pick.reshape(-1)
    output_rows = (
        jnp.zeros((row_count, width), jnp.bfloat16)
        .at[flat_pick]
        .set(back_out.reshape(row_count, width))
    )
    d_tokens = (
        jnp.zeros((row_count, width), jnp.bfloat16)
        .at[flat_pick]
        .set(back_dtok.reshape(row_count, width))
    )
    return (
        output_rows,
        d_tokens,
        sum_gains[0],
        sum_wq,
        sum_wk,
        sum_wv,
        sum_wo,
        sum_gains[1],
        sum_gains[2],
        sum_gains[3],
        sum_router,
        d_w_gate,
        d_w_up,
        d_w_down,
    )


MESH_ID = pl.DeviceIdType.MESH
ANY = pl.BlockSpec(memory_space=pl.ANY)
IN_VMEM = pl.BlockSpec(memory_space=pltpu.VMEM)
def cost_of(micros):
    return pl.CostEstimate(flops=0, bytes_accessed=micros * 3_000_000, transcendentals=0)


SELF, NEAR, FAR, BOTH_FLIPPED = 0, 1, 2, 3


def place_of(device):
    expert, tensor = device
    return expert // 2, expert % 2, tensor // 2, tensor % 2


def flipped(device, role):
    expert, tensor = device
    _, x, y, core = place_of(device)
    step_x, step_y = 1 - 2 * x, 2 - 4 * y
    if role == NEAR:
        return expert + (1 - core) * step_x, tensor + core * step_y
    if role == FAR:
        return expert + core * step_x, tensor + (1 - core) * step_y
    if role == BOTH_FLIPPED:
        return expert + step_x, tensor + step_y
    return expert, tensor


def moved_z(device, hops):
    expert, tensor = device
    return lax.rem(expert + 2 * hops, 8), tensor


def sibling(device):
    expert, tensor = device
    return expert, tensor + 1 - 2 * (tensor % 2)


def slot_of(device):
    return device[0] * 4 + device[1]


def here():
    return lax.axis_index(EXPERT), lax.axis_index(TENSOR)


def greet(partners):
    barrier = pltpu.get_barrier_semaphore()
    for partner in partners:
        pl.semaphore_signal(barrier, inc=1, device_id=partner, device_id_type=MESH_ID)
    pl.semaphore_wait(barrier, len(partners))


def push(source, target, send_sem, recv_sem, device):
    return pltpu.make_async_remote_copy(
        src_ref=source,
        dst_ref=target,
        send_sem=send_sem,
        recv_sem=recv_sem,
        device_id=device,
        device_id_type=MESH_ID,
    )


def hop(device, flips, hops):
    expert, tensor = device
    return lax.rem(expert + flips * (1 - 2 * lax.rem(expert, 2)) + 2 * hops, 8), tensor


def across_y(device):
    expert, tensor = device
    return expert, lax.rem(tensor + 2, 4)


class Line:
    def __init__(self, send_sem, recv_sem):
        self.send_sem, self.recv_sem = send_sem, recv_sem
        self.started = []

    def send(self, source, target, tag, recv_tag, device):
        copy = push(source, target, self.send_sem.at[tag], self.recv_sem.at[recv_tag], device)
        copy.start()
        self.started.append(copy)

    def wait(self, target, tag, device):
        push(target, target, self.send_sem.at[0], self.recv_sem.at[tag], device).wait_recv()

    def finish(self):
        for copy in self.started:
            copy.wait_send()


PIECES = ((0, 1), (1, 0), (3, 0), (1, 1), (3, 1), (2, 0), (2, 1))


def exchange_steps(source, out, gathered, line, local_sem):
    me = here()
    tensor = me[1]
    side, sib = across_y(me), sibling(me)

    def at(column, expert):
        return out.at[column, expert] if gathered else out.at[expert]

    local = pltpu.make_async_copy(source.at[me[0]], at(tensor, me[0]), local_sem)
    local.start()
    if gathered:
        line.send(source.at[me[0]], at(tensor, me[0]), 8, 8, side)
        line.send(source.at[me[0]], at(tensor, me[0]), 16, 16, sib)
    for k, flips in PIECES:
        target = hop(me, flips, k)
        line.send(
            source.at[target[0]], at(tensor, me[0]), k * 2 + flips, (4 - k) % 4 * 2 + flips, target
        )
    yield
    for k, flips in PIECES:
        expert = hop(me, flips, k)[0]
        tag = k * 2 + flips
        line.wait(at(tensor, expert), tag, sib)
        if gathered:
            line.send(at(tensor, expert), at(tensor, expert), 8 + tag, 8 + tag, side)
            line.send(at(tensor, expert), at(tensor, expert), 16 + tag, 16 + tag, sib)
        yield
    if gathered:
        for k, flips in ((0, 0),) + PIECES:
            expert = hop(me, flips, k)[0]
            tag = k * 2 + flips
            line.wait(at(side[1], expert), 8 + tag, sib)
            line.send(at(side[1], expert), at(side[1], expert), 24 + tag, 24 + tag, sib)
            yield
        for k, flips in ((0, 0),) + PIECES:
            expert = hop(me, flips, k)[0]
            tag = k * 2 + flips
            line.wait(at(sib[1], expert), 16 + tag, sib)
            line.wait(at(across_y(sib)[1], expert), 24 + tag, sib)
    local.wait()
    line.finish()


def gather_expert_steps(sources, outs, plans, line, local_sems):
    me = here()
    z = me[0] // 2
    beside = hop(me, 1, 0)
    locals_ = [
        pltpu.make_async_copy(source, out.at[me[0]], local_sems.at[n])
        for n, (source, out) in enumerate(zip(sources, outs))
    ]
    for copy in locals_:
        copy.start()
    items = [(n, i, i < s) for n, (c, s) in enumerate(plans) for i in range(c)]
    count = len(items)
    straight = [j for j in range(count) if items[j][2]]
    crossed = [j for j in range(count) if not items[j][2]]

    def window(ref, j):
        n, i, _ = items[j]
        step = sources[n].shape[0] // plans[n][0]
        return ref.at[pl.ds(i * step, step), :]

    def own(j):
        return window(sources[items[j][0]], j)

    def block_of(expert, j):
        return window(outs[items[j][0]].at[expert], j)

    def base(distance, up, j):
        return ((distance - 1) * 2 + up) * count + j

    def passes(ref, target, tag, up, held):
        @pl.when(held & ((z < 3) if up else (z > 0)))
        def _():
            push(
                ref, target, line.send_sem.at[tag], line.recv_sem.at[tag], hop(me, 0, 1 if up else 3)
            ).start()

    def came(column, distance, up):
        return lax.rem(column[0] + (8 - 2 * distance if up else 2 * distance), 8)

    def is_held(distance, up):
        return (z >= distance) if up else (z + distance <= 3)

    cross, over = 6 * count, 12 * count
    for j in crossed + straight:
        line.send(own(j), block_of(me[0], j), over + j, over + j, beside)
    for j in straight + crossed:
        for up in (1, 0):
            passes(own(j), block_of(me[0], j), base(1, up, j), up, z >= 0)
    yield
    for j in crossed:
        block = block_of(beside[0], j)
        line.wait(block, over + j, beside)
        for up in (1, 0):
            passes(block, block, cross + base(1, up, j), up, z >= 0)
    yield
    for distance in (1, 2, 3):
        for j in straight + crossed:
            for up in (1, 0):
                held = is_held(distance, up)
                block = block_of(came(me, distance, up), j)
                tag = base(distance, up, j)

                @pl.when(held)
                def _():
                    line.wait(block, tag, beside)

                if distance < 3:
                    passes(block, block, base(distance + 1, up, j), up, held)
                if items[j][2]:

                    @pl.when(held)
                    def _():
                        push(
                            block,
                            block,
                            line.send_sem.at[cross + tag],
                            line.recv_sem.at[cross + tag],
                            beside,
                        ).start()

            yield
        for j in crossed:
            for up in (1, 0):
                held = is_held(distance, up)
                block = block_of(came(beside, distance, up), j)
                tag = cross + base(distance, up, j)

                @pl.when(held)
                def _():
                    line.wait(block, tag, beside)

                if distance < 3:
                    passes(block, block, cross + base(distance + 1, up, j), up, held)
            yield
    for j in straight:
        line.wait(block_of(beside[0], j), over + j, beside)
    for distance in (1, 2, 3):
        for j in straight + crossed:
            for up in (1, 0):
                held = is_held(distance, up)
                block = block_of(came(beside, distance, up), j)
                tag = base(distance, up, j)
                sent_on = (z + 1 >= distance) & (z < 3) if up else (z - 1 + distance <= 3) & (z > 0)

                def sent(at):
                    push(block, block, line.send_sem.at[at], line.recv_sem.at[at], beside).wait_send()

                if items[j][2]:

                    @pl.when(held)
                    def _():
                        sent(cross + tag)
                        line.wait(block, cross + tag, beside)

                @pl.when(sent_on)
                def _():
                    sent(tag)
                    if not items[j][2]:
                        sent(cross + tag)

        yield
    for copy in locals_:
        copy.wait()
    line.finish()


def sum_rows(target, terms, step=16):
    def body(i, carry):
        window = pl.ds(pl.multiple_of(i * step, step), step)
        value = terms[0][window, :].astype(jnp.float32)
        for ref in terms[1:]:
            value = value + ref[window, :].astype(jnp.float32)
        target[window, :] = value.astype(target.dtype)
        return carry

    lax.fori_loop(0, target.shape[0] // step, body, 0)


def sum_expert_steps(part, out, mine, from_x, from_z, line, load_sem, step=16):
    me = here()
    beside = hop(me, 1, 0)
    loads = {}
    for k in (2, 1, 3, 0):
        line.send(part.at[hop(me, 1, k)[0]], from_x.at[k], k, k, beside)
        loads[k] = pltpu.make_async_copy(part.at[hop(me, 0, k)[0]], mine.at[k], load_sem.at[k])
        loads[k].start()
    yield
    for k in (2, 1, 3, 0):
        loads[k].wait()
        line.wait(from_x.at[k], k, beside)
        if k:
            sum_rows(mine.at[k], [mine.at[k], from_x.at[k]], step)
            line.send(mine.at[k], from_z.at[3 - k], 3 + k, 4 + 3 - k, hop(me, 0, k))
            yield
            yield
    for i in range(3):
        line.wait(from_z.at[i], 4 + i, beside)
    sum_rows(out, [mine.at[0], from_x.at[0], from_z.at[0], from_z.at[1], from_z.at[2]], step)
    line.finish()


CHAIN = (3, 0, 2, 1)


def sum_chain_steps(part, out, mine, from_x, arrive, from_b, line, load_sem, straight):
    me = here()
    z = me[0] // 2
    x = lax.rem(me[0], 2)
    low = z < 2
    near = jnp.where(low, z, 3 - z)
    behind = jnp.where(low, 0, 1)
    beside = hop(me, 1, 0)
    step = mine.shape[2]
    chunks = out.shape[0] // step
    streams = []
    for i in range(straight, chunks):
        streams += [(i, 1, None), (i, 0, None)]
    streams += [(i, 0, i) for i in range(straight)]
    first_x = len(streams) * 4
    first_b = first_x + straight * 4
    recv_x = len(streams) * 8
    recv_b = recv_x + straight * 4

    def plane(a):
        return jnp.where(low, a, 3 - a)

    def chunk_of(expert, i):
        return part.at[expert, pl.ds(i * step, step), :]

    def column(flip):
        return jnp.where(flip == 1, 1 - x, x)

    def load(s, a):
        i, flip, _ = streams[s]
        p = plane(a)
        return pltpu.make_async_copy(
            chunk_of(2 * p + column(flip), i), mine.at[s, p], load_sem.at[s * 4 + p]
        )

    for a in CHAIN:
        p = plane(a)
        for s, (i, _, at) in enumerate(streams):
            if at is not None:
                line.send(
                    chunk_of(2 * p + 1 - x, i), from_x.at[at, p], first_x + at * 4 + p,
                    recv_x + at * 4 + p, beside,
                )
            load(s, a).start()
    yield

    def own_terms(s, a):
        p = plane(a)
        load(s, a).wait()
        at = streams[s][2]
        if at is None:
            return [mine.at[s, p]]
        line.wait(from_x.at[at, p], recv_x + at * 4 + p, beside)
        return [mine.at[s, p], from_x.at[at, p]]

    def arrived(s, a, side):
        p = plane(a)
        ref = arrive.at[s, side, p]
        line.wait(ref, (s * 2 + side) * 4 + p, beside)
        return ref

    def passing(s, a, forward):
        p = plane(a)
        side = behind if forward else 1 - behind
        up = jnp.where(low, 1, 3) if forward else jnp.where(low, 3, 1)
        return push(
            mine.at[s, p],
            arrive.at[s, side, p],
            line.send_sem.at[s * 4 + p],
            line.recv_sem.at[(s * 2 + side) * 4 + p],
            hop(me, 0, up),
        )

    def pass_on(s, a, forward, sides):
        terms = own_terms(s, a) + [arrived(s, a, side) for side in sides]
        if len(terms) > 1:
            sum_rows(mine.at[s, plane(a)], terms)
        passing(s, a, forward).start()

    for a in CHAIN:
        for s in range(len(streams)):
            if a != 0:

                @pl.when(near == 0)
                def _():
                    pass_on(s, a, True, [])

            if a != 1:

                @pl.when(near == 1)
                def _():
                    pass_on(s, a, a != 0, [1 - behind if a == 0 else behind])

            yield

    def final(s, a, sides):
        i, flip, at = streams[s]
        terms = own_terms(s, a) + [arrived(s, a, side) for side in sides]
        if flip:
            total = mine.at[s, plane(a)]
            sum_rows(total, terms)
            j = i - straight
            push(
                total, from_b.at[j], line.send_sem.at[first_b + j], line.recv_sem.at[recv_b + j], beside
            ).start()
        else:
            sum_rows(out.at[pl.ds(i * step, step), :], terms)

    for s in sorted(range(len(streams)), key=lambda s: streams[s][2] is not None):

        @pl.when(near == 0)
        def _():
            final(s, 0, [1 - behind])

        @pl.when(near == 1)
        def _():
            final(s, 1, [behind, 1 - behind])

        yield
    for j in range(chunks - straight):
        rows = out.at[pl.ds((straight + j) * step, step), :]
        both = push(
            from_b.at[j], from_b.at[j], line.send_sem.at[first_b + j], line.recv_sem.at[recv_b + j], beside
        )
        both.wait()
        sum_rows(rows, [rows, from_b.at[j]])
    for a in CHAIN:
        for s in range(len(streams)):
            if a != 0:

                @pl.when(near == 0)
                def _():
                    passing(s, a, True).wait_send()

            if a != 1:

                @pl.when(near == 1)
                def _():
                    passing(s, a, a != 0).wait_send()

    line.finish()


def sum_everywhere_steps(part, out, mine, from_x, from_z, total, shares, line, load_sem):
    me = here()
    yield from sum_expert_steps(part, total, mine, from_x, from_z, line, load_sem, 8)
    peers = [across_y(me), sibling(me), across_y(sibling(me))]
    for i, peer in enumerate(peers):
        line.send(total, shares.at[me[1]], 7 + i, 7 + i, peer)
    shares[me[1]] = total[...]
    yield
    for i, peer in enumerate(peers):
        line.wait(shares.at[peer[1]], 7 + i, peer)
    sum_rows(out, [shares.at[i] for i in range(4)], 8)
    for i in range(3):
        line.started[-3 + i].wait_send()


def take_turns(steps):
    steps = list(steps)
    while steps:
        steps = [s for s in steps if next(s, steps) is not steps]


DMA = pltpu.SemaphoreType.DMA


GATHER_PLANS = ((1, 1), (4, 3), (2, 2))


def start_kernel(
    tokens, grads, weights, outs, small, o_tokens, o_grads, o_weights, o_outs, o_small, *sems
):
    me = here()
    pieces = [hop(me, flips, k) for k, flips in PIECES]
    greet(pieces + [across_y(me), sibling(me)])
    local = sems[7]
    take_turns(
        [
            exchange_steps(tokens, o_tokens, True, Line(sems[0], sems[1]), local.at[0]),
            exchange_steps(grads, o_grads, False, Line(sems[2], sems[3]), local.at[1]),
            gather_expert_steps(
                [small, weights, outs], [o_small, o_weights, o_outs], GATHER_PLANS,
                Line(sems[4], sems[5]), sems[6],
            ),
        ]
    )


def start_exchange(tokens, grads, weights, outs, small):
    piece = tokens.shape[1:]
    sds = jax.ShapeDtypeStruct
    return pl.pallas_call(
        start_kernel,
        out_shape=[
            sds((4, 8) + piece, tokens.dtype),
            sds((8,) + piece, grads.dtype),
            sds((8,) + weights.shape, weights.dtype),
            sds((8,) + outs.shape, outs.dtype),
            sds((8,) + small.shape, small.dtype),
        ],
        in_specs=[IN_VMEM] * 5,
        out_specs=[ANY] * 5,
        scratch_shapes=[DMA((32,)), DMA((32,)), DMA((8,)), DMA((8,))]
        + [DMA((13 * sum(c for c, _ in GATHER_PLANS),))] * 2
        + [DMA((3,)), DMA((2,))],
        compiler_params=pltpu.CompilerParams(
            collective_id=4, has_side_effects=True, vmem_limit_bytes=16 * 2**20
        ),
        cost_estimate=cost_of(100),
        name="start_exchange",
    )(tokens, grads, weights, outs, small)


def last_kernel(
    rows, more, part, small, o_rows, o_more, out, o_small,
    mine, from_x, arrive, from_b, mine_s, x_s, z_s, total_s, shares_s, *sems,
):
    me = here()
    pieces = [hop(me, flips, k) for k, flips in PIECES]
    greet(pieces + [across_y(me), sibling(me), across_y(sibling(me))])
    take_turns(
        [
            exchange_steps(more, o_more, True, Line(sems[2], sems[3]), sems[7].at[1]),
            exchange_steps(rows, o_rows, True, Line(sems[0], sems[1]), sems[7].at[0]),
            sum_everywhere_steps(
                small, o_small, mine_s, x_s, z_s, total_s, shares_s, Line(sems[8], sems[9]), sems[10]
            ),
            sum_chain_steps(
                part, out, mine, from_x, arrive, from_b, Line(sems[4], sems[5]), sems[6], from_x.shape[0]
            ),
        ]
    )


def last_exchange(rows, more, part, small):
    piece = rows.shape[1:]
    block, little = part.shape[1:], small.shape[1:]
    chunks, straight = 8, 7
    streams = 2 * chunks - straight
    chunk = (block[0] // chunks, block[1])
    first = (streams + straight) * 4
    sds = jax.ShapeDtypeStruct
    return pl.pallas_call(
        last_kernel,
        out_shape=[
            sds((4, 8) + piece, rows.dtype),
            sds((4, 8) + piece, more.dtype),
            sds(block, jnp.float32),
            sds(little, jnp.float32),
        ],
        in_specs=[IN_VMEM, IN_VMEM, ANY, ANY],
        out_specs=[ANY, ANY, IN_VMEM, IN_VMEM],
        scratch_shapes=[
            pltpu.VMEM((streams, 4) + chunk, part.dtype),
            pltpu.VMEM((straight, 4) + chunk, part.dtype),
            pltpu.VMEM((streams, 2, 4) + chunk, part.dtype),
            pltpu.VMEM((chunks - straight,) + chunk, part.dtype),
        ]
        + [pltpu.VMEM((n,) + little, jnp.float32) for n in (4, 4, 3)]
        + [pltpu.VMEM(little, jnp.float32), pltpu.VMEM((4,) + little, jnp.float32)]
        + [DMA((32,))] * 4
        + [DMA((first + chunks,)), DMA((first + streams * 4 + chunks,)), DMA((streams * 4,)), DMA((2,))]
        + [DMA((10,)), DMA((10,)), DMA((4,))],
        compiler_params=pltpu.CompilerParams(
            collective_id=5, has_side_effects=True, vmem_limit_bytes=46 * 2**20
        ),
        cost_estimate=cost_of(1),
        name="last_exchange",
    )(rows, more, part, small)


def gather_tensor_kernel(source, out, send_sem, recv_sem, local_sem):
    me = here()
    side, sib = across_y(me), sibling(me)
    greet([side, sib])
    line = Line(send_sem, recv_sem)
    halves = 4
    step = source.shape[0] // halves

    def part(ref, i):
        return ref.at[pl.ds(i * step, step), :]

    local = pltpu.make_async_copy(source, out.at[me[1]], local_sem)
    for i in range(halves):
        line.send(part(source, i), part(out.at[me[1]], i), i, i, side)
        line.send(part(source, i), part(out.at[me[1]], i), 4 + i, 4 + i, sib)
    local.start()
    for i in range(halves):
        got = part(out.at[side[1]], i)
        line.wait(got, i, sib)
        line.send(got, got, 8 + i, 8 + i, sib)
    for i in range(halves):
        line.wait(part(out.at[sib[1]], i), 4 + i, sib)
        line.wait(part(out.at[across_y(sib)[1]], i), 8 + i, sib)
    local.wait()
    line.finish()


def gather_tensor(rows):
    out = pl.pallas_call(
        gather_tensor_kernel,
        out_shape=jax.ShapeDtypeStruct((4,) + rows.shape, rows.dtype),
        in_specs=[IN_VMEM],
        out_specs=ANY,
        scratch_shapes=[DMA((12,)), DMA((12,)), DMA],
        compiler_params=pltpu.CompilerParams(
            collective_id=6, has_side_effects=True, vmem_limit_bytes=8 * 2**20
        ),
        cost_estimate=cost_of(15),
        name="gather_tensor",
    )(rows)
    return out.reshape((-1,) + rows.shape[1:])


def sum_tensor_into(make, part, out, from_sib, from_side, total, line):
    me = here()
    side, sib = across_y(me), sibling(me)
    pieces = 4
    step = out.shape[0] // pieces

    def rows(ref, i):
        return ref.at[pl.ds(i * step, step), :]

    for j, column in ((0, across_y(sib)[1]), (1, sib[1])):
        make(column)
        for i in range(pieces):
            line.send(
                rows(part.at[column], i), rows(from_sib.at[j], i), 4 * j + i, 4 * j + i, sib
            )
    make(side[1])
    for i in range(pieces):
        got = rows(from_sib.at[0], i)
        line.wait(got, i, sib)
        sum_rows(rows(total, i), [rows(part.at[side[1]], i), got])
        line.send(rows(total, i), rows(from_side, i), 8 + i, 8 + i, side)
    make(me[1])
    for i in range(pieces):
        got = rows(from_sib.at[1], i)
        line.wait(got, 4 + i, sib)
        line.wait(rows(from_side, i), 8 + i, sib)
        sum_rows(rows(out, i), [rows(part.at[me[1]], i), got, rows(from_side, i)])
    line.finish()


def sum_tensor_scratch(block):
    bf16 = jnp.bfloat16
    return [
        pltpu.VMEM((4,) + block, bf16),
        pltpu.VMEM((2,) + block, bf16),
        pltpu.VMEM(block, bf16),
        pltpu.VMEM(block, bf16),
        DMA((12,)),
        DMA((12,)),
    ]


def input_sum_kernel(left, right, out, part, from_sib, from_side, total, send_sem, recv_sem):
    me = here()
    greet([across_y(me), sibling(me)])

    def make(column):
        rows = pl.ds(pl.multiple_of(column * out.shape[0], out.shape[0]), out.shape[0])
        for c in range(4):
            span = right.shape[0] // 4
            cols = slice(c * span, (c + 1) * span)
            part[column, :, cols] = dot32(left[rows, :], right[cols, :], NT).astype(jnp.bfloat16)

    sum_tensor_into(make, part, out, from_sib, from_side, total, Line(send_sem, recv_sem))


def input_sum(left, right):
    block = (left.shape[0] // 4, right.shape[0])
    return pl.pallas_call(
        input_sum_kernel,
        out_shape=jax.ShapeDtypeStruct(block, jnp.float32),
        in_specs=[IN_VMEM] * 2,
        out_specs=IN_VMEM,
        scratch_shapes=sum_tensor_scratch(block),
        compiler_params=pltpu.CompilerParams(
            collective_id=7, has_side_effects=True, vmem_limit_bytes=32 * 2**20
        ),
        cost_estimate=cost_of(1),
        name="input_sum",
    )(left, right)


def rows_at(ref, slot, size, count=1):
    return ref.at[pl.ds(pl.multiple_of(slot * size, size), size * count), :]


class Plan:
    def __init__(self, send_sem, recv_sem):
        self.send_sem, self.recv_sem, self.made = send_sem, recv_sem, []

    def send(self, make):
        make().start()
        self.made.append(make)

    def finish(self):
        for make in self.made:
            make().wait_send()


def gather_plan(ins, outs, sizes, send_sem, recv_sem):
    me = here()
    near, far, sib = flipped(me, NEAR), flipped(me, FAR), sibling(me)
    plan = Plan(send_sem, recv_sem)
    count = len(ins)

    def send(k, role, device, tag, recv_tag):
        for i in range(count):

            def make(i=i):
                block = rows_at(outs[i], slot_of(moved_z(flipped(me, role), k)), sizes[i])
                source = ins[i] if (k, role) == (0, SELF) else block
                return push(source, block, send_sem.at[i, tag], recv_sem.at[i, recv_tag], device)

            plan.send(make)

    def arrive(k, role):
        for i in range(count):
            block = rows_at(outs[i], slot_of(moved_z(flipped(me, role), k)), sizes[i])
            push(block, block, send_sem.at[i, 0], recv_sem.at[i, k * 4 + role], near).wait_recv()

    def forward(k, role):
        if role == SELF:
            send(k, SELF, far, 4 + k, k * 4 + FAR)
            send(k, SELF, near, k, k * 4 + NEAR)
        if role == NEAR:
            send(k, NEAR, far, 8 + k, k * 4 + BOTH_FLIPPED)
        send(k, role, sib, 16 + k * 4 + role, 16 + k * 4 + role)

    def event(k, role):
        arrive(k, role)
        forward(k, role)

    def from_sibling(k, role):
        for i in range(count):
            block = rows_at(outs[i], 0, sizes[i])
            push(
                block, block, send_sem.at[i, 0], recv_sem.at[i, 16 + k * 4 + role], near
            ).wait_recv()

    def begin():
        forward(0, SELF)
        for d in (1, 3, 2):
            send(0, SELF, moved_z(me, d), 11 + d, (4 - d) * 4 + SELF)

    return plan, begin, event, from_sibling


def gate_columns(gates_ref, slot, columns, first):
    lane = lax.broadcasted_iota(jnp.int32, (128, 128), 1)
    for s in range(4):
        block = gates_ref[pl.ds(pl.multiple_of((slot + s) * 16, 16), 16), :]
        turned = jnp.concatenate([block, jnp.zeros((112, 128), jnp.float32)], axis=0).T
        for i in range(2):
            column = jnp.sum(jnp.where(lane == first + i, turned, 0.0), axis=1, keepdims=True)
            columns[i, pl.ds(s * 128, 128), :] = jnp.broadcast_to(column, (128, 128))


def tiles(count, width, body):
    def step(n, carry):
        body(pl.ds(pl.multiple_of(n * width, width), width))
        return carry

    lax.fori_loop(0, count, step, 0)


STAGES = ((0, 0), (0, 1), (1, 0), (1, 1), (3, 0), (3, 1), (2, 0), (2, 1))
BLOCK = 512


def stage_expert(me, j):
    half = j // 2
    k = half + jnp.where(half == 2, 1, 0) - jnp.where(half == 3, 1, 0)
    flips = lax.rem(j, 2)
    expert = me[0]
    return lax.rem(expert + flips * (1 - 2 * lax.rem(expert, 2)) + 2 * k, 8)


def forward_kernel(
    x_own, g_own, w_joined, w_down, x_out, g_out, pre_out, gated_out, y_out,
    x_all, g_all, columns, pre, gated, y, send_sem, recv_sem, local_sem, out_sem,
):
    me = here()
    core = lax.rem(me[1], 2)
    greet(
        [flipped(me, NEAR), flipped(me, FAR), sibling(me)] + [moved_z(me, d) for d in (1, 2, 3)]
    )
    plan, begin, event, from_sibling = gather_plan(
        [x_own, g_own], [x_all, g_all], [128, 16], send_sem, recv_sem
    )
    local = [
        pltpu.make_async_copy(x_own, rows_at(x_all, slot_of(me), 128), local_sem.at[0]),
        pltpu.make_async_copy(g_own, rows_at(g_all, slot_of(me), 16), local_sem.at[1]),
    ]
    begin()
    for copy in local:
        copy.start()
    for copy in local:
        copy.wait()
    before = {
        0: [(1, SELF), (0, NEAR), (0, FAR)],
        1: [(0, BOTH_FLIPPED)],
        3: [(1, BOTH_FLIPPED)],
        5: [(3, BOTH_FLIPPED)],
        7: [(2, BOTH_FLIPPED)],
    }
    middle = {
        0: [(3, SELF), (1, NEAR)],
        1: [(1, FAR)],
        2: [(2, SELF), (3, NEAR)],
        3: [(3, FAR)],
        4: [(2, NEAR)],
        5: [(2, FAR)],
    }
    half = w_joined.shape[1] // 2

    def results(expert, slot):
        return [
            pltpu.make_async_copy(
                rows_at(x_all, expert, BLOCK), rows_at(x_out, expert, BLOCK), out_sem.at[0, slot]
            ),
            pltpu.make_async_copy(pre.at[slot], rows_at(pre_out, expert, BLOCK), out_sem.at[1, slot]),
            pltpu.make_async_copy(
                gated.at[slot], rows_at(gated_out, expert, BLOCK), out_sem.at[2, slot]
            ),
            pltpu.make_async_copy(y.at[slot], rows_at(y_out, expert, BLOCK), out_sem.at[3, slot]),
        ]

    def block(j, carry):
        slot = lax.rem(j, 2)
        expert = stage_expert(me, j)
        for n, (k, flips) in enumerate(STAGES):

            @pl.when(j == n)
            def _():
                for at in before.get(n, []):
                    event(*at)
                if n:
                    from_sibling(k, 2 - core if flips else SELF)
                    from_sibling(k, BOTH_FLIPPED if flips else 1 + core)
                else:
                    from_sibling(k, SELF)
                    from_sibling(k, 1 + core)

        @pl.when(j >= 2)
        def _():
            for copy in results(stage_expert(me, j - 2), slot):
                copy.wait()

        gate_columns(g_all, expert * 4, columns, me[0] * 2)
        x_rows = rows_at(x_all, expert, BLOCK)

        def first(cols):
            pre[slot, :, cols] = jnp.dot(
                x_rows[...], w_joined[:, cols], preferred_element_type=jnp.float32
            )

        tiles(w_joined.shape[1] // 1024, 1024, first)
        for n in middle:

            @pl.when(j == n)
            def _():
                for at in middle[n]:
                    event(*at)

        def act(r):
            for c in range(half // 128):
                cols = slice(c * 128, (c + 1) * 128)
                g = pre[slot, r, cols]
                u = pre[slot, r, half + c * 128 : half + (c + 1) * 128]
                hidden = (g * (1.0 / (1.0 + jnp.exp(-g))) * u).astype(jnp.bfloat16)
                gate = columns[c * 128 * 2 // half, r, :]
                gated[slot, r, cols] = (hidden.astype(jnp.float32) * gate).astype(jnp.bfloat16)

        tiles(BLOCK // 64, 64, act)

        def second(cols):
            y[slot, :, cols] = jnp.dot(
                gated[slot], w_down[:, cols], preferred_element_type=jnp.float32
            ).astype(jnp.bfloat16)

        tiles(w_down.shape[1] // 1024, 1024, second)
        for copy in results(expert, slot):
            copy.start()
        return carry

    lax.fori_loop(0, 8, block, 0)
    for j in (6, 7):
        for copy in results(stage_expert(me, jnp.int32(j)), j % 2):
            copy.wait()
    g_out[...] = g_all[...]
    plan.finish()


def experts_forward(ffn_in, gates_own, w_joined, w_down):
    rows, width = ffn_in.shape[0] * 32, ffn_in.shape[1]
    joined, hidden = w_joined.shape[1], w_down.shape[0]
    bf16, f32, sds = jnp.bfloat16, jnp.float32, jax.ShapeDtypeStruct
    return pl.pallas_call(
        forward_kernel,
        out_shape=[
            sds((rows, width), bf16),
            sds((512, 128), f32),
            sds((rows, joined), f32),
            sds((rows, hidden), bf16),
            sds((rows, width), bf16),
        ],
        in_specs=[IN_VMEM] * 4,
        out_specs=[ANY, IN_VMEM, ANY, ANY, ANY],
        scratch_shapes=[
            pltpu.VMEM((rows, width), bf16),
            pltpu.VMEM((512, 128), f32),
            pltpu.VMEM((2, BLOCK, 128), f32),
            pltpu.VMEM((2, BLOCK, joined), f32),
            pltpu.VMEM((2, BLOCK, hidden), bf16),
            pltpu.VMEM((2, BLOCK, width), bf16),
            DMA((2, 32)),
            DMA((2, 32)),
            DMA((2,)),
            DMA((4, 2)),
        ],
        compiler_params=pltpu.CompilerParams(
            collective_id=1, has_side_effects=True, vmem_limit_bytes=48 * 2**20
        ),
        cost_estimate=cost_of(90),
        name="experts_forward",
    )(ffn_in, gates_own, w_joined, w_down)


def sum_plan(arrays, send_sem, recv_sem, load_sem):
    me = here()
    near, far, sib = flipped(me, NEAR), flipped(me, FAR), sibling(me)
    plan = Plan(send_sem, recv_sem)
    order = (2, 1, 3, 0)

    def send(i, source, target, tag, recv_tag, device):
        plan.send(
            lambda: push(source(), target(), send_sem.at[i, tag], recv_sem.at[i, recv_tag], device())
        )

    def arrive(i, ref, tag):
        push(ref, ref, send_sem.at[i, 0], recv_sem.at[i, tag], near).wait_recv()

    def load(i, k, role):
        part, _, size, mine = arrays[i][:4]
        tag = k * 4 + role
        return pltpu.make_async_copy(
            rows_at(part, slot_of(moved_z(flipped(me, role), k)), size), mine.at[tag], load_sem.at[i, tag]
        )

    def begin():
        for roles in ((BOTH_FLIPPED, FAR), (NEAR, SELF)):
            for k in order:
                for role in roles:
                    for i, (part, _, size, _, from_sib, _, _, _) in enumerate(arrays):
                        tag = k * 4 + role
                        send(
                            i,
                            lambda part=part, size=size, k=k, role=role: rows_at(
                                part, slot_of(moved_z(flipped(sib, role), k)), size
                            ),
                            lambda from_sib=from_sib, tag=tag: from_sib.at[tag],
                            tag,
                            tag,
                            lambda: sib,
                        )
                        load(i, k, role).start()

    def collect(i, k, role):
        tag = k * 4 + role
        load(i, k, role).wait()
        from_sib = arrays[i][4]
        arrive(i, from_sib.at[tag], tag)
        return [arrays[i][3].at[tag], from_sib.at[tag]]

    def first(k, role):
        for i, (_, _, _, mine, _, from_far, _, _) in enumerate(arrays):
            tag, at = k * 4 + role, k * 2 + (role == BOTH_FLIPPED)
            terms = collect(i, k, role)
            sum_rows(mine.at[tag], terms)
            send(
                i,
                lambda mine=mine, tag=tag: mine.at[tag],
                lambda from_far=from_far, at=at: from_far.at[at],
                16 + at,
                16 + at,
                lambda: far,
            )

    def second(k):
        for i, (_, _, _, mine, _, from_far, from_near, _) in enumerate(arrays):
            tag = k * 4 + NEAR
            terms = collect(i, k, NEAR)
            arrive(i, from_far.at[k * 2 + 1], 16 + k * 2 + 1)
            sum_rows(mine.at[tag], terms + [from_far.at[k * 2 + 1]])
            send(
                i,
                lambda mine=mine, tag=tag: mine.at[tag],
                lambda from_near=from_near, k=k: from_near.at[k],
                24 + k,
                24 + k,
                lambda: near,
            )

    def third(k):
        for i, (_, out, _, mine, _, from_far, from_near, from_z) in enumerate(arrays):
            tag = k * 4 + SELF
            terms = collect(i, k, SELF)
            arrive(i, from_far.at[k * 2], 16 + k * 2)
            arrive(i, from_near.at[k], 24 + k)
            terms = terms + [from_far.at[k * 2], from_near.at[k]]
            if k > 0:
                sum_rows(mine.at[tag], terms)
                send(
                    i,
                    lambda mine=mine, tag=tag: mine.at[tag],
                    lambda from_z=from_z, k=k: from_z.at[3 - k],
                    27 + k,
                    31 - k,
                    lambda k=k: moved_z(me, k),
                )
            else:
                for d in range(3):
                    arrive(i, from_z.at[d], 28 + d)
                    terms.append(from_z.at[d])
                sum_rows(out, terms)

    return plan, begin, first, second, third


def sum_scratch(size, width, dtype):
    return [pltpu.VMEM((n, size, width), dtype) for n in (16, 16, 8, 4, 3)]


SUM_BEFORE = {0: [(2, 3), (2, 2), (1, 3), (1, 2)], 3: [(2, "third")], 5: [(1, "third")]}
SUM_MIDDLE = {
    0: [(3, 3), (3, 2), (0, 3), (0, 2)],
    1: [(2, "second")],
    2: [(1, "second")],
    4: [(3, "second")],
    6: [(0, "second")],
}


def sum_events(table, j, first, second, third):
    for n, events in table.items():

        @pl.when(j == n)
        def _():
            for k, what in events:
                if what == "second":
                    second(k)
                elif what == "third":
                    third(k)
                else:
                    first(k, what)


def greet_all(me):
    greet(
        [flipped(me, NEAR), flipped(me, FAR), sibling(me)] + [moved_z(me, d) for d in (1, 2, 3)]
    )


def backward_kernel(
    y_part, grads, pre_all, gates, w_joined, w_down, mix_out, dpre_out, drow_out, gate_grads,
    mine, from_sib, from_far, from_near, from_z, dz, pre, raw, columns, products, dpre, drow,
    send_sem, recv_sem, load_sem, in_sem, out_sem,
):
    me = here()
    greet_all(me)
    plan, begin, first, second, third = sum_plan(
        [(y_part, mix_out, 128, mine, from_sib, from_far, from_near, from_z)],
        send_sem, recv_sem, load_sem,
    )
    half = w_joined.shape[1] // 2
    expert_lanes = half // 2

    def loads(block, slot):
        return [
            pltpu.make_async_copy(rows_at(grads, block, BLOCK), dz.at[slot], in_sem.at[0, slot]),
            pltpu.make_async_copy(rows_at(pre_all, block, BLOCK), pre.at[slot], in_sem.at[1, slot]),
        ]

    def results(block, slot):
        return [
            pltpu.make_async_copy(dpre.at[slot], rows_at(dpre_out, block, BLOCK), out_sem.at[0, slot]),
            pltpu.make_async_copy(drow.at[slot], rows_at(drow_out, block, BLOCK), out_sem.at[1, slot]),
        ]

    for copy in loads(0, 0):
        copy.start()
    begin()

    def step(j, carry):
        slot = lax.rem(j, 2)

        @pl.when(j < 7)
        def _():
            for copy in loads(j + 1, 1 - slot):
                copy.start()

        sum_events(SUM_BEFORE, j, first, second, third)
        for copy in loads(j, slot):
            copy.wait()

        @pl.when(j >= 2)
        def _():
            for copy in results(j - 2, slot):
                copy.wait()

        gate_columns(gates, j * 4, columns, me[0] * 2)
        raw[...] = lax.dot_general(
            dz[slot], w_down[...], (((1,), (1,)), ((), ())), preferred_element_type=jnp.float32
        )
        sum_events(SUM_MIDDLE, j, first, second, third)

        def act(r):
            for i in range(2):
                product = None
                for c in range(i * expert_lanes, (i + 1) * expert_lanes, 128):
                    g = pre[slot, r, c : c + 128]
                    u = pre[slot, r, half + c : half + c + 128]
                    t = raw[r, c : c + 128]
                    sig = 1.0 / (1.0 + jnp.exp(-g))
                    silu = g * sig
                    hidden = (silu * u).astype(jnp.bfloat16).astype(jnp.float32)
                    term = hidden * t
                    product = term if product is None else product + term
                    dh = t * columns[i, r, :]
                    dpre[slot, r, c : c + 128] = (
                        dh * u * sig * (1.0 + g * (1.0 - sig))
                    ).astype(jnp.bfloat16)
                    dpre[slot, r, half + c : half + c + 128] = (dh * silu).astype(jnp.bfloat16)
                products[i, r, :] = product

        tiles(BLOCK // 64, 64, act)
        place = lax.broadcasted_iota(jnp.int32, (16, 128), 0)
        for s in range(4):
            sums = jnp.zeros((16, 128), jnp.float32)
            for i in range(2):
                turned = products[i, pl.ds(s * 128, 128), :].T
                row = jnp.sum(turned, axis=0, keepdims=True)
                sums = jnp.where(place == me[0] * 2 + i, jnp.broadcast_to(row, (16, 128)), sums)
            gate_grads[pl.ds(pl.multiple_of((j * 4 + s) * 16, 16), 16), :] = sums

        def back(rows):
            drow[slot, :, rows] = lax.dot_general(
                dpre[slot],
                w_joined[rows, :],
                (((1,), (1,)), ((), ())),
                preferred_element_type=jnp.float32,
            ).astype(jnp.bfloat16)

        tiles(w_joined.shape[0] // 1024, 1024, back)
        for copy in results(j, slot):
            copy.start()
        return carry

    lax.fori_loop(0, 8, step, 0)
    third(3)
    third(0)
    for j in (6, 7):
        for copy in results(j, j % 2):
            copy.wait()
    plan.finish()


def experts_backward(y_part, grads, pre, gates, w_joined, w_down):
    rows, width = grads.shape
    joined, hidden = w_joined.shape[1], w_down.shape[0]
    bf16, f32, sds = jnp.bfloat16, jnp.float32, jax.ShapeDtypeStruct
    return pl.pallas_call(
        backward_kernel,
        out_shape=[
            sds((rows // 32, width), f32),
            sds((rows, joined), bf16),
            sds((rows, width), bf16),
            sds((512, 128), f32),
        ],
        in_specs=[ANY, ANY, ANY] + [IN_VMEM] * 3,
        out_specs=[IN_VMEM, ANY, ANY, IN_VMEM],
        scratch_shapes=sum_scratch(rows // 32, width, bf16)
        + [
            pltpu.VMEM((2, BLOCK, width), bf16),
            pltpu.VMEM((2, BLOCK, joined), f32),
            pltpu.VMEM((BLOCK, hidden), f32),
            pltpu.VMEM((2, BLOCK, 128), f32),
            pltpu.VMEM((2, BLOCK, 128), f32),
            pltpu.VMEM((2, BLOCK, joined), bf16),
            pltpu.VMEM((2, BLOCK, width), bf16),
            DMA((1, 32)),
            DMA((1, 32)),
            DMA((1, 16)),
            DMA((2, 2)),
            DMA((2, 2)),
        ],
        compiler_params=pltpu.CompilerParams(
            collective_id=2, has_side_effects=True, vmem_limit_bytes=56 * 2**20
        ),
        cost_estimate=cost_of(90),
        name="experts_backward",
    )(y_part, grads, pre, gates, w_joined, w_down)


def weights_kernel(
    drow, gate_grads, x_all, grads, dpre_all, gated_all, row_out, gate_out, d_gate, d_up, d_down,
    mine, from_sib, from_far, from_near, from_z, mine_g, sib_g, far_g, near_g, z_g,
    dpre, gated, tile, wide, send_sem, recv_sem, load_sem, in_sem, tile_sem, out_sem,
):
    me = here()
    greet_all(me)
    plan, begin, first, second, third = sum_plan(
        [
            (drow, row_out, 128, mine, from_sib, from_far, from_near, from_z),
            (gate_grads, gate_out, 16, mine_g, sib_g, far_g, near_g, z_g),
        ],
        send_sem, recv_sem, load_sem,
    )
    span = tile.shape[2]
    steps = x_all.shape[1] // span
    hidden = d_gate.shape[2]
    begin()
    held = [
        pltpu.make_async_copy(dpre_all, dpre, in_sem.at[0]),
        pltpu.make_async_copy(gated_all, gated, in_sem.at[1]),
    ]

    def columns_of(j):
        return pl.ds(pl.multiple_of(lax.rem(j, steps) * span, span), span)

    def fetch(j, slot, act):
        @pl.when(j < steps)
        def _():
            act(pltpu.make_async_copy(x_all.at[:, columns_of(j)], tile.at[slot], tile_sem.at[slot]))

        @pl.when((j >= steps) & (j < 2 * steps))
        def _():
            act(pltpu.make_async_copy(grads.at[:, columns_of(j)], tile.at[slot], tile_sem.at[slot]))

    def results(j, slot, act):
        cols = columns_of(j)

        @pl.when(j < steps)
        def _():
            for i in range(2):
                act(
                    pltpu.make_async_copy(
                        wide.at[slot, :, pl.ds(i * hidden, hidden)], d_gate.at[i, cols, :], out_sem.at[slot, i]
                    )
                )
                act(
                    pltpu.make_async_copy(
                        wide.at[slot, :, pl.ds((2 + i) * hidden, hidden)],
                        d_up.at[i, cols, :],
                        out_sem.at[slot, 2 + i],
                    )
                )

        @pl.when(j >= steps)
        def _():
            act(
                pltpu.make_async_copy(
                    wide.at[slot, :, pl.ds(0, span)], d_down.at[:, cols], out_sem.at[slot, 0]
                )
            )

    fetch(jnp.int32(0), 0, lambda copy: copy.start())
    for copy in held:
        copy.start()

    def step(j, carry):
        slot = lax.rem(j, 2)
        fetch(j + 1, 1 - slot, lambda copy: copy.start())
        sum_events(SUM_BEFORE, j, first, second, third)

        @pl.when(j == 0)
        def _():
            for copy in held:
                copy.wait()

        fetch(j, slot, lambda copy: copy.wait())

        @pl.when(j >= 2)
        def _():
            results(j - 2, slot, lambda copy: copy.wait())

        @pl.when(j < steps)
        def _():
            wide[slot] = lax.dot_general(
                tile[slot], dpre[...], (((0,), (0,)), ((), ())), preferred_element_type=jnp.float32
            )

        @pl.when(j >= steps)
        def _():
            wide[slot, :, 0:span] = lax.dot_general(
                gated[...], tile[slot], (((0,), (0,)), ((), ())), preferred_element_type=jnp.float32
            )

        results(j, slot, lambda copy: copy.start())
        sum_events(SUM_MIDDLE, j, first, second, third)
        return carry

    lax.fori_loop(0, 2 * steps, step, 0)
    third(3)
    third(0)
    for j in (2 * steps - 2, 2 * steps - 1):
        results(jnp.int32(j), j % 2, lambda copy: copy.wait())
    plan.finish()


def experts_weights(drow, gate_grads, x_all, grads, dpre, gated):
    rows, width = grads.shape
    joined, hidden = dpre.shape[1], gated.shape[1]
    span = width // 4
    bf16, f32, sds = jnp.bfloat16, jnp.float32, jax.ShapeDtypeStruct
    return pl.pallas_call(
        weights_kernel,
        out_shape=[
            sds((rows // 32, width), f32),
            sds((16, 128), f32),
            sds((2, width, joined // 4), f32),
            sds((2, width, joined // 4), f32),
            sds((hidden, width), f32),
        ],
        in_specs=[ANY] * 6,
        out_specs=[IN_VMEM, IN_VMEM, ANY, ANY, ANY],
        scratch_shapes=sum_scratch(rows // 32, width, bf16)
        + sum_scratch(16, 128, f32)
        + [
            pltpu.VMEM((rows, joined), bf16),
            pltpu.VMEM((rows, hidden), bf16),
            pltpu.VMEM((2, rows, span), bf16),
            pltpu.VMEM((2, span, joined), f32),
            DMA((2, 32)),
            DMA((2, 32)),
            DMA((2, 16)),
            DMA((2,)),
            DMA((2,)),
            DMA((2, 4)),
        ],
        compiler_params=pltpu.CompilerParams(
            collective_id=3, has_side_effects=True, vmem_limit_bytes=58 * 2**20
        ),
        cost_estimate=cost_of(90),
        name="experts_weights",
    )(drow, gate_grads, x_all, grads, dpre, gated)


def rotated(values, cosines, sines):
    return values * cosines + pltpu.roll(values, HEAD_DIM // 2, 1) * sines


def turned_back(values, cosines, sines):
    return values * cosines - pltpu.roll(values, HEAD_DIM // 2, 1) * sines


def mask_scores(spans_col, places_row, bias):
    place = places_row[0:1, :]

    def body(r):
        allowed = (place >= spans_col[r, 0:1]) & (place <= spans_col[r, 1:2])
        bias[r, :] = jnp.where(allowed, 0.0, -1e30)

    tiles(bias.shape[0] // 128, 128, body)


def attend_kernel(
    qkv, invs, gains, cosines, sines, spans, places, w_out,
    q_out, k_out, v_out, attended, lse, branch_own, bias,
    part, from_sib, from_side, total, send_sem, recv_sem,
):
    me = here()
    greet([across_y(me), sibling(me)])
    rows, local = q_out.shape
    mask_scores(spans, places, bias)

    def prepare(r):
        v_out[r, :] = qkv[r, 2 * local : 3 * local].astype(jnp.bfloat16)
        for h in range(local // HEAD_DIM):
            c = slice(h * HEAD_DIM, (h + 1) * HEAD_DIM)
            for i, target in ((0, q_out), (1, k_out)):
                normed = qkv[r, i * local + h * HEAD_DIM : i * local + (h + 1) * HEAD_DIM]
                normed = normed * invs[r, i : i + 1] * gains[i : i + 1, c]
                target[r, c] = rotated(normed, cosines[r, :], sines[r, :]).astype(jnp.bfloat16)

    tiles(rows // 128, 128, prepare)
    scale = 1.0 / math.sqrt(HEAD_DIM)
    for h in range(local // HEAD_DIM):
        c = slice(h * HEAD_DIM, (h + 1) * HEAD_DIM)

        def one(r, h=h, c=c):
            scores = dot32(q_out[r, c], k_out[:, c], NT) * scale + bias[r, :]
            top = jnp.max(scores, axis=-1, keepdims=True)
            log_total = top + jnp.log(jnp.sum(jnp.exp(scores - top), axis=-1, keepdims=True))
            lse[h, r, :] = log_total
            probs = jnp.exp(scores - log_total).astype(jnp.bfloat16)
            attended[r, c] = dot32(probs, v_out[:, c], NN).astype(jnp.bfloat16)

        tiles(rows // 128, 128, one)

    def make(column):
        own = branch_own.shape[0]
        places_of = pl.ds(pl.multiple_of(column * own, own), own)
        span = w_out.shape[2]
        for e in range(w_out.shape[0]):
            part[column, :, e * span : (e + 1) * span] = dot32(
                attended[places_of, :], w_out[e], NN
            ).astype(jnp.bfloat16)

    sum_tensor_into(make, part, branch_own, from_sib, from_side, total, Line(send_sem, recv_sem))


def attend(qkv, invs, gains, cosines, sines, spans, places, w_out):
    rows, local = qkv.shape[0], qkv.shape[1] // 3
    block = (rows // 4, w_out.shape[0] * w_out.shape[2])
    bf16, f32, sds = jnp.bfloat16, jnp.float32, jax.ShapeDtypeStruct
    return pl.pallas_call(
        attend_kernel,
        out_shape=[sds((rows, local), bf16)] * 4
        + [
            sds((local // HEAD_DIM, rows, 1), f32),
            sds(block, f32),
        ],
        in_specs=[IN_VMEM] * 8,
        out_specs=[IN_VMEM] * 6,
        scratch_shapes=[pltpu.VMEM((rows, rows), f32)] + sum_tensor_scratch(block),
        compiler_params=pltpu.CompilerParams(
            collective_id=9, has_side_effects=True, vmem_limit_bytes=24 * 2**20
        ),
        cost_estimate=cost_of(15),
        name="attend",
    )(qkv, invs, gains, cosines, sines, spans, places, w_out)


def attend_back_kernel(
    grad, w_out_far, q_far, k_far, v_far, lse, qkv_far, invs, gains, cosines, sines, spans, places,
    hat_grads, value_grad, dots, d_gains, bias, out_grad, probs_low, score_grad,
    w_out, q, k, v, qkv, sems,
):
    rows, local = q.shape
    fetched = [
        pltpu.make_async_copy(far, close, sems.at[i])
        for i, (far, close) in enumerate(
            ((w_out_far, w_out), (q_far, q), (k_far, k), (v_far, v), (qkv_far, qkv))
        )
    ]
    for copy in fetched:
        copy.start()
    mask_scores(spans, places, bias)
    span = w_out.shape[2]
    fetched[0].wait()

    def project(r):
        total = None
        for e in range(w_out.shape[0]):
            term = dot32(grad[r, e * span : (e + 1) * span], w_out[e], NT)
            total = term if total is None else total + term
        out_grad[r, :] = total.astype(jnp.bfloat16)

    tiles(rows // 128, 128, project)
    for copy in fetched[1:]:
        copy.wait()
    scale = 1.0 / math.sqrt(HEAD_DIM)
    dots[...] = jnp.zeros_like(dots)
    for h in range(local // HEAD_DIM):
        c = slice(h * HEAD_DIM, (h + 1) * HEAD_DIM)

        def one(r, h=h, c=c):
            scores = dot32(q[r, c], k[:, c], NT) * scale + bias[r, :]
            probs = jnp.exp(scores - lse[h, r, :])
            prob_grad = dot32(out_grad[r, c], v[:, c], NT)
            delta = jnp.sum(probs * prob_grad, axis=-1, keepdims=True)
            probs_low[r, :] = probs.astype(jnp.bfloat16)
            score_grad[r, :] = (probs * (prob_grad - delta) * scale).astype(jnp.bfloat16)

        tiles(rows // 128, 128, one)
        value_grad[:, c] = dot32(probs_low[...], out_grad[:, c], TN).astype(jnp.bfloat16)
        for i, turned in (
            (0, dot32(score_grad[...], k[:, c], NN)),
            (1, dot32(score_grad[...], q[:, c], TN)),
        ):
            at = slice(i * local + h * HEAD_DIM, i * local + (h + 1) * HEAD_DIM)
            norm_grad = turned_back(turned, cosines[...], sines[...])
            hat = qkv[:, at] * invs[:, i : i + 1]
            hat_grad = norm_grad * gains[i : i + 1, c]
            hat_grads[:, at] = hat_grad
            d_gains[i : i + 1, c] = jnp.sum(norm_grad * hat, axis=0, keepdims=True)
            dots[i] += jnp.sum(hat_grad * hat, axis=-1, keepdims=True)


def attend_back(grad, w_out, q, k, v, lse, qkv, invs, gains, cosines, sines, spans, places):
    rows, local = q.shape
    bf16, f32, sds = jnp.bfloat16, jnp.float32, jax.ShapeDtypeStruct
    return pl.pallas_call(
        attend_back_kernel,
        out_shape=[
            sds((rows, 2 * local), f32),
            sds((rows, local), bf16),
            sds((2, rows, 1), f32),
            sds((2, local), f32),
        ],
        in_specs=[IN_VMEM] + [ANY] * 4 + [IN_VMEM, ANY] + [IN_VMEM] * 6,
        out_specs=[IN_VMEM] * 4,
        scratch_shapes=[
            pltpu.VMEM((rows, rows), f32),
            pltpu.VMEM((rows, local), bf16),
            pltpu.VMEM((rows, rows), bf16),
            pltpu.VMEM((rows, rows), bf16),
        ]
        + [pltpu.VMEM(a.shape, a.dtype) for a in (w_out, q, k, v, qkv)]
        + [DMA((5,))],
        compiler_params=pltpu.CompilerParams(vmem_limit_bytes=62 * 2**20),
        cost_estimate=cost_of(5),
        name="attend_back",
    )(grad, w_out, q, k, v, lse, qkv, invs, gains, cosines, sines, spans, places)


def sum_few_kernel(part, out, shares, send_sem, recv_sem):
    me = here()
    peers = [across_y(sibling(me)), across_y(me), sibling(me)]
    greet(peers)
    line = Line(send_sem, recv_sem)
    for i, peer in enumerate(peers):
        line.send(part, shares.at[me[1]], i, i, peer)
    shares[me[1]] = part[...]
    for i, peer in enumerate(peers):
        line.wait(shares.at[peer[1]], i, peer)
    out[...] = (shares[0] + shares[1]) + (shares[2] + shares[3])
    line.finish()


def sum_few(rows):
    block = (rows.size // 128, 128)
    return pl.pallas_call(
        sum_few_kernel,
        out_shape=jax.ShapeDtypeStruct(block, jnp.float32),
        in_specs=[IN_VMEM],
        out_specs=IN_VMEM,
        scratch_shapes=[pltpu.VMEM((4,) + block, jnp.float32), DMA((3,)), DMA((3,))],
        compiler_params=pltpu.CompilerParams(
            collective_id=8, has_side_effects=True, vmem_limit_bytes=2**20
        ),
        cost_estimate=cost_of(1),
        name="sum_few",
    )(rows.reshape(block)).reshape(rows.shape)


BOTH = (EXPERT, TENSOR)


def dot32(left, right, dims):
    return lax.dot_general(left, right, (dims, ((), ())), preferred_element_type=jnp.float32)


NN = ((1,), (0,))
NT = ((1,), (1,))
TN = ((0,), (0,))


def rms_inv(values):
    return lax.rsqrt(jnp.mean(values * values, axis=-1, keepdims=True) + NORM_EPS)


def dense_body(
    tokens,
    attn_gain,
    w_query,
    w_key,
    w_value,
    w_out,
    query_gain,
    key_gain,
    ffn_gain,
    w_router,
    w_gate,
    w_up,
    w_down,
    doc_ids,
    routes,
    deal,
    out_grad,
):
    rows, width = tokens.shape
    parts = lax.axis_size(TENSOR)
    blocks = lax.axis_size(EXPERT)
    column = lax.axis_index(TENSOR)
    block = lax.axis_index(EXPERT)
    own = rows // parts
    share = rows // blocks
    piece = share // parts
    bf16, f32 = jnp.bfloat16, jnp.float32

    def reorder(per_place):
        grid = per_place.reshape((blocks, parts, piece) + per_place.shape[1:])
        return jnp.swapaxes(grid, 0, 1).reshape(per_place.shape)

    local_width = w_query.shape[1]
    head_count = local_width // HEAD_DIM
    expert_count = w_router.shape[1]
    qkv_own = jnp.concatenate([w_query, w_key, w_value], axis=1)
    gain_stack = jnp.stack([attn_gain, query_gain, key_gain, ffn_gain], axis=1)
    small_own = jnp.concatenate([w_router, gain_stack], axis=1)
    small_own = jnp.pad(small_own, ((0, 0), (0, 128 - small_own.shape[1])))
    deal_grid = deal.reshape(blocks, blocks, parts, piece)
    picks = lax.dynamic_slice(deal_grid, (0, block, column, 0), (blocks, 1, 1, piece)).reshape(-1)
    picks = picks - block * rows
    inputs, dealt_grads, qkv_full, out_full, small_full = start_exchange(
        tokens[picks].reshape(blocks, piece, width),
        out_grad[picks].reshape(blocks, piece, width),
        qkv_own,
        w_out,
        small_own,
    )
    own_low = lax.dynamic_slice_in_dim(inputs, column, 1, 0).reshape(own, width)
    inputs = inputs.reshape(rows, width).astype(f32)
    qkv_full = qkv_full.reshape(width, -1)
    small_full = small_full.reshape(width, -1)
    router_full = small_full[:, :expert_count]
    gain_full = small_full[:, expert_count : expert_count + 4].T.astype(f32)
    gain_attn, gain_ffn = gain_full[0], gain_full[3]
    gain_query = lax.dynamic_slice_in_dim(gain_full[1], column * local_width, local_width)
    gain_key = lax.dynamic_slice_in_dim(gain_full[2], column * local_width, local_width)
    own_grad_low = dealt_grads.reshape(own, width)
    grads_all = lax.all_gather(own_grad_low, BOTH, axis=0, tiled=True)
    own_in = own_low.astype(f32)
    own_grad = own_grad_low.astype(f32)

    scale = 1.0 / math.sqrt(HEAD_DIM)
    normed = (inputs * rms_inv(inputs) * gain_attn).astype(bf16)
    qkv = dot32(normed, qkv_full, NN)
    query_pre = qkv[:, :local_width]
    key_pre = qkv[:, local_width : 2 * local_width]
    squares = sum_few(
        jnp.stack([jnp.sum(query_pre * query_pre, axis=-1), jnp.sum(key_pre * key_pre, axis=-1)])
    )
    cosines, sines, starts = rope_tables(doc_ids, HEAD_DIM)
    cosines = reorder(jnp.concatenate([cosines, cosines], axis=1))
    sines = reorder(jnp.concatenate([-sines, sines], axis=1))
    positions = reorder(jnp.arange(rows, dtype=jnp.int32))
    spans = jnp.stack([reorder(starts), positions], axis=1)
    places = jnp.broadcast_to(positions[None], (8, rows))
    invs = lax.rsqrt(squares / width + NORM_EPS).T
    gains = jnp.stack([gain_query, gain_key])
    query_rot, key_rot, value_rows, attended, log_total, branch_own = attend(
        qkv, invs, gains, cosines, sines, spans, places, out_full
    )

    residual = own_in + branch_own
    resid_inv = rms_inv(residual)
    resid_hat = residual * resid_inv
    ffn_in = (resid_hat * gain_ffn).astype(bf16)
    logits = dot32(ffn_in, router_full, NN)
    router_probs = jax.nn.softmax(logits, axis=-1)
    local_experts = w_gate.shape[0]
    own_routes = lax.dynamic_slice(
        routes.reshape(blocks, parts, piece, -1),
        (0, column, 0, 0),
        (blocks, 1, piece, routes.shape[1]),
    ).reshape(own, -1)
    expert_ids = jnp.arange(expert_count, dtype=jnp.int32)
    routed = jnp.any(own_routes[:, :, None] == expert_ids[None, None, :], axis=1)
    gates_own = jnp.where(routed, router_probs, 0.0)

    hidden_width = w_gate.shape[2]
    joined_weight = jnp.concatenate(
        [w_gate[i] for i in range(local_experts)] + [w_up[i] for i in range(local_experts)], axis=1
    )
    down_weight = w_down.reshape(local_experts * hidden_width, width)
    rows_all, gates_all, pre_all, gated_all, mixed = experts_forward(
        ffn_in, gates_own.T, joined_weight, down_weight
    )
    mix_own, joined_grad, row_terms, gate_grads = experts_backward(
        mixed, grads_all, pre_all, gates_all, joined_weight, down_weight
    )
    output_own = (residual + mix_own).astype(bf16)
    row_own, gate_grad_own, d_w_gate, d_w_up, d_w_down = experts_weights(
        row_terms, gate_grads, rows_all, grads_all, joined_grad, gated_all
    )
    gate_grad_own = gate_grad_own.T
    d_w_down = d_w_down.reshape(w_down.shape)

    prob_grad = jnp.where(routed, gate_grad_own, 0.0)
    logit_grad = (
        router_probs * (prob_grad - jnp.sum(router_probs * prob_grad, axis=-1, keepdims=True))
    ).astype(bf16)
    d_router = dot32(ffn_in, logit_grad, TN)
    ffn_grad = row_own + dot32(logit_grad, router_full, NT)
    d_ffn_gain = jnp.sum(ffn_grad * resid_hat, axis=0)
    scaled_ffn = ffn_grad * gain_ffn
    resid_grad = own_grad + resid_inv * (
        scaled_ffn - resid_hat * jnp.mean(scaled_ffn * resid_hat, axis=-1, keepdims=True)
    )
    branch_grad = gather_tensor(resid_grad.astype(bf16))

    branch_cols = branch_grad.reshape(rows, blocks, width // blocks)
    d_wo = jnp.einsum("rk,red->ekd", attended, branch_cols, preferred_element_type=f32).astype(bf16)
    d_wo, branch_grad = lax.optimization_barrier((d_wo, branch_grad))
    sum_wo = lax.psum_scatter(d_wo, EXPERT, scatter_dimension=0, tiled=False)
    hat_grads, value_grad, dots, d_gains = attend_back(
        branch_grad, out_full, query_rot, key_rot, value_rows, log_total,
        qkv, invs, gains, cosines, sines, spans, places,
    )
    d_query_gain, d_key_gain = d_gains[0], d_gains[1]
    dots = sum_few(dots.reshape(2, rows)) / width

    def norm_back(i):
        part = slice(i * local_width, (i + 1) * local_width)
        inv = invs[:, i : i + 1]
        return (inv * (hat_grads[:, part] - qkv[:, part] * inv * dots[i][:, None])).astype(bf16)

    query_grad, key_grad = norm_back(0), norm_back(1)
    qkv_grad = jnp.concatenate([query_grad, key_grad, value_grad], axis=1)
    normed_grad = input_sum(qkv_grad, qkv_full)
    d_qkv = dot32(normed, qkv_grad, TN).astype(bf16)
    d_qkv, sum_wo = lax.optimization_barrier((d_qkv, sum_wo))

    own_inv = rms_inv(own_in)
    own_hat = own_in * own_inv
    d_attn_gain = jnp.sum(normed_grad * own_hat, axis=0)
    scaled_attn = normed_grad * gain_attn
    input_grad = resid_grad + own_inv * (
        scaled_attn - own_hat * jnp.mean(scaled_attn * own_hat, axis=-1, keepdims=True)
    )

    def widen(slots):
        return lax.dynamic_update_slice_in_dim(
            jnp.zeros((width,), f32), slots, column * local_width, 0
        )

    small = jnp.concatenate(
        [
            d_router.T,
            jnp.stack([d_attn_gain, widen(d_query_gain), widen(d_key_gain), d_ffn_gain]),
        ]
    )
    small = jnp.pad(small, ((0, 24 - small.shape[0]), (0, 0)))
    small = jnp.swapaxes(small.reshape(24, blocks, -1), 0, 1)

    back_out, back_in, sum_qkv, small = last_exchange(
        output_own.reshape(blocks, piece, width),
        input_grad.astype(bf16).reshape(blocks, piece, width),
        d_qkv.reshape(blocks, -1, d_qkv.shape[1]),
        small,
    )
    sum_router = small[:expert_count].T
    sum_gains = small[expert_count:]
    came = lax.dynamic_slice(deal_grid, (0, block, 0, 0), (blocks, 1, parts, piece))
    came = jnp.swapaxes(came.reshape(blocks, parts, piece), 0, 1).reshape(-1) - block * rows
    chooser = (jnp.arange(rows, dtype=jnp.int32)[:, None] == came[None, :]).astype(bf16)
    output = dot32(chooser, back_out.reshape(rows, width), NN).astype(bf16)
    d_tokens = dot32(chooser, back_in.reshape(rows, width), NN).astype(bf16)
    return (
        output,
        d_tokens,
        sum_gains[0],
        sum_qkv[:, :local_width],
        sum_qkv[:, local_width : 2 * local_width],
        sum_qkv[:, 2 * local_width :],
        sum_wo.astype(f32),
        sum_gains[1],
        sum_gains[2],
        sum_gains[3],
        sum_router,
        d_w_gate,
        d_w_up,
        d_w_down,
    )


def pick_body(*args):
    routes, experts = args[14], args[9].shape[1]
    mesh_fits = (lax.axis_size(EXPERT), lax.axis_size(TENSOR)) == (8, 4)
    body = dense_body if mesh_fits and experts <= 2 * routes.shape[1] else routed_body
    return body(*args)


def solution(mesh):
    in_specs = (
        P(EXPERT, None),
        P(EXPERT),
        P(EXPERT, TENSOR),
        P(EXPERT, TENSOR),
        P(EXPERT, TENSOR),
        P(TENSOR, EXPERT),
        P(EXPERT),
        P(EXPERT),
        P(EXPERT),
        P(EXPERT, None),
        P(EXPERT, None, TENSOR),
        P(EXPERT, None, TENSOR),
        P(EXPERT, TENSOR, None),
        P(EXPERT),
        P(EXPERT, None),
        P(),
        P(EXPERT, None),
    )
    out_specs = (
        P(EXPERT, None),
        P(EXPERT, None),
        P(EXPERT),
        P(EXPERT, TENSOR),
        P(EXPERT, TENSOR),
        P(EXPERT, TENSOR),
        P(TENSOR, EXPERT),
        P(EXPERT),
        P(EXPERT),
        P(EXPERT),
        P(EXPERT, None),
        P(EXPERT, None, TENSOR),
        P(EXPERT, None, TENSOR),
        P(EXPERT, TENSOR, None),
    )
    return jax.shard_map(pick_body, mesh=mesh, in_specs=in_specs, out_specs=out_specs, check_vma=False)
```
